32 devices in a mesh: dp: 2 (over y), ctx: 4 (over z), tp: 4 (over x, core).
Axes of the slice: x: 2, y: 2, z: 4, core: 2. Of those that a mesh axis runs over, the one named last changes fastest.
Arguments:
- tokens: bfloat16 [16, 1024, 768], P('dp', 'ctx'), may hold values from -6 to 6
- out_grad: bfloat16 [16, 1024, 768], P('dp', 'ctx'), may hold values from -6 to 6
- query_weight: bfloat16 [768, 768], P(('dp', 'ctx'), 'tp'), may hold values from -0.21875 to 0.21875
- key_weight: bfloat16 [768, 768], P(('dp', 'ctx'), 'tp'), may hold values from -0.21875 to 0.21875
- value_weight: bfloat16 [768, 768], P(('dp', 'ctx'), 'tp'), may hold values from -0.21875 to 0.21875
- output_weight: bfloat16 [768, 768], P(('dp', 'ctx'), 'tp'), may hold values from -4 to 4
- up_weight: bfloat16 [768, 3072], P(('dp', 'ctx'), 'tp'), may hold values from -0.21875 to 0.21875
- down_weight: bfloat16 [768, 3072], P(('dp', 'ctx'), 'tp'), may hold values from -0.109375 to 0.109375
- norm1_gain: bfloat16 [768], P(('dp', 'ctx')), may hold values from 0.5 to 1.5
- norm1_bias: bfloat16 [768], P(('dp', 'ctx')), may hold values from -4 to 4
- output_bias: bfloat16 [768], P(('dp', 'ctx')), may hold values from -4 to 4
- norm2_gain: bfloat16 [768], P(('dp', 'ctx')), may hold values from 0.5 to 1.5
- norm2_bias: bfloat16 [768], P(('dp', 'ctx')), may hold values from -4 to 4
- down_bias: bfloat16 [768], P(('dp', 'ctx')), may hold values from -4 to 4
- query_bias: bfloat16 [768], P('tp'), may hold values from -1.5 to 1.5
- value_bias: bfloat16 [768], P('tp'), may hold values from -0.75 to 0.75
- up_bias: bfloat16 [3072], P('tp'), may hold values from -6 to 6
Outputs:
- layer_out: bfloat16 [16, 1024, 768], P('dp', 'ctx')
- tokens_grad: float32 [16, 1024, 768], P('dp', 'ctx')
- query_weight_grad: float32 [768, 768], P(('dp', 'ctx'), 'tp')
- key_weight_grad: float32 [768, 768], P(('dp', 'ctx'), 'tp')
- value_weight_grad: float32 [768, 768], P(('dp', 'ctx'), 'tp')
- output_weight_grad: float32 [768, 768], P(('dp', 'ctx'), 'tp')
- up_weight_grad: float32 [768, 3072], P(('dp', 'ctx'), 'tp')
- down_weight_grad: float32 [768, 3072], P(('dp', 'ctx'), 'tp')
- norm1_gain_grad: float32 [768], P(('dp', 'ctx'))
- norm1_bias_grad: float32 [768], P(('dp', 'ctx'))
- output_bias_grad: float32 [768], P(('dp', 'ctx'))
- norm2_gain_grad: float32 [768], P(('dp', 'ctx'))
- norm2_bias_grad: float32 [768], P(('dp', 'ctx'))
- down_bias_grad: float32 [768], P(('dp', 'ctx'))
- query_bias_grad: float32 [768], P('tp')
- value_bias_grad: float32 [768], P('tp')
- up_bias_grad: float32 [3072], P('tp')
The draws below stay inside these ranges and needn't reach their ends.
All inputs are finite; a program needn't handle non-finite values.
Results may differ from the reference program's by a relative error of at most 0.011.
Values may be sent and summed in bfloat16 or wider, within the bound.
A program may use at most 192 MiB of HBM per device.

```python
import jax
import jax.numpy as jnp
from jax import lax

D = 768
HEADS = 12
HEAD_DIM = 64
FF = 3072
BLOCK = 256
HHD = 768
SEQS = 16
LEN = 1024


def strengthened(drawn, stream_key, source, target, shards_of, factor):
    owner, partner = [(jnp.arange(drawn.shape[position]) // (drawn.shape[position] // shards_of)).reshape([-1 if axis == position else 1 for axis in range(drawn.ndim)]) for position in (source, target)]
    chosen = jax.random.permutation(stream_key, shards_of)[partner]
    strong = (owner == chosen) | (owner == (partner + shards_of // 2) % shards_of)
    return jnp.where(strong, factor * drawn, drawn)


def level_of(own_key, extent, cuts, smallest, high):
    loudness, own = 1.0, jax.random.fold_in(own_key, 6)
    for axis_at, shards_of in cuts:
        steps = jnp.exp(jax.random.uniform(jax.random.fold_in(own, axis_at), (shards_of,), jnp.float32, smallest / len(cuts), high / len(cuts)))
        loudness = loudness * jnp.repeat(steps, extent[axis_at] // shards_of).reshape([-1 if axis == axis_at else 1 for axis in range(len(extent))])
    return loudness


def normal_values(own_key, extent, spread, most, cuts=(), held_as=jnp.bfloat16):
    drawn = jax.random.normal(own_key, extent, jnp.float32) * spread
    if len(cuts) > 0:
        drawn = level_of(own_key, extent, cuts, -0.22, 0.18) * drawn
    return jnp.clip(drawn, min=-most, max=most).astype(held_as)


def heavy_noise(rng, extent, spread, reach, split, heavy, held_as=jnp.bfloat16):
    entries = spread * jax.random.normal(rng, extent, jnp.float32)
    if split:
        entries = entries * level_of(rng, extent, split, -0.22, 0.18)
    return jnp.clip(strengthened(entries, jax.random.fold_in(rng, 3), *heavy), -reach, reach).astype(held_as)


def setup_inputs(seed: int = 0) -> dict:
    streams_of = jax.random.split(jax.random.key(seed), 18)
    tokens = normal_values(streams_of[0], (SEQS, LEN, D), 1.0, 6.0, ((0, 2), (1, 4)))
    out_grad = heavy_noise(streams_of[1], (SEQS, LEN, D), 1.0, 6.0, ((0, 2), (1, 4)), (0, 2, 2, 2.0))
    query_weight = normal_values(streams_of[2], (D, HHD), D ** -0.5, 0.21875, ((0, 8), (1, 4)))
    key_weight = normal_values(streams_of[3], (D, HHD), D ** -0.5, 0.21875, ((0, 8), (1, 4)))
    value_weight = normal_values(streams_of[4], (D, HHD), D ** -0.5, 0.21875, ((0, 8), (1, 4)))
    output_weight = normal_values(streams_of[5], (D, HHD), 2 ** -0.5, 4.0, ((0, 8), (1, 4)))
    up_weight = normal_values(streams_of[6], (D, FF), D ** -0.5, 0.21875, ((0, 8), (1, 4)))
    down_weight = normal_values(streams_of[7], (D, FF), FF ** -0.5, 0.109375, ((0, 8), (1, 4)))
    norm1_gain = jnp.clip(1.0 + 0.1 * jax.random.normal(streams_of[8], (D,), jnp.float32), 0.5, 1.5).astype(jnp.bfloat16)
    norm1_bias = normal_values(streams_of[9], (D,), 0.3, 4.0, ((0, 8),))
    output_bias = normal_values(streams_of[10], (D,), 0.3, 4.0, ((0, 8),))
    norm2_gain = jnp.clip(1.0 + 0.1 * jax.random.normal(streams_of[11], (D,), jnp.float32), 0.5, 1.5).astype(jnp.bfloat16)
    norm2_bias = normal_values(streams_of[12], (D,), 0.3, 4.0, ((0, 8),))
    down_bias = normal_values(streams_of[13], (D,), 0.3, 4.0, ((0, 8),))
    query_bias = normal_values(streams_of[14], (HHD,), 0.1, 1.5, ((0, 4),))
    value_bias = normal_values(streams_of[15], (HHD,), 0.05, 0.75, ((0, 4),))
    up_bias = normal_values(streams_of[16], (FF,), 0.5, 6.0, ((0, 4),))
    return {"tokens": tokens, "out_grad": out_grad, "query_weight": query_weight, "key_weight": key_weight, "value_weight": value_weight, "output_weight": output_weight, "up_weight": up_weight, "down_weight": down_weight, "norm1_gain": norm1_gain, "norm1_bias": norm1_bias, "output_bias": output_bias, "norm2_gain": norm2_gain, "norm2_bias": norm2_bias, "down_bias": down_bias, "query_bias": query_bias, "value_bias": value_bias, "up_bias": up_bias}


epsilon = 1e-05
highest = lax.Precision.HIGHEST

@jax.custom_vjp
def low(v):
    return lax.optimization_barrier(v.astype(jnp.bfloat16)).astype(jnp.float32)

@jax.custom_vjp
def low_back(v):
    return v

def low_keep(v):
    return (low(v), None)

def low_pass(kept, grad):
    return (grad,)

def back_keep(v):
    return (v, None)

def back_low(kept, grad):
    return (low(grad),)
low.defvjp(low_keep, low_pass)
low_back.defvjp(back_keep, back_low)

def matmul(left_side, right_side):
    return jnp.dot(left_side, right_side, precision=highest, preferred_element_type=jnp.float32)

def normalize(values):
    centred = values - lax.optimization_barrier(jnp.mean(values, axis=-1, keepdims=True))
    return centred * lax.rsqrt(lax.optimization_barrier(jnp.mean(centred * centred, axis=-1, keepdims=True)) + epsilon)

def layer_forward(sequence, query_weight, key_weight, value_weight, output_weight, up_weight, down_weight, norm1_gain, norm1_bias, output_bias, norm2_gain, norm2_bias, down_bias, query_bias, value_bias, up_bias):
    length = sequence.shape[0]
    normed = low(normalize(sequence) * norm1_gain + norm1_bias)
    queries = low(low_back(matmul(normed, query_weight) + query_bias)).reshape(length, HEADS, HEAD_DIM)
    keys_all = low(low_back(matmul(normed, key_weight))).reshape(length, HEADS, HEAD_DIM)
    values_all = low(low_back(matmul(normed, value_weight) + value_bias)).reshape(length, HEADS, HEAD_DIM)
    scores = low_back(jnp.einsum('qhd,khd->hqk', queries, keys_all, precision=highest) * HEAD_DIM ** (-0.5))
    positions = jnp.arange(length, dtype=jnp.int32) // BLOCK
    allowed = positions[None, :] <= positions[:, None]
    scores = jnp.where(allowed[None], scores, -jnp.inf)
    largest = lax.optimization_barrier(jnp.max(scores, axis=-1, keepdims=True))
    powers = jnp.exp(scores - largest)
    probabilities = powers / lax.optimization_barrier(jnp.sum(powers, axis=-1, keepdims=True))
    mixed_heads = jnp.einsum('hqk,khd->qhd', low(probabilities), values_all, precision=highest)
    mixed_heads = low(low_back(mixed_heads.reshape(length, HEADS * HEAD_DIM)))
    branch = low_back(matmul(mixed_heads, output_weight.T) + output_bias)
    hidden = sequence + branch
    normed_two = low(normalize(hidden) * norm2_gain + norm2_bias)
    upward = low_back(matmul(normed_two, up_weight) + up_bias)
    activated = low(jax.nn.gelu(upward, approximate=False))
    return hidden + matmul(activated, down_weight.T) + down_bias

def reference(tokens, out_grad, query_weight, key_weight, value_weight, output_weight, up_weight, down_weight, norm1_gain, norm1_bias, output_bias, norm2_gain, norm2_bias, down_bias, query_bias, value_bias, up_bias):
    params = tuple((weight.astype(jnp.float32) for weight in (query_weight, key_weight, value_weight, output_weight, up_weight, down_weight, norm1_gain, norm1_bias, output_bias, norm2_gain, norm2_bias, down_bias, query_bias, value_bias, up_bias)))

    def one_sequence(totals, seq_pair):
        sequence, cotangent = seq_pair
        output, pullback = jax.vjp(layer_forward, sequence, *params)
        gradients = pullback(cotangent)
        updated = tuple((former + latter for former, latter in zip(totals, gradients[1:])))
        return (updated, (output.astype(jnp.bfloat16), gradients[0]))
    zero_sums = tuple((jnp.zeros(weight.shape, jnp.float32) for weight in params))
    totals, (outputs, input_grads) = lax.scan(one_sequence, zero_sums, (tokens.astype(jnp.float32), out_grad.astype(jnp.float32)))
    return (outputs, input_grads, totals[0], totals[1], totals[2], totals[3], totals[4], totals[5], totals[6], totals[7], totals[8], totals[9], totals[10], totals[11], totals[12], totals[13], totals[14])
```

```python
import functools

import jax
import jax.numpy as jnp
from jax import lax
from jax.experimental import pallas as pl
from jax.experimental.pallas import tpu as pltpu
from jax.sharding import PartitionSpec as P

HEAD_DIM = 64
MESH = pl.DeviceIdType.MESH
F32 = jnp.float32
BF16 = jnp.bfloat16
VMEM_LIMIT = 66 * 1000 * 1000

epsilon = 1e-05
root_half = 0.7071067811865476
density_scale = 0.3989422804014327


def remote(src, dst, send_sem, recv_sem, device):
    return pltpu.make_async_remote_copy(
        src_ref=src,
        dst_ref=dst,
        send_sem=send_sem,
        recv_sem=recv_sem,
        device_id=device,
        device_id_type=MESH,
    )


def nn_dot(left, right):
    return lax.dot_general(left, right, (((1,), (0,)), ((), ())), preferred_element_type=F32)


def nt_dot(left, right):
    return lax.dot_general(left, right, (((1,), (1,)), ((), ())), preferred_element_type=F32)


def tn_dot(left, right):
    return lax.dot_general(left, right, (((0,), (0,)), ((), ())), preferred_element_type=F32)


def normalize(values):
    centred = values - jnp.mean(values, axis=-1, keepdims=True)
    spread = lax.rsqrt(jnp.mean(centred * centred, axis=-1, keepdims=True) + epsilon)
    return centred * spread, spread


def norm_back(grad_scaled, scaled, spread):
    inner = grad_scaled - jnp.mean(grad_scaled, axis=-1, keepdims=True)
    inner = inner - scaled * jnp.mean(grad_scaled * scaled, axis=-1, keepdims=True)
    return inner * spread


class Place:
    def __init__(self, sizes):
        self.n_dp, self.n_ctx, self.n_tp = sizes
        self.n_pair = self.n_tp // 2
        self.dp = lax.axis_index("dp")
        self.ctx = lax.axis_index("ctx")
        self.tp = lax.axis_index("tp")
        self.pair = self.tp // 2
        self.side = self.tp % 2

    def other_dp(self, k):
        d = (self.dp + k) % self.n_dp
        return d, (d, self.ctx, self.tp)

    def other_ctx(self, k):
        z = (self.ctx + k) % self.n_ctx
        return z, (self.dp, z, self.tp)

    def other_pair(self, k):
        p = (self.pair + k) % self.n_pair
        return p, (self.dp, self.ctx, 2 * p + self.side)

    def partner(self):
        return (self.dp, self.ctx, 2 * self.pair + 1 - self.side)

    def barrier(self, far):
        sem = pltpu.get_barrier_semaphore()
        count = 1
        pl.semaphore_signal(sem, inc=1, device_id=self.partner(), device_id_type=MESH)
        if far:
            for size, other in (
                (self.n_dp, self.other_dp),
                (self.n_ctx, self.other_ctx),
                (self.n_pair, self.other_pair),
            ):
                for k in range(1, size):
                    pl.semaphore_signal(sem, inc=1, device_id=other(k)[1], device_id_type=MESH)
                    count += 1
        pl.semaphore_wait(sem, count)


class Sends:
    def __init__(self, sems):
        self.sems = sems
        self.started = []

    def go(self, src, dst, recv_sem, device):
        copy = remote(src, dst, self.sems.at[len(self.started)], recv_sem, device)
        copy.start()
        self.started.append(copy)

    def finish(self):
        for copy in self.started:
            copy.wait_send()


def gather_body(sizes, half, *refs):
    here = Place(sizes)
    n_dp, n_ctx, n_pair = here.n_dp, here.n_ctx, here.n_pair
    d, z, p, c = here.dp, here.ctx, here.pair, here.side
    tokens, out_grad = refs[0:2]
    shards = refs[2:8]
    vec, bias = refs[8:10]
    tok_own, og_own = refs[10:12]
    full = refs[12:18]
    vec_all, bias_all = refs[18:20]
    own_sem, send_sem, rows_sem, line_sem, group_sem, vline_sem, vgroup_sem, bias_sem = refs[20:28]
    own_row = d * n_ctx + z
    mine = p * n_ctx + z
    rows = pl.ds(pl.multiple_of(c * half, half), half)

    here.barrier(True)
    sends = Sends(send_sem)
    own = [
        pltpu.make_async_copy(tokens.at[mine, rows], tok_own.at[z], own_sem.at[0]),
        pltpu.make_async_copy(out_grad.at[mine, rows], og_own.at[z], own_sem.at[1]),
        pltpu.make_async_copy(vec, vec_all.at[own_row], own_sem.at[2]),
        pltpu.make_async_copy(bias, bias_all.at[p], own_sem.at[3]),
    ]
    for a in range(6):
        own.append(pltpu.make_async_copy(shards[a], full[a].at[p, own_row], own_sem.at[4 + a]))
    for copy in own:
        copy.start()

    def send_rows(index, source, target):
        for k in range(1, n_ctx):
            zz, device = here.other_ctx(k)
            sends.go(
                source.at[p * n_ctx + zz, rows], target.at[z], rows_sem.at[index, z], device
            )

    def send_line(a):
        for k in range(1, n_ctx):
            zz, device = here.other_ctx(k)
            sends.go(shards[a], full[a].at[p, own_row], line_sem.at[a, z], device)

    send_rows(0, tokens, tok_own)
    for k in range(1, n_ctx):
        zz, device = here.other_ctx(k)
        sends.go(vec, vec_all.at[own_row], vline_sem.at[z], device)
    for k in range(1, n_pair):
        pp, device = here.other_pair(k)
        sends.go(bias, bias_all.at[p], bias_sem.at[p], device)
    for a in range(6):
        send_line(a)
    send_rows(1, out_grad, og_own)

    for copy in own:
        copy.wait()

    def group(a, pp, dd):
        return full[a].at[pp, pl.ds(dd * n_ctx, n_ctx)]

    def wait_line(a):
        for k in range(1, n_ctx):
            zz, device = here.other_ctx(k)
            slot = full[a].at[p, d * n_ctx + zz]
            remote(slot, slot, send_sem.at[0], line_sem.at[a, zz], device).wait_recv()

    def send_pair(a, dd):
        for k in range(1, n_pair):
            pp, device = here.other_pair(k)
            sends.go(group(a, p, dd), group(a, p, dd), group_sem.at[a, p, dd], device)

    def send_dp(a, pp):
        for k in range(1, n_dp):
            dd, device = here.other_dp(k)
            sends.go(group(a, pp, d), group(a, pp, d), group_sem.at[a, pp, d], device)

    def wait_group(a, pp, dd):
        slot = group(a, pp, dd)
        remote(slot, slot, send_sem.at[0], group_sem.at[a, pp, dd], here.partner()).wait_recv()

    for a in range(6):
        wait_line(a)
        send_dp(a, p)
        send_pair(a, d)
    for k in range(1, n_ctx):
        zz, device = here.other_ctx(k)
        slot = vec_all.at[d * n_ctx + zz]
        remote(slot, slot, send_sem.at[0], vline_sem.at[zz], device).wait_recv()
    for k in range(1, n_dp):
        dd, device = here.other_dp(k)
        slot = vec_all.at[pl.ds(d * n_ctx, n_ctx)]
        sends.go(slot, slot, vgroup_sem.at[d], device)
    pair_first = (True, True, True, True, False, True)
    for a in range(6):
        if pair_first[a]:
            for k in range(1, n_pair):
                pp = here.other_pair(k)[0]
                wait_group(a, pp, d)
                send_dp(a, pp)
        else:
            for k in range(1, n_dp):
                dd = here.other_dp(k)[0]
                wait_group(a, p, dd)
                send_pair(a, dd)
    for a in range(6):
        for k in range(1, n_dp):
            dd = here.other_dp(k)[0]
            if pair_first[a]:
                wait_group(a, p, dd)
            for j in range(1, n_pair):
                wait_group(a, here.other_pair(j)[0], dd)
        if not pair_first[a]:
            for j in range(1, n_pair):
                wait_group(a, here.other_pair(j)[0], d)
    for k in range(1, n_dp):
        dd, device = here.other_dp(k)
        slot = vec_all.at[pl.ds(dd * n_ctx, n_ctx)]
        remote(slot, slot, send_sem.at[0], vgroup_sem.at[dd], device).wait_recv()
    for k in range(1, n_pair):
        pp, device = here.other_pair(k)
        slot = bias_all.at[pp]
        remote(slot, slot, send_sem.at[0], bias_sem.at[pp], device).wait_recv()
    for index, target in ((0, tok_own), (1, og_own)):
        for k in range(1, n_ctx):
            zz, device = here.other_ctx(k)
            slot = target.at[zz]
            remote(slot, slot, send_sem.at[0], rows_sem.at[index, zz], device).wait_recv()
    sends.finish()


def gather_call(sizes, tokens, out_grad, shards, vec, bias):
    n_dp, n_ctx, n_tp = sizes
    n_pair = n_tp // 2
    seqs, block, width = tokens.shape
    half = block // 2
    any_spec = pl.BlockSpec(memory_space=pl.ANY)
    vmem_spec = pl.BlockSpec(memory_space=pltpu.VMEM)
    own = jax.ShapeDtypeStruct((n_ctx, half, width), BF16)
    out_shape = [own, own]
    out_shape += [jax.ShapeDtypeStruct((n_pair, n_dp * n_ctx) + s.shape, BF16) for s in shards]
    out_shape += [
        jax.ShapeDtypeStruct((n_dp * n_ctx,) + vec.shape, F32),
        jax.ShapeDtypeStruct((n_pair,) + bias.shape, F32),
    ]
    n_sends = (
        2 * (n_ctx - 1)
        + (n_ctx - 1)
        + (n_pair - 1)
        + 6 * (n_ctx - 1)
        + (n_dp - 1)
        + 6 * ((n_dp - 1) + (n_pair - 1) + (n_dp - 1) * (n_pair - 1))
    )
    dma = pltpu.SemaphoreType.DMA
    return pl.pallas_call(
        functools.partial(gather_body, sizes, half),
        out_shape=out_shape,
        in_specs=[any_spec] * 10,
        out_specs=[vmem_spec] * 10,
        scratch_shapes=[
            dma((10,)),
            dma((n_sends,)),
            dma((2, n_ctx)),
            dma((6, n_ctx)),
            dma((6, n_pair, n_dp)),
            dma((n_ctx,)),
            dma((n_dp,)),
            dma((n_pair,)),
        ],
        compiler_params=pltpu.CompilerParams(
            collective_id=0, has_side_effects=True, vmem_limit_bytes=VMEM_LIMIT
        ),
    )(tokens, out_grad, *shards, vec, bias)


def compute_body(sizes, *refs):
    here = Place(sizes)
    n_ctx, n_pair = here.n_ctx, here.n_pair
    c = here.side
    (tok, og, gq, gk, gv, go, gu, gd, vecs, bias) = refs[:10]
    (lo, tg, dwq, dwk, dwv, dwo, dwu, dwd, small) = refs[10:19]
    (
        xn1, wqkv, wo, qs, ks, vs, o32, mixed, hid, xn2, ogf, act, ug, bg, dm,
        dka, dva, dqkv, tra, trb, part, ssend, srecv, p_first, send_sem, recv_sem,
    ) = refs[19 : 19 + 23] + (refs[42 : 42 + n_ctx],) + refs[42 + n_ctx :]
    half, width = tok.shape[1], tok.shape[2]
    block = 2 * half
    cols = gq.shape[2]
    hw = n_pair * cols
    fw = gu.shape[2]
    lanes = 2 * HEAD_DIM
    n_twos = hw // lanes
    partner = here.partner()
    scale = HEAD_DIM ** -0.5
    first_head = lax.broadcasted_iota(jnp.int32, (1, lanes), 1) < HEAD_DIM
    zero16 = jnp.zeros((), BF16)

    def own_rows(b):
        return pl.ds(pl.multiple_of(b * block + c * half, half), half)

    def far_rows(b):
        return pl.ds(pl.multiple_of(b * block + (1 - c) * half, half), half)

    def block_rows(b):
        return pl.ds(pl.multiple_of(b * block, block), block)

    def exchange(stage, b, src, dst):
        return remote(src, dst, send_sem.at[stage, b], recv_sem.at[stage, b], partner)

    def rows_copy(stage, b, ref):
        return exchange(stage, b, ref.at[own_rows(b)], ref.at[own_rows(b)])

    def rows_arrive(stage, b, ref):
        exchange(stage, b, ref.at[far_rows(b)], ref.at[far_rows(b)]).wait_recv()

    def part_copy(stage, slot, b):
        return exchange(stage, b, ssend.at[slot, b], srecv.at[slot, b])

    here.barrier(False)

    gain_one, shift_one, out_shift = vecs[0:1, :], vecs[1:2, :], vecs[2:3, :]
    gain_two, shift_two, down_shift = vecs[3:4, :], vecs[4:5, :], vecs[5:6, :]

    @pl.loop(0, n_ctx)
    def _(b):
        exchange(0, b, og.at[b], ogf.at[own_rows(b)]).start()
        ogf[own_rows(b), :] = og[b]
        scaled, _ = normalize(tok[b].astype(F32))
        xn1[own_rows(b), :] = (scaled * gain_one + shift_one).astype(BF16)
        rows_copy(1, b, xn1).start()

    for i in range(n_pair):
        at = slice(i * cols, (i + 1) * cols)
        wqkv[:, i * cols : (i + 1) * cols] = gq[i]
        wqkv[:, hw + i * cols : hw + (i + 1) * cols] = gk[i]
        wqkv[:, 2 * hw + i * cols : 2 * hw + (i + 1) * cols] = gv[i]
        wo[:, at] = go[i]
    q_shift = bias[0, 0:1, :hw]
    v_shift = bias[0, 1:2, :hw]
    for i in range(1, n_pair):
        q_shift = q_shift + bias[i, 0:1, :hw]
        v_shift = v_shift + bias[i, 1:2, :hw]

    @pl.loop(0, n_ctx)
    def _(b):
        rows_arrive(1, b, xn1)
        product = nn_dot(xn1[block_rows(b), :], wqkv[...])
        qs[block_rows(b), :] = (product[:, :hw] + q_shift).astype(BF16) * jnp.asarray(scale, BF16)
        ks[block_rows(b), :] = product[:, hw : 2 * hw].astype(BF16)
        vs[block_rows(b), :] = (product[:, 2 * hw :] + v_shift).astype(BF16)

    for b in range(n_ctx):
        reach = (b + 1) * block
        here_rows = slice(b * block, (b + 1) * block)

        @pl.loop(0, n_twos)
        def _(j):
            at = pl.ds(pl.multiple_of(j * lanes, lanes), lanes)
            queries, keys, values = qs[here_rows, at], ks[:reach, at], vs[:reach, at]
            pieces = []
            for e in range(2):
                head = first_head if e == 0 else jnp.logical_not(first_head)
                scores = nt_dot(jnp.where(head, queries, zero16), keys)
                powers = jnp.exp(scores - jnp.max(scores, axis=-1, keepdims=True))
                inverse = 1.0 / jnp.sum(powers, axis=-1, keepdims=True)
                probs = (powers * inverse).astype(BF16)
                p_first[b][2 * j + e] = probs
                pieces.append(nn_dot(probs, values))
            out = jnp.where(first_head, pieces[0], pieces[1])
            o32[here_rows, at] = out
            mixed[here_rows, at] = out.astype(BF16)

        ssend[0, b] = nt_dot(mixed[far_rows(b), :], wo[...]).astype(BF16)
        part_copy(2, 0, b).start()
        hid[b] = nt_dot(mixed[own_rows(b), :], wo[...])

    @pl.loop(0, n_ctx)
    def _(b):
        part_copy(2, 0, b).wait()
        hidden = tok[b].astype(F32) + (hid[b] + srecv[0, b].astype(F32)) + out_shift
        hid[b] = hidden
        scaled, _ = normalize(hidden)
        xn2[own_rows(b), :] = (scaled * gain_two + shift_two).astype(BF16)
        rows_copy(3, b, xn2).start()

    small[...] = jnp.zeros_like(small)

    @pl.loop(0, n_ctx)
    def _(b):
        rows_arrive(0, b, ogf)
        rows_arrive(3, b, xn2)
        normed = xn2[block_rows(b), :]
        grads = ogf[block_rows(b), :]
        for i in range(n_pair):
            upward = nn_dot(normed, gu[i]) + bias[i, 2:3, :]
            big_phi = 0.5 + 0.5 * lax.erf(upward * root_half)
            act[i, block_rows(b), :] = (upward * big_phi).astype(BF16)
            slope = big_phi + upward * density_scale * jnp.exp(-0.5 * upward * upward)
            rows_grad = (nn_dot(grads, gd[i]) * slope).astype(BF16)
            ug[i, block_rows(b), :] = rows_grad
            small[8 + i : 9 + i, :] += jnp.sum(rows_grad.astype(F32), axis=0, keepdims=True)

        def through(ref, weight, rows):
            total = nt_dot(ref[0, rows, :], weight[0])
            for i in range(1, n_pair):
                total = total + nt_dot(ref[i, rows, :], weight[i])
            return total

        ssend[1, b] = through(act, gd, far_rows(b)).astype(BF16)
        part_copy(4, 1, b).start()
        ssend[0, b] = through(ug, gu, far_rows(b)).astype(BF16)
        part_copy(5, 0, b).start()
        part[0, b] = through(act, gd, own_rows(b))
        part[1, b] = through(ug, gu, own_rows(b))

    def transposed(ref, out):
        for b in range(n_ctx):
            out[:, b * block : (b + 1) * block] = ref[b * block : (b + 1) * block, :].T

    @pl.loop(0, n_ctx)
    def _(b):
        part_copy(4, 1, b).wait()
        lo[b] = (hid[b] + (part[0, b] + srecv[1, b].astype(F32)) + down_shift).astype(BF16)
        part_copy(5, 0, b).wait()
        grad_two = part[1, b] + srecv[0, b].astype(F32)
        scaled, spread = normalize(hid[b])
        own_grad = og[b].astype(F32)
        hidden_grad = own_grad + norm_back(grad_two * gain_two, scaled, spread)
        hid[b] = hidden_grad
        branch = hidden_grad.astype(BF16)
        bg[own_rows(b), :] = branch
        rows_copy(6, b, bg).start()
        small[2:3, :] += jnp.sum(branch.astype(F32), axis=0, keepdims=True)
        small[3:4, :] += jnp.sum(grad_two * scaled, axis=0, keepdims=True)
        small[4:5, :] += jnp.sum(grad_two, axis=0, keepdims=True)
        small[5:6, :] += jnp.sum(own_grad, axis=0, keepdims=True)

    transposed(xn2, tra)
    transposed(ogf, trb)
    step = 256

    @pl.loop(0, width // step)
    def _(r):
        rows = pl.ds(pl.multiple_of(r * step, step), step)
        for i in range(n_pair):
            dwu[i, rows, :] = nn_dot(tra[rows, :], ug[i]).astype(BF16)
            dwd[i, rows, :] = nn_dot(trb[rows, :], act[i]).astype(BF16)

    @pl.loop(0, n_ctx)
    def _(b):
        rows_arrive(6, b, bg)
        dm[block_rows(b), :] = nn_dot(bg[block_rows(b), :], wo[...]).astype(BF16)

    transposed(bg, trb)

    @pl.loop(0, width // step)
    def _(r):
        rows = pl.ds(pl.multiple_of(r * step, step), step)
        product = nn_dot(trb[rows, :], mixed[...])
        for i in range(n_pair):
            dwo[i, rows, :] = product[:, i * cols : (i + 1) * cols].astype(BF16)

    for b in reversed(range(n_ctx)):
        reach = (b + 1) * block
        here_rows = slice(b * block, (b + 1) * block)

        @pl.loop(0, n_twos)
        def _(j):
            at = pl.ds(pl.multiple_of(j * lanes, lanes), lanes)
            queries, keys, values = qs[here_rows, at], ks[:reach, at], vs[:reach, at]
            mix_grad, mix = dm[here_rows, at], o32[here_rows, at]
            towards = mix_grad.astype(F32) * mix
            query_parts, key_sum, value_sum = [], None, None
            for e in range(2):
                head = first_head if e == 0 else jnp.logical_not(first_head)
                grad_head = jnp.where(head, mix_grad, zero16)
                prob_grad = nt_dot(grad_head, values)
                centre = jnp.sum(jnp.where(head, towards, 0.0), axis=-1, keepdims=True)
                probs = p_first[b][2 * j + e]
                score_grad = (probs.astype(F32) * (prob_grad - centre)).astype(BF16)
                query_parts.append(nn_dot(score_grad, keys))
                key_term = tn_dot(score_grad, jnp.where(head, queries, zero16))
                value_term = tn_dot(probs, grad_head)
                key_sum = key_term if key_sum is None else key_sum + key_term
                value_sum = value_term if value_sum is None else value_sum + value_term
            query_grad = jnp.where(first_head, query_parts[0], query_parts[1]) * scale
            dqkv[here_rows, at] = query_grad.astype(BF16)
            if b == n_ctx - 1:
                dka[:, at] = key_sum
                dva[:, at] = value_sum
            else:
                dka[:reach, at] += key_sum
                dva[:reach, at] += value_sum

    @pl.loop(0, n_ctx)
    def _(b):
        dqkv[block_rows(b), hw : 2 * hw] = dka[block_rows(b), :].astype(BF16)
        dqkv[block_rows(b), 2 * hw :] = dva[block_rows(b), :].astype(BF16)
        small[6:7, :hw] += jnp.sum(dqkv[block_rows(b), :hw].astype(F32), axis=0, keepdims=True)
        small[7:8, :hw] += jnp.sum(dqkv[block_rows(b), 2 * hw :].astype(F32), axis=0, keepdims=True)
        ssend[1, b] = nt_dot(dqkv[far_rows(b), :], wqkv[...]).astype(BF16)
        part_copy(7, 1, b).start()
        part[0, b] = nt_dot(dqkv[own_rows(b), :], wqkv[...])

    transposed(xn1, tra)

    @pl.loop(0, width // step)
    def _(r):
        rows = pl.ds(pl.multiple_of(r * step, step), step)
        product = nn_dot(tra[rows, :], dqkv[...])
        for i in range(n_pair):
            dwq[i, rows, :] = product[:, i * cols : (i + 1) * cols].astype(BF16)
            dwk[i, rows, :] = product[:, hw + i * cols : hw + (i + 1) * cols].astype(BF16)
            dwv[i, rows, :] = product[:, 2 * hw + i * cols : 2 * hw + (i + 1) * cols].astype(BF16)

    @pl.loop(0, n_ctx)
    def _(b):
        part_copy(7, 1, b).wait()
        grad_one = part[0, b] + srecv[1, b].astype(F32)
        scaled, spread = normalize(tok[b].astype(F32))
        tg[b] = (hid[b] + norm_back(grad_one * gain_one, scaled, spread)).astype(BF16)
        small[0:1, :] += jnp.sum(grad_one * scaled, axis=0, keepdims=True)
        small[1:2, :] += jnp.sum(grad_one, axis=0, keepdims=True)
        exchange(0, b, og.at[b], ogf.at[own_rows(b)]).wait_send()
        rows_copy(1, b, xn1).wait_send()
        rows_copy(3, b, xn2).wait_send()
        rows_copy(6, b, bg).wait_send()


def compute_call(sizes, tok, og, weights, vecs, bias):
    n_dp, n_ctx, n_tp = sizes
    n_pair = n_tp // 2
    half, width = tok.shape[1:]
    block = 2 * half
    length = n_ctx * block
    cols = weights[0].shape[2]
    hw = n_pair * cols
    fw = weights[4].shape[2]
    heads = hw // HEAD_DIM
    vmem_spec = pl.BlockSpec(memory_space=pltpu.VMEM)
    shape = jax.ShapeDtypeStruct
    out_shape = [
        shape(tok.shape, BF16),
        shape(tok.shape, BF16),
    ]
    out_shape += [shape(w.shape, BF16) for w in weights]
    out_shape += [shape((16, width), F32)]
    vm = pltpu.VMEM
    scratch = [
        vm((length, width), BF16),
        vm((width, 3 * hw), BF16),
        vm((width, hw), BF16),
        vm((length, hw), BF16),
        vm((length, hw), BF16),
        vm((length, hw), BF16),
        vm((length, hw), F32),
        vm((length, hw), BF16),
        vm((n_ctx, half, width), F32),
        vm((length, width), BF16),
        vm((length, width), BF16),
        vm((n_pair, length, fw), BF16),
        vm((n_pair, length, fw), BF16),
        vm((length, width), BF16),
        vm((length, hw), BF16),
        vm((length, hw), F32),
        vm((length, hw), F32),
        vm((length, 3 * hw), BF16),
        vm((width, length), BF16),
        vm((width, length), BF16),
        vm((2, n_ctx, half, width), F32),
        vm((2, n_ctx, half, width), BF16),
        vm((2, n_ctx, half, width), BF16),
    ]
    scratch += [vm((heads, block, (b + 1) * block), BF16) for b in range(n_ctx)]
    scratch += [pltpu.SemaphoreType.DMA((8, n_ctx)), pltpu.SemaphoreType.DMA((8, n_ctx))]
    return pl.pallas_call(
        functools.partial(compute_body, sizes),
        out_shape=out_shape,
        in_specs=[vmem_spec] * 10,
        out_specs=[vmem_spec] * 9,
        scratch_shapes=scratch,
        compiler_params=pltpu.CompilerParams(
            collective_id=1, has_side_effects=True, vmem_limit_bytes=VMEM_LIMIT
        ),
    )(tok, og, *weights, vecs, bias)


def scatter_body(sizes, half, *refs):
    here = Place(sizes)
    n_dp, n_ctx, n_pair = here.n_dp, here.n_ctx, here.n_pair
    d, z, p, c = here.dp, here.ctx, here.pair, here.side
    rows_in = refs[0:2]
    grads = refs[2:8]
    small = refs[8]
    rows_out = refs[9:11]
    owned = refs[11:17]
    small_out = refs[17]
    it = iter(refs[18:])
    dp_land = [next(it) for _ in range(6)]
    dp_sum = [next(it) for _ in range(6)]
    keep = [next(it) for _ in range(6)]
    pair_land = [next(it) for _ in range(6)]
    pair_sum = [next(it) for _ in range(6)]
    ctx_land = [next(it) for _ in range(6)]
    side_land, small_b, ctx_small, small_c, pair_small, small_d, dp_small = [next(it) for _ in range(7)]
    own_sem, send_sem, line_sem, far_sem, side_sem, dp_sem, pair_sem, ctx_sem, small_sem = it
    mine = p * n_ctx + z
    rows = pl.ds(pl.multiple_of(c * half, half), half)

    here.barrier(True)
    sends = Sends(send_sem)

    for a in range(6):
        for k in range(1, n_dp):
            dd, device = here.other_dp(k)
            sends.go(
                grads[a].at[:, pl.ds(dd * n_ctx, n_ctx)],
                dp_land[a].at[k - 1],
                dp_sem.at[a, k - 1],
                device,
            )
    own = []
    for i in range(2):
        for k in range(1, n_ctx):
            zz, device = here.other_ctx(k)
            sends.go(rows_in[i].at[zz], rows_out[i].at[mine, rows], line_sem.at[i, z], device)
        own.append(pltpu.make_async_copy(rows_in[i].at[z], rows_out[i].at[mine, rows], own_sem.at[i]))
        own[-1].start()
    sends.go(small.at[pl.ds(0, 8)], side_land, small_sem.at[0, 0], here.partner())

    def small_arrive(stage, k, land):
        remote(land, land, send_sem.at[0], small_sem.at[stage, k - 1], here.partner()).wait_recv()

    for i in range(2):
        own[i].wait()
        for k in range(1, n_ctx):
            zz, device = here.other_ctx(k)
            slot = rows_out[i].at[p * n_ctx + zz, rows]
            remote(slot, slot, send_sem.at[0], line_sem.at[i, zz], device).wait_recv()
        for k in range(1, n_pair):
            pp, device = here.other_pair(k)
            slot = rows_out[i].at[pl.ds(p * n_ctx, n_ctx), rows]
            sends.go(slot, slot, far_sem.at[i, p], device)

    small_arrive(0, 1, side_land)
    small_b[0:8, :] = small[0:8, :] + side_land[...]
    small_b[8:16, :] = small[8:16, :]
    small_b[6:8, :] = small[6:8, :]
    for k in range(1, n_ctx):
        zz, device = here.other_ctx(k)
        sends.go(small_b, ctx_small.at[k - 1], small_sem.at[1, k - 1], device)

    for a in range(6):
        for k in range(1, n_dp):
            remote(
                dp_land[a].at[k - 1], dp_land[a].at[k - 1], send_sem.at[0], dp_sem.at[a, k - 1],
                here.partner(),
            ).wait_recv()
        for i in range(n_pair):
            total = grads[a][i, pl.ds(d * n_ctx, n_ctx)].astype(F32)
            for k in range(1, n_dp):
                total = total + dp_land[a][k - 1, i].astype(F32)
            dp_sum[a][i] = total.astype(BF16)
        for k in range(1, n_pair):
            pp, device = here.other_pair(k)
            sends.go(dp_sum[a].at[pp], pair_land[a].at[k - 1], pair_sem.at[a, k - 1], device)

    total = small_b[...]
    for k in range(1, n_ctx):
        small_arrive(1, k, ctx_small.at[k - 1])
        total = total + ctx_small[k - 1]
    small_c[...] = total
    for k in range(1, n_pair):
        pp, device = here.other_pair(k)
        sends.go(small_c, pair_small.at[k - 1], small_sem.at[2, k - 1], device)

    for a in range(6):
        for k in range(1, n_pair):
            remote(
                pair_land[a].at[k - 1], pair_land[a].at[k - 1], send_sem.at[0], pair_sem.at[a, k - 1],
                here.partner(),
            ).wait_recv()
        total = dp_sum[a][p].astype(F32)
        for k in range(1, n_pair):
            total = total + pair_land[a][k - 1].astype(F32)
        keep[a][...] = total
        pair_sum[a][...] = total.astype(BF16)
        for k in range(1, n_ctx):
            zz, device = here.other_ctx(k)
            sends.go(pair_sum[a].at[zz], ctx_land[a].at[k - 1], ctx_sem.at[a, k - 1], device)

    total = small_c[...]
    for k in range(1, n_pair):
        small_arrive(2, k, pair_small.at[k - 1])
        total = total + pair_small[k - 1]
    small_d[...] = total
    for k in range(1, n_dp):
        dd, device = here.other_dp(k)
        sends.go(small_d, dp_small.at[k - 1], small_sem.at[3, k - 1], device)

    for i in range(2):
        for k in range(1, n_pair):
            pp, device = here.other_pair(k)
            slot = rows_out[i].at[pl.ds(pp * n_ctx, n_ctx), rows]
            remote(slot, slot, send_sem.at[0], far_sem.at[i, pp], device).wait_recv()
        slot = rows_out[i].at[:, rows]
        sends.go(slot, slot, side_sem.at[i], here.partner())

    for a in range(6):
        total = keep[a][z]
        for k in range(1, n_ctx):
            remote(
                ctx_land[a].at[k - 1], ctx_land[a].at[k - 1], send_sem.at[0], ctx_sem.at[a, k - 1],
                here.partner(),
            ).wait_recv()
            total = total + ctx_land[a][k - 1].astype(F32)
        owned[a][...] = total

    total = small_d[...]
    for k in range(1, n_dp):
        small_arrive(3, k, dp_small.at[k - 1])
        total = total + dp_small[k - 1]
    small_out[...] = total
    other = pl.ds(pl.multiple_of((1 - c) * half, half), half)
    for i in range(2):
        slot = rows_out[i].at[:, other]
        remote(slot, slot, send_sem.at[0], side_sem.at[i], here.partner()).wait_recv()
    sends.finish()


def scatter_call(sizes, seqs, lo, tg, grads, small):
    n_dp, n_ctx, n_tp = sizes
    n_pair = n_tp // 2
    half, width = lo.shape[1:]
    vmem_spec = pl.BlockSpec(memory_space=pltpu.VMEM)
    shape = jax.ShapeDtypeStruct
    vm = pltpu.VMEM
    tail = [g.shape[2:] for g in grads]
    out_shape = [shape((seqs, 2 * half, width), BF16)] * 2
    out_shape += [shape(t, F32) for t in tail]
    out_shape += [shape(small.shape, F32)]
    scratch = [vm((n_dp - 1, n_pair, n_ctx) + t, BF16) for t in tail]
    scratch += [vm((n_pair, n_ctx) + t, BF16) for t in tail]
    scratch += [vm((n_ctx,) + t, F32) for t in tail]
    scratch += [vm((n_pair - 1, n_ctx) + t, BF16) for t in tail]
    scratch += [vm((n_ctx,) + t, BF16) for t in tail]
    scratch += [vm((n_ctx - 1,) + t, BF16) for t in tail]
    scratch += [
        vm((8, width), F32),
        vm((16, width), F32),
        vm((n_ctx - 1, 16, width), F32),
        vm((16, width), F32),
        vm((n_pair - 1, 16, width), F32),
        vm((16, width), F32),
        vm((n_dp - 1, 16, width), F32),
    ]
    n_sends = (
        6 * ((n_dp - 1) + (n_pair - 1) + (n_ctx - 1))
        + 2 * ((n_ctx - 1) + (n_pair - 1) + 1)
        + 1 + (n_ctx - 1) + (n_pair - 1) + (n_dp - 1)
    )
    dma = pltpu.SemaphoreType.DMA
    most = max(n_dp, n_ctx, n_pair)
    scratch += [
        dma((2,)),
        dma((n_sends,)),
        dma((2, n_ctx)),
        dma((2, n_pair)),
        dma((2,)),
        dma((6, n_dp - 1)),
        dma((6, n_pair - 1)),
        dma((6, n_ctx - 1)),
        dma((4, most)),
    ]
    return pl.pallas_call(
        functools.partial(scatter_body, sizes, half),
        out_shape=out_shape,
        in_specs=[vmem_spec] * 9,
        out_specs=[vmem_spec] * 9,
        scratch_shapes=scratch,
        compiler_params=pltpu.CompilerParams(
            collective_id=2, has_side_effects=True, vmem_limit_bytes=VMEM_LIMIT
        ),
    )(lo, tg, *grads, small)


def per_device(
    tokens,
    out_grad,
    query_weight,
    key_weight,
    value_weight,
    output_weight,
    up_weight,
    down_weight,
    norm1_gain,
    norm1_bias,
    output_bias,
    norm2_gain,
    norm2_bias,
    down_bias,
    query_bias,
    value_bias,
    up_bias,
):
    sizes = (lax.axis_size("dp"), lax.axis_size("ctx"), lax.axis_size("tp"))
    n_dp, n_ctx, n_tp = sizes
    n_pair = n_tp // 2
    seqs, block, width = tokens.shape
    assert seqs == n_ctx * n_pair
    share = norm1_gain.shape[0]
    cols = query_bias.shape[0]
    pair = lax.axis_index("tp") // 2
    row = lax.axis_index("dp") * n_ctx + lax.axis_index("ctx")

    six = jnp.stack(
        [norm1_gain, norm1_bias, output_bias, norm2_gain, norm2_bias, down_bias]
    ).astype(F32)
    vec = jnp.pad(six, ((0, 2), (0, 128 - share)))
    columns = jnp.arange(width) // cols == pair
    narrow = [jnp.where(columns, jnp.tile(b.astype(F32), width // cols), 0.0) for b in (query_bias, value_bias)]
    bias = jnp.pad(jnp.stack(narrow + [up_bias.astype(F32)]), ((0, 5), (0, 0)))

    shards = (query_weight, key_weight, value_weight, output_weight, up_weight, down_weight)
    gathered = gather_call(sizes, tokens, out_grad, shards, vec, bias)
    tok, og = gathered[0:2]
    weights = [w.reshape(n_pair, width, w.shape[3]) for w in gathered[2:8]]
    vecs = gathered[8][:, :, :share].transpose(1, 0, 2).reshape(8, width)
    results = compute_call(sizes, tok, og, weights, vecs, gathered[9])
    lo, tg = results[0:2]
    grads = [
        g.reshape(n_pair, n_dp * n_ctx, s.shape[0], s.shape[1]) for g, s in zip(results[2:8], shards)
    ]
    final = scatter_call(sizes, seqs, lo, tg, grads, results[8])
    layer_out, tokens_grad = final[0], final[1].astype(F32)
    small = final[8]
    owned = [lax.dynamic_slice_in_dim(small[i], row * share, share) for i in range(6)]
    shifts = [lax.dynamic_slice_in_dim(small[6 + i], pair * cols, cols) for i in range(2)]
    up_total = lax.dynamic_index_in_dim(small[8 : 8 + n_pair], pair, 0, keepdims=False)
    return (layer_out, tokens_grad, *final[2:8], *owned, *shifts, up_total)


def solution(mesh):
    rows_spec = P("dp", "ctx", None)
    weight_spec = P(("dp", "ctx"), "tp")
    vector_spec = P(("dp", "ctx"))
    column_spec = P("tp")
    common = (rows_spec,) * 2 + (weight_spec,) * 6 + (vector_spec,) * 6 + (column_spec,) * 3
    return jax.shard_map(
        per_device, mesh=mesh, in_specs=common, out_specs=common, check_vma=False
    )
```

```python
import functools

import jax
import jax.numpy as jnp
from jax import lax
from jax.experimental import pallas as pl
from jax.experimental.pallas import tpu as pltpu
from jax.sharding import PartitionSpec as P

HEAD_DIM = 64
MESH = pl.DeviceIdType.MESH
F32 = jnp.float32
BF16 = jnp.bfloat16
VMEM_LIMIT = 66 * 1000 * 1000

epsilon = 1e-05
root_half = 0.7071067811865476
density_scale = 0.3989422804014327


def remote(src, dst, send_sem, recv_sem, device):
    return pltpu.make_async_remote_copy(
        src_ref=src,
        dst_ref=dst,
        send_sem=send_sem,
        recv_sem=recv_sem,
        device_id=device,
        device_id_type=MESH,
    )


def nn_dot(left, right):
    return lax.dot_general(left, right, (((1,), (0,)), ((), ())), preferred_element_type=F32)


def nt_dot(left, right):
    return lax.dot_general(left, right, (((1,), (1,)), ((), ())), preferred_element_type=F32)


def tn_dot(left, right):
    return lax.dot_general(left, right, (((0,), (0,)), ((), ())), preferred_element_type=F32)


def normalize(values):
    centred = values - jnp.mean(values, axis=-1, keepdims=True)
    spread = lax.rsqrt(jnp.mean(centred * centred, axis=-1, keepdims=True) + epsilon)
    return centred * spread, spread


def norm_back(grad_scaled, scaled, spread):
    inner = grad_scaled - jnp.mean(grad_scaled, axis=-1, keepdims=True)
    inner = inner - scaled * jnp.mean(grad_scaled * scaled, axis=-1, keepdims=True)
    return inner * spread


class Place:
    def __init__(self, sizes):
        self.n_dp, self.n_ctx, self.n_tp = sizes
        self.n_pair = self.n_tp // 2
        self.dp = lax.axis_index("dp")
        self.ctx = lax.axis_index("ctx")
        self.tp = lax.axis_index("tp")
        self.pair = self.tp // 2
        self.side = self.tp % 2

    def other_dp(self, k):
        d = (self.dp + k) % self.n_dp
        return d, (d, self.ctx, self.tp)

    def other_ctx(self, k):
        z = (self.ctx + k) % self.n_ctx
        return z, (self.dp, z, self.tp)

    def other_pair(self, k):
        p = (self.pair + k) % self.n_pair
        return p, (self.dp, self.ctx, 2 * p + self.side)

    def partner(self):
        return (self.dp, self.ctx, 2 * self.pair + 1 - self.side)

    def barrier(self, far):
        sem = pltpu.get_barrier_semaphore()
        count = 1
        pl.semaphore_signal(sem, inc=1, device_id=self.partner(), device_id_type=MESH)
        if far:
            for size, other in (
                (self.n_dp, self.other_dp),
                (self.n_ctx, self.other_ctx),
                (self.n_pair, self.other_pair),
            ):
                for k in range(1, size):
                    pl.semaphore_signal(sem, inc=1, device_id=other(k)[1], device_id_type=MESH)
                    count += 1
        pl.semaphore_wait(sem, count)


class Sends:
    def __init__(self, sems):
        self.sems = sems
        self.started = []

    def go(self, src, dst, recv_sem, device):
        copy = remote(src, dst, self.sems.at[len(self.started)], recv_sem, device)
        copy.start()
        self.started.append(copy)

    def finish(self):
        for copy in self.started:
            copy.wait_send()


def gather_body(sizes, half, *refs):
    here = Place(sizes)
    n_dp, n_ctx, n_pair = here.n_dp, here.n_ctx, here.n_pair
    d, z, p, c = here.dp, here.ctx, here.pair, here.side
    tokens, out_grad = refs[0:2]
    shards = refs[2:8]
    vec, bias = refs[8:10]
    tok_own, og_own = refs[10:12]
    full = refs[12:18]
    vec_all, bias_all = refs[18:20]
    own_sem, send_sem, rows_sem, line_sem, group_sem, vline_sem, vgroup_sem, bias_sem = refs[20:28]
    own_row = d * n_ctx + z
    mine = p * n_ctx + z
    rows = pl.ds(pl.multiple_of(c * half, half), half)

    here.barrier(True)
    sends = Sends(send_sem)
    own = [
        pltpu.make_async_copy(tokens.at[mine, rows], tok_own.at[z], own_sem.at[0]),
        pltpu.make_async_copy(out_grad.at[mine, rows], og_own.at[z], own_sem.at[1]),
        pltpu.make_async_copy(vec, vec_all.at[own_row], own_sem.at[2]),
        pltpu.make_async_copy(bias, bias_all.at[p], own_sem.at[3]),
    ]
    for a in range(6):
        own.append(pltpu.make_async_copy(shards[a], full[a].at[p, own_row], own_sem.at[4 + a]))
    for copy in own:
        copy.start()

    def send_rows(index, source, target):
        for k in range(1, n_ctx):
            zz, device = here.other_ctx(k)
            sends.go(
                source.at[p * n_ctx + zz, rows], target.at[z], rows_sem.at[index, z], device
            )

    def send_line(a):
        for k in range(1, n_ctx):
            zz, device = here.other_ctx(k)
            sends.go(shards[a], full[a].at[p, own_row], line_sem.at[a, z], device)

    send_rows(0, tokens, tok_own)
    for k in range(1, n_ctx):
        zz, device = here.other_ctx(k)
        sends.go(vec, vec_all.at[own_row], vline_sem.at[z], device)
    for k in range(1, n_pair):
        pp, device = here.other_pair(k)
        sends.go(bias, bias_all.at[p], bias_sem.at[p], device)
    for a in range(6):
        send_line(a)
    send_rows(1, out_grad, og_own)

    for copy in own:
        copy.wait()

    def group(a, pp, dd):
        return full[a].at[pp, pl.ds(dd * n_ctx, n_ctx)]

    def wait_line(a):
        for k in range(1, n_ctx):
            zz, device = here.other_ctx(k)
            slot = full[a].at[p, d * n_ctx + zz]
            remote(slot, slot, send_sem.at[0], line_sem.at[a, zz], device).wait_recv()

    def send_pair(a, dd):
        for k in range(1, n_pair):
            pp, device = here.other_pair(k)
            sends.go(group(a, p, dd), group(a, p, dd), group_sem.at[a, p, dd], device)

    def send_dp(a, pp):
        for k in range(1, n_dp):
            dd, device = here.other_dp(k)
            sends.go(group(a, pp, d), group(a, pp, d), group_sem.at[a, pp, d], device)

    def wait_group(a, pp, dd):
        slot = group(a, pp, dd)
        remote(slot, slot, send_sem.at[0], group_sem.at[a, pp, dd], here.partner()).wait_recv()

    for a in range(6):
        wait_line(a)
        send_dp(a, p)
        send_pair(a, d)
    for k in range(1, n_ctx):
        zz, device = here.other_ctx(k)
        slot = vec_all.at[d * n_ctx + zz]
        remote(slot, slot, send_sem.at[0], vline_sem.at[zz], device).wait_recv()
    for k in range(1, n_dp):
        dd, device = here.other_dp(k)
        slot = vec_all.at[pl.ds(d * n_ctx, n_ctx)]
        sends.go(slot, slot, vgroup_sem.at[d], device)
    pair_first = (True, True, True, True, False, True)
    for a in range(6):
        if pair_first[a]:
            for k in range(1, n_pair):
                pp = here.other_pair(k)[0]
                wait_group(a, pp, d)
                send_dp(a, pp)
        else:
            for k in range(1, n_dp):
                dd = here.other_dp(k)[0]
                wait_group(a, p, dd)
                send_pair(a, dd)
    for a in range(6):
        for k in range(1, n_dp):
            dd = here.other_dp(k)[0]
            if pair_first[a]:
                wait_group(a, p, dd)
            for j in range(1, n_pair):
                wait_group(a, here.other_pair(j)[0], dd)
        if not pair_first[a]:
            for j in range(1, n_pair):
                wait_group(a, here.other_pair(j)[0], d)
    for k in range(1, n_dp):
        dd, device = here.other_dp(k)
        slot = vec_all.at[pl.ds(dd * n_ctx, n_ctx)]
        remote(slot, slot, send_sem.at[0], vgroup_sem.at[dd], device).wait_recv()
    for k in range(1, n_pair):
        pp, device = here.other_pair(k)
        slot = bias_all.at[pp]
        remote(slot, slot, send_sem.at[0], bias_sem.at[pp], device).wait_recv()
    for index, target in ((0, tok_own), (1, og_own)):
        for k in range(1, n_ctx):
            zz, device = here.other_ctx(k)
            slot = target.at[zz]
            remote(slot, slot, send_sem.at[0], rows_sem.at[index, zz], device).wait_recv()
    sends.finish()


def gather_call(sizes, tokens, out_grad, shards, vec, bias):
    n_dp, n_ctx, n_tp = sizes
    n_pair = n_tp // 2
    seqs, block, width = tokens.shape
    half = block // 2
    any_spec = pl.BlockSpec(memory_space=pl.ANY)
    vmem_spec = pl.BlockSpec(memory_space=pltpu.VMEM)
    own = jax.ShapeDtypeStruct((n_ctx, half, width), BF16)
    out_shape = [own, own]
    out_shape += [jax.ShapeDtypeStruct((n_pair, n_dp * n_ctx) + s.shape, BF16) for s in shards]
    out_shape += [
        jax.ShapeDtypeStruct((n_dp * n_ctx,) + vec.shape, F32),
        jax.ShapeDtypeStruct((n_pair,) + bias.shape, F32),
    ]
    n_sends = (
        2 * (n_ctx - 1)
        + (n_ctx - 1)
        + (n_pair - 1)
        + 6 * (n_ctx - 1)
        + (n_dp - 1)
        + 6 * ((n_dp - 1) + (n_pair - 1) + (n_dp - 1) * (n_pair - 1))
    )
    dma = pltpu.SemaphoreType.DMA
    return pl.pallas_call(
        functools.partial(gather_body, sizes, half),
        out_shape=out_shape,
        in_specs=[any_spec] * 10,
        out_specs=[vmem_spec] * 10,
        scratch_shapes=[
            dma((10,)),
            dma((n_sends,)),
            dma((2, n_ctx)),
            dma((6, n_ctx)),
            dma((6, n_pair, n_dp)),
            dma((n_ctx,)),
            dma((n_dp,)),
            dma((n_pair,)),
        ],
        compiler_params=pltpu.CompilerParams(
            collective_id=0, has_side_effects=True, vmem_limit_bytes=VMEM_LIMIT
        ),
    )(tokens, out_grad, *shards, vec, bias)


def compute_body(sizes, *refs):
    here = Place(sizes)
    n_ctx, n_pair = here.n_ctx, here.n_pair
    c = here.side
    (tok, og, gq, gk, gv, go, gu, gd, vecs, bias) = refs[:10]
    (lo, tg, dwq, dwk, dwv, dwo, dwu, dwd, small) = refs[10:19]
    (
        xn1, wqkv, wo, qs, ks, vs, o32, mixed, hid, xn2, ogf, act, ug, bg, dm,
        dka, dva, dqkv, tra, trb, part, ssend, srecv, p_first, send_sem, recv_sem,
    ) = refs[19 : 19 + 23] + (refs[42 : 42 + n_ctx],) + refs[42 + n_ctx :]
    half, width = tok.shape[1], tok.shape[2]
    block = 2 * half
    cols = gq.shape[2]
    hw = n_pair * cols
    fw = gu.shape[2]
    lanes = 2 * HEAD_DIM
    n_twos = hw // lanes
    partner = here.partner()
    scale = HEAD_DIM ** -0.5
    first_head = lax.broadcasted_iota(jnp.int32, (1, lanes), 1) < HEAD_DIM
    zero16 = jnp.zeros((), BF16)

    def own_rows(b):
        return pl.ds(pl.multiple_of(b * block + c * half, half), half)

    def far_rows(b):
        return pl.ds(pl.multiple_of(b * block + (1 - c) * half, half), half)

    def block_rows(b):
        return pl.ds(pl.multiple_of(b * block, block), block)

    def exchange(stage, b, src, dst):
        return remote(src, dst, send_sem.at[stage, b], recv_sem.at[stage, b], partner)

    def rows_copy(stage, b, ref):
        return exchange(stage, b, ref.at[own_rows(b)], ref.at[own_rows(b)])

    def rows_arrive(stage, b, ref):
        exchange(stage, b, ref.at[far_rows(b)], ref.at[far_rows(b)]).wait_recv()

    def part_copy(stage, slot, b):
        return exchange(stage, b, ssend.at[slot, b], srecv.at[slot, b])

    here.barrier(False)

    gain_one, shift_one, out_shift = vecs[0:1, :], vecs[1:2, :], vecs[2:3, :]
    gain_two, shift_two, down_shift = vecs[3:4, :], vecs[4:5, :], vecs[5:6, :]

    @pl.loop(0, n_ctx)
    def _(b):
        exchange(0, b, og.at[b], ogf.at[own_rows(b)]).start()
        ogf[own_rows(b), :] = og[b]
        scaled, _ = normalize(tok[b].astype(F32))
        xn1[own_rows(b), :] = (scaled * gain_one + shift_one).astype(BF16)
        rows_copy(1, b, xn1).start()

    for i in range(n_pair):
        at = slice(i * cols, (i + 1) * cols)
        wqkv[:, i * cols : (i + 1) * cols] = gq[i]
        wqkv[:, hw + i * cols : hw + (i + 1) * cols] = gk[i]
        wqkv[:, 2 * hw + i * cols : 2 * hw + (i + 1) * cols] = gv[i]
        wo[:, at] = go[i]
    q_shift = bias[0, 0:1, :hw]
    v_shift = bias[0, 1:2, :hw]
    for i in range(1, n_pair):
        q_shift = q_shift + bias[i, 0:1, :hw]
        v_shift = v_shift + bias[i, 1:2, :hw]

    @pl.loop(0, n_ctx)
    def _(b):
        rows_arrive(1, b, xn1)
        product = nn_dot(xn1[block_rows(b), :], wqkv[...])
        qs[block_rows(b), :] = (product[:, :hw] + q_shift).astype(BF16) * jnp.asarray(scale, BF16)
        ks[block_rows(b), :] = product[:, hw : 2 * hw].astype(BF16)
        vs[block_rows(b), :] = (product[:, 2 * hw :] + v_shift).astype(BF16)

    for b in range(n_ctx):
        reach = (b + 1) * block
        here_rows = slice(b * block, (b + 1) * block)

        @pl.loop(0, n_twos)
        def _(j):
            at = pl.ds(pl.multiple_of(j * lanes, lanes), lanes)
            queries, keys, values = qs[here_rows, at], ks[:reach, at], vs[:reach, at]
            pieces = []
            for e in range(2):
                head = first_head if e == 0 else jnp.logical_not(first_head)
                scores = nt_dot(jnp.where(head, queries, zero16), keys)
                powers = jnp.exp(scores - jnp.max(scores, axis=-1, keepdims=True))
                inverse = 1.0 / jnp.sum(powers, axis=-1, keepdims=True)
                probs = (powers * inverse).astype(BF16)
                p_first[b][2 * j + e] = probs
                pieces.append(nn_dot(probs, values))
            out = jnp.where(first_head, pieces[0], pieces[1])
            o32[here_rows, at] = out
            mixed[here_rows, at] = out.astype(BF16)

        ssend[0, b] = nt_dot(mixed[far_rows(b), :], wo[...]).astype(BF16)
        part_copy(2, 0, b).start()
        hid[b] = nt_dot(mixed[own_rows(b), :], wo[...])

    @pl.loop(0, n_ctx)
    def _(b):
        part_copy(2, 0, b).wait()
        hidden = tok[b].astype(F32) + (hid[b] + srecv[0, b].astype(F32)) + out_shift
        hid[b] = hidden
        scaled, _ = normalize(hidden)
        xn2[own_rows(b), :] = (scaled * gain_two + shift_two).astype(BF16)
        rows_copy(3, b, xn2).start()

    small[...] = jnp.zeros_like(small)

    @pl.loop(0, n_ctx)
    def _(b):
        rows_arrive(0, b, ogf)
        rows_arrive(3, b, xn2)
        normed = xn2[block_rows(b), :]
        grads = ogf[block_rows(b), :]
        for i in range(n_pair):
            upward = nn_dot(normed, gu[i]) + bias[i, 2:3, :]
            big_phi = 0.5 + 0.5 * lax.erf(upward * root_half)
            act[i, block_rows(b), :] = (upward * big_phi).astype(BF16)
            slope = big_phi + upward * density_scale * jnp.exp(-0.5 * upward * upward)
            rows_grad = (nn_dot(grads, gd[i]) * slope).astype(BF16)
            ug[i, block_rows(b), :] = rows_grad
            small[8 + i : 9 + i, :] += jnp.sum(rows_grad.astype(F32), axis=0, keepdims=True)

        def through(ref, weight, rows):
            total = nt_dot(ref[0, rows, :], weight[0])
            for i in range(1, n_pair):
                total = total + nt_dot(ref[i, rows, :], weight[i])
            return total

        ssend[1, b] = through(act, gd, far_rows(b)).astype(BF16)
        part_copy(4, 1, b).start()
        ssend[0, b] = through(ug, gu, far_rows(b)).astype(BF16)
        part_copy(5, 0, b).start()
        part[0, b] = through(act, gd, own_rows(b))
        part[1, b] = through(ug, gu, own_rows(b))

    def transposed(ref, out):
        for b in range(n_ctx):
            out[:, b * block : (b + 1) * block] = ref[b * block : (b + 1) * block, :].T

    @pl.loop(0, n_ctx)
    def _(b):
        part_copy(4, 1, b).wait()
        lo[b] = (hid[b] + (part[0, b] + srecv[1, b].astype(F32)) + down_shift).astype(BF16)
        part_copy(5, 0, b).wait()
        grad_two = part[1, b] + srecv[0, b].astype(F32)
        scaled, spread = normalize(hid[b])
        own_grad = og[b].astype(F32)
        hidden_grad = own_grad + norm_back(grad_two * gain_two, scaled, spread)
        hid[b] = hidden_grad
        branch = hidden_grad.astype(BF16)
        bg[own_rows(b), :] = branch
        rows_copy(6, b, bg).start()
        small[2:3, :] += jnp.sum(branch.astype(F32), axis=0, keepdims=True)
        small[3:4, :] += jnp.sum(grad_two * scaled, axis=0, keepdims=True)
        small[4:5, :] += jnp.sum(grad_two, axis=0, keepdims=True)
        small[5:6, :] += jnp.sum(own_grad, axis=0, keepdims=True)

    transposed(xn2, tra)
    transposed(ogf, trb)
    step = 256

    @pl.loop(0, width // step)
    def _(r):
        rows = pl.ds(pl.multiple_of(r * step, step), step)
        for i in range(n_pair):
            dwu[i, rows, :] = nn_dot(tra[rows, :], ug[i]).astype(BF16)
            dwd[i, rows, :] = nn_dot(trb[rows, :], act[i]).astype(BF16)

    @pl.loop(0, n_ctx)
    def _(b):
        rows_arrive(6, b, bg)
        dm[block_rows(b), :] = nn_dot(bg[block_rows(b), :], wo[...]).astype(BF16)

    transposed(bg, trb)

    @pl.loop(0, width // step)
    def _(r):
        rows = pl.ds(pl.multiple_of(r * step, step), step)
        product = nn_dot(trb[rows, :], mixed[...])
        for i in range(n_pair):
            dwo[i, rows, :] = product[:, i * cols : (i + 1) * cols].astype(BF16)

    for b in reversed(range(n_ctx)):
        reach = (b + 1) * block
        here_rows = slice(b * block, (b + 1) * block)

        @pl.loop(0, n_twos)
        def _(j):
            at = pl.ds(pl.multiple_of(j * lanes, lanes), lanes)
            queries, keys, values = qs[here_rows, at], ks[:reach, at], vs[:reach, at]
            mix_grad, mix = dm[here_rows, at], o32[here_rows, at]
            towards = mix_grad.astype(F32) * mix
            query_parts, key_sum, value_sum = [], None, None
            for e in range(2):
                head = first_head if e == 0 else jnp.logical_not(first_head)
                grad_head = jnp.where(head, mix_grad, zero16)
                prob_grad = nt_dot(grad_head, values)
                centre = jnp.sum(jnp.where(head, towards, 0.0), axis=-1, keepdims=True)
                probs = p_first[b][2 * j + e]
                score_grad = (probs.astype(F32) * (prob_grad - centre)).astype(BF16)
                query_parts.append(nn_dot(score_grad, keys))
                key_term = tn_dot(score_grad, jnp.where(head, queries, zero16))
                value_term = tn_dot(probs, grad_head)
                key_sum = key_term if key_sum is None else key_sum + key_term
                value_sum = value_term if value_sum is None else value_sum + value_term
            query_grad = jnp.where(first_head, query_parts[0], query_parts[1]) * scale
            dqkv[here_rows, at] = query_grad.astype(BF16)
            if b == n_ctx - 1:
                dka[:, at] = key_sum
                dva[:, at] = value_sum
            else:
                dka[:reach, at] += key_sum
                dva[:reach, at] += value_sum

    @pl.loop(0, n_ctx)
    def _(b):
        dqkv[block_rows(b), hw : 2 * hw] = dka[block_rows(b), :].astype(BF16)
        dqkv[block_rows(b), 2 * hw :] = dva[block_rows(b), :].astype(BF16)
        small[6:7, :hw] += jnp.sum(dqkv[block_rows(b), :hw].astype(F32), axis=0, keepdims=True)
        small[7:8, :hw] += jnp.sum(dqkv[block_rows(b), 2 * hw :].astype(F32), axis=0, keepdims=True)
        ssend[1, b] = nt_dot(dqkv[far_rows(b), :], wqkv[...]).astype(BF16)
        part_copy(7, 1, b).start()
        part[0, b] = nt_dot(dqkv[own_rows(b), :], wqkv[...])

    transposed(xn1, tra)

    @pl.loop(0, width // step)
    def _(r):
        rows = pl.ds(pl.multiple_of(r * step, step), step)
        product = nn_dot(tra[rows, :], dqkv[...])
        for i in range(n_pair):
            dwq[i, rows, :] = product[:, i * cols : (i + 1) * cols].astype(BF16)
            dwk[i, rows, :] = product[:, hw + i * cols : hw + (i + 1) * cols].astype(BF16)
            dwv[i, rows, :] = product[:, 2 * hw + i * cols : 2 * hw + (i + 1) * cols].astype(BF16)

    @pl.loop(0, n_ctx)
    def _(b):
        part_copy(7, 1, b).wait()
        grad_one = part[0, b] + srecv[1, b].astype(F32)
        scaled, spread = normalize(tok[b].astype(F32))
        tg[b] = (hid[b] + norm_back(grad_one * gain_one, scaled, spread)).astype(BF16)
        small[0:1, :] += jnp.sum(grad_one * scaled, axis=0, keepdims=True)
        small[1:2, :] += jnp.sum(grad_one, axis=0, keepdims=True)
        exchange(0, b, og.at[b], ogf.at[own_rows(b)]).wait_send()
        rows_copy(1, b, xn1).wait_send()
        rows_copy(3, b, xn2).wait_send()
        rows_copy(6, b, bg).wait_send()


def compute_call(sizes, tok, og, weights, vecs, bias):
    n_dp, n_ctx, n_tp = sizes
    n_pair = n_tp // 2
    half, width = tok.shape[1:]
    block = 2 * half
    length = n_ctx * block
    cols = weights[0].shape[2]
    hw = n_pair * cols
    fw = weights[4].shape[2]
    heads = hw // HEAD_DIM
    vmem_spec = pl.BlockSpec(memory_space=pltpu.VMEM)
    shape = jax.ShapeDtypeStruct
    out_shape = [
        shape(tok.shape, BF16),
        shape(tok.shape, BF16),
    ]
    out_shape += [shape(w.shape, BF16) for w in weights]
    out_shape += [shape((16, width), F32)]
    vm = pltpu.VMEM
    scratch = [
        vm((length, width), BF16),
        vm((width, 3 * hw), BF16),
        vm((width, hw), BF16),
        vm((length, hw), BF16),
        vm((length, hw), BF16),
        vm((length, hw), BF16),
        vm((length, hw), F32),
        vm((length, hw), BF16),
        vm((n_ctx, half, width), F32),
        vm((length, width), BF16),
        vm((length, width), BF16),
        vm((n_pair, length, fw), BF16),
        vm((n_pair, length, fw), BF16),
        vm((length, width), BF16),
        vm((length, hw), BF16),
        vm((length, hw), F32),
        vm((length, hw), F32),
        vm((length, 3 * hw), BF16),
        vm((width, length), BF16),
        vm((width, length), BF16),
        vm((2, n_ctx, half, width), F32),
        vm((2, n_ctx, half, width), BF16),
        vm((2, n_ctx, half, width), BF16),
    ]
    scratch += [vm((heads, block, (b + 1) * block), BF16) for b in range(n_ctx)]
    scratch += [pltpu.SemaphoreType.DMA((8, n_ctx)), pltpu.SemaphoreType.DMA((8, n_ctx))]
    return pl.pallas_call(
        functools.partial(compute_body, sizes),
        out_shape=out_shape,
        in_specs=[vmem_spec] * 10,
        out_specs=[vmem_spec] * 9,
        scratch_shapes=scratch,
        compiler_params=pltpu.CompilerParams(
            collective_id=1, has_side_effects=True, vmem_limit_bytes=VMEM_LIMIT
        ),
    )(tok, og, *weights, vecs, bias)


def scatter_body(sizes, half, *refs):
    here = Place(sizes)
    n_dp, n_ctx, n_pair = here.n_dp, here.n_ctx, here.n_pair
    d, z, p, c = here.dp, here.ctx, here.pair, here.side
    rows_in = refs[0:2]
    grads = refs[2:8]
    small = refs[8]
    rows_out = refs[9:11]
    owned = refs[11:17]
    small_out = refs[17]
    it = iter(refs[18:])
    dp_land = [next(it) for _ in range(6)]
    dp_sum = [next(it) for _ in range(6)]
    keep = [next(it) for _ in range(6)]
    pair_land = [next(it) for _ in range(6)]
    pair_sum = [next(it) for _ in range(6)]
    ctx_land = [next(it) for _ in range(6)]
    side_land, small_b, ctx_small, small_c, pair_small, small_d, dp_small = [next(it) for _ in range(7)]
    own_sem, send_sem, line_sem, far_sem, side_sem, dp_sem, pair_sem, ctx_sem, small_sem = it
    mine = p * n_ctx + z
    rows = pl.ds(pl.multiple_of(c * half, half), half)

    here.barrier(True)
    sends = Sends(send_sem)

    for a in range(6):
        for k in range(1, n_dp):
            dd, device = here.other_dp(k)
            sends.go(
                grads[a].at[:, pl.ds(dd * n_ctx, n_ctx)],
                dp_land[a].at[k - 1],
                dp_sem.at[a, k - 1],
                device,
            )
    own = []
    for i in range(2):
        for k in range(1, n_ctx):
            zz, device = here.other_ctx(k)
            sends.go(rows_in[i].at[zz], rows_out[i].at[mine, rows], line_sem.at[i, z], device)
        own.append(pltpu.make_async_copy(rows_in[i].at[z], rows_out[i].at[mine, rows], own_sem.at[i]))
        own[-1].start()
    sends.go(small.at[pl.ds(0, 8)], side_land, small_sem.at[0, 0], here.partner())

    def small_arrive(stage, k, land):
        remote(land, land, send_sem.at[0], small_sem.at[stage, k - 1], here.partner()).wait_recv()

    for i in range(2):
        own[i].wait()
        for k in range(1, n_ctx):
            zz, device = here.other_ctx(k)
            slot = rows_out[i].at[p * n_ctx + zz, rows]
            remote(slot, slot, send_sem.at[0], line_sem.at[i, zz], device).wait_recv()
        for k in range(1, n_pair):
            pp, device = here.other_pair(k)
            slot = rows_out[i].at[pl.ds(p * n_ctx, n_ctx), rows]
            sends.go(slot, slot, far_sem.at[i, p], device)

    small_arrive(0, 1, side_land)
    small_b[0:8, :] = small[0:8, :] + side_land[...]
    small_b[8:16, :] = small[8:16, :]
    small_b[6:8, :] = small[6:8, :]
    for k in range(1, n_ctx):
        zz, device = here.other_ctx(k)
        sends.go(small_b, ctx_small.at[k - 1], small_sem.at[1, k - 1], device)

    for a in range(6):
        for k in range(1, n_dp):
            remote(
                dp_land[a].at[k - 1], dp_land[a].at[k - 1], send_sem.at[0], dp_sem.at[a, k - 1],
                here.partner(),
            ).wait_recv()
        for i in range(n_pair):
            total = grads[a][i, pl.ds(d * n_ctx, n_ctx)].astype(F32)
            for k in range(1, n_dp):
                total = total + dp_land[a][k - 1, i].astype(F32)
            dp_sum[a][i] = total.astype(BF16)
        for k in range(1, n_pair):
            pp, device = here.other_pair(k)
            sends.go(dp_sum[a].at[pp], pair_land[a].at[k - 1], pair_sem.at[a, k - 1], device)

    total = small_b[...]
    for k in range(1, n_ctx):
        small_arrive(1, k, ctx_small.at[k - 1])
        total = total + ctx_small[k - 1]
    small_c[...] = total
    for k in range(1, n_pair):
        pp, device = here.other_pair(k)
        sends.go(small_c, pair_small.at[k - 1], small_sem.at[2, k - 1], device)

    for a in range(6):
        for k in range(1, n_pair):
            remote(
                pair_land[a].at[k - 1], pair_land[a].at[k - 1], send_sem.at[0], pair_sem.at[a, k - 1],
                here.partner(),
            ).wait_recv()
        total = dp_sum[a][p].astype(F32)
        for k in range(1, n_pair):
            total = total + pair_land[a][k - 1].astype(F32)
        keep[a][...] = total
        pair_sum[a][...] = total.astype(BF16)
        for k in range(1, n_ctx):
            zz, device = here.other_ctx(k)
            sends.go(pair_sum[a].at[zz], ctx_land[a].at[k - 1], ctx_sem.at[a, k - 1], device)

    total = small_c[...]
    for k in range(1, n_pair):
        small_arrive(2, k, pair_small.at[k - 1])
        total = total + pair_small[k - 1]
    small_d[...] = total
    for k in range(1, n_dp):
        dd, device = here.other_dp(k)
        sends.go(small_d, dp_small.at[k - 1], small_sem.at[3, k - 1], device)

    for i in range(2):
        for k in range(1, n_pair):
            pp, device = here.other_pair(k)
            slot = rows_out[i].at[pl.ds(pp * n_ctx, n_ctx), rows]
            remote(slot, slot, send_sem.at[0], far_sem.at[i, pp], device).wait_recv()
        slot = rows_out[i].at[:, rows]
        sends.go(slot, slot, side_sem.at[i], here.partner())

    for a in range(6):
        total = keep[a][z]
        for k in range(1, n_ctx):
            remote(
                ctx_land[a].at[k - 1], ctx_land[a].at[k - 1], send_sem.at[0], ctx_sem.at[a, k - 1],
                here.partner(),
            ).wait_recv()
            total = total + ctx_land[a][k - 1].astype(F32)
        owned[a][...] = total

    total = small_d[...]
    for k in range(1, n_dp):
        small_arrive(3, k, dp_small.at[k - 1])
        total = total + dp_small[k - 1]
    small_out[...] = total
    other = pl.ds(pl.multiple_of((1 - c) * half, half), half)
    for i in range(2):
        slot = rows_out[i].at[:, other]
        remote(slot, slot, send_sem.at[0], side_sem.at[i], here.partner()).wait_recv()
    sends.finish()


def scatter_call(sizes, seqs, lo, tg, grads, small):
    n_dp, n_ctx, n_tp = sizes
    n_pair = n_tp // 2
    half, width = lo.shape[1:]
    vmem_spec = pl.BlockSpec(memory_space=pltpu.VMEM)
    shape = jax.ShapeDtypeStruct
    vm = pltpu.VMEM
    tail = [g.shape[2:] for g in grads]
    out_shape = [shape((seqs, 2 * half, width), BF16)] * 2
    out_shape += [shape(t, F32) for t in tail]
    out_shape += [shape(small.shape, F32)]
    scratch = [vm((n_dp - 1, n_pair, n_ctx) + t, BF16) for t in tail]
    scratch += [vm((n_pair, n_ctx) + t, BF16) for t in tail]
    scratch += [vm((n_ctx,) + t, F32) for t in tail]
    scratch += [vm((n_pair - 1, n_ctx) + t, BF16) for t in tail]
    scratch += [vm((n_ctx,) + t, BF16) for t in tail]
    scratch += [vm((n_ctx - 1,) + t, BF16) for t in tail]
    scratch += [
        vm((8, width), F32),
        vm((16, width), F32),
        vm((n_ctx - 1, 16, width), F32),
        vm((16, width), F32),
        vm((n_pair - 1, 16, width), F32),
        vm((16, width), F32),
        vm((n_dp - 1, 16, width), F32),
    ]
    n_sends = (
        6 * ((n_dp - 1) + (n_pair - 1) + (n_ctx - 1))
        + 2 * ((n_ctx - 1) + (n_pair - 1) + 1)
        + 1 + (n_ctx - 1) + (n_pair - 1) + (n_dp - 1)
    )
    dma = pltpu.SemaphoreType.DMA
    most = max(n_dp, n_ctx, n_pair)
    scratch += [
        dma((2,)),
        dma((n_sends,)),
        dma((2, n_ctx)),
        dma((2, n_pair)),
        dma((2,)),
        dma((6, n_dp - 1)),
        dma((6, n_pair - 1)),
        dma((6, n_ctx - 1)),
        dma((4, most)),
    ]
    return pl.pallas_call(
        functools.partial(scatter_body, sizes, half),
        out_shape=out_shape,
        in_specs=[vmem_spec] * 9,
        out_specs=[vmem_spec] * 9,
        scratch_shapes=scratch,
        compiler_params=pltpu.CompilerParams(
            collective_id=2, has_side_effects=True, vmem_limit_bytes=VMEM_LIMIT
        ),
    )(lo, tg, *grads, small)


def fused_body(sizes, dims, *refs):
    here = Place(sizes)
    n_dp, n_ctx, n_pair = here.n_dp, here.n_ctx, here.n_pair
    d, z, p, c = here.dp, here.ctx, here.pair, here.side
    half, width, share, cols, fw = dims
    block = 2 * half
    hw = n_pair * cols
    lanes = 2 * HEAD_DIM
    n_twos = hw // lanes
    n_rows = n_dp * n_ctx
    two = n_ctx // 2
    it = iter(refs)

    def take(n):
        return [next(it) for _ in range(n)]

    tokens, out_grad, pack = take(3)
    shards = take(3)
    rows_out = take(2)
    owned = take(3)
    small_out = next(it)
    full = take(3)
    pack_all, vecs, cold = take(3)
    tok, og, lo, tg = take(4)
    (
        xn1, wqkv, wo, qs, ks, vs, o32, mixed, hid, xn2, ogf, act, ug, bg, dm, dqkv, tra, trb,
        wide, ssend, srecv, dwd, small,
    ) = take(23)
    p_first = take(n_ctx)
    dp_one, pair_one, pair_two, dp_two, ctx_land = take(3), take(3), take(3), take(3), take(3)
    side_land, small_b, ctx_small, small_c, pair_small, small_d, dp_small = take(7)
    (
        own_sem, put_sem, rows_sem, line_sem, pair_sem, dp_sem, diag_dp_sem, diag_pair_sem, swap_send,
        swap_recv, scatter_sem, ctx_sem, out_line, out_pair, out_side, small_sem,
    ) = take(16)
    partner = here.partner()
    own_row = d * n_ctx + z
    mine = p * n_ctx + z
    scale = HEAD_DIM ** -0.5
    first_head = lax.broadcasted_iota(jnp.int32, (1, lanes), 1) < HEAD_DIM
    zero16 = jnp.zeros((), BF16)
    side_rows = pl.ds(pl.multiple_of(c * half, half), half)
    sends = Sends(put_sem)

    def arrive(slot, sem):
        remote(slot, slot, put_sem.at[0], sem, partner).wait_recv()

    def shard_rows(r, count=1):
        return pl.ds(pl.multiple_of(r * share, 16), count * share)

    def slot(a, pp, dd, zz, count=1):
        return full[a].at[pp, shard_rows(dd * n_ctx + zz, count)]

    gather_own = [pltpu.make_async_copy(shards[a], slot(a, p, d, z), own_sem.at[a]) for a in range(3)]

    def gather_start(a):
        gather_own[a].start()
        for k in range(1, n_ctx):
            zz, device = here.other_ctx(k)
            sends.go(shards[a], slot(a, p, d, z), line_sem.at[a, z], device)

    def gather_hop(a):
        gather_own[a].wait()
        for k in range(1, n_ctx):
            zz = here.other_ctx(k)[0]
            arrive(slot(a, p, d, zz), line_sem.at[a, zz])
        group = slot(a, p, d, 0, n_ctx)
        for k in range(1, n_pair):
            sends.go(group, group, pair_sem.at[a, p], here.other_pair(k)[1])
        for k in range(1, n_dp):
            sends.go(group, group, dp_sem.at[a, d], here.other_dp(k)[1])

    def gather_turn(a):
        for k in range(1, n_pair):
            pp = here.other_pair(k)[0]
            arrive(slot(a, pp, d, 0, n_ctx), pair_sem.at[a, pp])
            first = slot(a, pp, d, 0, two)
            for j in range(1, n_dp):
                sends.go(first, first, diag_dp_sem.at[a, pp, d], here.other_dp(j)[1])
        for k in range(1, n_dp):
            dd = here.other_dp(k)[0]
            arrive(slot(a, p, dd, 0, n_ctx), dp_sem.at[a, dd])
            second = slot(a, p, dd, two, n_ctx - two)
            for j in range(1, n_pair):
                sends.go(second, second, diag_pair_sem.at[a, p, dd], here.other_pair(j)[1])

    def gather_end(a):
        for k in range(1, n_pair):
            pp = here.other_pair(k)[0]
            for j in range(1, n_dp):
                dd = here.other_dp(j)[0]
                arrive(slot(a, pp, dd, 0, two), diag_dp_sem.at[a, pp, dd])
                arrive(slot(a, pp, dd, two, n_ctx - two), diag_pair_sem.at[a, pp, dd])

    def pack_start():
        pack_own.start()
        for k in range(1, n_ctx):
            sends.go(pack, pack_all.at[p, own_row], line_sem.at[3, z], here.other_ctx(k)[1])

    def pack_hop():
        pack_own.wait()
        for k in range(1, n_ctx):
            zz = here.other_ctx(k)[0]
            arrive(pack_all.at[p, d * n_ctx + zz], line_sem.at[3, zz])
        group = pack_all.at[p, pl.ds(d * n_ctx, n_ctx)]
        for k in range(1, n_pair):
            sends.go(group, group, pair_sem.at[3, p], here.other_pair(k)[1])
        for k in range(1, n_dp):
            sends.go(group, group, dp_sem.at[3, d], here.other_dp(k)[1])

    def pack_end():
        for k in range(1, n_pair):
            pp = here.other_pair(k)[0]
            arrive(pack_all.at[pp, pl.ds(d * n_ctx, n_ctx)], pair_sem.at[3, pp])
        for k in range(1, n_dp):
            dd = here.other_dp(k)[0]
            arrive(pack_all.at[p, pl.ds(dd * n_ctx, n_ctx)], dp_sem.at[3, dd])

    pack_own = pltpu.make_async_copy(pack, pack_all.at[p, own_row], own_sem.at[3])

    rows_own = [
        pltpu.make_async_copy(source.at[mine, side_rows], target.at[z], own_sem.at[4 + i])
        for i, (source, target) in enumerate(((tokens, tok), (out_grad, og)))
    ]

    def rows_start(i, source, target):
        rows_own[i].start()
        for k in range(1, n_ctx):
            zz, device = here.other_ctx(k)
            sends.go(source.at[p * n_ctx + zz, side_rows], target.at[z], rows_sem.at[i, z], device)

    def grad_rows(ref, pp, dd, second):
        return ref.at[pp, shard_rows(dd * n_ctx + (two if second else 0), two)]

    def scatter_start(a, ref):
        for k in range(1, n_dp):
            dd, device = here.other_dp(k)
            for i in range(n_pair):
                sends.go(grad_rows(ref, i, dd, False), dp_one[a].at[k - 1, i], scatter_sem.at[a, 0, k - 1, i], device)
        for k in range(1, n_pair):
            pp, device = here.other_pair(k)
            for i in range(n_dp):
                sends.go(grad_rows(ref, pp, i, True), pair_one[a].at[k - 1, i], scatter_sem.at[a, 1, k - 1, i], device)

    def add_into(target, parts):
        total = target[...].astype(F32)
        for part in parts:
            total = total + part[...].astype(F32)
        target[...] = total.astype(BF16)

    def scatter_turn(a, ref):
        for i in range(n_pair):
            for k in range(1, n_dp):
                arrive(dp_one[a].at[k - 1, i], scatter_sem.at[a, 0, k - 1, i])
            add_into(grad_rows(ref, i, d, False), [dp_one[a].at[k - 1, i] for k in range(1, n_dp)])
        for k in range(1, n_pair):
            pp, device = here.other_pair(k)
            sends.go(grad_rows(ref, pp, d, False), pair_two[a].at[k - 1], scatter_sem.at[a, 2, k - 1, 0], device)
        for i in range(n_dp):
            for k in range(1, n_pair):
                arrive(pair_one[a].at[k - 1, i], scatter_sem.at[a, 1, k - 1, i])
            add_into(grad_rows(ref, p, i, True), [pair_one[a].at[k - 1, i] for k in range(1, n_pair)])
        for k in range(1, n_dp):
            dd, device = here.other_dp(k)
            sends.go(grad_rows(ref, p, dd, True), dp_two[a].at[k - 1], scatter_sem.at[a, 3, k - 1, 0], device)

    def scatter_line(a, ref):
        for k in range(1, n_pair):
            arrive(pair_two[a].at[k - 1], scatter_sem.at[a, 2, k - 1, 0])
        add_into(grad_rows(ref, p, d, False), [pair_two[a].at[k - 1] for k in range(1, n_pair)])
        for k in range(1, n_dp):
            arrive(dp_two[a].at[k - 1], scatter_sem.at[a, 3, k - 1, 0])
        add_into(grad_rows(ref, p, d, True), [dp_two[a].at[k - 1] for k in range(1, n_dp)])
        for k in range(1, n_ctx):
            zz, device = here.other_ctx(k)
            sends.go(ref.at[p, shard_rows(d * n_ctx + zz)], ctx_land[a].at[k - 1], ctx_sem.at[a, k - 1], device)

    def scatter_end(a, ref):
        total = ref[p, shard_rows(own_row), :].astype(F32)
        for k in range(1, n_ctx):
            arrive(ctx_land[a].at[k - 1], ctx_sem.at[a, k - 1])
            total = total + ctx_land[a][k - 1].astype(F32)
        owned[a][...] = total

    def out_slot(i, s, rows):
        return rows_out[i].at[s, rows]

    def out_start(i, source):
        for k in range(1, n_ctx):
            zz, device = here.other_ctx(k)
            sends.go(source.at[zz], out_slot(i, mine, side_rows), out_line.at[i, z], device)
        copy = pltpu.make_async_copy(source.at[z], out_slot(i, mine, side_rows), own_sem.at[6 + i])
        copy.start()
        return copy

    def out_pass(i, s):
        piece = out_slot(i, s, side_rows)
        for j in range(1, n_pair):
            sends.go(piece, piece, out_pair.at[i, s], here.other_pair(j)[1])
        sends.go(piece, piece, out_side.at[i, s], partner)

    def out_hop(i, copy):
        copy.wait()
        out_pass(i, mine)
        for k in range(1, n_ctx):
            zz = here.other_ctx(k)[0]
            s = p * n_ctx + zz
            arrive(out_slot(i, s, side_rows), out_line.at[i, zz])
            out_pass(i, s)

    def out_cross(i):
        for j in range(1, n_pair):
            pp = here.other_pair(j)[0]
            for k in range(n_ctx):
                s = pp * n_ctx + (z + k) % n_ctx
                piece = out_slot(i, s, side_rows)
                arrive(piece, out_pair.at[i, s])
                sends.go(piece, piece, out_side.at[i, s], partner)

    far_side = pl.ds(pl.multiple_of((1 - c) * half, half), half)

    def out_end(i):
        for s in range(n_pair * n_ctx):
            arrive(out_slot(i, s, far_side), out_side.at[i, s])

    def own_rows(b):
        return pl.ds(pl.multiple_of(b * block + c * half, half), half)

    def far_rows(b):
        return pl.ds(pl.multiple_of(b * block + (1 - c) * half, half), half)

    def block_rows(b):
        return pl.ds(pl.multiple_of(b * block, block), block)

    def swap(stage, b, src, dst):
        return remote(src, dst, swap_send.at[stage, b], swap_recv.at[stage, b], partner)

    def rows_copy(stage, b, ref):
        return swap(stage, b, ref.at[own_rows(b)], ref.at[own_rows(b)])

    def rows_arrive(stage, b, ref):
        swap(stage, b, ref.at[far_rows(b)], ref.at[far_rows(b)]).wait_recv()

    def part_copy(stage, place, b):
        return swap(stage, b, ssend.at[place, b], srecv.at[place, b])

    def part_store(i, b, value):
        wide[i, pl.ds(pl.multiple_of(b * block, block), half), :] = value[:, :hw]
        wide[i, pl.ds(pl.multiple_of(b * block + half, half), half), :] = value[:, hw:]

    def part_load(i, b):
        left = wide[i, pl.ds(pl.multiple_of(b * block, block), half), :]
        right = wide[i, pl.ds(pl.multiple_of(b * block + half, half), half), :]
        return jnp.concatenate([left, right], axis=1)

    here.barrier(True)
    gather_start(0)
    pack_start()
    rows_start(0, tokens, tok)
    gather_start(1)
    gather_start(2)
    rows_start(1, out_grad, og)

    small[...] = jnp.zeros_like(small)
    gather_hop(0)
    pack_hop()
    pack_end()
    for r in range(n_rows):
        own_part = pack_all[p, r]
        vecs[0:8, r * share : (r + 1) * share] = own_part[0:8, :share]
    for i in range(n_pair):
        piece = pack_all[i, d * n_ctx]
        for line in range(2):
            for w in range(0, cols, 128):
                n = min(128, cols - w)
                row = 6 + 2 * line + w // 128
                cold[line : line + 1, i * cols + w : i * cols + w + n] = piece[row : row + 1, :n]
        for w in range(0, fw, 128):
            row = 10 + w // 128
            cold[2 + i : 3 + i, w : w + 128] = piece[row : row + 1, :]
    gain_one, shift_one, out_shift = vecs[0:1, :], vecs[1:2, :], vecs[2:3, :]
    gain_two, shift_two, down_shift = vecs[3:4, :], vecs[4:5, :], vecs[5:6, :]

    rows_own[0].wait()
    for k in range(n_ctx):
        b = (z + k) % n_ctx
        if k > 0:
            arrive(tok.at[b], rows_sem.at[0, b])
        scaled, _ = normalize(tok[b].astype(F32))
        xn1[own_rows(b), :] = (scaled * gain_one + shift_one).astype(BF16)
        rows_copy(1, b, xn1).start()

    gather_turn(0)
    gather_end(0)
    for i in range(n_pair):
        for a, base in enumerate((0, hw, 2 * hw)):
            wqkv[:, base + i * cols : base + (i + 1) * cols] = full[0][i, :, a * cols : (a + 1) * cols]
        wo[:, i * cols : (i + 1) * cols] = full[0][i, :, 3 * cols : 4 * cols]
    gather_hop(1)
    q_shift, v_shift = cold[0:1, :hw], cold[1:2, :hw]

    @pl.loop(0, n_ctx)
    def _(b):
        rows_arrive(1, b, xn1)
        product = nn_dot(xn1[block_rows(b), :], wqkv[...])
        qs[block_rows(b), :] = (product[:, :hw] + q_shift).astype(BF16) * jnp.asarray(scale, BF16)
        ks[block_rows(b), :] = product[:, hw : 2 * hw].astype(BF16)
        vs[block_rows(b), :] = (product[:, 2 * hw :] + v_shift).astype(BF16)

    gather_hop(2)

    for b in range(n_ctx):
        reach = (b + 1) * block
        here_rows = slice(b * block, (b + 1) * block)

        @pl.loop(0, n_twos)
        def _(j):
            at = pl.ds(pl.multiple_of(j * lanes, lanes), lanes)
            queries, keys, values = qs[here_rows, at], ks[:reach, at], vs[:reach, at]
            pieces = []
            for e in range(2):
                head = first_head if e == 0 else jnp.logical_not(first_head)
                scores = nt_dot(jnp.where(head, queries, zero16), keys)
                powers = jnp.exp(scores - jnp.max(scores, axis=-1, keepdims=True))
                inverse = 1.0 / jnp.sum(powers, axis=-1, keepdims=True)
                probs = (powers * inverse).astype(BF16)
                p_first[b][2 * j + e] = probs
                pieces.append(nn_dot(probs, values))
            out = jnp.where(first_head, pieces[0], pieces[1])
            o32[here_rows, at] = out
            mixed[here_rows, at] = out.astype(BF16)

        ssend[0, b] = nt_dot(mixed[far_rows(b), :], wo[...]).astype(BF16)
        part_copy(2, 0, b).start()
        hid[b] = nt_dot(mixed[own_rows(b), :], wo[...])
        if b == 2:
            gather_turn(1)

    gather_end(1)
    gather_turn(2)

    @pl.loop(0, n_ctx)
    def _(b):
        part_copy(2, 0, b).wait()
        hidden = tok[b].astype(F32) + (hid[b] + srecv[0, b].astype(F32)) + out_shift
        hid[b] = hidden
        scaled, _ = normalize(hidden)
        xn2[own_rows(b), :] = (scaled * gain_two + shift_two).astype(BF16)
        rows_copy(3, b, xn2).start()

    rows_own[1].wait()
    for k in range(n_ctx):
        b = (z + k) % n_ctx
        if k > 0:
            arrive(og.at[b], rows_sem.at[1, b])
        ogf[own_rows(b), :] = og[b]
        swap(0, b, og.at[b], ogf.at[own_rows(b)]).start()

    @pl.loop(0, n_ctx)
    def _(b):
        rows_arrive(3, b, xn2)
        normed = xn2[block_rows(b), :]
        for i in range(n_pair):
            upward = nn_dot(normed, full[1][i]) + cold[2 + i : 3 + i, :fw]
            big_phi = 0.5 + 0.5 * lax.erf(upward * root_half)
            act[i, block_rows(b), :] = (upward * big_phi).astype(BF16)
            slope = big_phi + upward * density_scale * jnp.exp(-0.5 * upward * upward)
            ug[i, block_rows(b), :] = slope.astype(BF16)
        rows_arrive(0, b, ogf)

    step = 256

    def transposed(ref, out):
        for b in range(n_ctx):
            out[:, b * block : (b + 1) * block] = ref[b * block : (b + 1) * block, :].T

    transposed(ogf, trb)

    @pl.loop(0, width // step)
    def _(r):
        rows = pl.ds(pl.multiple_of(r * step, step), step)
        for i in range(n_pair):
            dwd[i, rows, :] = nn_dot(trb[rows, :], act[i]).astype(BF16)

    gathered = len(sends.started)
    scatter_start(2, dwd)
    gather_end(2)

    def through(ref, weight, rows):
        total = nt_dot(ref[0, rows, :], weight[0])
        for i in range(1, n_pair):
            total = total + nt_dot(ref[i, rows, :], weight[i])
        return total

    @pl.loop(0, n_ctx)
    def _(b):
        grads = ogf[block_rows(b), :]
        for i in range(n_pair):
            slope = ug[i, block_rows(b), :].astype(F32)
            rows_grad = (nn_dot(grads, full[2][i]) * slope).astype(BF16)
            ug[i, block_rows(b), :] = rows_grad
            small[8 + i : 9 + i, :] += jnp.sum(rows_grad.astype(F32), axis=0, keepdims=True)
        ssend[0, b] = through(ug, full[1], far_rows(b)).astype(BF16)
        part_copy(5, 0, b).start()
        ssend[1, b] = through(act, full[2], far_rows(b)).astype(BF16)
        part_copy(4, 1, b).start()
        part_store(1, b, through(ug, full[1], own_rows(b)))
        part_store(0, b, through(act, full[2], own_rows(b)))

    transposed(xn2, tra)
    for copy in sends.started[:gathered]:
        copy.wait_send()

    @pl.loop(0, width // step)
    def _(r):
        rows = pl.ds(pl.multiple_of(r * step, step), step)
        for i in range(n_pair):
            full[1][i, rows, :] = nn_dot(tra[rows, :], ug[i]).astype(BF16)

    scatter_start(1, full[1])

    @pl.loop(0, n_ctx)
    def _(b):
        part_copy(5, 0, b).wait()
        grad_two = part_load(1, b) + srecv[0, b].astype(F32)
        part_copy(4, 1, b).wait()
        lo[b] = (hid[b] + (part_load(0, b) + srecv[1, b].astype(F32)) + down_shift).astype(BF16)
        scaled, spread = normalize(hid[b])
        own_grad = og[b].astype(F32)
        hidden_grad = own_grad + norm_back(grad_two * gain_two, scaled, spread)
        hid[b] = hidden_grad
        branch = hidden_grad.astype(BF16)
        bg[own_rows(b), :] = branch
        rows_copy(6, b, bg).start()
        small[2:3, :] += jnp.sum(branch.astype(F32), axis=0, keepdims=True)
        small[3:4, :] += jnp.sum(grad_two * scaled, axis=0, keepdims=True)
        small[4:5, :] += jnp.sum(grad_two, axis=0, keepdims=True)
        small[5:6, :] += jnp.sum(own_grad, axis=0, keepdims=True)

    lo_copy = out_start(0, lo)

    @pl.loop(0, n_ctx)
    def _(b):
        rows_arrive(6, b, bg)
        dm[block_rows(b), :] = nn_dot(bg[block_rows(b), :], wo[...]).astype(BF16)

    transposed(bg, trb)

    @pl.loop(0, width // step)
    def _(r):
        rows = pl.ds(pl.multiple_of(r * step, step), step)
        product = nn_dot(trb[rows, :], mixed[...])
        for i in range(n_pair):
            full[0][i, rows, 3 * cols : 4 * cols] = product[:, i * cols : (i + 1) * cols].astype(BF16)

    scatter_turn(2, dwd)

    for b in reversed(range(n_ctx)):
        reach = (b + 1) * block
        here_rows = slice(b * block, (b + 1) * block)

        @pl.loop(0, n_twos)
        def _(j):
            at = pl.ds(pl.multiple_of(j * lanes, lanes), lanes)
            queries, keys, values = qs[here_rows, at], ks[:reach, at], vs[:reach, at]
            mix_grad, mix = dm[here_rows, at], o32[here_rows, at]
            towards = mix_grad.astype(F32) * mix
            query_parts, key_sum, value_sum = [], None, None
            for e in range(2):
                head = first_head if e == 0 else jnp.logical_not(first_head)
                grad_head = jnp.where(head, mix_grad, zero16)
                prob_grad = nt_dot(grad_head, values)
                centre = jnp.sum(jnp.where(head, towards, 0.0), axis=-1, keepdims=True)
                probs = p_first[b][2 * j + e]
                score_grad = (probs.astype(F32) * (prob_grad - centre)).astype(BF16)
                query_parts.append(nn_dot(score_grad, keys))
                key_term = tn_dot(score_grad, jnp.where(head, queries, zero16))
                value_term = tn_dot(probs, grad_head)
                key_sum = key_term if key_sum is None else key_sum + key_term
                value_sum = value_term if value_sum is None else value_sum + value_term
            query_grad = jnp.where(first_head, query_parts[0], query_parts[1]) * scale
            dqkv[here_rows, at] = query_grad.astype(BF16)
            if b == n_ctx - 1:
                wide[0, :, at] = key_sum
                wide[1, :, at] = value_sum
            else:
                wide[0, :reach, at] += key_sum
                wide[1, :reach, at] += value_sum

        if b == n_ctx - 1:
            scatter_turn(1, full[1])
            out_hop(0, lo_copy)
        if b == n_ctx - 2:
            scatter_line(2, dwd)
            out_cross(0)

    scatter_line(1, full[1])

    @pl.loop(0, n_ctx)
    def _(b):
        dqkv[block_rows(b), hw : 2 * hw] = wide[0, block_rows(b), :].astype(BF16)
        dqkv[block_rows(b), 2 * hw :] = wide[1, block_rows(b), :].astype(BF16)
        small[6:7, :hw] += jnp.sum(dqkv[block_rows(b), :hw].astype(F32), axis=0, keepdims=True)
        small[7:8, :hw] += jnp.sum(dqkv[block_rows(b), 2 * hw :].astype(F32), axis=0, keepdims=True)
        ssend[1, b] = nt_dot(dqkv[far_rows(b), :], wqkv[...]).astype(BF16)
        part_copy(7, 1, b).start()

    transposed(xn1, tra)

    @pl.loop(0, width // step)
    def _(r):
        rows = pl.ds(pl.multiple_of(r * step, step), step)
        product = nn_dot(tra[rows, :], dqkv[...])
        for i in range(n_pair):
            for a in range(3):
                full[0][i, rows, a * cols : (a + 1) * cols] = product[
                    :, a * hw + i * cols : a * hw + (i + 1) * cols
                ].astype(BF16)

    scatter_start(0, full[0])

    @pl.loop(0, n_ctx)
    def _(b):
        own_part = nt_dot(dqkv[own_rows(b), :], wqkv[...])
        part_copy(7, 1, b).wait()
        grad_one = own_part + srecv[1, b].astype(F32)
        scaled, spread = normalize(tok[b].astype(F32))
        tg[b] = (hid[b] + norm_back(grad_one * gain_one, scaled, spread)).astype(BF16)
        small[0:1, :] += jnp.sum(grad_one * scaled, axis=0, keepdims=True)
        small[1:2, :] += jnp.sum(grad_one, axis=0, keepdims=True)
        swap(0, b, og.at[b], ogf.at[own_rows(b)]).wait_send()
        rows_copy(1, b, xn1).wait_send()
        rows_copy(3, b, xn2).wait_send()
        rows_copy(6, b, bg).wait_send()

    tg_copy = out_start(1, tg)
    sends.go(small.at[pl.ds(0, 8)], side_land, small_sem.at[0, 0], partner)
    scatter_turn(0, full[0])
    arrive(side_land, small_sem.at[0, 0])
    small_b[0:6, :] = small[0:6, :] + side_land[0:6, :]
    small_b[6:16, :] = small[6:16, :]
    for k in range(1, n_ctx):
        sends.go(small_b, ctx_small.at[k - 1], small_sem.at[1, k - 1], here.other_ctx(k)[1])
    scatter_end(1, full[1])
    scatter_end(2, dwd)
    out_end(0)
    scatter_line(0, full[0])
    total = small_b[...]
    for k in range(1, n_ctx):
        arrive(ctx_small.at[k - 1], small_sem.at[1, k - 1])
        total = total + ctx_small[k - 1]
    small_c[...] = total
    for k in range(1, n_pair):
        sends.go(small_c, pair_small.at[k - 1], small_sem.at[2, k - 1], here.other_pair(k)[1])
    out_hop(1, tg_copy)
    total = small_c[...]
    for k in range(1, n_pair):
        arrive(pair_small.at[k - 1], small_sem.at[2, k - 1])
        total = total + pair_small[k - 1]
    small_d[...] = total
    for k in range(1, n_dp):
        sends.go(small_d, dp_small.at[k - 1], small_sem.at[3, k - 1], here.other_dp(k)[1])
    out_cross(1)
    scatter_end(0, full[0])
    total = small_d[...]
    for k in range(1, n_dp):
        arrive(dp_small.at[k - 1], small_sem.at[3, k - 1])
        total = total + dp_small[k - 1]
    small_out[...] = total
    out_end(1)
    for copy in sends.started[gathered:]:
        copy.wait_send()


def fused_call(sizes, tokens, out_grad, pack, shards, cols):
    n_dp, n_ctx, n_tp = sizes
    n_pair = n_tp // 2
    seqs, block, width = tokens.shape
    half = block // 2
    length = n_ctx * block
    share = shards[0].shape[0]
    fw = shards[1].shape[1]
    hw = n_pair * cols
    heads = hw // HEAD_DIM
    two = n_ctx // 2
    any_spec = pl.BlockSpec(memory_space=pl.ANY)
    vmem_spec = pl.BlockSpec(memory_space=pltpu.VMEM)
    shape = jax.ShapeDtypeStruct
    vm = pltpu.VMEM
    dma = pltpu.SemaphoreType.DMA
    out_shape = [shape(tokens.shape, BF16)] * 2
    out_shape += [shape(s.shape, F32) for s in shards]
    out_shape += [shape((16, width), F32)]
    scratch = [vm((n_pair, width, s.shape[1]), BF16) for s in shards]
    scratch += [
        vm((n_pair, n_dp * n_ctx) + pack.shape, F32),
        vm((8, width), F32),
        vm((8, width), F32),
    ]
    scratch += [vm((n_ctx, half, width), BF16)] * 4
    scratch += [
        vm((length, width), BF16),
        vm((width, 3 * hw), BF16),
        vm((width, hw), BF16),
        vm((length, hw), BF16),
        vm((length, hw), BF16),
        vm((length, hw), BF16),
        vm((length, hw), F32),
        vm((length, hw), BF16),
        vm((n_ctx, half, width), F32),
        vm((length, width), BF16),
        vm((length, width), BF16),
        vm((n_pair, length, fw), BF16),
        vm((n_pair, length, fw), BF16),
        vm((length, width), BF16),
        vm((length, hw), BF16),
        vm((length, 3 * hw), BF16),
        vm((width, length), BF16),
        vm((width, length), BF16),
        vm((2, length, hw), F32),
        vm((2, n_ctx, half, width), BF16),
        vm((2, n_ctx, half, width), BF16),
        vm((n_pair, width, fw), BF16),
        vm((16, width), F32),
    ]
    scratch += [vm((heads, block, (b + 1) * block), BF16) for b in range(n_ctx)]
    wide = [s.shape[1] for s in shards]
    scratch += [vm((n_dp - 1, n_pair, two * share, w), BF16) for w in wide]
    scratch += [vm((n_pair - 1, n_dp, two * share, w), BF16) for w in wide]
    scratch += [vm((n_pair - 1, two * share, w), BF16) for w in wide]
    scratch += [vm((n_dp - 1, two * share, w), BF16) for w in wide]
    scratch += [vm((n_ctx - 1, share, w), BF16) for w in wide]
    scratch += [
        vm((8, width), F32),
        vm((16, width), F32),
        vm((n_ctx - 1, 16, width), F32),
        vm((16, width), F32),
        vm((n_pair - 1, 16, width), F32),
        vm((16, width), F32),
        vm((n_dp - 1, 16, width), F32),
    ]
    most = max(n_dp, n_ctx, n_pair)
    scratch += [
        dma((8,)),
        dma((200,)),
        dma((2, n_ctx)),
        dma((4, n_ctx)),
        dma((4, n_pair)),
        dma((4, n_dp)),
        dma((3, n_pair, n_dp)),
        dma((3, n_pair, n_dp)),
        dma((8, n_ctx)),
        dma((8, n_ctx)),
        dma((3, 4, most, most)),
        dma((3, n_ctx)),
        dma((2, n_ctx)),
        dma((2, seqs)),
        dma((2, seqs)),
        dma((4, most)),
    ]
    return pl.pallas_call(
        functools.partial(fused_body, sizes, (half, width, share, cols, fw)),
        out_shape=out_shape,
        in_specs=[any_spec] * 6,
        out_specs=[any_spec] * 2 + [vmem_spec] * 4,
        scratch_shapes=scratch,
        compiler_params=pltpu.CompilerParams(
            collective_id=3, has_side_effects=True, vmem_limit_bytes=67043328
        ),
    )(tokens, out_grad, pack, *shards)


def finish_body(n_ctx, share, cols, *refs):
    lo_in, tg_in, attn, up, down, small = refs[:6]
    lo, tg, dq, dk, dv, do, du, dd = refs[6:14]
    vectors = refs[14:20]
    shifts = refs[20:22]
    up_shift = refs[22]
    lo[...] = lo_in[...]
    tg[...] = tg_in[...].astype(F32)
    row = lax.axis_index("dp") * n_ctx + lax.axis_index("ctx")
    pair = lax.axis_index("tp") // 2
    width = small.shape[1]

    @pl.when(pl.program_id(0) == 0)
    def _():
        for i, ref in enumerate((dq, dk, dv, do)):
            ref[...] = attn[:, i * cols : (i + 1) * cols]
        du[...] = up[...]
        dd[...] = down[...]
        turned = pltpu.roll(small[0:8, :], (width - row * share) % width, 1)
        for i, ref in enumerate(vectors):
            ref[...] = turned[i : i + 1, :share]
        turned = pltpu.roll(small[0:8, :], (width - pair * cols) % width, 1)
        for i, ref in enumerate(shifts):
            ref[...] = turned[6 + i : 7 + i, :cols]
        up_shift[...] = small[pl.ds(8 + pair, 1), :]


def finish_call(sizes, cols, lo, tg, attn, up, down, small):
    n_dp, n_ctx, n_tp = sizes
    seqs, block, width = lo.shape
    share = attn.shape[0]
    shape = jax.ShapeDtypeStruct
    rows = pl.BlockSpec((1, block, width), lambda i: (i, 0, 0))

    def whole(s):
        return pl.BlockSpec(s, lambda i: (0, 0))

    out_tail = [(share, cols)] * 4 + [up.shape] * 2 + [(1, share)] * 6 + [(1, cols)] * 2 + [(1, up.shape[1])]
    return pl.pallas_call(
        functools.partial(finish_body, n_ctx, share, cols),
        grid=(seqs,),
        out_shape=[shape(lo.shape, BF16), shape(lo.shape, F32)] + [shape(s, F32) for s in out_tail],
        in_specs=[rows, rows] + [whole(x.shape) for x in (attn, up, down, small)],
        out_specs=[rows, rows] + [whole(s) for s in out_tail],
    )(lo, tg, attn, up, down, small)


def fused_layer(sizes, tokens, out_grad, shards, vectors, column_biases):
    cols = shards[0].shape[1]
    share = shards[0].shape[0]
    attn = jnp.concatenate(shards[:4], axis=1)
    pieces = [jnp.pad(v.astype(F32), (0, 128 - share)) for v in vectors]
    pieces += [jnp.pad(b.astype(F32), (0, (-b.shape[0]) % 128)) for b in column_biases]
    pack = jnp.concatenate(pieces).reshape(-1, 128)
    results = fused_call(sizes, tokens, out_grad, pack, (attn, shards[4], shards[5]), cols)
    final = finish_call(sizes, cols, *results)
    return (*final[:8], *[v.reshape(v.shape[1]) for v in final[8:]])


def per_device(
    tokens,
    out_grad,
    query_weight,
    key_weight,
    value_weight,
    output_weight,
    up_weight,
    down_weight,
    norm1_gain,
    norm1_bias,
    output_bias,
    norm2_gain,
    norm2_bias,
    down_bias,
    query_bias,
    value_bias,
    up_bias,
):
    sizes = (lax.axis_size("dp"), lax.axis_size("ctx"), lax.axis_size("tp"))
    n_dp, n_ctx, n_tp = sizes
    n_pair = n_tp // 2
    seqs, block, width = tokens.shape
    assert seqs == n_ctx * n_pair
    share = norm1_gain.shape[0]
    cols = query_bias.shape[0]
    pair = lax.axis_index("tp") // 2
    row = lax.axis_index("dp") * n_ctx + lax.axis_index("ctx")
    shards = (query_weight, key_weight, value_weight, output_weight, up_weight, down_weight)
    vectors = (norm1_gain, norm1_bias, output_bias, norm2_gain, norm2_bias, down_bias)
    if share % 16 == 0 and n_ctx % 2 == 0:
        return fused_layer(
            sizes, tokens, out_grad, shards, vectors, (query_bias, value_bias, up_bias)
        )

    six = jnp.stack(vectors).astype(F32)
    vec = jnp.pad(six, ((0, 2), (0, 128 - share)))
    columns = jnp.arange(width) // cols == pair
    narrow = [jnp.where(columns, jnp.tile(b.astype(F32), width // cols), 0.0) for b in (query_bias, value_bias)]
    bias = jnp.pad(jnp.stack(narrow + [up_bias.astype(F32)]), ((0, 5), (0, 0)))

    gathered = gather_call(sizes, tokens, out_grad, shards, vec, bias)
    tok, og = gathered[0:2]
    weights = [w.reshape(n_pair, width, w.shape[3]) for w in gathered[2:8]]
    vecs = gathered[8][:, :, :share].transpose(1, 0, 2).reshape(8, width)
    results = compute_call(sizes, tok, og, weights, vecs, gathered[9])
    lo, tg = results[0:2]
    grads = [
        g.reshape(n_pair, n_dp * n_ctx, s.shape[0], s.shape[1]) for g, s in zip(results[2:8], shards)
    ]
    final = scatter_call(sizes, seqs, lo, tg, grads, results[8])
    layer_out, tokens_grad = final[0], final[1].astype(F32)
    small = final[8]
    owned = [lax.dynamic_slice_in_dim(small[i], row * share, share) for i in range(6)]
    shifts = [lax.dynamic_slice_in_dim(small[6 + i], pair * cols, cols) for i in range(2)]
    up_total = lax.dynamic_index_in_dim(small[8 : 8 + n_pair], pair, 0, keepdims=False)
    return (layer_out, tokens_grad, *final[2:8], *owned, *shifts, up_total)


def solution(mesh):
    rows_spec = P("dp", "ctx", None)
    weight_spec = P(("dp", "ctx"), "tp")
    vector_spec = P(("dp", "ctx"))
    column_spec = P("tp")
    common = (rows_spec,) * 2 + (weight_spec,) * 6 + (vector_spec,) * 6 + (column_spec,) * 3
    return jax.shard_map(
        per_device, mesh=mesh, in_specs=common, out_specs=common, check_vma=False
    )
```

```python
import functools

import jax
import jax.numpy as jnp
from jax import lax
from jax.experimental import pallas as pl
from jax.experimental.pallas import tpu as pltpu
from jax.sharding import PartitionSpec as P

HEAD_DIM = 64
MESH = pl.DeviceIdType.MESH
F32 = jnp.float32
BF16 = jnp.bfloat16
VMEM_LIMIT = 66 * 1000 * 1000

epsilon = 1e-05
root_half = 0.7071067811865476
density_scale = 0.3989422804014327


def remote(src, dst, send_sem, recv_sem, device):
    return pltpu.make_async_remote_copy(
        src_ref=src,
        dst_ref=dst,
        send_sem=send_sem,
        recv_sem=recv_sem,
        device_id=device,
        device_id_type=MESH,
    )


def nn_dot(left, right):
    return lax.dot_general(left, right, (((1,), (0,)), ((), ())), preferred_element_type=F32)


def nt_dot(left, right):
    return lax.dot_general(left, right, (((1,), (1,)), ((), ())), preferred_element_type=F32)


def tn_dot(left, right):
    return lax.dot_general(left, right, (((0,), (0,)), ((), ())), preferred_element_type=F32)


def normalize(values):
    centred = values - jnp.mean(values, axis=-1, keepdims=True)
    spread = lax.rsqrt(jnp.mean(centred * centred, axis=-1, keepdims=True) + epsilon)
    return centred * spread, spread


def norm_back(grad_scaled, scaled, spread):
    inner = grad_scaled - jnp.mean(grad_scaled, axis=-1, keepdims=True)
    inner = inner - scaled * jnp.mean(grad_scaled * scaled, axis=-1, keepdims=True)
    return inner * spread


class Place:
    def __init__(self, sizes):
        self.n_dp, self.n_ctx, self.n_tp = sizes
        self.n_pair = self.n_tp // 2
        self.dp = lax.axis_index("dp")
        self.ctx = lax.axis_index("ctx")
        self.tp = lax.axis_index("tp")
        self.pair = self.tp // 2
        self.side = self.tp % 2

    def other_dp(self, k):
        d = (self.dp + k) % self.n_dp
        return d, (d, self.ctx, self.tp)

    def other_ctx(self, k):
        z = (self.ctx + k) % self.n_ctx
        return z, (self.dp, z, self.tp)

    def other_pair(self, k):
        p = (self.pair + k) % self.n_pair
        return p, (self.dp, self.ctx, 2 * p + self.side)

    def partner(self):
        return (self.dp, self.ctx, 2 * self.pair + 1 - self.side)

    def barrier(self, far):
        sem = pltpu.get_barrier_semaphore()
        count = 1
        pl.semaphore_signal(sem, inc=1, device_id=self.partner(), device_id_type=MESH)
        if far:
            for size, other in (
                (self.n_dp, self.other_dp),
                (self.n_ctx, self.other_ctx),
                (self.n_pair, self.other_pair),
            ):
                for k in range(1, size):
                    pl.semaphore_signal(sem, inc=1, device_id=other(k)[1], device_id_type=MESH)
                    count += 1
        pl.semaphore_wait(sem, count)


class Sends:
    def __init__(self, sems):
        self.sems = sems
        self.started = []

    def go(self, src, dst, recv_sem, device):
        copy = remote(src, dst, self.sems.at[len(self.started)], recv_sem, device)
        copy.start()
        self.started.append(copy)

    def finish(self):
        for copy in self.started:
            copy.wait_send()


def gather_body(sizes, half, *refs):
    here = Place(sizes)
    n_dp, n_ctx, n_pair = here.n_dp, here.n_ctx, here.n_pair
    d, z, p, c = here.dp, here.ctx, here.pair, here.side
    tokens, out_grad = refs[0:2]
    shards = refs[2:8]
    vec, bias = refs[8:10]
    tok_own, og_own = refs[10:12]
    full = refs[12:18]
    vec_all, bias_all = refs[18:20]
    own_sem, send_sem, rows_sem, line_sem, group_sem, vline_sem, vgroup_sem, bias_sem = refs[20:28]
    own_row = d * n_ctx + z
    mine = p * n_ctx + z
    rows = pl.ds(pl.multiple_of(c * half, half), half)

    here.barrier(True)
    sends = Sends(send_sem)
    own = [
        pltpu.make_async_copy(tokens.at[mine, rows], tok_own.at[z], own_sem.at[0]),
        pltpu.make_async_copy(out_grad.at[mine, rows], og_own.at[z], own_sem.at[1]),
        pltpu.make_async_copy(vec, vec_all.at[own_row], own_sem.at[2]),
        pltpu.make_async_copy(bias, bias_all.at[p], own_sem.at[3]),
    ]
    for a in range(6):
        own.append(pltpu.make_async_copy(shards[a], full[a].at[p, own_row], own_sem.at[4 + a]))
    for copy in own:
        copy.start()

    def send_rows(index, source, target):
        for k in range(1, n_ctx):
            zz, device = here.other_ctx(k)
            sends.go(
                source.at[p * n_ctx + zz, rows], target.at[z], rows_sem.at[index, z], device
            )

    def send_line(a):
        for k in range(1, n_ctx):
            zz, device = here.other_ctx(k)
            sends.go(shards[a], full[a].at[p, own_row], line_sem.at[a, z], device)

    send_rows(0, tokens, tok_own)
    for k in range(1, n_ctx):
        zz, device = here.other_ctx(k)
        sends.go(vec, vec_all.at[own_row], vline_sem.at[z], device)
    for k in range(1, n_pair):
        pp, device = here.other_pair(k)
        sends.go(bias, bias_all.at[p], bias_sem.at[p], device)
    for a in range(6):
        send_line(a)
    send_rows(1, out_grad, og_own)

    for copy in own:
        copy.wait()

    def group(a, pp, dd):
        return full[a].at[pp, pl.ds(dd * n_ctx, n_ctx)]

    def wait_line(a):
        for k in range(1, n_ctx):
            zz, device = here.other_ctx(k)
            slot = full[a].at[p, d * n_ctx + zz]
            remote(slot, slot, send_sem.at[0], line_sem.at[a, zz], device).wait_recv()

    def send_pair(a, dd):
        for k in range(1, n_pair):
            pp, device = here.other_pair(k)
            sends.go(group(a, p, dd), group(a, p, dd), group_sem.at[a, p, dd], device)

    def send_dp(a, pp):
        for k in range(1, n_dp):
            dd, device = here.other_dp(k)
            sends.go(group(a, pp, d), group(a, pp, d), group_sem.at[a, pp, d], device)

    def wait_group(a, pp, dd):
        slot = group(a, pp, dd)
        remote(slot, slot, send_sem.at[0], group_sem.at[a, pp, dd], here.partner()).wait_recv()

    for a in range(6):
        wait_line(a)
        send_dp(a, p)
        send_pair(a, d)
    for k in range(1, n_ctx):
        zz, device = here.other_ctx(k)
        slot = vec_all.at[d * n_ctx + zz]
        remote(slot, slot, send_sem.at[0], vline_sem.at[zz], device).wait_recv()
    for k in range(1, n_dp):
        dd, device = here.other_dp(k)
        slot = vec_all.at[pl.ds(d * n_ctx, n_ctx)]
        sends.go(slot, slot, vgroup_sem.at[d], device)
    pair_first = (True, True, True, True, False, True)
    for a in range(6):
        if pair_first[a]:
            for k in range(1, n_pair):
                pp = here.other_pair(k)[0]
                wait_group(a, pp, d)
                send_dp(a, pp)
        else:
            for k in range(1, n_dp):
                dd = here.other_dp(k)[0]
                wait_group(a, p, dd)
                send_pair(a, dd)
    for a in range(6):
        for k in range(1, n_dp):
            dd = here.other_dp(k)[0]
            if pair_first[a]:
                wait_group(a, p, dd)
            for j in range(1, n_pair):
                wait_group(a, here.other_pair(j)[0], dd)
        if not pair_first[a]:
            for j in range(1, n_pair):
                wait_group(a, here.other_pair(j)[0], d)
    for k in range(1, n_dp):
        dd, device = here.other_dp(k)
        slot = vec_all.at[pl.ds(dd * n_ctx, n_ctx)]
        remote(slot, slot, send_sem.at[0], vgroup_sem.at[dd], device).wait_recv()
    for k in range(1, n_pair):
        pp, device = here.other_pair(k)
        slot = bias_all.at[pp]
        remote(slot, slot, send_sem.at[0], bias_sem.at[pp], device).wait_recv()
    for index, target in ((0, tok_own), (1, og_own)):
        for k in range(1, n_ctx):
            zz, device = here.other_ctx(k)
            slot = target.at[zz]
            remote(slot, slot, send_sem.at[0], rows_sem.at[index, zz], device).wait_recv()
    sends.finish()


def gather_call(sizes, tokens, out_grad, shards, vec, bias):
    n_dp, n_ctx, n_tp = sizes
    n_pair = n_tp // 2
    seqs, block, width = tokens.shape
    half = block // 2
    any_spec = pl.BlockSpec(memory_space=pl.ANY)
    vmem_spec = pl.BlockSpec(memory_space=pltpu.VMEM)
    own = jax.ShapeDtypeStruct((n_ctx, half, width), BF16)
    out_shape = [own, own]
    out_shape += [jax.ShapeDtypeStruct((n_pair, n_dp * n_ctx) + s.shape, BF16) for s in shards]
    out_shape += [
        jax.ShapeDtypeStruct((n_dp * n_ctx,) + vec.shape, F32),
        jax.ShapeDtypeStruct((n_pair,) + bias.shape, F32),
    ]
    n_sends = (
        2 * (n_ctx - 1)
        + (n_ctx - 1)
        + (n_pair - 1)
        + 6 * (n_ctx - 1)
        + (n_dp - 1)
        + 6 * ((n_dp - 1) + (n_pair - 1) + (n_dp - 1) * (n_pair - 1))
    )
    dma = pltpu.SemaphoreType.DMA
    return pl.pallas_call(
        functools.partial(gather_body, sizes, half),
        out_shape=out_shape,
        in_specs=[any_spec] * 10,
        out_specs=[vmem_spec] * 10,
        scratch_shapes=[
            dma((10,)),
            dma((n_sends,)),
            dma((2, n_ctx)),
            dma((6, n_ctx)),
            dma((6, n_pair, n_dp)),
            dma((n_ctx,)),
            dma((n_dp,)),
            dma((n_pair,)),
        ],
        compiler_params=pltpu.CompilerParams(
            collective_id=0, has_side_effects=True, vmem_limit_bytes=VMEM_LIMIT
        ),
    )(tokens, out_grad, *shards, vec, bias)


def compute_body(sizes, *refs):
    here = Place(sizes)
    n_ctx, n_pair = here.n_ctx, here.n_pair
    c = here.side
    (tok, og, gq, gk, gv, go, gu, gd, vecs, bias) = refs[:10]
    (lo, tg, dwq, dwk, dwv, dwo, dwu, dwd, small) = refs[10:19]
    (
        xn1, wqkv, wo, qs, ks, vs, o32, mixed, hid, xn2, ogf, act, ug, bg, dm,
        dka, dva, dqkv, tra, trb, part, ssend, srecv, p_first, send_sem, recv_sem,
    ) = refs[19 : 19 + 23] + (refs[42 : 42 + n_ctx],) + refs[42 + n_ctx :]
    half, width = tok.shape[1], tok.shape[2]
    block = 2 * half
    cols = gq.shape[2]
    hw = n_pair * cols
    fw = gu.shape[2]
    lanes = 2 * HEAD_DIM
    n_twos = hw // lanes
    partner = here.partner()
    scale = HEAD_DIM ** -0.5
    first_head = lax.broadcasted_iota(jnp.int32, (1, lanes), 1) < HEAD_DIM
    zero16 = jnp.zeros((), BF16)

    def own_rows(b):
        return pl.ds(pl.multiple_of(b * block + c * half, half), half)

    def far_rows(b):
        return pl.ds(pl.multiple_of(b * block + (1 - c) * half, half), half)

    def block_rows(b):
        return pl.ds(pl.multiple_of(b * block, block), block)

    def exchange(stage, b, src, dst):
        return remote(src, dst, send_sem.at[stage, b], recv_sem.at[stage, b], partner)

    def rows_copy(stage, b, ref):
        return exchange(stage, b, ref.at[own_rows(b)], ref.at[own_rows(b)])

    def rows_arrive(stage, b, ref):
        exchange(stage, b, ref.at[far_rows(b)], ref.at[far_rows(b)]).wait_recv()

    def part_copy(stage, slot, b):
        return exchange(stage, b, ssend.at[slot, b], srecv.at[slot, b])

    here.barrier(False)

    gain_one, shift_one, out_shift = vecs[0:1, :], vecs[1:2, :], vecs[2:3, :]
    gain_two, shift_two, down_shift = vecs[3:4, :], vecs[4:5, :], vecs[5:6, :]

    @pl.loop(0, n_ctx)
    def _(b):
        exchange(0, b, og.at[b], ogf.at[own_rows(b)]).start()
        ogf[own_rows(b), :] = og[b]
        scaled, _ = normalize(tok[b].astype(F32))
        xn1[own_rows(b), :] = (scaled * gain_one + shift_one).astype(BF16)
        rows_copy(1, b, xn1).start()

    for i in range(n_pair):
        at = slice(i * cols, (i + 1) * cols)
        wqkv[:, i * cols : (i + 1) * cols] = gq[i]
        wqkv[:, hw + i * cols : hw + (i + 1) * cols] = gk[i]
        wqkv[:, 2 * hw + i * cols : 2 * hw + (i + 1) * cols] = gv[i]
        wo[:, at] = go[i]
    q_shift = bias[0, 0:1, :hw]
    v_shift = bias[0, 1:2, :hw]
    for i in range(1, n_pair):
        q_shift = q_shift + bias[i, 0:1, :hw]
        v_shift = v_shift + bias[i, 1:2, :hw]

    @pl.loop(0, n_ctx)
    def _(b):
        rows_arrive(1, b, xn1)
        product = nn_dot(xn1[block_rows(b), :], wqkv[...])
        qs[block_rows(b), :] = (product[:, :hw] + q_shift).astype(BF16) * jnp.asarray(scale, BF16)
        ks[block_rows(b), :] = product[:, hw : 2 * hw].astype(BF16)
        vs[block_rows(b), :] = (product[:, 2 * hw :] + v_shift).astype(BF16)

    for b in range(n_ctx):
        reach = (b + 1) * block
        here_rows = slice(b * block, (b + 1) * block)

        @pl.loop(0, n_twos)
        def _(j):
            at = pl.ds(pl.multiple_of(j * lanes, lanes), lanes)
            queries, keys, values = qs[here_rows, at], ks[:reach, at], vs[:reach, at]
            pieces = []
            for e in range(2):
                head = first_head if e == 0 else jnp.logical_not(first_head)
                scores = nt_dot(jnp.where(head, queries, zero16), keys)
                powers = jnp.exp(scores - jnp.max(scores, axis=-1, keepdims=True))
                inverse = 1.0 / jnp.sum(powers, axis=-1, keepdims=True)
                probs = (powers * inverse).astype(BF16)
                p_first[b][2 * j + e] = probs
                pieces.append(nn_dot(probs, values))
            out = jnp.where(first_head, pieces[0], pieces[1])
            o32[here_rows, at] = out
            mixed[here_rows, at] = out.astype(BF16)

        ssend[0, b] = nt_dot(mixed[far_rows(b), :], wo[...]).astype(BF16)
        part_copy(2, 0, b).start()
        hid[b] = nt_dot(mixed[own_rows(b), :], wo[...])

    @pl.loop(0, n_ctx)
    def _(b):
        part_copy(2, 0, b).wait()
        hidden = tok[b].astype(F32) + (hid[b] + srecv[0, b].astype(F32)) + out_shift
        hid[b] = hidden
        scaled, _ = normalize(hidden)
        xn2[own_rows(b), :] = (scaled * gain_two + shift_two).astype(BF16)
        rows_copy(3, b, xn2).start()

    small[...] = jnp.zeros_like(small)

    @pl.loop(0, n_ctx)
    def _(b):
        rows_arrive(0, b, ogf)
        rows_arrive(3, b, xn2)
        normed = xn2[block_rows(b), :]
        grads = ogf[block_rows(b), :]
        for i in range(n_pair):
            upward = nn_dot(normed, gu[i]) + bias[i, 2:3, :]
            big_phi = 0.5 + 0.5 * lax.erf(upward * root_half)
            act[i, block_rows(b), :] = (upward * big_phi).astype(BF16)
            slope = big_phi + upward * density_scale * jnp.exp(-0.5 * upward * upward)
            rows_grad = (nn_dot(grads, gd[i]) * slope).astype(BF16)
            ug[i, block_rows(b), :] = rows_grad
            small[8 + i : 9 + i, :] += jnp.sum(rows_grad.astype(F32), axis=0, keepdims=True)

        def through(ref, weight, rows):
            total = nt_dot(ref[0, rows, :], weight[0])
            for i in range(1, n_pair):
                total = total + nt_dot(ref[i, rows, :], weight[i])
            return total

        ssend[1, b] = through(act, gd, far_rows(b)).astype(BF16)
        part_copy(4, 1, b).start()
        ssend[0, b] = through(ug, gu, far_rows(b)).astype(BF16)
        part_copy(5, 0, b).start()
        part[0, b] = through(act, gd, own_rows(b))
        part[1, b] = through(ug, gu, own_rows(b))

    def transposed(ref, out):
        for b in range(n_ctx):
            out[:, b * block : (b + 1) * block] = ref[b * block : (b + 1) * block, :].T

    @pl.loop(0, n_ctx)
    def _(b):
        part_copy(4, 1, b).wait()
        lo[b] = (hid[b] + (part[0, b] + srecv[1, b].astype(F32)) + down_shift).astype(BF16)
        part_copy(5, 0, b).wait()
        grad_two = part[1, b] + srecv[0, b].astype(F32)
        scaled, spread = normalize(hid[b])
        own_grad = og[b].astype(F32)
        hidden_grad = own_grad + norm_back(grad_two * gain_two, scaled, spread)
        hid[b] = hidden_grad
        branch = hidden_grad.astype(BF16)
        bg[own_rows(b), :] = branch
        rows_copy(6, b, bg).start()
        small[2:3, :] += jnp.sum(branch.astype(F32), axis=0, keepdims=True)
        small[3:4, :] += jnp.sum(grad_two * scaled, axis=0, keepdims=True)
        small[4:5, :] += jnp.sum(grad_two, axis=0, keepdims=True)
        small[5:6, :] += jnp.sum(own_grad, axis=0, keepdims=True)

    transposed(xn2, tra)
    transposed(ogf, trb)
    step = 256

    @pl.loop(0, width // step)
    def _(r):
        rows = pl.ds(pl.multiple_of(r * step, step), step)
        for i in range(n_pair):
            dwu[i, rows, :] = nn_dot(tra[rows, :], ug[i]).astype(BF16)
            dwd[i, rows, :] = nn_dot(trb[rows, :], act[i]).astype(BF16)

    @pl.loop(0, n_ctx)
    def _(b):
        rows_arrive(6, b, bg)
        dm[block_rows(b), :] = nn_dot(bg[block_rows(b), :], wo[...]).astype(BF16)

    transposed(bg, trb)

    @pl.loop(0, width // step)
    def _(r):
        rows = pl.ds(pl.multiple_of(r * step, step), step)
        product = nn_dot(trb[rows, :], mixed[...])
        for i in range(n_pair):
            dwo[i, rows, :] = product[:, i * cols : (i + 1) * cols].astype(BF16)

    for b in reversed(range(n_ctx)):
        reach = (b + 1) * block
        here_rows = slice(b * block, (b + 1) * block)

        @pl.loop(0, n_twos)
        def _(j):
            at = pl.ds(pl.multiple_of(j * lanes, lanes), lanes)
            queries, keys, values = qs[here_rows, at], ks[:reach, at], vs[:reach, at]
            mix_grad, mix = dm[here_rows, at], o32[here_rows, at]
            towards = mix_grad.astype(F32) * mix
            query_parts, key_sum, value_sum = [], None, None
            for e in range(2):
                head = first_head if e == 0 else jnp.logical_not(first_head)
                grad_head = jnp.where(head, mix_grad, zero16)
                prob_grad = nt_dot(grad_head, values)
                centre = jnp.sum(jnp.where(head, towards, 0.0), axis=-1, keepdims=True)
                probs = p_first[b][2 * j + e]
                score_grad = (probs.astype(F32) * (prob_grad - centre)).astype(BF16)
                query_parts.append(nn_dot(score_grad, keys))
                key_term = tn_dot(score_grad, jnp.where(head, queries, zero16))
                value_term = tn_dot(probs, grad_head)
                key_sum = key_term if key_sum is None else key_sum + key_term
                value_sum = value_term if value_sum is None else value_sum + value_term
            query_grad = jnp.where(first_head, query_parts[0], query_parts[1]) * scale
            dqkv[here_rows, at] = query_grad.astype(BF16)
            if b == n_ctx - 1:
                dka[:, at] = key_sum
                dva[:, at] = value_sum
            else:
                dka[:reach, at] += key_sum
                dva[:reach, at] += value_sum

    @pl.loop(0, n_ctx)
    def _(b):
        dqkv[block_rows(b), hw : 2 * hw] = dka[block_rows(b), :].astype(BF16)
        dqkv[block_rows(b), 2 * hw :] = dva[block_rows(b), :].astype(BF16)
        small[6:7, :hw] += jnp.sum(dqkv[block_rows(b), :hw].astype(F32), axis=0, keepdims=True)
        small[7:8, :hw] += jnp.sum(dqkv[block_rows(b), 2 * hw :].astype(F32), axis=0, keepdims=True)
        ssend[1, b] = nt_dot(dqkv[far_rows(b), :], wqkv[...]).astype(BF16)
        part_copy(7, 1, b).start()
        part[0, b] = nt_dot(dqkv[own_rows(b), :], wqkv[...])

    transposed(xn1, tra)

    @pl.loop(0, width // step)
    def _(r):
        rows = pl.ds(pl.multiple_of(r * step, step), step)
        product = nn_dot(tra[rows, :], dqkv[...])
        for i in range(n_pair):
            dwq[i, rows, :] = product[:, i * cols : (i + 1) * cols].astype(BF16)
            dwk[i, rows, :] = product[:, hw + i * cols : hw + (i + 1) * cols].astype(BF16)
            dwv[i, rows, :] = product[:, 2 * hw + i * cols : 2 * hw + (i + 1) * cols].astype(BF16)

    @pl.loop(0, n_ctx)
    def _(b):
        part_copy(7, 1, b).wait()
        grad_one = part[0, b] + srecv[1, b].astype(F32)
        scaled, spread = normalize(tok[b].astype(F32))
        tg[b] = (hid[b] + norm_back(grad_one * gain_one, scaled, spread)).astype(BF16)
        small[0:1, :] += jnp.sum(grad_one * scaled, axis=0, keepdims=True)
        small[1:2, :] += jnp.sum(grad_one, axis=0, keepdims=True)
        exchange(0, b, og.at[b], ogf.at[own_rows(b)]).wait_send()
        rows_copy(1, b, xn1).wait_send()
        rows_copy(3, b, xn2).wait_send()
        rows_copy(6, b, bg).wait_send()


def compute_call(sizes, tok, og, weights, vecs, bias):
    n_dp, n_ctx, n_tp = sizes
    n_pair = n_tp // 2
    half, width = tok.shape[1:]
    block = 2 * half
    length = n_ctx * block
    cols = weights[0].shape[2]
    hw = n_pair * cols
    fw = weights[4].shape[2]
    heads = hw // HEAD_DIM
    vmem_spec = pl.BlockSpec(memory_space=pltpu.VMEM)
    shape = jax.ShapeDtypeStruct
    out_shape = [
        shape(tok.shape, BF16),
        shape(tok.shape, BF16),
    ]
    out_shape += [shape(w.shape, BF16) for w in weights]
    out_shape += [shape((16, width), F32)]
    vm = pltpu.VMEM
    scratch = [
        vm((length, width), BF16),
        vm((width, 3 * hw), BF16),
        vm((width, hw), BF16),
        vm((length, hw), BF16),
        vm((length, hw), BF16),
        vm((length, hw), BF16),
        vm((length, hw), F32),
        vm((length, hw), BF16),
        vm((n_ctx, half, width), F32),
        vm((length, width), BF16),
        vm((length, width), BF16),
        vm((n_pair, length, fw), BF16),
        vm((n_pair, length, fw), BF16),
        vm((length, width), BF16),
        vm((length, hw), BF16),
        vm((length, hw), F32),
        vm((length, hw), F32),
        vm((length, 3 * hw), BF16),
        vm((width, length), BF16),
        vm((width, length), BF16),
        vm((2, n_ctx, half, width), F32),
        vm((2, n_ctx, half, width), BF16),
        vm((2, n_ctx, half, width), BF16),
    ]
    scratch += [vm((heads, block, (b + 1) * block), BF16) for b in range(n_ctx)]
    scratch += [pltpu.SemaphoreType.DMA((8, n_ctx)), pltpu.SemaphoreType.DMA((8, n_ctx))]
    return pl.pallas_call(
        functools.partial(compute_body, sizes),
        out_shape=out_shape,
        in_specs=[vmem_spec] * 10,
        out_specs=[vmem_spec] * 9,
        scratch_shapes=scratch,
        compiler_params=pltpu.CompilerParams(
            collective_id=1, has_side_effects=True, vmem_limit_bytes=VMEM_LIMIT
        ),
    )(tok, og, *weights, vecs, bias)


def scatter_body(sizes, half, *refs):
    here = Place(sizes)
    n_dp, n_ctx, n_pair = here.n_dp, here.n_ctx, here.n_pair
    d, z, p, c = here.dp, here.ctx, here.pair, here.side
    rows_in = refs[0:2]
    grads = refs[2:8]
    small = refs[8]
    rows_out = refs[9:11]
    owned = refs[11:17]
    small_out = refs[17]
    it = iter(refs[18:])
    dp_land = [next(it) for _ in range(6)]
    dp_sum = [next(it) for _ in range(6)]
    keep = [next(it) for _ in range(6)]
    pair_land = [next(it) for _ in range(6)]
    pair_sum = [next(it) for _ in range(6)]
    ctx_land = [next(it) for _ in range(6)]
    side_land, small_b, ctx_small, small_c, pair_small, small_d, dp_small = [next(it) for _ in range(7)]
    own_sem, send_sem, line_sem, far_sem, side_sem, dp_sem, pair_sem, ctx_sem, small_sem = it
    mine = p * n_ctx + z
    rows = pl.ds(pl.multiple_of(c * half, half), half)

    here.barrier(True)
    sends = Sends(send_sem)

    for a in range(6):
        for k in range(1, n_dp):
            dd, device = here.other_dp(k)
            sends.go(
                grads[a].at[:, pl.ds(dd * n_ctx, n_ctx)],
                dp_land[a].at[k - 1],
                dp_sem.at[a, k - 1],
                device,
            )
    own = []
    for i in range(2):
        for k in range(1, n_ctx):
            zz, device = here.other_ctx(k)
            sends.go(rows_in[i].at[zz], rows_out[i].at[mine, rows], line_sem.at[i, z], device)
        own.append(pltpu.make_async_copy(rows_in[i].at[z], rows_out[i].at[mine, rows], own_sem.at[i]))
        own[-1].start()
    sends.go(small.at[pl.ds(0, 8)], side_land, small_sem.at[0, 0], here.partner())

    def small_arrive(stage, k, land):
        remote(land, land, send_sem.at[0], small_sem.at[stage, k - 1], here.partner()).wait_recv()

    for i in range(2):
        own[i].wait()
        for k in range(1, n_ctx):
            zz, device = here.other_ctx(k)
            slot = rows_out[i].at[p * n_ctx + zz, rows]
            remote(slot, slot, send_sem.at[0], line_sem.at[i, zz], device).wait_recv()
        for k in range(1, n_pair):
            pp, device = here.other_pair(k)
            slot = rows_out[i].at[pl.ds(p * n_ctx, n_ctx), rows]
            sends.go(slot, slot, far_sem.at[i, p], device)

    small_arrive(0, 1, side_land)
    small_b[0:8, :] = small[0:8, :] + side_land[...]
    small_b[8:16, :] = small[8:16, :]
    small_b[6:8, :] = small[6:8, :]
    for k in range(1, n_ctx):
        zz, device = here.other_ctx(k)
        sends.go(small_b, ctx_small.at[k - 1], small_sem.at[1, k - 1], device)

    for a in range(6):
        for k in range(1, n_dp):
            remote(
                dp_land[a].at[k - 1], dp_land[a].at[k - 1], send_sem.at[0], dp_sem.at[a, k - 1],
                here.partner(),
            ).wait_recv()
        for i in range(n_pair):
            total = grads[a][i, pl.ds(d * n_ctx, n_ctx)].astype(F32)
            for k in range(1, n_dp):
                total = total + dp_land[a][k - 1, i].astype(F32)
            dp_sum[a][i] = total.astype(BF16)
        for k in range(1, n_pair):
            pp, device = here.other_pair(k)
            sends.go(dp_sum[a].at[pp], pair_land[a].at[k - 1], pair_sem.at[a, k - 1], device)

    total = small_b[...]
    for k in range(1, n_ctx):
        small_arrive(1, k, ctx_small.at[k - 1])
        total = total + ctx_small[k - 1]
    small_c[...] = total
    for k in range(1, n_pair):
        pp, device = here.other_pair(k)
        sends.go(small_c, pair_small.at[k - 1], small_sem.at[2, k - 1], device)

    for a in range(6):
        for k in range(1, n_pair):
            remote(
                pair_land[a].at[k - 1], pair_land[a].at[k - 1], send_sem.at[0], pair_sem.at[a, k - 1],
                here.partner(),
            ).wait_recv()
        total = dp_sum[a][p].astype(F32)
        for k in range(1, n_pair):
            total = total + pair_land[a][k - 1].astype(F32)
        keep[a][...] = total
        pair_sum[a][...] = total.astype(BF16)
        for k in range(1, n_ctx):
            zz, device = here.other_ctx(k)
            sends.go(pair_sum[a].at[zz], ctx_land[a].at[k - 1], ctx_sem.at[a, k - 1], device)

    total = small_c[...]
    for k in range(1, n_pair):
        small_arrive(2, k, pair_small.at[k - 1])
        total = total + pair_small[k - 1]
    small_d[...] = total
    for k in range(1, n_dp):
        dd, device = here.other_dp(k)
        sends.go(small_d, dp_small.at[k - 1], small_sem.at[3, k - 1], device)

    for i in range(2):
        for k in range(1, n_pair):
            pp, device = here.other_pair(k)
            slot = rows_out[i].at[pl.ds(pp * n_ctx, n_ctx), rows]
            remote(slot, slot, send_sem.at[0], far_sem.at[i, pp], device).wait_recv()
        slot = rows_out[i].at[:, rows]
        sends.go(slot, slot, side_sem.at[i], here.partner())

    for a in range(6):
        total = keep[a][z]
        for k in range(1, n_ctx):
            remote(
                ctx_land[a].at[k - 1], ctx_land[a].at[k - 1], send_sem.at[0], ctx_sem.at[a, k - 1],
                here.partner(),
            ).wait_recv()
            total = total + ctx_land[a][k - 1].astype(F32)
        owned[a][...] = total

    total = small_d[...]
    for k in range(1, n_dp):
        small_arrive(3, k, dp_small.at[k - 1])
        total = total + dp_small[k - 1]
    small_out[...] = total
    other = pl.ds(pl.multiple_of((1 - c) * half, half), half)
    for i in range(2):
        slot = rows_out[i].at[:, other]
        remote(slot, slot, send_sem.at[0], side_sem.at[i], here.partner()).wait_recv()
    sends.finish()


def scatter_call(sizes, seqs, lo, tg, grads, small):
    n_dp, n_ctx, n_tp = sizes
    n_pair = n_tp // 2
    half, width = lo.shape[1:]
    vmem_spec = pl.BlockSpec(memory_space=pltpu.VMEM)
    shape = jax.ShapeDtypeStruct
    vm = pltpu.VMEM
    tail = [g.shape[2:] for g in grads]
    out_shape = [shape((seqs, 2 * half, width), BF16)] * 2
    out_shape += [shape(t, F32) for t in tail]
    out_shape += [shape(small.shape, F32)]
    scratch = [vm((n_dp - 1, n_pair, n_ctx) + t, BF16) for t in tail]
    scratch += [vm((n_pair, n_ctx) + t, BF16) for t in tail]
    scratch += [vm((n_ctx,) + t, F32) for t in tail]
    scratch += [vm((n_pair - 1, n_ctx) + t, BF16) for t in tail]
    scratch += [vm((n_ctx,) + t, BF16) for t in tail]
    scratch += [vm((n_ctx - 1,) + t, BF16) for t in tail]
    scratch += [
        vm((8, width), F32),
        vm((16, width), F32),
        vm((n_ctx - 1, 16, width), F32),
        vm((16, width), F32),
        vm((n_pair - 1, 16, width), F32),
        vm((16, width), F32),
        vm((n_dp - 1, 16, width), F32),
    ]
    n_sends = (
        6 * ((n_dp - 1) + (n_pair - 1) + (n_ctx - 1))
        + 2 * ((n_ctx - 1) + (n_pair - 1) + 1)
        + 1 + (n_ctx - 1) + (n_pair - 1) + (n_dp - 1)
    )
    dma = pltpu.SemaphoreType.DMA
    most = max(n_dp, n_ctx, n_pair)
    scratch += [
        dma((2,)),
        dma((n_sends,)),
        dma((2, n_ctx)),
        dma((2, n_pair)),
        dma((2,)),
        dma((6, n_dp - 1)),
        dma((6, n_pair - 1)),
        dma((6, n_ctx - 1)),
        dma((4, most)),
    ]
    return pl.pallas_call(
        functools.partial(scatter_body, sizes, half),
        out_shape=out_shape,
        in_specs=[vmem_spec] * 9,
        out_specs=[vmem_spec] * 9,
        scratch_shapes=scratch,
        compiler_params=pltpu.CompilerParams(
            collective_id=2, has_side_effects=True, vmem_limit_bytes=VMEM_LIMIT
        ),
    )(lo, tg, *grads, small)


def fused_body(sizes, dims, *refs):
    here = Place(sizes)
    n_dp, n_ctx, n_pair = here.n_dp, here.n_ctx, here.n_pair
    d, z, p, c = here.dp, here.ctx, here.pair, here.side
    half, width, share, cols, fw = dims
    block = 2 * half
    hw = n_pair * cols
    lanes = 2 * HEAD_DIM
    n_twos = hw // lanes
    n_rows = n_dp * n_ctx
    two = n_ctx // 2
    it = iter(refs)

    def take(n):
        return [next(it) for _ in range(n)]

    tokens, out_grad = take(2)
    narrow_shards = take(4)
    shards = [None] + take(2)
    vectors, column_biases = take(6), take(3)
    rows_out = take(2)
    owned = take(3)
    small_out = next(it)
    full = take(3)
    pack_all, vecs, cold = take(3)
    tok, og, lo, tg = take(4)
    (
        xn1, wqkv, wo, qs, ks, vs, o32, mixed, hid, xn2, ogf, act, ug, bg, dm, dqkv, tra, trb,
        wide, whole, ssend, srecv, dwd, small,
    ) = take(24)
    p_first = take(n_ctx)
    first_land, second_land, ctx_land = take(3), take(3), take(3)
    side_land, small_b, ctx_small, small_c, pair_small, small_d, dp_small = take(7)
    (
        own_sem, put_sem, rows_sem, line_sem, pair_sem, dp_sem, diag_dp_sem, diag_pair_sem, swap_send,
        swap_recv, first_sem, second_sem, ctx_sem, out_line, out_pair, out_side, small_sem,
    ) = take(17)
    partner = here.partner()
    own_row = d * n_ctx + z
    mine = p * n_ctx + z
    scale = HEAD_DIM ** -0.5
    first_head = lax.broadcasted_iota(jnp.int32, (1, lanes), 1) < HEAD_DIM
    zero16 = jnp.zeros((), BF16)
    side_rows = pl.ds(pl.multiple_of(c * half, half), half)
    far_side = pl.ds(pl.multiple_of((1 - c) * half, half), half)
    sends = Sends(put_sem)

    def arrive(slot, sem):
        remote(slot, slot, put_sem.at[0], sem, partner).wait_recv()

    def far_first():
        upper = z // two
        order = []
        for i in range(n_ctx - 1):
            down = n_ctx - 1 - i
            down = down - (z - down + n_ctx) // n_ctx
            up = i + (i - z + n_ctx) // n_ctx
            zz = upper * up + (1 - upper) * down
            order.append((zz, (d, zz, here.tp)))
        return order

    line_order = far_first()

    def shard_rows(r, count=1):
        return pl.ds(pl.multiple_of(r * share, 16), count * share)

    def slot(a, pp, dd, zz, count=1):
        return full[a].at[pp, shard_rows(dd * n_ctx + zz, count)]

    gather_own = [None] + [
        pltpu.make_async_copy(shards[a], slot(a, p, d, z), own_sem.at[a]) for a in (1, 2)
    ]

    def gather_start(a):
        source = slot(a, p, d, z) if a == 0 else shards[a]
        for zz, device in line_order:
            sends.go(source, slot(a, p, d, z), line_sem.at[a, z], device)

    def gather_hop(a):
        if a > 0:
            gather_own[a].wait()
        for k in range(1, n_ctx):
            zz = here.other_ctx(k)[0]
            arrive(slot(a, p, d, zz), line_sem.at[a, zz])
        group = slot(a, p, d, 0, n_ctx)
        for k in range(1, n_pair):
            sends.go(group, group, pair_sem.at[a, p], here.other_pair(k)[1])
        for k in range(1, n_dp):
            sends.go(group, group, dp_sem.at[a, d], here.other_dp(k)[1])

    def gather_turn(a):
        for k in range(1, n_pair):
            pp = here.other_pair(k)[0]
            arrive(slot(a, pp, d, 0, n_ctx), pair_sem.at[a, pp])
            first = slot(a, pp, d, 0, two)
            for j in range(1, n_dp):
                sends.go(first, first, diag_dp_sem.at[a, pp, d], here.other_dp(j)[1])
        for k in range(1, n_dp):
            dd = here.other_dp(k)[0]
            arrive(slot(a, p, dd, 0, n_ctx), dp_sem.at[a, dd])
            second = slot(a, p, dd, two, n_ctx - two)
            for j in range(1, n_pair):
                sends.go(second, second, diag_pair_sem.at[a, p, dd], here.other_pair(j)[1])

    def gather_end(a):
        for k in range(1, n_pair):
            pp = here.other_pair(k)[0]
            for j in range(1, n_dp):
                dd = here.other_dp(j)[0]
                arrive(slot(a, pp, dd, 0, two), diag_dp_sem.at[a, pp, dd])
                arrive(slot(a, pp, dd, two, n_ctx - two), diag_pair_sem.at[a, pp, dd])

    def pack_start():
        own = pack_all.at[p, own_row]
        for zz, device in line_order:
            sends.go(own, own, line_sem.at[3, z], device)

    def pack_hop():
        for k in range(1, n_ctx):
            zz = here.other_ctx(k)[0]
            arrive(pack_all.at[p, d * n_ctx + zz], line_sem.at[3, zz])
        group = pack_all.at[p, pl.ds(d * n_ctx, n_ctx)]
        for k in range(1, n_pair):
            sends.go(group, group, pair_sem.at[3, p], here.other_pair(k)[1])
        for k in range(1, n_dp):
            sends.go(group, group, dp_sem.at[3, d], here.other_dp(k)[1])

    def pack_end():
        for k in range(1, n_pair):
            pp = here.other_pair(k)[0]
            arrive(pack_all.at[pp, pl.ds(d * n_ctx, n_ctx)], pair_sem.at[3, pp])
        for k in range(1, n_dp):
            dd = here.other_dp(k)[0]
            arrive(pack_all.at[p, pl.ds(dd * n_ctx, n_ctx)], dp_sem.at[3, dd])

    rows_own = [
        pltpu.make_async_copy(source.at[mine, side_rows], target.at[z], own_sem.at[4 + i])
        for i, (source, target) in enumerate(((tokens, tok), (out_grad, og)))
    ]

    def rows_start(i, source, target):
        for zz, device in line_order:
            sends.go(source.at[p * n_ctx + zz, side_rows], target.at[z], rows_sem.at[i, z], device)

    def grad_slot(ref, pp, dd, k):
        return ref.at[pp, shard_rows(dd * n_ctx + (z + k) % n_ctx)]

    def pair_leads(a, k):
        return a == 2 and k % 2 == 1

    def scatter_start(a, ref, ks):
        for k in ks:
            if pair_leads(a, k):
                for j in range(1, n_pair):
                    pp, device = here.other_pair(j)
                    for i in range(n_dp):
                        sends.go(grad_slot(ref, pp, i, k), first_land[a].at[j - 1, i, k], first_sem.at[a, j - 1, i, k], device)
            else:
                for j in range(1, n_dp):
                    dd, device = here.other_dp(j)
                    for i in range(n_pair):
                        sends.go(grad_slot(ref, i, dd, k), first_land[a].at[j - 1, i, k], first_sem.at[a, j - 1, i, k], device)

    def add_into(target, parts):
        total = target[...].astype(F32)
        for part in parts:
            total = total + part[...].astype(F32)
        target[...] = total.astype(BF16)

    def scatter_turn(a, ref, ks):
        for k in ks:
            leads = pair_leads(a, k)
            n_lead, n_next = (n_pair, n_dp) if leads else (n_dp, n_pair)
            for i in range(n_next):
                parts = [first_land[a].at[j - 1, i, k] for j in range(1, n_lead)]
                for j in range(1, n_lead):
                    arrive(parts[j - 1], first_sem.at[a, j - 1, i, k])
                target = grad_slot(ref, p, i, k) if leads else grad_slot(ref, i, d, k)
                add_into(target, parts)
            for j in range(1, n_next):
                other, device = here.other_dp(j) if leads else here.other_pair(j)
                source = grad_slot(ref, p, other, k) if leads else grad_slot(ref, other, d, k)
                sends.go(source, second_land[a].at[j - 1, k], second_sem.at[a, j - 1, k], device)

    def scatter_line(a, ref, ks):
        for k in ks:
            n_next = n_dp if pair_leads(a, k) else n_pair
            parts = [second_land[a].at[j - 1, k] for j in range(1, n_next)]
            for j in range(1, n_next):
                arrive(parts[j - 1], second_sem.at[a, j - 1, k])
            add_into(grad_slot(ref, p, d, k), parts)
            if k > 0:
                sends.go(grad_slot(ref, p, d, k), ctx_land[a].at[k - 1], ctx_sem.at[a, k - 1], here.other_ctx(k)[1])

    def scatter_end(a, ref):
        total = ref[p, shard_rows(own_row), :].astype(F32)
        for k in range(1, n_ctx):
            arrive(ctx_land[a].at[k - 1], ctx_sem.at[a, k - 1])
            total = total + ctx_land[a][k - 1].astype(F32)
        owned[a][...] = total

    near = list(range(1, n_ctx)) + [0]
    early, late = near[:two], near[two:]

    def out_slot(i, s, rows):
        return rows_out[i].at[s, rows]

    def out_start(i, source):
        for zz, device in line_order:
            sends.go(source.at[zz], out_slot(i, mine, side_rows), out_line.at[i, z], device)
        copy = pltpu.make_async_copy(source.at[z], out_slot(i, mine, side_rows), own_sem.at[6 + i])
        copy.start()
        return copy

    def out_pass(i, s, source):
        piece = out_slot(i, s, side_rows)
        for j in range(1, n_pair):
            sends.go(source, piece, out_pair.at[i, s], here.other_pair(j)[1])
        sends.go(source, piece, out_side.at[i, s], partner)

    def out_hop(i):
        for k in range(1, n_ctx):
            s = p * n_ctx + here.other_ctx(k)[0]
            piece = out_slot(i, s, side_rows)
            arrive(piece, out_line.at[i, here.other_ctx(k)[0]])
            out_pass(i, s, piece)

    def out_cross(i):
        for j in range(1, n_pair):
            pp = here.other_pair(j)[0]
            for k in range(n_ctx):
                s = pp * n_ctx + (z + k) % n_ctx
                piece = out_slot(i, s, side_rows)
                arrive(piece, out_pair.at[i, s])
                sends.go(piece, piece, out_side.at[i, s], partner)

    def out_end(i):
        for s in range(n_pair * n_ctx):
            arrive(out_slot(i, s, far_side), out_side.at[i, s])

    def own_rows(b):
        return pl.ds(pl.multiple_of(b * block + c * half, half), half)

    def far_rows(b):
        return pl.ds(pl.multiple_of(b * block + (1 - c) * half, half), half)

    def block_rows(b):
        return pl.ds(pl.multiple_of(b * block, block), block)

    def swap(stage, b, src, dst):
        return remote(src, dst, swap_send.at[stage, b], swap_recv.at[stage, b], partner)

    def rows_copy(stage, b, ref):
        return swap(stage, b, ref.at[own_rows(b)], ref.at[own_rows(b)])

    def rows_arrive(stage, b, ref):
        swap(stage, b, ref.at[far_rows(b)], ref.at[far_rows(b)]).wait_recv()

    def part_copy(stage, place, b):
        return swap(stage, b, ssend.at[place, b], srecv.at[place, b])

    def part_store(i, b, value):
        wide[i, pl.ds(pl.multiple_of(b * block, block), half), :] = value[:, :hw]
        wide[i, pl.ds(pl.multiple_of(b * block + half, half), half), :] = value[:, hw:]

    def part_load(i, b):
        left = wide[i, pl.ds(pl.multiple_of(b * block, block), half), :]
        right = wide[i, pl.ds(pl.multiple_of(b * block + half, half), half), :]
        return jnp.concatenate([left, right], axis=1)

    rows_own[0].start()
    rows_own[1].start()
    gather_own[1].start()
    gather_own[2].start()
    for a in range(4):
        full[0][p, shard_rows(own_row), a * cols : (a + 1) * cols] = narrow_shards[a][...]
    own_pack = pack_all.at[p, own_row]
    own_pack[...] = jnp.zeros(own_pack.shape, F32)
    for i in range(6):
        own_pack[i : i + 1, :share] = vectors[i][...].astype(F32)
    row = 6
    for ref in column_biases:
        n = ref.shape[1]
        for w in range(0, n, 128):
            m = min(128, n - w)
            own_pack[row : row + 1, :m] = ref[:, w : w + m].astype(F32)
            row += 1
    small[...] = jnp.zeros_like(small)
    here.barrier(True)
    pack_start()
    gather_start(0)
    gather_start(1)
    rows_start(0, tokens, tok)
    gather_start(2)
    rows_start(1, out_grad, og)
    pack_hop()
    pack_end()
    for r in range(n_rows):
        own_part = pack_all[p, r]
        vecs[0:8, r * share : (r + 1) * share] = own_part[0:8, :share]
    for i in range(n_pair):
        piece = pack_all[i, d * n_ctx]
        for line in range(2):
            for w in range(0, cols, 128):
                n = min(128, cols - w)
                row = 6 + 2 * line + w // 128
                cold[line : line + 1, i * cols + w : i * cols + w + n] = piece[row : row + 1, :n]
        for w in range(0, fw, 128):
            row = 10 + w // 128
            cold[2 + i : 3 + i, w : w + 128] = piece[row : row + 1, :]
    gain_one, shift_one, out_shift = vecs[0:1, :], vecs[1:2, :], vecs[2:3, :]
    gain_two, shift_two, down_shift = vecs[3:4, :], vecs[4:5, :], vecs[5:6, :]

    def norm_one(b):
        scaled, _ = normalize(tok[b].astype(F32))
        xn1[own_rows(b), :] = (scaled * gain_one + shift_one).astype(BF16)
        rows_copy(1, b, xn1).start()

    rows_own[0].wait()
    norm_one(z)
    gather_hop(0)
    gather_turn(0)
    gather_hop(1)
    for k in range(1, n_ctx):
        b = here.other_ctx(k)[0]
        arrive(tok.at[b], rows_sem.at[0, b])
        norm_one(b)
    gather_end(0)
    for i in range(n_pair):
        for a, base in enumerate((0, hw, 2 * hw)):
            wqkv[:, base + i * cols : base + (i + 1) * cols] = full[0][i, :, a * cols : (a + 1) * cols]
        wo[:, i * cols : (i + 1) * cols] = full[0][i, :, 3 * cols : 4 * cols]
    q_shift, v_shift = cold[0:1, :hw], cold[1:2, :hw]

    @pl.loop(0, n_ctx)
    def _(b):
        rows_arrive(1, b, xn1)
        product = nn_dot(xn1[block_rows(b), :], wqkv[...])
        qs[block_rows(b), :] = (product[:, :hw] + q_shift).astype(BF16) * jnp.asarray(scale, BF16)
        ks[block_rows(b), :] = product[:, hw : 2 * hw].astype(BF16)
        vs[block_rows(b), :] = (product[:, 2 * hw :] + v_shift).astype(BF16)

    for b in range(n_ctx):
        reach = (b + 1) * block
        here_rows = slice(b * block, (b + 1) * block)

        @pl.loop(0, n_twos)
        def _(j):
            at = pl.ds(pl.multiple_of(j * lanes, lanes), lanes)
            queries, keys, values = qs[here_rows, at], ks[:reach, at], vs[:reach, at]
            pieces = []
            for e in range(2):
                head = first_head if e == 0 else jnp.logical_not(first_head)
                scores = nt_dot(jnp.where(head, queries, zero16), keys)
                powers = jnp.exp(scores - jnp.max(scores, axis=-1, keepdims=True))
                inverse = 1.0 / jnp.sum(powers, axis=-1, keepdims=True)
                probs = (powers * inverse).astype(BF16)
                p_first[b][2 * j + e] = probs
                pieces.append(nn_dot(probs, values))
            out = jnp.where(first_head, pieces[0], pieces[1])
            o32[here_rows, at] = out
            mixed[here_rows, at] = out.astype(BF16)

        whole[b % 2] = nt_dot(mixed[here_rows, :], wo[...])
        ssend[0, b] = whole[b % 2, far_side, :].astype(BF16)
        part_copy(2, 0, b).start()
        hid[b] = whole[b % 2, side_rows, :]
        if b == 0:
            gather_turn(1)
        if b == 1:
            gather_hop(2)

    @pl.loop(0, n_ctx)
    def _(b):
        part_copy(2, 0, b).wait()
        hidden = tok[b].astype(F32) + (hid[b] + srecv[0, b].astype(F32)) + out_shift
        hid[b] = hidden
        scaled, _ = normalize(hidden)
        xn2[own_rows(b), :] = (scaled * gain_two + shift_two).astype(BF16)
        rows_copy(3, b, xn2).start()

    gather_end(1)

    @pl.loop(0, n_ctx)
    def _(b):
        rows_arrive(3, b, xn2)
        normed = xn2[block_rows(b), :]
        for i in range(n_pair):
            upward = nn_dot(normed, full[1][i]) + cold[2 + i : 3 + i, :fw]
            big_phi = 0.5 + 0.5 * lax.erf(upward * root_half)
            act[i, block_rows(b), :] = (upward * big_phi).astype(BF16)
            slope = big_phi + upward * density_scale * jnp.exp(-0.5 * upward * upward)
            ug[i, block_rows(b), :] = slope.astype(BF16)

    rows_own[1].wait()
    for k in range(n_ctx):
        b = (z + k) % n_ctx
        if k > 0:
            arrive(og.at[b], rows_sem.at[1, b])
        swap(0, b, og.at[b], ogf.at[own_rows(b)]).start()
        ogf[own_rows(b), :] = og[b]
    for b in range(n_ctx):
        rows_arrive(0, b, ogf)

    step = 256

    def transposed(ref, out):
        for b in range(n_ctx):
            out[:, b * block : (b + 1) * block] = ref[b * block : (b + 1) * block, :].T

    transposed(ogf, trb)
    gather_turn(2)
    gathered = len(sends.started)

    @pl.loop(0, width // step)
    def _(r):
        rows = pl.ds(pl.multiple_of(r * step, step), step)
        for i in range(n_pair):
            dwd[i, rows, :] = nn_dot(trb[rows, :], act[i]).astype(BF16)

    scatter_start(2, dwd, near)
    gather_end(2)

    def through(ref, weight, rows):
        total = nt_dot(ref[0, rows, :], weight[0])
        for i in range(1, n_pair):
            total = total + nt_dot(ref[i, rows, :], weight[i])
        return total

    @pl.loop(0, n_ctx)
    def _(b):
        grads = ogf[block_rows(b), :]
        for i in range(n_pair):
            slope = ug[i, block_rows(b), :].astype(F32)
            rows_grad = (nn_dot(grads, full[2][i]) * slope).astype(BF16)
            ug[i, block_rows(b), :] = rows_grad
            small[8 + i : 9 + i, :] += jnp.sum(rows_grad.astype(F32), axis=0, keepdims=True)
        whole[0] = through(ug, full[1], block_rows(b))
        ssend[0, b] = whole[0, far_side, :].astype(BF16)
        part_copy(5, 0, b).start()
        part_store(1, b, whole[0, side_rows, :])
        whole[1] = through(act, full[2], block_rows(b))
        ssend[1, b] = whole[1, far_side, :].astype(BF16)
        part_copy(4, 1, b).start()
        part_store(0, b, whole[1, side_rows, :])

    transposed(xn2, tra)
    scatter_turn(2, dwd, near)
    for copy in sends.started[:gathered]:
        copy.wait_send()

    @pl.loop(0, width // step)
    def _(r):
        rows = pl.ds(pl.multiple_of(r * step, step), step)
        for i in range(n_pair):
            full[1][i, rows, :] = nn_dot(tra[rows, :], ug[i]).astype(BF16)

    scatter_start(1, full[1], near)

    @pl.loop(0, n_ctx)
    def _(b):
        part_copy(5, 0, b).wait()
        grad_two = part_load(1, b) + srecv[0, b].astype(F32)
        part_copy(4, 1, b).wait()
        lo[b] = (hid[b] + (part_load(0, b) + srecv[1, b].astype(F32)) + down_shift).astype(BF16)
        scaled, spread = normalize(hid[b])
        own_grad = og[b].astype(F32)
        hidden_grad = own_grad + norm_back(grad_two * gain_two, scaled, spread)
        hid[b] = hidden_grad
        branch = hidden_grad.astype(BF16)
        bg[own_rows(b), :] = branch
        rows_copy(6, b, bg).start()
        small[2:3, :] += jnp.sum(branch.astype(F32), axis=0, keepdims=True)
        small[3:4, :] += jnp.sum(grad_two * scaled, axis=0, keepdims=True)
        small[4:5, :] += jnp.sum(grad_two, axis=0, keepdims=True)
        small[5:6, :] += jnp.sum(own_grad, axis=0, keepdims=True)

    lo_copy = out_start(0, lo)
    out_pass(0, mine, lo.at[z])

    @pl.loop(0, n_ctx)
    def _(b):
        rows_arrive(6, b, bg)
        dm[block_rows(b), :] = nn_dot(bg[block_rows(b), :], wo[...]).astype(BF16)

    transposed(bg, trb)

    @pl.loop(0, width // step)
    def _(r):
        rows = pl.ds(pl.multiple_of(r * step, step), step)
        product = nn_dot(trb[rows, :], mixed[...])
        for i in range(n_pair):
            full[0][i, rows, 3 * cols : 4 * cols] = product[:, i * cols : (i + 1) * cols].astype(BF16)

    for b in reversed(range(n_ctx)):
        reach = (b + 1) * block
        here_rows = slice(b * block, (b + 1) * block)

        @pl.loop(0, n_twos)
        def _(j):
            at = pl.ds(pl.multiple_of(j * lanes, lanes), lanes)
            queries, keys, values = qs[here_rows, at], ks[:reach, at], vs[:reach, at]
            mix_grad, mix = dm[here_rows, at], o32[here_rows, at]
            towards = mix_grad.astype(F32) * mix
            query_parts, key_sum, value_sum = [], None, None
            for e in range(2):
                head = first_head if e == 0 else jnp.logical_not(first_head)
                grad_head = jnp.where(head, mix_grad, zero16)
                prob_grad = nt_dot(grad_head, values)
                centre = jnp.sum(jnp.where(head, towards, 0.0), axis=-1, keepdims=True)
                probs = p_first[b][2 * j + e]
                score_grad = (probs.astype(F32) * (prob_grad - centre)).astype(BF16)
                query_parts.append(nn_dot(score_grad, keys))
                key_term = tn_dot(score_grad, jnp.where(head, queries, zero16))
                value_term = tn_dot(probs, grad_head)
                key_sum = key_term if key_sum is None else key_sum + key_term
                value_sum = value_term if value_sum is None else value_sum + value_term
            query_grad = jnp.where(first_head, query_parts[0], query_parts[1]) * scale
            dqkv[here_rows, at] = query_grad.astype(BF16)
            if b == n_ctx - 1:
                wide[0, :, at] = key_sum
                wide[1, :, at] = value_sum
            else:
                wide[0, :reach, at] += key_sum
                wide[1, :reach, at] += value_sum

        if b == 3:
            scatter_line(2, dwd, near)
        if b == 1:
            scatter_turn(1, full[1], early)
        if b == 0:
            out_hop(0)

    @pl.loop(0, n_ctx)
    def _(b):
        dqkv[block_rows(b), hw : 2 * hw] = wide[0, block_rows(b), :].astype(BF16)
        dqkv[block_rows(b), 2 * hw :] = wide[1, block_rows(b), :].astype(BF16)
        small[6:7, :hw] += jnp.sum(dqkv[block_rows(b), :hw].astype(F32), axis=0, keepdims=True)
        small[7:8, :hw] += jnp.sum(dqkv[block_rows(b), 2 * hw :].astype(F32), axis=0, keepdims=True)
        whole[0] = nt_dot(dqkv[block_rows(b), :], wqkv[...])
        ssend[1, b] = whole[0, far_side, :].astype(BF16)
        part_copy(7, 1, b).start()
        part_store(0, b, whole[0, side_rows, :])

    transposed(xn1, tra)

    @pl.loop(0, width // step)
    def _(r):
        rows = pl.ds(pl.multiple_of(r * step, step), step)
        product = nn_dot(tra[rows, :], dqkv[...])
        for i in range(n_pair):
            for a in range(3):
                full[0][i, rows, a * cols : (a + 1) * cols] = product[
                    :, a * hw + i * cols : a * hw + (i + 1) * cols
                ].astype(BF16)

    scatter_start(0, full[0], near)

    @pl.loop(0, n_ctx)
    def _(b):
        part_copy(7, 1, b).wait()
        grad_one = part_load(0, b) + srecv[1, b].astype(F32)
        scaled, spread = normalize(tok[b].astype(F32))
        tg[b] = (hid[b] + norm_back(grad_one * gain_one, scaled, spread)).astype(BF16)
        small[0:1, :] += jnp.sum(grad_one * scaled, axis=0, keepdims=True)
        small[1:2, :] += jnp.sum(grad_one, axis=0, keepdims=True)

    sends.go(small.at[pl.ds(0, 8)], side_land, small_sem.at[0, 0], partner)
    tg_copy = out_start(1, tg)
    out_pass(1, mine, tg.at[z])
    scatter_turn(1, full[1], late)
    arrive(side_land, small_sem.at[0, 0])
    small_b[0:6, :] = small[0:6, :] + side_land[0:6, :]
    small_b[6:16, :] = small[6:16, :]
    for k in range(1, n_pair):
        sends.go(small_b, pair_small.at[k - 1], small_sem.at[2, k - 1], here.other_pair(k)[1])
    out_cross(0)
    scatter_line(1, full[1], early)
    scatter_turn(0, full[0], early)
    out_hop(1)
    scatter_line(1, full[1], late)
    scatter_turn(0, full[0], late)
    total = small_b[...]
    for k in range(1, n_pair):
        arrive(pair_small.at[k - 1], small_sem.at[2, k - 1])
        total = total + pair_small[k - 1]
    small_c[...] = total
    for k in range(1, n_dp):
        sends.go(small_c, dp_small.at[k - 1], small_sem.at[3, k - 1], here.other_dp(k)[1])
    scatter_line(0, full[0], near)
    scatter_end(2, dwd)
    scatter_end(1, full[1])
    out_end(0)
    total = small_c[...]
    for k in range(1, n_dp):
        arrive(dp_small.at[k - 1], small_sem.at[3, k - 1])
        total = total + dp_small[k - 1]
    small_d[...] = total
    for k in range(1, n_ctx):
        sends.go(small_d, ctx_small.at[k - 1], small_sem.at[1, k - 1], here.other_ctx(k)[1])
    out_cross(1)
    scatter_end(0, full[0])
    total = small_d[...]
    for k in range(1, n_ctx):
        arrive(ctx_small.at[k - 1], small_sem.at[1, k - 1])
        total = total + ctx_small[k - 1]
    small_out[...] = total
    out_end(1)
    lo_copy.wait()
    tg_copy.wait()

    @pl.loop(0, n_ctx)
    def _(b):
        swap(0, b, og.at[b], ogf.at[own_rows(b)]).wait_send()
        rows_copy(1, b, xn1).wait_send()
        rows_copy(3, b, xn2).wait_send()
        rows_copy(6, b, bg).wait_send()

    for copy in sends.started[gathered:]:
        copy.wait_send()


def fused_call(sizes, tokens, out_grad, shards, vectors, column_biases):
    n_dp, n_ctx, n_tp = sizes
    n_pair = n_tp // 2
    seqs, block, width = tokens.shape
    half = block // 2
    length = n_ctx * block
    share, cols = shards[0].shape
    fw = shards[4].shape[1]
    widths = [4 * cols, fw, fw]
    hw = n_pair * cols
    heads = hw // HEAD_DIM
    two = n_ctx // 2
    any_spec = pl.BlockSpec(memory_space=pl.ANY)
    vmem_spec = pl.BlockSpec(memory_space=pltpu.VMEM)
    shape = jax.ShapeDtypeStruct
    vm = pltpu.VMEM
    dma = pltpu.SemaphoreType.DMA
    out_shape = [shape(tokens.shape, BF16)] * 2
    out_shape += [shape((share, w), F32) for w in widths]
    out_shape += [shape((16, width), F32)]
    scratch = [vm((n_pair, width, w), BF16) for w in widths]
    scratch += [
        vm((n_pair, n_dp * n_ctx, 16, 128), F32),
        vm((8, width), F32),
        vm((8, width), F32),
    ]
    scratch += [vm((n_ctx, half, width), BF16)] * 4
    scratch += [
        vm((length, width), BF16),
        vm((width, 3 * hw), BF16),
        vm((width, hw), BF16),
        vm((length, hw), BF16),
        vm((length, hw), BF16),
        vm((length, hw), BF16),
        vm((length, hw), F32),
        vm((length, hw), BF16),
        vm((n_ctx, half, width), F32),
        vm((length, width), BF16),
        vm((length, width), BF16),
        vm((n_pair, length, fw), BF16),
        vm((n_pair, length, fw), BF16),
        vm((length, width), BF16),
        vm((length, hw), BF16),
        vm((length, 3 * hw), BF16),
        vm((width, length), BF16),
        vm((width, length), BF16),
        vm((2, length, hw), F32),
        vm((2, block, width), F32),
        vm((2, n_ctx, half, width), BF16),
        vm((2, n_ctx, half, width), BF16),
        vm((n_pair, width, fw), BF16),
        vm((16, width), F32),
    ]
    scratch += [vm((heads, block, (b + 1) * block), BF16) for b in range(n_ctx)]
    lead, after = max(n_dp, n_pair) - 1, max(n_dp, n_pair)
    scratch += [vm((lead, after, n_ctx, share, w), BF16) for w in widths]
    scratch += [vm((lead, n_ctx, share, w), BF16) for w in widths]
    scratch += [vm((n_ctx - 1, share, w), BF16) for w in widths]
    scratch += [
        vm((8, width), F32),
        vm((16, width), F32),
        vm((n_ctx - 1, 16, width), F32),
        vm((16, width), F32),
        vm((n_pair - 1, 16, width), F32),
        vm((16, width), F32),
        vm((n_dp - 1, 16, width), F32),
    ]
    most = max(n_dp, n_ctx, n_pair)
    scratch += [
        dma((8,)),
        dma((260,)),
        dma((2, n_ctx)),
        dma((4, n_ctx)),
        dma((4, n_pair)),
        dma((4, n_dp)),
        dma((3, n_pair, n_dp)),
        dma((3, n_pair, n_dp)),
        dma((8, n_ctx)),
        dma((8, n_ctx)),
        dma((3, lead, after, n_ctx)),
        dma((3, lead, n_ctx)),
        dma((3, n_ctx)),
        dma((2, n_ctx)),
        dma((2, seqs)),
        dma((2, seqs)),
        dma((4, most)),
    ]
    return pl.pallas_call(
        functools.partial(fused_body, sizes, (half, width, share, cols, fw)),
        out_shape=out_shape,
        in_specs=[any_spec] * 2 + [vmem_spec] * 4 + [any_spec] * 2 + [vmem_spec] * 9,
        out_specs=[any_spec] * 2 + [vmem_spec] * 4,
        scratch_shapes=scratch,
        compiler_params=pltpu.CompilerParams(
            collective_id=3, has_side_effects=True, vmem_limit_bytes=67043328
        ),
    )(tokens, out_grad, *shards, *vectors, *column_biases)


def finish_body(n_ctx, share, cols, *refs):
    lo_in, tg_in, attn, up, down, small = refs[:6]
    lo, tg, dq, dk, dv, do, du, dd = refs[6:14]
    vectors = refs[14:20]
    shifts = refs[20:22]
    up_shift = refs[22]
    lo[...] = lo_in[...]
    tg[...] = tg_in[...].astype(F32)
    row = lax.axis_index("dp") * n_ctx + lax.axis_index("ctx")
    pair = lax.axis_index("tp") // 2
    width = small.shape[1]

    @pl.when(pl.program_id(0) == 0)
    def _():
        for i, ref in enumerate((dq, dk, dv, do)):
            ref[...] = attn[:, i * cols : (i + 1) * cols]
        du[...] = up[...]
        dd[...] = down[...]
        turned = pltpu.roll(small[0:8, :], (width - row * share) % width, 1)
        for i, ref in enumerate(vectors):
            ref[...] = turned[i : i + 1, :share]
        turned = pltpu.roll(small[0:8, :], (width - pair * cols) % width, 1)
        for i, ref in enumerate(shifts):
            ref[...] = turned[6 + i : 7 + i, :cols]
        row_of = small[pl.ds(8 + pair, 1), :]
        for i in range(up_shift.shape[0]):
            up_shift[i : i + 1, :] = row_of[:, i * 128 : (i + 1) * 128]


def finish_call(sizes, cols, lo, tg, attn, up, down, small):
    n_dp, n_ctx, n_tp = sizes
    seqs, block, width = lo.shape
    share = attn.shape[0]
    shape = jax.ShapeDtypeStruct
    rows = pl.BlockSpec((1, block, width), lambda i: (i, 0, 0))

    def whole(s):
        return pl.BlockSpec(s, lambda i: (0, 0))

    out_tail = [(share, cols)] * 4 + [up.shape] * 2 + [(1, share)] * 6 + [(1, cols)] * 2 + [(up.shape[1] // 128, 128)]
    return pl.pallas_call(
        functools.partial(finish_body, n_ctx, share, cols),
        grid=(seqs,),
        out_shape=[shape(lo.shape, BF16), shape(lo.shape, F32)] + [shape(s, F32) for s in out_tail],
        in_specs=[rows, rows] + [whole(x.shape) for x in (attn, up, down, small)],
        out_specs=[rows, rows] + [whole(s) for s in out_tail],
    )(lo, tg, attn, up, down, small)


def fused_layer(sizes, tokens, out_grad, shards, vectors, column_biases):
    cols = shards[0].shape[1]
    lines = [v.reshape(1, -1) for v in (*vectors, *column_biases)]
    results = fused_call(sizes, tokens, out_grad, shards, lines[:6], lines[6:])
    final = finish_call(sizes, cols, *results)
    return (*final[:8], *[v.reshape(-1) for v in final[8:]])


def per_device(
    tokens,
    out_grad,
    query_weight,
    key_weight,
    value_weight,
    output_weight,
    up_weight,
    down_weight,
    norm1_gain,
    norm1_bias,
    output_bias,
    norm2_gain,
    norm2_bias,
    down_bias,
    query_bias,
    value_bias,
    up_bias,
):
    sizes = (lax.axis_size("dp"), lax.axis_size("ctx"), lax.axis_size("tp"))
    n_dp, n_ctx, n_tp = sizes
    n_pair = n_tp // 2
    seqs, block, width = tokens.shape
    assert seqs == n_ctx * n_pair
    share = norm1_gain.shape[0]
    cols = query_bias.shape[0]
    pair = lax.axis_index("tp") // 2
    row = lax.axis_index("dp") * n_ctx + lax.axis_index("ctx")
    shards = (query_weight, key_weight, value_weight, output_weight, up_weight, down_weight)
    vectors = (norm1_gain, norm1_bias, output_bias, norm2_gain, norm2_bias, down_bias)
    if share % 16 == 0 and n_ctx % 2 == 0:
        return fused_layer(
            sizes, tokens, out_grad, shards, vectors, (query_bias, value_bias, up_bias)
        )

    six = jnp.stack(vectors).astype(F32)
    vec = jnp.pad(six, ((0, 2), (0, 128 - share)))
    columns = jnp.arange(width) // cols == pair
    narrow = [jnp.where(columns, jnp.tile(b.astype(F32), width // cols), 0.0) for b in (query_bias, value_bias)]
    bias = jnp.pad(jnp.stack(narrow + [up_bias.astype(F32)]), ((0, 5), (0, 0)))

    gathered = gather_call(sizes, tokens, out_grad, shards, vec, bias)
    tok, og = gathered[0:2]
    weights = [w.reshape(n_pair, width, w.shape[3]) for w in gathered[2:8]]
    vecs = gathered[8][:, :, :share].transpose(1, 0, 2).reshape(8, width)
    results = compute_call(sizes, tok, og, weights, vecs, gathered[9])
    lo, tg = results[0:2]
    grads = [
        g.reshape(n_pair, n_dp * n_ctx, s.shape[0], s.shape[1]) for g, s in zip(results[2:8], shards)
    ]
    final = scatter_call(sizes, seqs, lo, tg, grads, results[8])
    layer_out, tokens_grad = final[0], final[1].astype(F32)
    small = final[8]
    owned = [lax.dynamic_slice_in_dim(small[i], row * share, share) for i in range(6)]
    shifts = [lax.dynamic_slice_in_dim(small[6 + i], pair * cols, cols) for i in range(2)]
    up_total = lax.dynamic_index_in_dim(small[8 : 8 + n_pair], pair, 0, keepdims=False)
    return (layer_out, tokens_grad, *final[2:8], *owned, *shifts, up_total)


def solution(mesh):
    rows_spec = P("dp", "ctx", None)
    weight_spec = P(("dp", "ctx"), "tp")
    vector_spec = P(("dp", "ctx"))
    column_spec = P("tp")
    common = (rows_spec,) * 2 + (weight_spec,) * 6 + (vector_spec,) * 6 + (column_spec,) * 3
    return jax.shard_map(
        per_device, mesh=mesh, in_specs=common, out_specs=common, check_vma=False
    )
```

```python
import functools

import jax
import jax.numpy as jnp
from jax import lax
from jax.experimental import pallas as pl
from jax.experimental.pallas import tpu as pltpu
from jax.sharding import PartitionSpec as P

HEAD_DIM = 64
MESH = pl.DeviceIdType.MESH
F32 = jnp.float32
BF16 = jnp.bfloat16
VMEM_LIMIT = 66 * 1000 * 1000

epsilon = 1e-05
root_half = 0.7071067811865476
density_scale = 0.3989422804014327


def remote(src, dst, send_sem, recv_sem, device):
    return pltpu.make_async_remote_copy(
        src_ref=src,
        dst_ref=dst,
        send_sem=send_sem,
        recv_sem=recv_sem,
        device_id=device,
        device_id_type=MESH,
    )


def nn_dot(left, right):
    return lax.dot_general(left, right, (((1,), (0,)), ((), ())), preferred_element_type=F32)


def nt_dot(left, right):
    return lax.dot_general(left, right, (((1,), (1,)), ((), ())), preferred_element_type=F32)


def tn_dot(left, right):
    return lax.dot_general(left, right, (((0,), (0,)), ((), ())), preferred_element_type=F32)


def normalize(values):
    centred = values - jnp.mean(values, axis=-1, keepdims=True)
    spread = lax.rsqrt(jnp.mean(centred * centred, axis=-1, keepdims=True) + epsilon)
    return centred * spread, spread


def norm_back(grad_scaled, scaled, spread):
    inner = grad_scaled - jnp.mean(grad_scaled, axis=-1, keepdims=True)
    inner = inner - scaled * jnp.mean(grad_scaled * scaled, axis=-1, keepdims=True)
    return inner * spread


class Place:
    def __init__(self, sizes):
        self.n_dp, self.n_ctx, self.n_tp = sizes
        self.n_pair = self.n_tp // 2
        self.dp = lax.axis_index("dp")
        self.ctx = lax.axis_index("ctx")
        self.tp = lax.axis_index("tp")
        self.pair = self.tp // 2
        self.side = self.tp % 2

    def other_dp(self, k):
        d = (self.dp + k) % self.n_dp
        return d, (d, self.ctx, self.tp)

    def other_ctx(self, k):
        z = (self.ctx + k) % self.n_ctx
        return z, (self.dp, z, self.tp)

    def other_pair(self, k):
        p = (self.pair + k) % self.n_pair
        return p, (self.dp, self.ctx, 2 * p + self.side)

    def partner(self):
        return (self.dp, self.ctx, 2 * self.pair + 1 - self.side)

    def barrier(self, far):
        sem = pltpu.get_barrier_semaphore()
        count = 1
        pl.semaphore_signal(sem, inc=1, device_id=self.partner(), device_id_type=MESH)
        if far:
            for size, other in (
                (self.n_dp, self.other_dp),
                (self.n_ctx, self.other_ctx),
                (self.n_pair, self.other_pair),
            ):
                for k in range(1, size):
                    pl.semaphore_signal(sem, inc=1, device_id=other(k)[1], device_id_type=MESH)
                    count += 1
        pl.semaphore_wait(sem, count)


class Sends:
    def __init__(self, sems):
        self.sems = sems
        self.started = []

    def go(self, src, dst, recv_sem, device):
        copy = remote(src, dst, self.sems.at[len(self.started)], recv_sem, device)
        copy.start()
        self.started.append(copy)

    def finish(self):
        for copy in self.started:
            copy.wait_send()


def gather_body(sizes, half, *refs):
    here = Place(sizes)
    n_dp, n_ctx, n_pair = here.n_dp, here.n_ctx, here.n_pair
    d, z, p, c = here.dp, here.ctx, here.pair, here.side
    tokens, out_grad = refs[0:2]
    shards = refs[2:8]
    vec, bias = refs[8:10]
    tok_own, og_own = refs[10:12]
    full = refs[12:18]
    vec_all, bias_all = refs[18:20]
    own_sem, send_sem, rows_sem, line_sem, group_sem, vline_sem, vgroup_sem, bias_sem = refs[20:28]
    own_row = d * n_ctx + z
    mine = p * n_ctx + z
    rows = pl.ds(pl.multiple_of(c * half, half), half)

    here.barrier(True)
    sends = Sends(send_sem)
    own = [
        pltpu.make_async_copy(tokens.at[mine, rows], tok_own.at[z], own_sem.at[0]),
        pltpu.make_async_copy(out_grad.at[mine, rows], og_own.at[z], own_sem.at[1]),
        pltpu.make_async_copy(vec, vec_all.at[own_row], own_sem.at[2]),
        pltpu.make_async_copy(bias, bias_all.at[p], own_sem.at[3]),
    ]
    for a in range(6):
        own.append(pltpu.make_async_copy(shards[a], full[a].at[p, own_row], own_sem.at[4 + a]))
    for copy in own:
        copy.start()

    def send_rows(index, source, target):
        for k in range(1, n_ctx):
            zz, device = here.other_ctx(k)
            sends.go(
                source.at[p * n_ctx + zz, rows], target.at[z], rows_sem.at[index, z], device
            )

    def send_line(a):
        for k in range(1, n_ctx):
            zz, device = here.other_ctx(k)
            sends.go(shards[a], full[a].at[p, own_row], line_sem.at[a, z], device)

    send_rows(0, tokens, tok_own)
    for k in range(1, n_ctx):
        zz, device = here.other_ctx(k)
        sends.go(vec, vec_all.at[own_row], vline_sem.at[z], device)
    for k in range(1, n_pair):
        pp, device = here.other_pair(k)
        sends.go(bias, bias_all.at[p], bias_sem.at[p], device)
    for a in range(6):
        send_line(a)
    send_rows(1, out_grad, og_own)

    for copy in own:
        copy.wait()

    def group(a, pp, dd):
        return full[a].at[pp, pl.ds(dd * n_ctx, n_ctx)]

    def wait_line(a):
        for k in range(1, n_ctx):
            zz, device = here.other_ctx(k)
            slot = full[a].at[p, d * n_ctx + zz]
            remote(slot, slot, send_sem.at[0], line_sem.at[a, zz], device).wait_recv()

    def send_pair(a, dd):
        for k in range(1, n_pair):
            pp, device = here.other_pair(k)
            sends.go(group(a, p, dd), group(a, p, dd), group_sem.at[a, p, dd], device)

    def send_dp(a, pp):
        for k in range(1, n_dp):
            dd, device = here.other_dp(k)
            sends.go(group(a, pp, d), group(a, pp, d), group_sem.at[a, pp, d], device)

    def wait_group(a, pp, dd):
        slot = group(a, pp, dd)
        remote(slot, slot, send_sem.at[0], group_sem.at[a, pp, dd], here.partner()).wait_recv()

    for a in range(6):
        wait_line(a)
        send_dp(a, p)
        send_pair(a, d)
    for k in range(1, n_ctx):
        zz, device = here.other_ctx(k)
        slot = vec_all.at[d * n_ctx + zz]
        remote(slot, slot, send_sem.at[0], vline_sem.at[zz], device).wait_recv()
    for k in range(1, n_dp):
        dd, device = here.other_dp(k)
        slot = vec_all.at[pl.ds(d * n_ctx, n_ctx)]
        sends.go(slot, slot, vgroup_sem.at[d], device)
    pair_first = (True, True, True, True, False, True)
    for a in range(6):
        if pair_first[a]:
            for k in range(1, n_pair):
                pp = here.other_pair(k)[0]
                wait_group(a, pp, d)
                send_dp(a, pp)
        else:
            for k in range(1, n_dp):
                dd = here.other_dp(k)[0]
                wait_group(a, p, dd)
                send_pair(a, dd)
    for a in range(6):
        for k in range(1, n_dp):
            dd = here.other_dp(k)[0]
            if pair_first[a]:
                wait_group(a, p, dd)
            for j in range(1, n_pair):
                wait_group(a, here.other_pair(j)[0], dd)
        if not pair_first[a]:
            for j in range(1, n_pair):
                wait_group(a, here.other_pair(j)[0], d)
    for k in range(1, n_dp):
        dd, device = here.other_dp(k)
        slot = vec_all.at[pl.ds(dd * n_ctx, n_ctx)]
        remote(slot, slot, send_sem.at[0], vgroup_sem.at[dd], device).wait_recv()
    for k in range(1, n_pair):
        pp, device = here.other_pair(k)
        slot = bias_all.at[pp]
        remote(slot, slot, send_sem.at[0], bias_sem.at[pp], device).wait_recv()
    for index, target in ((0, tok_own), (1, og_own)):
        for k in range(1, n_ctx):
            zz, device = here.other_ctx(k)
            slot = target.at[zz]
            remote(slot, slot, send_sem.at[0], rows_sem.at[index, zz], device).wait_recv()
    sends.finish()


def gather_call(sizes, tokens, out_grad, shards, vec, bias):
    n_dp, n_ctx, n_tp = sizes
    n_pair = n_tp // 2
    seqs, block, width = tokens.shape
    half = block // 2
    any_spec = pl.BlockSpec(memory_space=pl.ANY)
    vmem_spec = pl.BlockSpec(memory_space=pltpu.VMEM)
    own = jax.ShapeDtypeStruct((n_ctx, half, width), BF16)
    out_shape = [own, own]
    out_shape += [jax.ShapeDtypeStruct((n_pair, n_dp * n_ctx) + s.shape, BF16) for s in shards]
    out_shape += [
        jax.ShapeDtypeStruct((n_dp * n_ctx,) + vec.shape, F32),
        jax.ShapeDtypeStruct((n_pair,) + bias.shape, F32),
    ]
    n_sends = (
        2 * (n_ctx - 1)
        + (n_ctx - 1)
        + (n_pair - 1)
        + 6 * (n_ctx - 1)
        + (n_dp - 1)
        + 6 * ((n_dp - 1) + (n_pair - 1) + (n_dp - 1) * (n_pair - 1))
    )
    dma = pltpu.SemaphoreType.DMA
    return pl.pallas_call(
        functools.partial(gather_body, sizes, half),
        out_shape=out_shape,
        in_specs=[any_spec] * 10,
        out_specs=[vmem_spec] * 10,
        scratch_shapes=[
            dma((10,)),
            dma((n_sends,)),
            dma((2, n_ctx)),
            dma((6, n_ctx)),
            dma((6, n_pair, n_dp)),
            dma((n_ctx,)),
            dma((n_dp,)),
            dma((n_pair,)),
        ],
        compiler_params=pltpu.CompilerParams(
            collective_id=0, has_side_effects=True, vmem_limit_bytes=VMEM_LIMIT
        ),
    )(tokens, out_grad, *shards, vec, bias)


def compute_body(sizes, *refs):
    here = Place(sizes)
    n_ctx, n_pair = here.n_ctx, here.n_pair
    c = here.side
    (tok, og, gq, gk, gv, go, gu, gd, vecs, bias) = refs[:10]
    (lo, tg, dwq, dwk, dwv, dwo, dwu, dwd, small) = refs[10:19]
    (
        xn1, wqkv, wo, qs, ks, vs, o32, mixed, hid, xn2, ogf, act, ug, bg, dm,
        dka, dva, dqkv, tra, trb, part, ssend, srecv, p_first, send_sem, recv_sem,
    ) = refs[19 : 19 + 23] + (refs[42 : 42 + n_ctx],) + refs[42 + n_ctx :]
    half, width = tok.shape[1], tok.shape[2]
    block = 2 * half
    cols = gq.shape[2]
    hw = n_pair * cols
    fw = gu.shape[2]
    lanes = 2 * HEAD_DIM
    n_twos = hw // lanes
    partner = here.partner()
    scale = HEAD_DIM ** -0.5
    first_head = lax.broadcasted_iota(jnp.int32, (1, lanes), 1) < HEAD_DIM
    zero16 = jnp.zeros((), BF16)

    def own_rows(b):
        return pl.ds(pl.multiple_of(b * block + c * half, half), half)

    def far_rows(b):
        return pl.ds(pl.multiple_of(b * block + (1 - c) * half, half), half)

    def block_rows(b):
        return pl.ds(pl.multiple_of(b * block, block), block)

    def exchange(stage, b, src, dst):
        return remote(src, dst, send_sem.at[stage, b], recv_sem.at[stage, b], partner)

    def rows_copy(stage, b, ref):
        return exchange(stage, b, ref.at[own_rows(b)], ref.at[own_rows(b)])

    def rows_arrive(stage, b, ref):
        exchange(stage, b, ref.at[far_rows(b)], ref.at[far_rows(b)]).wait_recv()

    def part_copy(stage, slot, b):
        return exchange(stage, b, ssend.at[slot, b], srecv.at[slot, b])

    here.barrier(False)

    gain_one, shift_one, out_shift = vecs[0:1, :], vecs[1:2, :], vecs[2:3, :]
    gain_two, shift_two, down_shift = vecs[3:4, :], vecs[4:5, :], vecs[5:6, :]

    @pl.loop(0, n_ctx)
    def _(b):
        exchange(0, b, og.at[b], ogf.at[own_rows(b)]).start()
        ogf[own_rows(b), :] = og[b]
        scaled, _ = normalize(tok[b].astype(F32))
        xn1[own_rows(b), :] = (scaled * gain_one + shift_one).astype(BF16)
        rows_copy(1, b, xn1).start()

    for i in range(n_pair):
        at = slice(i * cols, (i + 1) * cols)
        wqkv[:, i * cols : (i + 1) * cols] = gq[i]
        wqkv[:, hw + i * cols : hw + (i + 1) * cols] = gk[i]
        wqkv[:, 2 * hw + i * cols : 2 * hw + (i + 1) * cols] = gv[i]
        wo[:, at] = go[i]
    q_shift = bias[0, 0:1, :hw]
    v_shift = bias[0, 1:2, :hw]
    for i in range(1, n_pair):
        q_shift = q_shift + bias[i, 0:1, :hw]
        v_shift = v_shift + bias[i, 1:2, :hw]

    @pl.loop(0, n_ctx)
    def _(b):
        rows_arrive(1, b, xn1)
        product = nn_dot(xn1[block_rows(b), :], wqkv[...])
        qs[block_rows(b), :] = (product[:, :hw] + q_shift).astype(BF16) * jnp.asarray(scale, BF16)
        ks[block_rows(b), :] = product[:, hw : 2 * hw].astype(BF16)
        vs[block_rows(b), :] = (product[:, 2 * hw :] + v_shift).astype(BF16)

    for b in range(n_ctx):
        reach = (b + 1) * block
        here_rows = slice(b * block, (b + 1) * block)

        @pl.loop(0, n_twos)
        def _(j):
            at = pl.ds(pl.multiple_of(j * lanes, lanes), lanes)
            queries, keys, values = qs[here_rows, at], ks[:reach, at], vs[:reach, at]
            pieces = []
            for e in range(2):
                head = first_head if e == 0 else jnp.logical_not(first_head)
                scores = nt_dot(jnp.where(head, queries, zero16), keys)
                powers = jnp.exp(scores - jnp.max(scores, axis=-1, keepdims=True))
                inverse = 1.0 / jnp.sum(powers, axis=-1, keepdims=True)
                probs = (powers * inverse).astype(BF16)
                p_first[b][2 * j + e] = probs
                pieces.append(nn_dot(probs, values))
            out = jnp.where(first_head, pieces[0], pieces[1])
            o32[here_rows, at] = out
            mixed[here_rows, at] = out.astype(BF16)

        ssend[0, b] = nt_dot(mixed[far_rows(b), :], wo[...]).astype(BF16)
        part_copy(2, 0, b).start()
        hid[b] = nt_dot(mixed[own_rows(b), :], wo[...])

    @pl.loop(0, n_ctx)
    def _(b):
        part_copy(2, 0, b).wait()
        hidden = tok[b].astype(F32) + (hid[b] + srecv[0, b].astype(F32)) + out_shift
        hid[b] = hidden
        scaled, _ = normalize(hidden)
        xn2[own_rows(b), :] = (scaled * gain_two + shift_two).astype(BF16)
        rows_copy(3, b, xn2).start()

    small[...] = jnp.zeros_like(small)

    @pl.loop(0, n_ctx)
    def _(b):
        rows_arrive(0, b, ogf)
        rows_arrive(3, b, xn2)
        normed = xn2[block_rows(b), :]
        grads = ogf[block_rows(b), :]
        for i in range(n_pair):
            upward = nn_dot(normed, gu[i]) + bias[i, 2:3, :]
            big_phi = 0.5 + 0.5 * lax.erf(upward * root_half)
            act[i, block_rows(b), :] = (upward * big_phi).astype(BF16)
            slope = big_phi + upward * density_scale * jnp.exp(-0.5 * upward * upward)
            rows_grad = (nn_dot(grads, gd[i]) * slope).astype(BF16)
            ug[i, block_rows(b), :] = rows_grad
            small[8 + i : 9 + i, :] += jnp.sum(rows_grad.astype(F32), axis=0, keepdims=True)

        def through(ref, weight, rows):
            total = nt_dot(ref[0, rows, :], weight[0])
            for i in range(1, n_pair):
                total = total + nt_dot(ref[i, rows, :], weight[i])
            return total

        ssend[1, b] = through(act, gd, far_rows(b)).astype(BF16)
        part_copy(4, 1, b).start()
        ssend[0, b] = through(ug, gu, far_rows(b)).astype(BF16)
        part_copy(5, 0, b).start()
        part[0, b] = through(act, gd, own_rows(b))
        part[1, b] = through(ug, gu, own_rows(b))

    def transposed(ref, out):
        for b in range(n_ctx):
            out[:, b * block : (b + 1) * block] = ref[b * block : (b + 1) * block, :].T

    @pl.loop(0, n_ctx)
    def _(b):
        part_copy(4, 1, b).wait()
        lo[b] = (hid[b] + (part[0, b] + srecv[1, b].astype(F32)) + down_shift).astype(BF16)
        part_copy(5, 0, b).wait()
        grad_two = part[1, b] + srecv[0, b].astype(F32)
        scaled, spread = normalize(hid[b])
        own_grad = og[b].astype(F32)
        hidden_grad = own_grad + norm_back(grad_two * gain_two, scaled, spread)
        hid[b] = hidden_grad
        branch = hidden_grad.astype(BF16)
        bg[own_rows(b), :] = branch
        rows_copy(6, b, bg).start()
        small[2:3, :] += jnp.sum(branch.astype(F32), axis=0, keepdims=True)
        small[3:4, :] += jnp.sum(grad_two * scaled, axis=0, keepdims=True)
        small[4:5, :] += jnp.sum(grad_two, axis=0, keepdims=True)
        small[5:6, :] += jnp.sum(own_grad, axis=0, keepdims=True)

    transposed(xn2, tra)
    transposed(ogf, trb)
    step = 256

    @pl.loop(0, width // step)
    def _(r):
        rows = pl.ds(pl.multiple_of(r * step, step), step)
        for i in range(n_pair):
            dwu[i, rows, :] = nn_dot(tra[rows, :], ug[i]).astype(BF16)
            dwd[i, rows, :] = nn_dot(trb[rows, :], act[i]).astype(BF16)

    @pl.loop(0, n_ctx)
    def _(b):
        rows_arrive(6, b, bg)
        dm[block_rows(b), :] = nn_dot(bg[block_rows(b), :], wo[...]).astype(BF16)

    transposed(bg, trb)

    @pl.loop(0, width // step)
    def _(r):
        rows = pl.ds(pl.multiple_of(r * step, step), step)
        product = nn_dot(trb[rows, :], mixed[...])
        for i in range(n_pair):
            dwo[i, rows, :] = product[:, i * cols : (i + 1) * cols].astype(BF16)

    for b in reversed(range(n_ctx)):
        reach = (b + 1) * block
        here_rows = slice(b * block, (b + 1) * block)

        @pl.loop(0, n_twos)
        def _(j):
            at = pl.ds(pl.multiple_of(j * lanes, lanes), lanes)
            queries, keys, values = qs[here_rows, at], ks[:reach, at], vs[:reach, at]
            mix_grad, mix = dm[here_rows, at], o32[here_rows, at]
            towards = mix_grad.astype(F32) * mix
            query_parts, key_sum, value_sum = [], None, None
            for e in range(2):
                head = first_head if e == 0 else jnp.logical_not(first_head)
                grad_head = jnp.where(head, mix_grad, zero16)
                prob_grad = nt_dot(grad_head, values)
                centre = jnp.sum(jnp.where(head, towards, 0.0), axis=-1, keepdims=True)
                probs = p_first[b][2 * j + e]
                score_grad = (probs.astype(F32) * (prob_grad - centre)).astype(BF16)
                query_parts.append(nn_dot(score_grad, keys))
                key_term = tn_dot(score_grad, jnp.where(head, queries, zero16))
                value_term = tn_dot(probs, grad_head)
                key_sum = key_term if key_sum is None else key_sum + key_term
                value_sum = value_term if value_sum is None else value_sum + value_term
            query_grad = jnp.where(first_head, query_parts[0], query_parts[1]) * scale
            dqkv[here_rows, at] = query_grad.astype(BF16)
            if b == n_ctx - 1:
                dka[:, at] = key_sum
                dva[:, at] = value_sum
            else:
                dka[:reach, at] += key_sum
                dva[:reach, at] += value_sum

    @pl.loop(0, n_ctx)
    def _(b):
        dqkv[block_rows(b), hw : 2 * hw] = dka[block_rows(b), :].astype(BF16)
        dqkv[block_rows(b), 2 * hw :] = dva[block_rows(b), :].astype(BF16)
        small[6:7, :hw] += jnp.sum(dqkv[block_rows(b), :hw].astype(F32), axis=0, keepdims=True)
        small[7:8, :hw] += jnp.sum(dqkv[block_rows(b), 2 * hw :].astype(F32), axis=0, keepdims=True)
        ssend[1, b] = nt_dot(dqkv[far_rows(b), :], wqkv[...]).astype(BF16)
        part_copy(7, 1, b).start()
        part[0, b] = nt_dot(dqkv[own_rows(b), :], wqkv[...])

    transposed(xn1, tra)

    @pl.loop(0, width // step)
    def _(r):
        rows = pl.ds(pl.multiple_of(r * step, step), step)
        product = nn_dot(tra[rows, :], dqkv[...])
        for i in range(n_pair):
            dwq[i, rows, :] = product[:, i * cols : (i + 1) * cols].astype(BF16)
            dwk[i, rows, :] = product[:, hw + i * cols : hw + (i + 1) * cols].astype(BF16)
            dwv[i, rows, :] = product[:, 2 * hw + i * cols : 2 * hw + (i + 1) * cols].astype(BF16)

    @pl.loop(0, n_ctx)
    def _(b):
        part_copy(7, 1, b).wait()
        grad_one = part[0, b] + srecv[1, b].astype(F32)
        scaled, spread = normalize(tok[b].astype(F32))
        tg[b] = (hid[b] + norm_back(grad_one * gain_one, scaled, spread)).astype(BF16)
        small[0:1, :] += jnp.sum(grad_one * scaled, axis=0, keepdims=True)
        small[1:2, :] += jnp.sum(grad_one, axis=0, keepdims=True)
        exchange(0, b, og.at[b], ogf.at[own_rows(b)]).wait_send()
        rows_copy(1, b, xn1).wait_send()
        rows_copy(3, b, xn2).wait_send()
        rows_copy(6, b, bg).wait_send()


def compute_call(sizes, tok, og, weights, vecs, bias):
    n_dp, n_ctx, n_tp = sizes
    n_pair = n_tp // 2
    half, width = tok.shape[1:]
    block = 2 * half
    length = n_ctx * block
    cols = weights[0].shape[2]
    hw = n_pair * cols
    fw = weights[4].shape[2]
    heads = hw // HEAD_DIM
    vmem_spec = pl.BlockSpec(memory_space=pltpu.VMEM)
    shape = jax.ShapeDtypeStruct
    out_shape = [
        shape(tok.shape, BF16),
        shape(tok.shape, BF16),
    ]
    out_shape += [shape(w.shape, BF16) for w in weights]
    out_shape += [shape((16, width), F32)]
    vm = pltpu.VMEM
    scratch = [
        vm((length, width), BF16),
        vm((width, 3 * hw), BF16),
        vm((width, hw), BF16),
        vm((length, hw), BF16),
        vm((length, hw), BF16),
        vm((length, hw), BF16),
        vm((length, hw), F32),
        vm((length, hw), BF16),
        vm((n_ctx, half, width), F32),
        vm((length, width), BF16),
        vm((length, width), BF16),
        vm((n_pair, length, fw), BF16),
        vm((n_pair, length, fw), BF16),
        vm((length, width), BF16),
        vm((length, hw), BF16),
        vm((length, hw), F32),
        vm((length, hw), F32),
        vm((length, 3 * hw), BF16),
        vm((width, length), BF16),
        vm((width, length), BF16),
        vm((2, n_ctx, half, width), F32),
        vm((2, n_ctx, half, width), BF16),
        vm((2, n_ctx, half, width), BF16),
    ]
    scratch += [vm((heads, block, (b + 1) * block), BF16) for b in range(n_ctx)]
    scratch += [pltpu.SemaphoreType.DMA((8, n_ctx)), pltpu.SemaphoreType.DMA((8, n_ctx))]
    return pl.pallas_call(
        functools.partial(compute_body, sizes),
        out_shape=out_shape,
        in_specs=[vmem_spec] * 10,
        out_specs=[vmem_spec] * 9,
        scratch_shapes=scratch,
        compiler_params=pltpu.CompilerParams(
            collective_id=1, has_side_effects=True, vmem_limit_bytes=VMEM_LIMIT
        ),
    )(tok, og, *weights, vecs, bias)


def scatter_body(sizes, half, *refs):
    here = Place(sizes)
    n_dp, n_ctx, n_pair = here.n_dp, here.n_ctx, here.n_pair
    d, z, p, c = here.dp, here.ctx, here.pair, here.side
    rows_in = refs[0:2]
    grads = refs[2:8]
    small = refs[8]
    rows_out = refs[9:11]
    owned = refs[11:17]
    small_out = refs[17]
    it = iter(refs[18:])
    dp_land = [next(it) for _ in range(6)]
    dp_sum = [next(it) for _ in range(6)]
    keep = [next(it) for _ in range(6)]
    pair_land = [next(it) for _ in range(6)]
    pair_sum = [next(it) for _ in range(6)]
    ctx_land = [next(it) for _ in range(6)]
    side_land, small_b, ctx_small, small_c, pair_small, small_d, dp_small = [next(it) for _ in range(7)]
    own_sem, send_sem, line_sem, far_sem, side_sem, dp_sem, pair_sem, ctx_sem, small_sem = it
    mine = p * n_ctx + z
    rows = pl.ds(pl.multiple_of(c * half, half), half)

    here.barrier(True)
    sends = Sends(send_sem)

    for a in range(6):
        for k in range(1, n_dp):
            dd, device = here.other_dp(k)
            sends.go(
                grads[a].at[:, pl.ds(dd * n_ctx, n_ctx)],
                dp_land[a].at[k - 1],
                dp_sem.at[a, k - 1],
                device,
            )
    own = []
    for i in range(2):
        for k in range(1, n_ctx):
            zz, device = here.other_ctx(k)
            sends.go(rows_in[i].at[zz], rows_out[i].at[mine, rows], line_sem.at[i, z], device)
        own.append(pltpu.make_async_copy(rows_in[i].at[z], rows_out[i].at[mine, rows], own_sem.at[i]))
        own[-1].start()
    sends.go(small.at[pl.ds(0, 8)], side_land, small_sem.at[0, 0], here.partner())

    def small_arrive(stage, k, land):
        remote(land, land, send_sem.at[0], small_sem.at[stage, k - 1], here.partner()).wait_recv()

    for i in range(2):
        own[i].wait()
        for k in range(1, n_ctx):
            zz, device = here.other_ctx(k)
            slot = rows_out[i].at[p * n_ctx + zz, rows]
            remote(slot, slot, send_sem.at[0], line_sem.at[i, zz], device).wait_recv()
        for k in range(1, n_pair):
            pp, device = here.other_pair(k)
            slot = rows_out[i].at[pl.ds(p * n_ctx, n_ctx), rows]
            sends.go(slot, slot, far_sem.at[i, p], device)

    small_arrive(0, 1, side_land)
    small_b[0:8, :] = small[0:8, :] + side_land[...]
    small_b[8:16, :] = small[8:16, :]
    small_b[6:8, :] = small[6:8, :]
    for k in range(1, n_ctx):
        zz, device = here.other_ctx(k)
        sends.go(small_b, ctx_small.at[k - 1], small_sem.at[1, k - 1], device)

    for a in range(6):
        for k in range(1, n_dp):
            remote(
                dp_land[a].at[k - 1], dp_land[a].at[k - 1], send_sem.at[0], dp_sem.at[a, k - 1],
                here.partner(),
            ).wait_recv()
        for i in range(n_pair):
            total = grads[a][i, pl.ds(d * n_ctx, n_ctx)].astype(F32)
            for k in range(1, n_dp):
                total = total + dp_land[a][k - 1, i].astype(F32)
            dp_sum[a][i] = total.astype(BF16)
        for k in range(1, n_pair):
            pp, device = here.other_pair(k)
            sends.go(dp_sum[a].at[pp], pair_land[a].at[k - 1], pair_sem.at[a, k - 1], device)

    total = small_b[...]
    for k in range(1, n_ctx):
        small_arrive(1, k, ctx_small.at[k - 1])
        total = total + ctx_small[k - 1]
    small_c[...] = total
    for k in range(1, n_pair):
        pp, device = here.other_pair(k)
        sends.go(small_c, pair_small.at[k - 1], small_sem.at[2, k - 1], device)

    for a in range(6):
        for k in range(1, n_pair):
            remote(
                pair_land[a].at[k - 1], pair_land[a].at[k - 1], send_sem.at[0], pair_sem.at[a, k - 1],
                here.partner(),
            ).wait_recv()
        total = dp_sum[a][p].astype(F32)
        for k in range(1, n_pair):
            total = total + pair_land[a][k - 1].astype(F32)
        keep[a][...] = total
        pair_sum[a][...] = total.astype(BF16)
        for k in range(1, n_ctx):
            zz, device = here.other_ctx(k)
            sends.go(pair_sum[a].at[zz], ctx_land[a].at[k - 1], ctx_sem.at[a, k - 1], device)

    total = small_c[...]
    for k in range(1, n_pair):
        small_arrive(2, k, pair_small.at[k - 1])
        total = total + pair_small[k - 1]
    small_d[...] = total
    for k in range(1, n_dp):
        dd, device = here.other_dp(k)
        sends.go(small_d, dp_small.at[k - 1], small_sem.at[3, k - 1], device)

    for i in range(2):
        for k in range(1, n_pair):
            pp, device = here.other_pair(k)
            slot = rows_out[i].at[pl.ds(pp * n_ctx, n_ctx), rows]
            remote(slot, slot, send_sem.at[0], far_sem.at[i, pp], device).wait_recv()
        slot = rows_out[i].at[:, rows]
        sends.go(slot, slot, side_sem.at[i], here.partner())

    for a in range(6):
        total = keep[a][z]
        for k in range(1, n_ctx):
            remote(
                ctx_land[a].at[k - 1], ctx_land[a].at[k - 1], send_sem.at[0], ctx_sem.at[a, k - 1],
                here.partner(),
            ).wait_recv()
            total = total + ctx_land[a][k - 1].astype(F32)
        owned[a][...] = total

    total = small_d[...]
    for k in range(1, n_dp):
        small_arrive(3, k, dp_small.at[k - 1])
        total = total + dp_small[k - 1]
    small_out[...] = total
    other = pl.ds(pl.multiple_of((1 - c) * half, half), half)
    for i in range(2):
        slot = rows_out[i].at[:, other]
        remote(slot, slot, send_sem.at[0], side_sem.at[i], here.partner()).wait_recv()
    sends.finish()


def scatter_call(sizes, seqs, lo, tg, grads, small):
    n_dp, n_ctx, n_tp = sizes
    n_pair = n_tp // 2
    half, width = lo.shape[1:]
    vmem_spec = pl.BlockSpec(memory_space=pltpu.VMEM)
    shape = jax.ShapeDtypeStruct
    vm = pltpu.VMEM
    tail = [g.shape[2:] for g in grads]
    out_shape = [shape((seqs, 2 * half, width), BF16)] * 2
    out_shape += [shape(t, F32) for t in tail]
    out_shape += [shape(small.shape, F32)]
    scratch = [vm((n_dp - 1, n_pair, n_ctx) + t, BF16) for t in tail]
    scratch += [vm((n_pair, n_ctx) + t, BF16) for t in tail]
    scratch += [vm((n_ctx,) + t, F32) for t in tail]
    scratch += [vm((n_pair - 1, n_ctx) + t, BF16) for t in tail]
    scratch += [vm((n_ctx,) + t, BF16) for t in tail]
    scratch += [vm((n_ctx - 1,) + t, BF16) for t in tail]
    scratch += [
        vm((8, width), F32),
        vm((16, width), F32),
        vm((n_ctx - 1, 16, width), F32),
        vm((16, width), F32),
        vm((n_pair - 1, 16, width), F32),
        vm((16, width), F32),
        vm((n_dp - 1, 16, width), F32),
    ]
    n_sends = (
        6 * ((n_dp - 1) + (n_pair - 1) + (n_ctx - 1))
        + 2 * ((n_ctx - 1) + (n_pair - 1) + 1)
        + 1 + (n_ctx - 1) + (n_pair - 1) + (n_dp - 1)
    )
    dma = pltpu.SemaphoreType.DMA
    most = max(n_dp, n_ctx, n_pair)
    scratch += [
        dma((2,)),
        dma((n_sends,)),
        dma((2, n_ctx)),
        dma((2, n_pair)),
        dma((2,)),
        dma((6, n_dp - 1)),
        dma((6, n_pair - 1)),
        dma((6, n_ctx - 1)),
        dma((4, most)),
    ]
    return pl.pallas_call(
        functools.partial(scatter_body, sizes, half),
        out_shape=out_shape,
        in_specs=[vmem_spec] * 9,
        out_specs=[vmem_spec] * 9,
        scratch_shapes=scratch,
        compiler_params=pltpu.CompilerParams(
            collective_id=2, has_side_effects=True, vmem_limit_bytes=VMEM_LIMIT
        ),
    )(lo, tg, *grads, small)


def fused_body(sizes, dims, *refs):
    here = Place(sizes)
    n_dp, n_ctx, n_pair = here.n_dp, here.n_ctx, here.n_pair
    d, z, p, c = here.dp, here.ctx, here.pair, here.side
    half, width, share, cols, fw = dims
    block = 2 * half
    hw = n_pair * cols
    lanes = 2 * HEAD_DIM
    n_twos = hw // lanes
    n_rows = n_dp * n_ctx
    two = n_ctx // 2
    it = iter(refs)

    def take(n):
        return [next(it) for _ in range(n)]

    tokens, out_grad = take(2)
    narrow_shards = take(4)
    shards = [None] + take(2)
    vectors, column_biases = take(6), take(3)
    rows_out = take(2)
    owned = take(3)
    small_out = next(it)
    full = take(3)
    pack_all, vecs, cold = take(3)
    tok, og, lo, tg = take(4)
    (
        xn1, wqkv, wo, qs, ks, vs, o32, mixed, hid, xn2, ogf, act, ug, bg, dm, dqkv, tra, trb,
        wide, whole, ssend, srecv, dwd, small,
    ) = take(24)
    p_first = take(n_ctx)
    first_land, second_land, ctx_land = take(3), take(3), take(3)
    side_land, small_b, ctx_small, small_c, pair_small, small_d, dp_small = take(7)
    (
        own_sem, put_sem, rows_sem, line_sem, pair_sem, dp_sem, diag_dp_sem, diag_pair_sem, swap_send,
        swap_recv, first_sem, second_sem, ctx_sem, out_line, out_pair, out_side, small_sem,
        side_sem,
    ) = take(18)
    partner = here.partner()
    own_row = d * n_ctx + z
    mine = p * n_ctx + z
    scale = HEAD_DIM ** -0.5
    first_head = lax.broadcasted_iota(jnp.int32, (1, lanes), 1) < HEAD_DIM
    zero16 = jnp.zeros((), BF16)
    side_rows = pl.ds(pl.multiple_of(c * half, half), half)
    far_side = pl.ds(pl.multiple_of((1 - c) * half, half), half)
    sends = Sends(put_sem)

    def arrive(slot, sem):
        remote(slot, slot, put_sem.at[0], sem, partner).wait_recv()

    def far_first():
        upper = z // two
        order = []
        for i in range(n_ctx - 1):
            down = n_ctx - 1 - i
            down = down - (z - down + n_ctx) // n_ctx
            up = i + (i - z + n_ctx) // n_ctx
            zz = upper * up + (1 - upper) * down
            order.append((zz, (d, zz, here.tp)))
        return order

    line_order = far_first()

    def flipped(h):
        zz = z + h - 2 * h * ((z // h) % 2)
        return zz, (d, zz, here.tp)

    strides = [1 << i for i in range(n_ctx.bit_length() - 1)]

    def shard_rows(r, count=1):
        return pl.ds(pl.multiple_of(r * share, 16), count * share)

    def slot(a, pp, dd, zz, count=1):
        return full[a].at[pp, shard_rows(dd * n_ctx + zz, count)]

    gather_own = [None] + [
        pltpu.make_async_copy(shards[a], slot(a, p, d, z), own_sem.at[a]) for a in (1, 2)
    ]

    def gather_give(a, h):
        device = flipped(h)[1]
        for i in range(n_ctx // (2 * h)):
            zz = (z + 2 * h * i) % n_ctx
            source = shards[a] if a > 0 and i == 0 else slot(a, p, d, zz)
            sends.go(source, slot(a, p, d, zz), line_sem.at[a, zz], device)

    def gather_take(a, h):
        q = flipped(h)[0]
        for i in range(n_ctx // (2 * h)):
            zz = (q + 2 * h * i) % n_ctx
            arrive(slot(a, p, d, zz), line_sem.at[a, zz])

    def gather_start(a):
        gather_give(a, strides[-1])

    def gather_next(a):
        for h in reversed(strides[:-1]):
            gather_take(a, 2 * h)
            gather_give(a, h)

    def gather_hop(a):
        if a > 0:
            gather_own[a].wait()
        gather_take(a, 1)
        group = slot(a, p, d, 0, n_ctx)
        for k in range(1, n_pair):
            sends.go(group, group, pair_sem.at[a, p], here.other_pair(k)[1])
        for k in range(1, n_dp):
            sends.go(group, group, dp_sem.at[a, d], here.other_dp(k)[1])

    def gather_turn(a):
        for k in range(1, n_pair):
            pp = here.other_pair(k)[0]
            arrive(slot(a, pp, d, 0, n_ctx), pair_sem.at[a, pp])
            first = slot(a, pp, d, 0, two)
            for j in range(1, n_dp):
                sends.go(first, first, diag_dp_sem.at[a, pp, d], here.other_dp(j)[1])
        for k in range(1, n_dp):
            dd = here.other_dp(k)[0]
            arrive(slot(a, p, dd, 0, n_ctx), dp_sem.at[a, dd])
            second = slot(a, p, dd, two, n_ctx - two)
            for j in range(1, n_pair):
                sends.go(second, second, diag_pair_sem.at[a, p, dd], here.other_pair(j)[1])

    def gather_end(a):
        for k in range(1, n_pair):
            pp = here.other_pair(k)[0]
            for j in range(1, n_dp):
                dd = here.other_dp(j)[0]
                arrive(slot(a, pp, dd, 0, two), diag_dp_sem.at[a, pp, dd])
                arrive(slot(a, pp, dd, two, n_ctx - two), diag_pair_sem.at[a, pp, dd])

    def pack_start():
        own = pack_all.at[p, own_row]
        for zz, device in line_order:
            sends.go(own, own, line_sem.at[3, z], device)

    def pack_hop():
        for k in range(1, n_ctx):
            zz = here.other_ctx(k)[0]
            arrive(pack_all.at[p, d * n_ctx + zz], line_sem.at[3, zz])
        group = pack_all.at[p, pl.ds(d * n_ctx, n_ctx)]
        for k in range(1, n_pair):
            sends.go(group, group, pair_sem.at[3, p], here.other_pair(k)[1])
        for k in range(1, n_dp):
            sends.go(group, group, dp_sem.at[3, d], here.other_dp(k)[1])

    def pack_end():
        for k in range(1, n_pair):
            pp = here.other_pair(k)[0]
            arrive(pack_all.at[pp, pl.ds(d * n_ctx, n_ctx)], pair_sem.at[3, pp])
        for k in range(1, n_dp):
            dd = here.other_dp(k)[0]
            arrive(pack_all.at[p, pl.ds(dd * n_ctx, n_ctx)], dp_sem.at[3, dd])

    rows_own = [
        pltpu.make_async_copy(source.at[mine, side_rows], target.at[z], own_sem.at[4 + i])
        for i, (source, target) in enumerate(((tokens, tok), (out_grad, og)))
    ]

    def rows_start(i, source, target):
        for zz, device in line_order:
            sends.go(source.at[p * n_ctx + zz, side_rows], target.at[z], rows_sem.at[i, z], device)

    def grad_slot(ref, pp, dd, k):
        return ref.at[pp, shard_rows(dd * n_ctx + (z + k) % n_ctx)]

    def pair_leads(a, k):
        return k == 1 if a == 0 else near.index(k) % 2 == 0

    def scatter_start(a, ref, ks):
        for k in ks:
            if pair_leads(a, k):
                for j in range(1, n_pair):
                    pp, device = here.other_pair(j)
                    for i in range(n_dp):
                        sends.go(grad_slot(ref, pp, i, k), first_land[a].at[j - 1, i, k], first_sem.at[a, j - 1, i, k], device)
            else:
                for j in range(1, n_dp):
                    dd, device = here.other_dp(j)
                    for i in range(n_pair):
                        sends.go(grad_slot(ref, i, dd, k), first_land[a].at[j - 1, i, k], first_sem.at[a, j - 1, i, k], device)

    def add_into(target, parts):
        total = target[...].astype(F32)
        for part in parts:
            total = total + part[...].astype(F32)
        target[...] = total.astype(BF16)

    def scatter_turn(a, ref, ks):
        for k in ks:
            leads = pair_leads(a, k)
            n_lead, n_next = (n_pair, n_dp) if leads else (n_dp, n_pair)
            for i in range(n_next):
                parts = [first_land[a].at[j - 1, i, k] for j in range(1, n_lead)]
                for j in range(1, n_lead):
                    arrive(parts[j - 1], first_sem.at[a, j - 1, i, k])
                target = grad_slot(ref, p, i, k) if leads else grad_slot(ref, i, d, k)
                add_into(target, parts)
            for j in range(1, n_next):
                other, device = here.other_dp(j) if leads else here.other_pair(j)
                source = grad_slot(ref, p, other, k) if leads else grad_slot(ref, other, d, k)
                sends.go(source, second_land[a].at[j - 1, k], second_sem.at[a, j - 1, k], device)

    def scatter_line(a, ref, ks):
        for k in ks:
            n_next = n_dp if pair_leads(a, k) else n_pair
            parts = [second_land[a].at[j - 1, k] for j in range(1, n_next)]
            for j in range(1, n_next):
                arrive(parts[j - 1], second_sem.at[a, j - 1, k])
            add_into(grad_slot(ref, p, d, k), parts)
            if k % 2 == 1:
                scatter_give(a, ref, 1, k)

    def scatter_give(a, ref, h, k):
        zz, device = flipped(h)
        at = n_ctx - n_ctx // h + ((z + k - zz + n_ctx) % n_ctx) // (2 * h)
        sends.go(grad_slot(ref, p, d, k), ctx_land[a].at[at], ctx_sem.at[a, at], device)

    def scatter_across(a, ref):
        for h in strides[1:]:
            for i in range(n_ctx // h):
                at = n_ctx - 2 * n_ctx // h + i
                arrive(ctx_land[a].at[at], ctx_sem.at[a, at])
                add_into(grad_slot(ref, p, d, i * h), [ctx_land[a].at[at]])
            for k in range(h, n_ctx, 2 * h):
                scatter_give(a, ref, h, k)

    def scatter_end(a, ref):
        last = n_ctx - 2
        arrive(ctx_land[a].at[last], ctx_sem.at[a, last])
        owned[a][...] = ref[p, shard_rows(own_row), :].astype(F32) + ctx_land[a][last].astype(F32)

    near = [k for h in strides for k in range(h, n_ctx, 2 * h)] + [0]
    early, late = near[:two], near[two:]
    others = list(range(1, n_ctx))

    def out_slot(i, s, rows):
        return rows_out[i].at[s, rows]

    def out_start(i, source):
        for zz, device in line_order:
            sends.go(source.at[zz], out_slot(i, mine, side_rows), out_line.at[i, z], device)
        copy = pltpu.make_async_copy(source.at[z], out_slot(i, mine, side_rows), own_sem.at[6 + i])
        copy.start()
        return copy

    def out_pass(i, s, source):
        piece = out_slot(i, s, side_rows)
        for j in range(1, n_pair):
            sends.go(source, piece, out_pair.at[i, s], here.other_pair(j)[1])
        sends.go(source, piece, out_side.at[i, s], partner)

    def out_hop(i, ks):
        for k in ks:
            s = p * n_ctx + here.other_ctx(k)[0]
            piece = out_slot(i, s, side_rows)
            arrive(piece, out_line.at[i, here.other_ctx(k)[0]])
            out_pass(i, s, piece)

    def out_cross(i):
        for j in range(1, n_pair):
            pp = here.other_pair(j)[0]
            for k in range(n_ctx):
                s = pp * n_ctx + (z + k) % n_ctx
                piece = out_slot(i, s, side_rows)
                arrive(piece, out_pair.at[i, s])
                sends.go(piece, piece, out_side.at[i, s], partner)

    def out_end(i):
        for s in range(n_pair * n_ctx):
            arrive(out_slot(i, s, far_side), out_side.at[i, s])

    def own_rows(b):
        return pl.ds(pl.multiple_of(b * block + c * half, half), half)

    def far_rows(b):
        return pl.ds(pl.multiple_of(b * block + (1 - c) * half, half), half)

    def block_rows(b):
        return pl.ds(pl.multiple_of(b * block, block), block)

    def swap(stage, b, src, dst):
        return remote(src, dst, swap_send.at[stage, b], swap_recv.at[stage, b], partner)

    def rows_copy(stage, b, ref):
        return swap(stage, b, ref.at[own_rows(b)], ref.at[own_rows(b)])

    def rows_arrive(stage, b, ref):
        swap(stage, b, ref.at[far_rows(b)], ref.at[far_rows(b)]).wait_recv()

    def part_copy(stage, place, b):
        return swap(stage, b, ssend.at[place, b], srecv.at[place, b])

    def part_store(i, b, value):
        wide[i, pl.ds(pl.multiple_of(b * block, block), half), :] = value[:, :hw]
        wide[i, pl.ds(pl.multiple_of(b * block + half, half), half), :] = value[:, hw:]

    def part_load(i, b):
        left = wide[i, pl.ds(pl.multiple_of(b * block, block), half), :]
        right = wide[i, pl.ds(pl.multiple_of(b * block + half, half), half), :]
        return jnp.concatenate([left, right], axis=1)

    rows_own[0].start()
    rows_own[1].start()
    gather_own[1].start()
    gather_own[2].start()
    for a in range(4):
        full[0][p, shard_rows(own_row), a * cols : (a + 1) * cols] = narrow_shards[a][...]
    own_pack = pack_all.at[p, own_row]
    own_pack[...] = jnp.zeros(own_pack.shape, F32)
    for i in range(6):
        own_pack[i : i + 1, :share] = vectors[i][...].astype(F32)
    row = 6
    for ref in column_biases:
        n = ref.shape[1]
        for w in range(0, n, 128):
            m = min(128, n - w)
            own_pack[row : row + 1, :m] = ref[:, w : w + m].astype(F32)
            row += 1
    small[...] = jnp.zeros_like(small)
    here.barrier(True)
    pack_start()
    gather_start(0)
    gather_next(0)
    gather_start(1)
    pack_hop()
    pack_end()
    for r in range(n_rows):
        own_part = pack_all[p, r]
        vecs[0:8, r * share : (r + 1) * share] = own_part[0:8, :share]
    for i in range(n_pair):
        piece = pack_all[i, d * n_ctx]
        for line in range(2):
            for w in range(0, cols, 128):
                n = min(128, cols - w)
                row = 6 + 2 * line + w // 128
                cold[line : line + 1, i * cols + w : i * cols + w + n] = piece[row : row + 1, :n]
        for w in range(0, fw, 128):
            row = 10 + w // 128
            cold[2 + i : 3 + i, w : w + 128] = piece[row : row + 1, :]
    gain_one, shift_one, out_shift = vecs[0:1, :], vecs[1:2, :], vecs[2:3, :]
    gain_two, shift_two, down_shift = vecs[3:4, :], vecs[4:5, :], vecs[5:6, :]

    def norm_one(b):
        scaled, _ = normalize(tok[b].astype(F32))
        xn1[own_rows(b), :] = (scaled * gain_one + shift_one).astype(BF16)
        rows_copy(1, b, xn1).start()

    rows_own[0].wait()
    norm_one(z)
    gather_hop(0)
    gather_next(1)
    pl.semaphore_signal(side_sem, inc=1, device_id=partner, device_id_type=MESH)
    pl.semaphore_wait(side_sem, 1)
    rows_start(0, tokens, tok)
    gather_start(2)
    gather_turn(0)
    gather_hop(1)
    for k in range(1, n_ctx):
        b = here.other_ctx(k)[0]
        arrive(tok.at[b], rows_sem.at[0, b])
        norm_one(b)
    gather_end(0)
    for i in range(n_pair):
        for a, base in enumerate((0, hw, 2 * hw)):
            wqkv[:, base + i * cols : base + (i + 1) * cols] = full[0][i, :, a * cols : (a + 1) * cols]
        wo[:, i * cols : (i + 1) * cols] = full[0][i, :, 3 * cols : 4 * cols]
    q_shift, v_shift = cold[0:1, :hw], cold[1:2, :hw]

    @pl.loop(0, n_ctx)
    def _(b):
        rows_arrive(1, b, xn1)
        product = nn_dot(xn1[block_rows(b), :], wqkv[...])
        qs[block_rows(b), :] = (product[:, :hw] + q_shift).astype(BF16) * jnp.asarray(scale, BF16)
        ks[block_rows(b), :] = product[:, hw : 2 * hw].astype(BF16)
        vs[block_rows(b), :] = (product[:, 2 * hw :] + v_shift).astype(BF16)

    gather_next(2)

    for b in range(n_ctx):
        reach = (b + 1) * block
        here_rows = slice(b * block, (b + 1) * block)

        @pl.loop(0, n_twos)
        def _(j):
            at = pl.ds(pl.multiple_of(j * lanes, lanes), lanes)
            queries, keys, values = qs[here_rows, at], ks[:reach, at], vs[:reach, at]
            pieces = []
            for e in range(2):
                head = first_head if e == 0 else jnp.logical_not(first_head)
                scores = nt_dot(jnp.where(head, queries, zero16), keys)
                powers = jnp.exp(scores - jnp.max(scores, axis=-1, keepdims=True))
                inverse = 1.0 / jnp.sum(powers, axis=-1, keepdims=True)
                probs = (powers * inverse).astype(BF16)
                p_first[b][2 * j + e] = probs
                pieces.append(nn_dot(probs, values))
            out = jnp.where(first_head, pieces[0], pieces[1])
            o32[here_rows, at] = out
            mixed[here_rows, at] = out.astype(BF16)

        whole[b % 2] = nt_dot(mixed[here_rows, :], wo[...])
        ssend[0, b] = whole[b % 2, far_side, :].astype(BF16)
        part_copy(2, 0, b).start()
        hid[b] = whole[b % 2, side_rows, :]
        if b == 1:
            gather_turn(1)
            rows_start(1, out_grad, og)
        if b == 2:
            gather_hop(2)

    @pl.loop(0, n_ctx)
    def _(b):
        part_copy(2, 0, b).wait()
        hidden = tok[b].astype(F32) + (hid[b] + srecv[0, b].astype(F32)) + out_shift
        hid[b] = hidden
        scaled, _ = normalize(hidden)
        xn2[own_rows(b), :] = (scaled * gain_two + shift_two).astype(BF16)
        rows_copy(3, b, xn2).start()

    gather_end(1)

    @pl.loop(0, n_ctx)
    def _(b):
        rows_arrive(3, b, xn2)
        normed = xn2[block_rows(b), :]
        for i in range(n_pair):
            upward = nn_dot(normed, full[1][i]) + cold[2 + i : 3 + i, :fw]
            big_phi = 0.5 + 0.5 * lax.erf(upward * root_half)
            act[i, block_rows(b), :] = (upward * big_phi).astype(BF16)
            slope = big_phi + upward * density_scale * jnp.exp(-0.5 * upward * upward)
            ug[i, block_rows(b), :] = slope.astype(BF16)

    rows_own[1].wait()
    for k in range(n_ctx):
        b = (z + k) % n_ctx
        if k > 0:
            arrive(og.at[b], rows_sem.at[1, b])
        swap(0, b, og.at[b], ogf.at[own_rows(b)]).start()
        ogf[own_rows(b), :] = og[b]
    for b in range(n_ctx):
        rows_arrive(0, b, ogf)

    step = 256

    def transposed(ref, out):
        for b in range(n_ctx):
            out[:, b * block : (b + 1) * block] = ref[b * block : (b + 1) * block, :].T

    transposed(ogf, trb)

    @pl.loop(0, width // step)
    def _(r):
        rows = pl.ds(pl.multiple_of(r * step, step), step)
        for i in range(n_pair):
            dwd[i, rows, :] = nn_dot(trb[rows, :], act[i]).astype(BF16)

    gather_turn(2)
    gathered = len(sends.started)
    scatter_start(2, dwd, near)

    def slope_back(i, b):
        slope = ug[i, block_rows(b), :].astype(F32)
        rows_grad = (nn_dot(ogf[block_rows(b), :], full[2][i]) * slope).astype(BF16)
        ug[i, block_rows(b), :] = rows_grad
        small[pl.ds(8 + i, 1), :] += jnp.sum(rows_grad.astype(F32), axis=0, keepdims=True)

    @pl.loop(0, n_ctx)
    def _(b):
        slope_back(p, b)

    gather_end(2)

    def through(ref, weight, rows):
        total = nt_dot(ref[0, rows, :], weight[0])
        for i in range(1, n_pair):
            total = total + nt_dot(ref[i, rows, :], weight[i])
        return total

    def units_back(b):
        for k in range(1, n_pair):
            slope_back(here.other_pair(k)[0], b)
        whole[0] = through(ug, full[1], block_rows(b))
        ssend[0, b] = whole[0, far_side, :].astype(BF16)
        part_copy(5, 0, b).start()
        part_store(1, b, whole[0, side_rows, :])
        whole[1] = through(act, full[2], block_rows(b))
        ssend[1, b] = whole[1, far_side, :].astype(BF16)
        part_copy(4, 1, b).start()
        part_store(0, b, whole[1, side_rows, :])

    pl.loop(0, two)(units_back)
    scatter_turn(2, dwd, early)
    pl.loop(two, n_ctx)(units_back)
    transposed(xn2, tra)
    scatter_turn(2, dwd, late)
    for copy in sends.started[:gathered]:
        copy.wait_send()

    @pl.loop(0, width // step)
    def _(r):
        rows = pl.ds(pl.multiple_of(r * step, step), step)
        for i in range(n_pair):
            full[1][i, rows, :] = nn_dot(tra[rows, :], ug[i]).astype(BF16)

    scatter_start(1, full[1], near)
    scatter_line(2, dwd, early)

    @pl.loop(0, n_ctx)
    def _(b):
        part_copy(5, 0, b).wait()
        grad_two = part_load(1, b) + srecv[0, b].astype(F32)
        part_copy(4, 1, b).wait()
        lo[b] = (hid[b] + (part_load(0, b) + srecv[1, b].astype(F32)) + down_shift).astype(BF16)
        scaled, spread = normalize(hid[b])
        own_grad = og[b].astype(F32)
        hidden_grad = own_grad + norm_back(grad_two * gain_two, scaled, spread)
        hid[b] = hidden_grad
        branch = hidden_grad.astype(BF16)
        bg[own_rows(b), :] = branch
        rows_copy(6, b, bg).start()
        small[2:3, :] += jnp.sum(branch.astype(F32), axis=0, keepdims=True)
        small[3:4, :] += jnp.sum(grad_two * scaled, axis=0, keepdims=True)
        small[4:5, :] += jnp.sum(grad_two, axis=0, keepdims=True)
        small[5:6, :] += jnp.sum(own_grad, axis=0, keepdims=True)

    lo_copy = out_start(0, lo)
    out_pass(0, mine, lo.at[z])

    @pl.loop(0, n_ctx)
    def _(b):
        rows_arrive(6, b, bg)
        dm[block_rows(b), :] = nn_dot(bg[block_rows(b), :], wo[...]).astype(BF16)

    scatter_line(2, dwd, late)
    transposed(bg, trb)

    @pl.loop(0, width // step)
    def _(r):
        rows = pl.ds(pl.multiple_of(r * step, step), step)
        product = nn_dot(trb[rows, :], mixed[...])
        for i in range(n_pair):
            full[0][i, rows, 3 * cols : 4 * cols] = product[:, i * cols : (i + 1) * cols].astype(BF16)

    for b in reversed(range(n_ctx)):
        reach = (b + 1) * block
        here_rows = slice(b * block, (b + 1) * block)

        @pl.loop(0, n_twos)
        def _(j):
            at = pl.ds(pl.multiple_of(j * lanes, lanes), lanes)
            queries, keys, values = qs[here_rows, at], ks[:reach, at], vs[:reach, at]
            mix_grad, mix = dm[here_rows, at], o32[here_rows, at]
            towards = mix_grad.astype(F32) * mix
            query_parts, key_sum, value_sum = [], None, None
            for e in range(2):
                head = first_head if e == 0 else jnp.logical_not(first_head)
                grad_head = jnp.where(head, mix_grad, zero16)
                prob_grad = nt_dot(grad_head, values)
                centre = jnp.sum(jnp.where(head, towards, 0.0), axis=-1, keepdims=True)
                probs = p_first[b][2 * j + e]
                score_grad = (probs.astype(F32) * (prob_grad - centre)).astype(BF16)
                query_parts.append(nn_dot(score_grad, keys))
                key_term = tn_dot(score_grad, jnp.where(head, queries, zero16))
                value_term = tn_dot(probs, grad_head)
                key_sum = key_term if key_sum is None else key_sum + key_term
                value_sum = value_term if value_sum is None else value_sum + value_term
            query_grad = jnp.where(first_head, query_parts[0], query_parts[1]) * scale
            dqkv[here_rows, at] = query_grad.astype(BF16)
            if b == n_ctx - 1:
                wide[0, :, at] = key_sum
                wide[1, :, at] = value_sum
            else:
                wide[0, :reach, at] += key_sum
                wide[1, :reach, at] += value_sum

        if b == 1:
            scatter_turn(1, full[1], near)
        if b == 0:
            out_hop(0, others)

    @pl.loop(0, n_ctx)
    def _(b):
        dqkv[block_rows(b), hw : 2 * hw] = wide[0, block_rows(b), :].astype(BF16)
        dqkv[block_rows(b), 2 * hw :] = wide[1, block_rows(b), :].astype(BF16)
        small[6:7, :hw] += jnp.sum(dqkv[block_rows(b), :hw].astype(F32), axis=0, keepdims=True)
        small[7:8, :hw] += jnp.sum(dqkv[block_rows(b), 2 * hw :].astype(F32), axis=0, keepdims=True)
        whole[0] = nt_dot(dqkv[block_rows(b), :], wqkv[...])
        ssend[1, b] = whole[0, far_side, :].astype(BF16)
        part_copy(7, 1, b).start()
        part_store(0, b, whole[0, side_rows, :])

    transposed(xn1, tra)

    @pl.loop(0, width // step)
    def _(r):
        rows = pl.ds(pl.multiple_of(r * step, step), step)
        product = nn_dot(tra[rows, :], dqkv[...])
        for i in range(n_pair):
            for a in range(3):
                full[0][i, rows, a * cols : (a + 1) * cols] = product[
                    :, a * hw + i * cols : a * hw + (i + 1) * cols
                ].astype(BF16)

    scatter_start(0, full[0], near)

    @pl.loop(0, n_ctx)
    def _(b):
        part_copy(7, 1, b).wait()
        grad_one = part_load(0, b) + srecv[1, b].astype(F32)
        scaled, spread = normalize(tok[b].astype(F32))
        tg[b] = (hid[b] + norm_back(grad_one * gain_one, scaled, spread)).astype(BF16)
        small[0:1, :] += jnp.sum(grad_one * scaled, axis=0, keepdims=True)
        small[1:2, :] += jnp.sum(grad_one, axis=0, keepdims=True)

    sends.go(small.at[pl.ds(0, 8)], side_land, small_sem.at[0, 0], partner)
    tg_copy = out_start(1, tg)
    out_pass(1, mine, tg.at[z])
    scatter_line(1, full[1], near)
    scatter_across(2, dwd)
    arrive(side_land, small_sem.at[0, 0])
    small_b[0:6, :] = small[0:6, :] + side_land[0:6, :]
    small_b[6:16, :] = small[6:16, :]
    for k in range(1, n_pair):
        sends.go(small_b, pair_small.at[k - 1], small_sem.at[2, k - 1], here.other_pair(k)[1])
    scatter_turn(0, full[0], early)
    out_cross(0)
    scatter_line(0, full[0], early)
    scatter_turn(0, full[0], late)
    out_hop(1, others)
    scatter_across(1, full[1])
    total = small_b[...]
    for k in range(1, n_pair):
        arrive(pair_small.at[k - 1], small_sem.at[2, k - 1])
        total = total + pair_small[k - 1]
    small_c[...] = total
    for k in range(1, n_dp):
        sends.go(small_c, dp_small.at[k - 1], small_sem.at[3, k - 1], here.other_dp(k)[1])
    scatter_line(0, full[0], late)
    scatter_across(0, full[0])
    scatter_end(2, dwd)
    scatter_end(1, full[1])
    out_end(0)
    total = small_c[...]
    for k in range(1, n_dp):
        arrive(dp_small.at[k - 1], small_sem.at[3, k - 1])
        total = total + dp_small[k - 1]
    small_d[...] = total
    for k in range(1, n_ctx):
        sends.go(small_d, ctx_small.at[k - 1], small_sem.at[1, k - 1], here.other_ctx(k)[1])
    out_cross(1)
    scatter_end(0, full[0])
    total = small_d[...]
    for k in range(1, n_ctx):
        arrive(ctx_small.at[k - 1], small_sem.at[1, k - 1])
        total = total + ctx_small[k - 1]
    small_out[...] = total
    out_end(1)
    lo_copy.wait()
    tg_copy.wait()

    @pl.loop(0, n_ctx)
    def _(b):
        swap(0, b, og.at[b], ogf.at[own_rows(b)]).wait_send()
        rows_copy(1, b, xn1).wait_send()
        rows_copy(3, b, xn2).wait_send()
        rows_copy(6, b, bg).wait_send()

    for copy in sends.started[gathered:]:
        copy.wait_send()


def fused_call(sizes, tokens, out_grad, shards, vectors, column_biases):
    n_dp, n_ctx, n_tp = sizes
    n_pair = n_tp // 2
    seqs, block, width = tokens.shape
    half = block // 2
    length = n_ctx * block
    share, cols = shards[0].shape
    fw = shards[4].shape[1]
    widths = [4 * cols, fw, fw]
    hw = n_pair * cols
    heads = hw // HEAD_DIM
    two = n_ctx // 2
    any_spec = pl.BlockSpec(memory_space=pl.ANY)
    vmem_spec = pl.BlockSpec(memory_space=pltpu.VMEM)
    shape = jax.ShapeDtypeStruct
    vm = pltpu.VMEM
    dma = pltpu.SemaphoreType.DMA
    out_shape = [shape(tokens.shape, BF16)] * 2
    out_shape += [shape((share, w), F32) for w in widths]
    out_shape += [shape((16, width), F32)]
    scratch = [vm((n_pair, width, w), BF16) for w in widths]
    scratch += [
        vm((n_pair, n_dp * n_ctx, 16, 128), F32),
        vm((8, width), F32),
        vm((8, width), F32),
    ]
    scratch += [vm((n_ctx, half, width), BF16)] * 4
    scratch += [
        vm((length, width), BF16),
        vm((width, 3 * hw), BF16),
        vm((width, hw), BF16),
        vm((length, hw), BF16),
        vm((length, hw), BF16),
        vm((length, hw), BF16),
        vm((length, hw), F32),
        vm((length, hw), BF16),
        vm((n_ctx, half, width), F32),
        vm((length, width), BF16),
        vm((length, width), BF16),
        vm((n_pair, length, fw), BF16),
        vm((n_pair, length, fw), BF16),
        vm((length, width), BF16),
        vm((length, hw), BF16),
        vm((length, 3 * hw), BF16),
        vm((width, length), BF16),
        vm((width, length), BF16),
        vm((2, length, hw), F32),
        vm((2, block, width), F32),
        vm((2, n_ctx, half, width), BF16),
        vm((2, n_ctx, half, width), BF16),
        vm((n_pair, width, fw), BF16),
        vm((16, width), F32),
    ]
    scratch += [vm((heads, block, (b + 1) * block), BF16) for b in range(n_ctx)]
    lead, after = max(n_dp, n_pair) - 1, max(n_dp, n_pair)
    scratch += [vm((lead, after, n_ctx, share, w), BF16) for w in widths]
    scratch += [vm((lead, n_ctx, share, w), BF16) for w in widths]
    scratch += [vm((n_ctx - 1, share, w), BF16) for w in widths]
    scratch += [
        vm((8, width), F32),
        vm((16, width), F32),
        vm((n_ctx - 1, 16, width), F32),
        vm((16, width), F32),
        vm((n_pair - 1, 16, width), F32),
        vm((16, width), F32),
        vm((n_dp - 1, 16, width), F32),
    ]
    most = max(n_dp, n_ctx, n_pair)
    scratch += [
        dma((8,)),
        dma((260,)),
        dma((2, n_ctx)),
        dma((4, n_ctx)),
        dma((4, n_pair)),
        dma((4, n_dp)),
        dma((3, n_pair, n_dp)),
        dma((3, n_pair, n_dp)),
        dma((8, n_ctx)),
        dma((8, n_ctx)),
        dma((3, lead, after, n_ctx)),
        dma((3, lead, n_ctx)),
        dma((3, n_ctx)),
        dma((2, n_ctx)),
        dma((2, seqs)),
        dma((2, seqs)),
        dma((4, most)),
        pltpu.SemaphoreType.REGULAR,
    ]
    return pl.pallas_call(
        functools.partial(fused_body, sizes, (half, width, share, cols, fw)),
        out_shape=out_shape,
        in_specs=[any_spec] * 2 + [vmem_spec] * 4 + [any_spec] * 2 + [vmem_spec] * 9,
        out_specs=[any_spec] * 2 + [vmem_spec] * 4,
        scratch_shapes=scratch,
        compiler_params=pltpu.CompilerParams(
            collective_id=3, has_side_effects=True, vmem_limit_bytes=67043328
        ),
    )(tokens, out_grad, *shards, *vectors, *column_biases)


def finish_body(n_ctx, share, cols, *refs):
    lo_in, tg_in, attn, up, down, small = refs[:6]
    lo, tg, dq, dk, dv, do, du, dd = refs[6:14]
    vectors = refs[14:20]
    shifts = refs[20:22]
    up_shift = refs[22]
    lo[...] = lo_in[...]
    tg[...] = tg_in[...].astype(F32)
    row = lax.axis_index("dp") * n_ctx + lax.axis_index("ctx")
    pair = lax.axis_index("tp") // 2
    width = small.shape[1]

    @pl.when(pl.program_id(0) == 0)
    def _():
        for i, ref in enumerate((dq, dk, dv, do)):
            ref[...] = attn[:, i * cols : (i + 1) * cols]
        du[...] = up[...]
        dd[...] = down[...]
        turned = pltpu.roll(small[0:8, :], (width - row * share) % width, 1)
        for i, ref in enumerate(vectors):
            ref[...] = turned[i : i + 1, :share]
        turned = pltpu.roll(small[0:8, :], (width - pair * cols) % width, 1)
        for i, ref in enumerate(shifts):
            ref[...] = turned[6 + i : 7 + i, :cols]
        row_of = small[pl.ds(8 + pair, 1), :]
        for i in range(up_shift.shape[0]):
            up_shift[i : i + 1, :] = row_of[:, i * 128 : (i + 1) * 128]


def finish_call(sizes, cols, lo, tg, attn, up, down, small):
    n_dp, n_ctx, n_tp = sizes
    seqs, block, width = lo.shape
    share = attn.shape[0]
    shape = jax.ShapeDtypeStruct
    rows = pl.BlockSpec((1, block, width), lambda i: (i, 0, 0))

    def whole(s):
        return pl.BlockSpec(s, lambda i: (0, 0))

    out_tail = [(share, cols)] * 4 + [up.shape] * 2 + [(1, share)] * 6 + [(1, cols)] * 2 + [(up.shape[1] // 128, 128)]
    return pl.pallas_call(
        functools.partial(finish_body, n_ctx, share, cols),
        grid=(seqs,),
        out_shape=[shape(lo.shape, BF16), shape(lo.shape, F32)] + [shape(s, F32) for s in out_tail],
        in_specs=[rows, rows] + [whole(x.shape) for x in (attn, up, down, small)],
        out_specs=[rows, rows] + [whole(s) for s in out_tail],
    )(lo, tg, attn, up, down, small)


def fused_layer(sizes, tokens, out_grad, shards, vectors, column_biases):
    cols = shards[0].shape[1]
    lines = [v.reshape(1, -1) for v in (*vectors, *column_biases)]
    results = fused_call(sizes, tokens, out_grad, shards, lines[:6], lines[6:])
    final = finish_call(sizes, cols, *results)
    return (*final[:8], *[v.reshape(-1) for v in final[8:]])


def per_device(
    tokens,
    out_grad,
    query_weight,
    key_weight,
    value_weight,
    output_weight,
    up_weight,
    down_weight,
    norm1_gain,
    norm1_bias,
    output_bias,
    norm2_gain,
    norm2_bias,
    down_bias,
    query_bias,
    value_bias,
    up_bias,
):
    sizes = (lax.axis_size("dp"), lax.axis_size("ctx"), lax.axis_size("tp"))
    n_dp, n_ctx, n_tp = sizes
    n_pair = n_tp // 2
    seqs, block, width = tokens.shape
    assert seqs == n_ctx * n_pair
    share = norm1_gain.shape[0]
    cols = query_bias.shape[0]
    pair = lax.axis_index("tp") // 2
    row = lax.axis_index("dp") * n_ctx + lax.axis_index("ctx")
    shards = (query_weight, key_weight, value_weight, output_weight, up_weight, down_weight)
    vectors = (norm1_gain, norm1_bias, output_bias, norm2_gain, norm2_bias, down_bias)
    if share % 16 == 0 and n_ctx % 2 == 0:
        return fused_layer(
            sizes, tokens, out_grad, shards, vectors, (query_bias, value_bias, up_bias)
        )

    six = jnp.stack(vectors).astype(F32)
    vec = jnp.pad(six, ((0, 2), (0, 128 - share)))
    columns = jnp.arange(width) // cols == pair
    narrow = [jnp.where(columns, jnp.tile(b.astype(F32), width // cols), 0.0) for b in (query_bias, value_bias)]
    bias = jnp.pad(jnp.stack(narrow + [up_bias.astype(F32)]), ((0, 5), (0, 0)))

    gathered = gather_call(sizes, tokens, out_grad, shards, vec, bias)
    tok, og = gathered[0:2]
    weights = [w.reshape(n_pair, width, w.shape[3]) for w in gathered[2:8]]
    vecs = gathered[8][:, :, :share].transpose(1, 0, 2).reshape(8, width)
    results = compute_call(sizes, tok, og, weights, vecs, gathered[9])
    lo, tg = results[0:2]
    grads = [
        g.reshape(n_pair, n_dp * n_ctx, s.shape[0], s.shape[1]) for g, s in zip(results[2:8], shards)
    ]
    final = scatter_call(sizes, seqs, lo, tg, grads, results[8])
    layer_out, tokens_grad = final[0], final[1].astype(F32)
    small = final[8]
    owned = [lax.dynamic_slice_in_dim(small[i], row * share, share) for i in range(6)]
    shifts = [lax.dynamic_slice_in_dim(small[6 + i], pair * cols, cols) for i in range(2)]
    up_total = lax.dynamic_index_in_dim(small[8 : 8 + n_pair], pair, 0, keepdims=False)
    return (layer_out, tokens_grad, *final[2:8], *owned, *shifts, up_total)


def solution(mesh):
    rows_spec = P("dp", "ctx", None)
    weight_spec = P(("dp", "ctx"), "tp")
    vector_spec = P(("dp", "ctx"))
    column_spec = P("tp")
    common = (rows_spec,) * 2 + (weight_spec,) * 6 + (vector_spec,) * 6 + (column_spec,) * 3
    return jax.shard_map(
        per_device, mesh=mesh, in_specs=common, out_specs=common, check_vma=False
    )
```

```python
import functools

import jax
import jax.numpy as jnp
from jax import lax
from jax.experimental import pallas as pl
from jax.experimental.pallas import tpu as pltpu
from jax.sharding import PartitionSpec as P

HEAD_DIM = 64
MESH = pl.DeviceIdType.MESH
F32 = jnp.float32
BF16 = jnp.bfloat16
VMEM_LIMIT = 66 * 1000 * 1000

epsilon = 1e-05
root_half = 0.7071067811865476
density_scale = 0.3989422804014327


def remote(src, dst, send_sem, recv_sem, device):
    return pltpu.make_async_remote_copy(
        src_ref=src,
        dst_ref=dst,
        send_sem=send_sem,
        recv_sem=recv_sem,
        device_id=device,
        device_id_type=MESH,
    )


def nn_dot(left, right):
    return lax.dot_general(left, right, (((1,), (0,)), ((), ())), preferred_element_type=F32)


def nt_dot(left, right):
    return lax.dot_general(left, right, (((1,), (1,)), ((), ())), preferred_element_type=F32)


def tn_dot(left, right):
    return lax.dot_general(left, right, (((0,), (0,)), ((), ())), preferred_element_type=F32)


def normalize(values):
    centred = values - jnp.mean(values, axis=-1, keepdims=True)
    spread = lax.rsqrt(jnp.mean(centred * centred, axis=-1, keepdims=True) + epsilon)
    return centred * spread, spread


def norm_back(grad_scaled, scaled, spread):
    inner = grad_scaled - jnp.mean(grad_scaled, axis=-1, keepdims=True)
    inner = inner - scaled * jnp.mean(grad_scaled * scaled, axis=-1, keepdims=True)
    return inner * spread


class Place:
    def __init__(self, sizes):
        self.n_dp, self.n_ctx, self.n_tp = sizes
        self.n_pair = self.n_tp // 2
        self.dp = lax.axis_index("dp")
        self.ctx = lax.axis_index("ctx")
        self.tp = lax.axis_index("tp")
        self.pair = self.tp // 2
        self.side = self.tp % 2

    def other_dp(self, k):
        d = (self.dp + k) % self.n_dp
        return d, (d, self.ctx, self.tp)

    def other_ctx(self, k):
        z = (self.ctx + k) % self.n_ctx
        return z, (self.dp, z, self.tp)

    def other_pair(self, k):
        p = (self.pair + k) % self.n_pair
        return p, (self.dp, self.ctx, 2 * p + self.side)

    def partner(self):
        return (self.dp, self.ctx, 2 * self.pair + 1 - self.side)

    def barrier(self, far):
        sem = pltpu.get_barrier_semaphore()
        count = 1
        pl.semaphore_signal(sem, inc=1, device_id=self.partner(), device_id_type=MESH)
        if far:
            for size, other in (
                (self.n_dp, self.other_dp),
                (self.n_ctx, self.other_ctx),
                (self.n_pair, self.other_pair),
            ):
                for k in range(1, size):
                    pl.semaphore_signal(sem, inc=1, device_id=other(k)[1], device_id_type=MESH)
                    count += 1
        pl.semaphore_wait(sem, count)


class Sends:
    def __init__(self, sems):
        self.sems = sems
        self.started = []

    def go(self, src, dst, recv_sem, device):
        copy = remote(src, dst, self.sems.at[len(self.started)], recv_sem, device)
        copy.start()
        self.started.append(copy)

    def finish(self):
        for copy in self.started:
            copy.wait_send()


def gather_body(sizes, half, *refs):
    here = Place(sizes)
    n_dp, n_ctx, n_pair = here.n_dp, here.n_ctx, here.n_pair
    d, z, p, c = here.dp, here.ctx, here.pair, here.side
    tokens, out_grad = refs[0:2]
    shards = refs[2:8]
    vec, bias = refs[8:10]
    tok_own, og_own = refs[10:12]
    full = refs[12:18]
    vec_all, bias_all = refs[18:20]
    own_sem, send_sem, rows_sem, line_sem, group_sem, vline_sem, vgroup_sem, bias_sem = refs[20:28]
    own_row = d * n_ctx + z
    mine = p * n_ctx + z
    rows = pl.ds(pl.multiple_of(c * half, half), half)

    here.barrier(True)
    sends = Sends(send_sem)
    own = [
        pltpu.make_async_copy(tokens.at[mine, rows], tok_own.at[z], own_sem.at[0]),
        pltpu.make_async_copy(out_grad.at[mine, rows], og_own.at[z], own_sem.at[1]),
        pltpu.make_async_copy(vec, vec_all.at[own_row], own_sem.at[2]),
        pltpu.make_async_copy(bias, bias_all.at[p], own_sem.at[3]),
    ]
    for a in range(6):
        own.append(pltpu.make_async_copy(shards[a], full[a].at[p, own_row], own_sem.at[4 + a]))
    for copy in own:
        copy.start()

    def send_rows(index, source, target):
        for k in range(1, n_ctx):
            zz, device = here.other_ctx(k)
            sends.go(
                source.at[p * n_ctx + zz, rows], target.at[z], rows_sem.at[index, z], device
            )

    def send_line(a):
        for k in range(1, n_ctx):
            zz, device = here.other_ctx(k)
            sends.go(shards[a], full[a].at[p, own_row], line_sem.at[a, z], device)

    send_rows(0, tokens, tok_own)
    for k in range(1, n_ctx):
        zz, device = here.other_ctx(k)
        sends.go(vec, vec_all.at[own_row], vline_sem.at[z], device)
    for k in range(1, n_pair):
        pp, device = here.other_pair(k)
        sends.go(bias, bias_all.at[p], bias_sem.at[p], device)
    for a in range(6):
        send_line(a)
    send_rows(1, out_grad, og_own)

    for copy in own:
        copy.wait()

    def group(a, pp, dd):
        return full[a].at[pp, pl.ds(dd * n_ctx, n_ctx)]

    def wait_line(a):
        for k in range(1, n_ctx):
            zz, device = here.other_ctx(k)
            slot = full[a].at[p, d * n_ctx + zz]
            remote(slot, slot, send_sem.at[0], line_sem.at[a, zz], device).wait_recv()

    def send_pair(a, dd):
        for k in range(1, n_pair):
            pp, device = here.other_pair(k)
            sends.go(group(a, p, dd), group(a, p, dd), group_sem.at[a, p, dd], device)

    def send_dp(a, pp):
        for k in range(1, n_dp):
            dd, device = here.other_dp(k)
            sends.go(group(a, pp, d), group(a, pp, d), group_sem.at[a, pp, d], device)

    def wait_group(a, pp, dd):
        slot = group(a, pp, dd)
        remote(slot, slot, send_sem.at[0], group_sem.at[a, pp, dd], here.partner()).wait_recv()

    for a in range(6):
        wait_line(a)
        send_dp(a, p)
        send_pair(a, d)
    for k in range(1, n_ctx):
        zz, device = here.other_ctx(k)
        slot = vec_all.at[d * n_ctx + zz]
        remote(slot, slot, send_sem.at[0], vline_sem.at[zz], device).wait_recv()
    for k in range(1, n_dp):
        dd, device = here.other_dp(k)
        slot = vec_all.at[pl.ds(d * n_ctx, n_ctx)]
        sends.go(slot, slot, vgroup_sem.at[d], device)
    pair_first = (True, True, True, True, False, True)
    for a in range(6):
        if pair_first[a]:
            for k in range(1, n_pair):
                pp = here.other_pair(k)[0]
                wait_group(a, pp, d)
                send_dp(a, pp)
        else:
            for k in range(1, n_dp):
                dd = here.other_dp(k)[0]
                wait_group(a, p, dd)
                send_pair(a, dd)
    for a in range(6):
        for k in range(1, n_dp):
            dd = here.other_dp(k)[0]
            if pair_first[a]:
                wait_group(a, p, dd)
            for j in range(1, n_pair):
                wait_group(a, here.other_pair(j)[0], dd)
        if not pair_first[a]:
            for j in range(1, n_pair):
                wait_group(a, here.other_pair(j)[0], d)
    for k in range(1, n_dp):
        dd, device = here.other_dp(k)
        slot = vec_all.at[pl.ds(dd * n_ctx, n_ctx)]
        remote(slot, slot, send_sem.at[0], vgroup_sem.at[dd], device).wait_recv()
    for k in range(1, n_pair):
        pp, device = here.other_pair(k)
        slot = bias_all.at[pp]
        remote(slot, slot, send_sem.at[0], bias_sem.at[pp], device).wait_recv()
    for index, target in ((0, tok_own), (1, og_own)):
        for k in range(1, n_ctx):
            zz, device = here.other_ctx(k)
            slot = target.at[zz]
            remote(slot, slot, send_sem.at[0], rows_sem.at[index, zz], device).wait_recv()
    sends.finish()


def gather_call(sizes, tokens, out_grad, shards, vec, bias):
    n_dp, n_ctx, n_tp = sizes
    n_pair = n_tp // 2
    seqs, block, width = tokens.shape
    half = block // 2
    any_spec = pl.BlockSpec(memory_space=pl.ANY)
    vmem_spec = pl.BlockSpec(memory_space=pltpu.VMEM)
    own = jax.ShapeDtypeStruct((n_ctx, half, width), BF16)
    out_shape = [own, own]
    out_shape += [jax.ShapeDtypeStruct((n_pair, n_dp * n_ctx) + s.shape, BF16) for s in shards]
    out_shape += [
        jax.ShapeDtypeStruct((n_dp * n_ctx,) + vec.shape, F32),
        jax.ShapeDtypeStruct((n_pair,) + bias.shape, F32),
    ]
    n_sends = (
        2 * (n_ctx - 1)
        + (n_ctx - 1)
        + (n_pair - 1)
        + 6 * (n_ctx - 1)
        + (n_dp - 1)
        + 6 * ((n_dp - 1) + (n_pair - 1) + (n_dp - 1) * (n_pair - 1))
    )
    dma = pltpu.SemaphoreType.DMA
    return pl.pallas_call(
        functools.partial(gather_body, sizes, half),
        out_shape=out_shape,
        in_specs=[any_spec] * 10,
        out_specs=[vmem_spec] * 10,
        scratch_shapes=[
            dma((10,)),
            dma((n_sends,)),
            dma((2, n_ctx)),
            dma((6, n_ctx)),
            dma((6, n_pair, n_dp)),
            dma((n_ctx,)),
            dma((n_dp,)),
            dma((n_pair,)),
        ],
        compiler_params=pltpu.CompilerParams(
            collective_id=0, has_side_effects=True, vmem_limit_bytes=VMEM_LIMIT
        ),
    )(tokens, out_grad, *shards, vec, bias)


def compute_body(sizes, *refs):
    here = Place(sizes)
    n_ctx, n_pair = here.n_ctx, here.n_pair
    c = here.side
    (tok, og, gq, gk, gv, go, gu, gd, vecs, bias) = refs[:10]
    (lo, tg, dwq, dwk, dwv, dwo, dwu, dwd, small) = refs[10:19]
    (
        xn1, wqkv, wo, qs, ks, vs, o32, mixed, hid, xn2, ogf, act, ug, bg, dm,
        dka, dva, dqkv, tra, trb, part, ssend, srecv, p_first, send_sem, recv_sem,
    ) = refs[19 : 19 + 23] + (refs[42 : 42 + n_ctx],) + refs[42 + n_ctx :]
    half, width = tok.shape[1], tok.shape[2]
    block = 2 * half
    cols = gq.shape[2]
    hw = n_pair * cols
    fw = gu.shape[2]
    lanes = 2 * HEAD_DIM
    n_twos = hw // lanes
    partner = here.partner()
    scale = HEAD_DIM ** -0.5
    first_head = lax.broadcasted_iota(jnp.int32, (1, lanes), 1) < HEAD_DIM
    zero16 = jnp.zeros((), BF16)

    def own_rows(b):
        return pl.ds(pl.multiple_of(b * block + c * half, half), half)

    def far_rows(b):
        return pl.ds(pl.multiple_of(b * block + (1 - c) * half, half), half)

    def block_rows(b):
        return pl.ds(pl.multiple_of(b * block, block), block)

    def exchange(stage, b, src, dst):
        return remote(src, dst, send_sem.at[stage, b], recv_sem.at[stage, b], partner)

    def rows_copy(stage, b, ref):
        return exchange(stage, b, ref.at[own_rows(b)], ref.at[own_rows(b)])

    def rows_arrive(stage, b, ref):
        exchange(stage, b, ref.at[far_rows(b)], ref.at[far_rows(b)]).wait_recv()

    def part_copy(stage, slot, b):
        return exchange(stage, b, ssend.at[slot, b], srecv.at[slot, b])

    here.barrier(False)

    gain_one, shift_one, out_shift = vecs[0:1, :], vecs[1:2, :], vecs[2:3, :]
    gain_two, shift_two, down_shift = vecs[3:4, :], vecs[4:5, :], vecs[5:6, :]

    @pl.loop(0, n_ctx)
    def _(b):
        exchange(0, b, og.at[b], ogf.at[own_rows(b)]).start()
        ogf[own_rows(b), :] = og[b]
        scaled, _ = normalize(tok[b].astype(F32))
        xn1[own_rows(b), :] = (scaled * gain_one + shift_one).astype(BF16)
        rows_copy(1, b, xn1).start()

    for i in range(n_pair):
        at = slice(i * cols, (i + 1) * cols)
        wqkv[:, i * cols : (i + 1) * cols] = gq[i]
        wqkv[:, hw + i * cols : hw + (i + 1) * cols] = gk[i]
        wqkv[:, 2 * hw + i * cols : 2 * hw + (i + 1) * cols] = gv[i]
        wo[:, at] = go[i]
    q_shift = bias[0, 0:1, :hw]
    v_shift = bias[0, 1:2, :hw]
    for i in range(1, n_pair):
        q_shift = q_shift + bias[i, 0:1, :hw]
        v_shift = v_shift + bias[i, 1:2, :hw]

    @pl.loop(0, n_ctx)
    def _(b):
        rows_arrive(1, b, xn1)
        product = nn_dot(xn1[block_rows(b), :], wqkv[...])
        qs[block_rows(b), :] = (product[:, :hw] + q_shift).astype(BF16) * jnp.asarray(scale, BF16)
        ks[block_rows(b), :] = product[:, hw : 2 * hw].astype(BF16)
        vs[block_rows(b), :] = (product[:, 2 * hw :] + v_shift).astype(BF16)

    for b in range(n_ctx):
        reach = (b + 1) * block
        here_rows = slice(b * block, (b + 1) * block)

        @pl.loop(0, n_twos)
        def _(j):
            at = pl.ds(pl.multiple_of(j * lanes, lanes), lanes)
            queries, keys, values = qs[here_rows, at], ks[:reach, at], vs[:reach, at]
            pieces = []
            for e in range(2):
                head = first_head if e == 0 else jnp.logical_not(first_head)
                scores = nt_dot(jnp.where(head, queries, zero16), keys)
                powers = jnp.exp(scores - jnp.max(scores, axis=-1, keepdims=True))
                inverse = 1.0 / jnp.sum(powers, axis=-1, keepdims=True)
                probs = (powers * inverse).astype(BF16)
                p_first[b][2 * j + e] = probs
                pieces.append(nn_dot(probs, values))
            out = jnp.where(first_head, pieces[0], pieces[1])
            o32[here_rows, at] = out
            mixed[here_rows, at] = out.astype(BF16)

        ssend[0, b] = nt_dot(mixed[far_rows(b), :], wo[...]).astype(BF16)
        part_copy(2, 0, b).start()
        hid[b] = nt_dot(mixed[own_rows(b), :], wo[...])

    @pl.loop(0, n_ctx)
    def _(b):
        part_copy(2, 0, b).wait()
        hidden = tok[b].astype(F32) + (hid[b] + srecv[0, b].astype(F32)) + out_shift
        hid[b] = hidden
        scaled, _ = normalize(hidden)
        xn2[own_rows(b), :] = (scaled * gain_two + shift_two).astype(BF16)
        rows_copy(3, b, xn2).start()

    small[...] = jnp.zeros_like(small)

    @pl.loop(0, n_ctx)
    def _(b):
        rows_arrive(0, b, ogf)
        rows_arrive(3, b, xn2)
        normed = xn2[block_rows(b), :]
        grads = ogf[block_rows(b), :]
        for i in range(n_pair):
            upward = nn_dot(normed, gu[i]) + bias[i, 2:3, :]
            big_phi = 0.5 + 0.5 * lax.erf(upward * root_half)
            act[i, block_rows(b), :] = (upward * big_phi).astype(BF16)
            slope = big_phi + upward * density_scale * jnp.exp(-0.5 * upward * upward)
            rows_grad = (nn_dot(grads, gd[i]) * slope).astype(BF16)
            ug[i, block_rows(b), :] = rows_grad
            small[8 + i : 9 + i, :] += jnp.sum(rows_grad.astype(F32), axis=0, keepdims=True)

        def through(ref, weight, rows):
            total = nt_dot(ref[0, rows, :], weight[0])
            for i in range(1, n_pair):
                total = total + nt_dot(ref[i, rows, :], weight[i])
            return total

        ssend[1, b] = through(act, gd, far_rows(b)).astype(BF16)
        part_copy(4, 1, b).start()
        ssend[0, b] = through(ug, gu, far_rows(b)).astype(BF16)
        part_copy(5, 0, b).start()
        part[0, b] = through(act, gd, own_rows(b))
        part[1, b] = through(ug, gu, own_rows(b))

    def transposed(ref, out):
        for b in range(n_ctx):
            out[:, b * block : (b + 1) * block] = ref[b * block : (b + 1) * block, :].T

    @pl.loop(0, n_ctx)
    def _(b):
        part_copy(4, 1, b).wait()
        lo[b] = (hid[b] + (part[0, b] + srecv[1, b].astype(F32)) + down_shift).astype(BF16)
        part_copy(5, 0, b).wait()
        grad_two = part[1, b] + srecv[0, b].astype(F32)
        scaled, spread = normalize(hid[b])
        own_grad = og[b].astype(F32)
        hidden_grad = own_grad + norm_back(grad_two * gain_two, scaled, spread)
        hid[b] = hidden_grad
        branch = hidden_grad.astype(BF16)
        bg[own_rows(b), :] = branch
        rows_copy(6, b, bg).start()
        small[2:3, :] += jnp.sum(branch.astype(F32), axis=0, keepdims=True)
        small[3:4, :] += jnp.sum(grad_two * scaled, axis=0, keepdims=True)
        small[4:5, :] += jnp.sum(grad_two, axis=0, keepdims=True)
        small[5:6, :] += jnp.sum(own_grad, axis=0, keepdims=True)

    transposed(xn2, tra)
    transposed(ogf, trb)
    step = 256

    @pl.loop(0, width // step)
    def _(r):
        rows = pl.ds(pl.multiple_of(r * step, step), step)
        for i in range(n_pair):
            dwu[i, rows, :] = nn_dot(tra[rows, :], ug[i]).astype(BF16)
            dwd[i, rows, :] = nn_dot(trb[rows, :], act[i]).astype(BF16)

    @pl.loop(0, n_ctx)
    def _(b):
        rows_arrive(6, b, bg)
        dm[block_rows(b), :] = nn_dot(bg[block_rows(b), :], wo[...]).astype(BF16)

    transposed(bg, trb)

    @pl.loop(0, width // step)
    def _(r):
        rows = pl.ds(pl.multiple_of(r * step, step), step)
        product = nn_dot(trb[rows, :], mixed[...])
        for i in range(n_pair):
            dwo[i, rows, :] = product[:, i * cols : (i + 1) * cols].astype(BF16)

    for b in reversed(range(n_ctx)):
        reach = (b + 1) * block
        here_rows = slice(b * block, (b + 1) * block)

        @pl.loop(0, n_twos)
        def _(j):
            at = pl.ds(pl.multiple_of(j * lanes, lanes), lanes)
            queries, keys, values = qs[here_rows, at], ks[:reach, at], vs[:reach, at]
            mix_grad, mix = dm[here_rows, at], o32[here_rows, at]
            towards = mix_grad.astype(F32) * mix
            query_parts, key_sum, value_sum = [], None, None
            for e in range(2):
                head = first_head if e == 0 else jnp.logical_not(first_head)
                grad_head = jnp.where(head, mix_grad, zero16)
                prob_grad = nt_dot(grad_head, values)
                centre = jnp.sum(jnp.where(head, towards, 0.0), axis=-1, keepdims=True)
                probs = p_first[b][2 * j + e]
                score_grad = (probs.astype(F32) * (prob_grad - centre)).astype(BF16)
                query_parts.append(nn_dot(score_grad, keys))
                key_term = tn_dot(score_grad, jnp.where(head, queries, zero16))
                value_term = tn_dot(probs, grad_head)
                key_sum = key_term if key_sum is None else key_sum + key_term
                value_sum = value_term if value_sum is None else value_sum + value_term
            query_grad = jnp.where(first_head, query_parts[0], query_parts[1]) * scale
            dqkv[here_rows, at] = query_grad.astype(BF16)
            if b == n_ctx - 1:
                dka[:, at] = key_sum
                dva[:, at] = value_sum
            else:
                dka[:reach, at] += key_sum
                dva[:reach, at] += value_sum

    @pl.loop(0, n_ctx)
    def _(b):
        dqkv[block_rows(b), hw : 2 * hw] = dka[block_rows(b), :].astype(BF16)
        dqkv[block_rows(b), 2 * hw :] = dva[block_rows(b), :].astype(BF16)
        small[6:7, :hw] += jnp.sum(dqkv[block_rows(b), :hw].astype(F32), axis=0, keepdims=True)
        small[7:8, :hw] += jnp.sum(dqkv[block_rows(b), 2 * hw :].astype(F32), axis=0, keepdims=True)
        ssend[1, b] = nt_dot(dqkv[far_rows(b), :], wqkv[...]).astype(BF16)
        part_copy(7, 1, b).start()
        part[0, b] = nt_dot(dqkv[own_rows(b), :], wqkv[...])

    transposed(xn1, tra)

    @pl.loop(0, width // step)
    def _(r):
        rows = pl.ds(pl.multiple_of(r * step, step), step)
        product = nn_dot(tra[rows, :], dqkv[...])
        for i in range(n_pair):
            dwq[i, rows, :] = product[:, i * cols : (i + 1) * cols].astype(BF16)
            dwk[i, rows, :] = product[:, hw + i * cols : hw + (i + 1) * cols].astype(BF16)
            dwv[i, rows, :] = product[:, 2 * hw + i * cols : 2 * hw + (i + 1) * cols].astype(BF16)

    @pl.loop(0, n_ctx)
    def _(b):
        part_copy(7, 1, b).wait()
        grad_one = part[0, b] + srecv[1, b].astype(F32)
        scaled, spread = normalize(tok[b].astype(F32))
        tg[b] = (hid[b] + norm_back(grad_one * gain_one, scaled, spread)).astype(BF16)
        small[0:1, :] += jnp.sum(grad_one * scaled, axis=0, keepdims=True)
        small[1:2, :] += jnp.sum(grad_one, axis=0, keepdims=True)
        exchange(0, b, og.at[b], ogf.at[own_rows(b)]).wait_send()
        rows_copy(1, b, xn1).wait_send()
        rows_copy(3, b, xn2).wait_send()
        rows_copy(6, b, bg).wait_send()


def compute_call(sizes, tok, og, weights, vecs, bias):
    n_dp, n_ctx, n_tp = sizes
    n_pair = n_tp // 2
    half, width = tok.shape[1:]
    block = 2 * half
    length = n_ctx * block
    cols = weights[0].shape[2]
    hw = n_pair * cols
    fw = weights[4].shape[2]
    heads = hw // HEAD_DIM
    vmem_spec = pl.BlockSpec(memory_space=pltpu.VMEM)
    shape = jax.ShapeDtypeStruct
    out_shape = [
        shape(tok.shape, BF16),
        shape(tok.shape, BF16),
    ]
    out_shape += [shape(w.shape, BF16) for w in weights]
    out_shape += [shape((16, width), F32)]
    vm = pltpu.VMEM
    scratch = [
        vm((length, width), BF16),
        vm((width, 3 * hw), BF16),
        vm((width, hw), BF16),
        vm((length, hw), BF16),
        vm((length, hw), BF16),
        vm((length, hw), BF16),
        vm((length, hw), F32),
        vm((length, hw), BF16),
        vm((n_ctx, half, width), F32),
        vm((length, width), BF16),
        vm((length, width), BF16),
        vm((n_pair, length, fw), BF16),
        vm((n_pair, length, fw), BF16),
        vm((length, width), BF16),
        vm((length, hw), BF16),
        vm((length, hw), F32),
        vm((length, hw), F32),
        vm((length, 3 * hw), BF16),
        vm((width, length), BF16),
        vm((width, length), BF16),
        vm((2, n_ctx, half, width), F32),
        vm((2, n_ctx, half, width), BF16),
        vm((2, n_ctx, half, width), BF16),
    ]
    scratch += [vm((heads, block, (b + 1) * block), BF16) for b in range(n_ctx)]
    scratch += [pltpu.SemaphoreType.DMA((8, n_ctx)), pltpu.SemaphoreType.DMA((8, n_ctx))]
    return pl.pallas_call(
        functools.partial(compute_body, sizes),
        out_shape=out_shape,
        in_specs=[vmem_spec] * 10,
        out_specs=[vmem_spec] * 9,
        scratch_shapes=scratch,
        compiler_params=pltpu.CompilerParams(
            collective_id=1, has_side_effects=True, vmem_limit_bytes=VMEM_LIMIT
        ),
    )(tok, og, *weights, vecs, bias)


def scatter_body(sizes, half, *refs):
    here = Place(sizes)
    n_dp, n_ctx, n_pair = here.n_dp, here.n_ctx, here.n_pair
    d, z, p, c = here.dp, here.ctx, here.pair, here.side
    rows_in = refs[0:2]
    grads = refs[2:8]
    small = refs[8]
    rows_out = refs[9:11]
    owned = refs[11:17]
    small_out = refs[17]
    it = iter(refs[18:])
    dp_land = [next(it) for _ in range(6)]
    dp_sum = [next(it) for _ in range(6)]
    keep = [next(it) for _ in range(6)]
    pair_land = [next(it) for _ in range(6)]
    pair_sum = [next(it) for _ in range(6)]
    ctx_land = [next(it) for _ in range(6)]
    side_land, small_b, ctx_small, small_c, pair_small, small_d, dp_small = [next(it) for _ in range(7)]
    own_sem, send_sem, line_sem, far_sem, side_sem, dp_sem, pair_sem, ctx_sem, small_sem = it
    mine = p * n_ctx + z
    rows = pl.ds(pl.multiple_of(c * half, half), half)

    here.barrier(True)
    sends = Sends(send_sem)

    for a in range(6):
        for k in range(1, n_dp):
            dd, device = here.other_dp(k)
            sends.go(
                grads[a].at[:, pl.ds(dd * n_ctx, n_ctx)],
                dp_land[a].at[k - 1],
                dp_sem.at[a, k - 1],
                device,
            )
    own = []
    for i in range(2):
        for k in range(1, n_ctx):
            zz, device = here.other_ctx(k)
            sends.go(rows_in[i].at[zz], rows_out[i].at[mine, rows], line_sem.at[i, z], device)
        own.append(pltpu.make_async_copy(rows_in[i].at[z], rows_out[i].at[mine, rows], own_sem.at[i]))
        own[-1].start()
    sends.go(small.at[pl.ds(0, 8)], side_land, small_sem.at[0, 0], here.partner())

    def small_arrive(stage, k, land):
        remote(land, land, send_sem.at[0], small_sem.at[stage, k - 1], here.partner()).wait_recv()

    for i in range(2):
        own[i].wait()
        for k in range(1, n_ctx):
            zz, device = here.other_ctx(k)
            slot = rows_out[i].at[p * n_ctx + zz, rows]
            remote(slot, slot, send_sem.at[0], line_sem.at[i, zz], device).wait_recv()
        for k in range(1, n_pair):
            pp, device = here.other_pair(k)
            slot = rows_out[i].at[pl.ds(p * n_ctx, n_ctx), rows]
            sends.go(slot, slot, far_sem.at[i, p], device)

    small_arrive(0, 1, side_land)
    small_b[0:8, :] = small[0:8, :] + side_land[...]
    small_b[8:16, :] = small[8:16, :]
    small_b[6:8, :] = small[6:8, :]
    for k in range(1, n_ctx):
        zz, device = here.other_ctx(k)
        sends.go(small_b, ctx_small.at[k - 1], small_sem.at[1, k - 1], device)

    for a in range(6):
        for k in range(1, n_dp):
            remote(
                dp_land[a].at[k - 1], dp_land[a].at[k - 1], send_sem.at[0], dp_sem.at[a, k - 1],
                here.partner(),
            ).wait_recv()
        for i in range(n_pair):
            total = grads[a][i, pl.ds(d * n_ctx, n_ctx)].astype(F32)
            for k in range(1, n_dp):
                total = total + dp_land[a][k - 1, i].astype(F32)
            dp_sum[a][i] = total.astype(BF16)
        for k in range(1, n_pair):
            pp, device = here.other_pair(k)
            sends.go(dp_sum[a].at[pp], pair_land[a].at[k - 1], pair_sem.at[a, k - 1], device)

    total = small_b[...]
    for k in range(1, n_ctx):
        small_arrive(1, k, ctx_small.at[k - 1])
        total = total + ctx_small[k - 1]
    small_c[...] = total
    for k in range(1, n_pair):
        pp, device = here.other_pair(k)
        sends.go(small_c, pair_small.at[k - 1], small_sem.at[2, k - 1], device)

    for a in range(6):
        for k in range(1, n_pair):
            remote(
                pair_land[a].at[k - 1], pair_land[a].at[k - 1], send_sem.at[0], pair_sem.at[a, k - 1],
                here.partner(),
            ).wait_recv()
        total = dp_sum[a][p].astype(F32)
        for k in range(1, n_pair):
            total = total + pair_land[a][k - 1].astype(F32)
        keep[a][...] = total
        pair_sum[a][...] = total.astype(BF16)
        for k in range(1, n_ctx):
            zz, device = here.other_ctx(k)
            sends.go(pair_sum[a].at[zz], ctx_land[a].at[k - 1], ctx_sem.at[a, k - 1], device)

    total = small_c[...]
    for k in range(1, n_pair):
        small_arrive(2, k, pair_small.at[k - 1])
        total = total + pair_small[k - 1]
    small_d[...] = total
    for k in range(1, n_dp):
        dd, device = here.other_dp(k)
        sends.go(small_d, dp_small.at[k - 1], small_sem.at[3, k - 1], device)

    for i in range(2):
        for k in range(1, n_pair):
            pp, device = here.other_pair(k)
            slot = rows_out[i].at[pl.ds(pp * n_ctx, n_ctx), rows]
            remote(slot, slot, send_sem.at[0], far_sem.at[i, pp], device).wait_recv()
        slot = rows_out[i].at[:, rows]
        sends.go(slot, slot, side_sem.at[i], here.partner())

    for a in range(6):
        total = keep[a][z]
        for k in range(1, n_ctx):
            remote(
                ctx_land[a].at[k - 1], ctx_land[a].at[k - 1], send_sem.at[0], ctx_sem.at[a, k - 1],
                here.partner(),
            ).wait_recv()
            total = total + ctx_land[a][k - 1].astype(F32)
        owned[a][...] = total

    total = small_d[...]
    for k in range(1, n_dp):
        small_arrive(3, k, dp_small.at[k - 1])
        total = total + dp_small[k - 1]
    small_out[...] = total
    other = pl.ds(pl.multiple_of((1 - c) * half, half), half)
    for i in range(2):
        slot = rows_out[i].at[:, other]
        remote(slot, slot, send_sem.at[0], side_sem.at[i], here.partner()).wait_recv()
    sends.finish()


def scatter_call(sizes, seqs, lo, tg, grads, small):
    n_dp, n_ctx, n_tp = sizes
    n_pair = n_tp // 2
    half, width = lo.shape[1:]
    vmem_spec = pl.BlockSpec(memory_space=pltpu.VMEM)
    shape = jax.ShapeDtypeStruct
    vm = pltpu.VMEM
    tail = [g.shape[2:] for g in grads]
    out_shape = [shape((seqs, 2 * half, width), BF16)] * 2
    out_shape += [shape(t, F32) for t in tail]
    out_shape += [shape(small.shape, F32)]
    scratch = [vm((n_dp - 1, n_pair, n_ctx) + t, BF16) for t in tail]
    scratch += [vm((n_pair, n_ctx) + t, BF16) for t in tail]
    scratch += [vm((n_ctx,) + t, F32) for t in tail]
    scratch += [vm((n_pair - 1, n_ctx) + t, BF16) for t in tail]
    scratch += [vm((n_ctx,) + t, BF16) for t in tail]
    scratch += [vm((n_ctx - 1,) + t, BF16) for t in tail]
    scratch += [
        vm((8, width), F32),
        vm((16, width), F32),
        vm((n_ctx - 1, 16, width), F32),
        vm((16, width), F32),
        vm((n_pair - 1, 16, width), F32),
        vm((16, width), F32),
        vm((n_dp - 1, 16, width), F32),
    ]
    n_sends = (
        6 * ((n_dp - 1) + (n_pair - 1) + (n_ctx - 1))
        + 2 * ((n_ctx - 1) + (n_pair - 1) + 1)
        + 1 + (n_ctx - 1) + (n_pair - 1) + (n_dp - 1)
    )
    dma = pltpu.SemaphoreType.DMA
    most = max(n_dp, n_ctx, n_pair)
    scratch += [
        dma((2,)),
        dma((n_sends,)),
        dma((2, n_ctx)),
        dma((2, n_pair)),
        dma((2,)),
        dma((6, n_dp - 1)),
        dma((6, n_pair - 1)),
        dma((6, n_ctx - 1)),
        dma((4, most)),
    ]
    return pl.pallas_call(
        functools.partial(scatter_body, sizes, half),
        out_shape=out_shape,
        in_specs=[vmem_spec] * 9,
        out_specs=[vmem_spec] * 9,
        scratch_shapes=scratch,
        compiler_params=pltpu.CompilerParams(
            collective_id=2, has_side_effects=True, vmem_limit_bytes=VMEM_LIMIT
        ),
    )(lo, tg, *grads, small)


def fused_body(sizes, dims, *refs):
    here = Place(sizes)
    n_dp, n_ctx, n_pair = here.n_dp, here.n_ctx, here.n_pair
    d, z, p, c = here.dp, here.ctx, here.pair, here.side
    half, width, share, cols, fw = dims
    block = 2 * half
    hw = n_pair * cols
    lanes = 2 * HEAD_DIM
    n_twos = hw // lanes
    n_rows = n_dp * n_ctx
    two = n_ctx // 2
    it = iter(refs)

    def take(n):
        return [next(it) for _ in range(n)]

    tokens, out_grad = take(2)
    narrow_shards = take(4)
    shards = [None] + take(2)
    vectors, column_biases = take(6), take(3)
    rows_out = take(2)
    owned_out = take(3)
    small_out = next(it)
    full = take(3)
    pack_all, vecs, cold = take(3)
    tok, og, lo, tg = take(4)
    (
        xn1, wqkv, wo, qs, ks, vs, o32, mixed, hid, xn2, ogf, act, ug, bg, dm, dqkv, tra, trb,
        wide, whole, ssend, srecv, dwd, small,
    ) = take(24)
    p_first = take(n_ctx)
    first_land, second_land, ctx_land = take(3), take(3), take(3)
    side_land, small_b, ctx_small, small_c, pair_small, small_d, dp_small = take(7)
    owned = take(3)
    small_e = next(it)
    (
        own_sem, put_sem, rows_sem, line_sem, pair_sem, dp_sem, diag_dp_sem, diag_pair_sem, swap_send,
        swap_recv, first_sem, second_sem, ctx_sem, out_line, out_pair, out_side, small_sem,
        side_sem,
    ) = take(18)
    partner = here.partner()
    own_row = d * n_ctx + z
    mine = p * n_ctx + z
    scale = HEAD_DIM ** -0.5
    first_head = lax.broadcasted_iota(jnp.int32, (1, lanes), 1) < HEAD_DIM
    zero16 = jnp.zeros((), BF16)
    side_rows = pl.ds(pl.multiple_of(c * half, half), half)
    far_side = pl.ds(pl.multiple_of((1 - c) * half, half), half)
    sends = Sends(put_sem)

    def arrive(slot, sem):
        remote(slot, slot, put_sem.at[0], sem, partner).wait_recv()

    def far_first():
        upper = z // two
        order = []
        for i in range(n_ctx - 1):
            down = n_ctx - 1 - i
            down = down - (z - down + n_ctx) // n_ctx
            up = i + (i - z + n_ctx) // n_ctx
            zz = upper * up + (1 - upper) * down
            order.append((zz, (d, zz, here.tp)))
        return order

    line_order = far_first()

    def flipped(h):
        zz = z + h - 2 * h * ((z // h) % 2)
        return zz, (d, zz, here.tp)

    strides = [1 << i for i in range(n_ctx.bit_length() - 1)]

    def shard_rows(r, count=1):
        return pl.ds(pl.multiple_of(r * share, 16), count * share)

    def slot(a, pp, dd, zz, count=1):
        return full[a].at[pp, shard_rows(dd * n_ctx + zz, count)]

    gather_own = [None] + [
        pltpu.make_async_copy(shards[a], slot(a, p, d, z), own_sem.at[a]) for a in (1, 2)
    ]

    def gather_give(a, h):
        device = flipped(h)[1]
        for i in range(n_ctx // (2 * h)):
            zz = (z + 2 * h * i) % n_ctx
            source = shards[a] if a > 0 and i == 0 else slot(a, p, d, zz)
            sends.go(source, slot(a, p, d, zz), line_sem.at[a, zz], device)

    def gather_take(a, h):
        q = flipped(h)[0]
        for i in range(n_ctx // (2 * h)):
            zz = (q + 2 * h * i) % n_ctx
            arrive(slot(a, p, d, zz), line_sem.at[a, zz])

    def gather_start(a):
        gather_give(a, strides[-1])

    def gather_next(a):
        for h in reversed(strides[:-1]):
            gather_take(a, 2 * h)
            gather_give(a, h)

    def gather_hop(a):
        if a > 0:
            gather_own[a].wait()
        gather_take(a, 1)
        group = slot(a, p, d, 0, n_ctx)
        for k in range(1, n_pair):
            sends.go(group, group, pair_sem.at[a, p], here.other_pair(k)[1])
        for k in range(1, n_dp):
            sends.go(group, group, dp_sem.at[a, d], here.other_dp(k)[1])

    def gather_turn(a):
        for k in range(1, n_pair):
            pp = here.other_pair(k)[0]
            arrive(slot(a, pp, d, 0, n_ctx), pair_sem.at[a, pp])
            first = slot(a, pp, d, 0, two)
            for j in range(1, n_dp):
                sends.go(first, first, diag_dp_sem.at[a, pp, d], here.other_dp(j)[1])
        for k in range(1, n_dp):
            dd = here.other_dp(k)[0]
            arrive(slot(a, p, dd, 0, n_ctx), dp_sem.at[a, dd])
            second = slot(a, p, dd, two, n_ctx - two)
            for j in range(1, n_pair):
                sends.go(second, second, diag_pair_sem.at[a, p, dd], here.other_pair(j)[1])

    def gather_end(a):
        for k in range(1, n_pair):
            pp = here.other_pair(k)[0]
            for j in range(1, n_dp):
                dd = here.other_dp(j)[0]
                arrive(slot(a, pp, dd, 0, two), diag_dp_sem.at[a, pp, dd])
                arrive(slot(a, pp, dd, two, n_ctx - two), diag_pair_sem.at[a, pp, dd])

    def pack_start():
        own = pack_all.at[p, own_row]
        for zz, device in line_order:
            sends.go(own, own, line_sem.at[3, z], device)

    def pack_hop():
        for k in range(1, n_ctx):
            zz = here.other_ctx(k)[0]
            arrive(pack_all.at[p, d * n_ctx + zz], line_sem.at[3, zz])
        group = pack_all.at[p, pl.ds(d * n_ctx, n_ctx)]
        for k in range(1, n_pair):
            sends.go(group, group, pair_sem.at[3, p], here.other_pair(k)[1])
        for k in range(1, n_dp):
            sends.go(group, group, dp_sem.at[3, d], here.other_dp(k)[1])

    def pack_end():
        for k in range(1, n_pair):
            pp = here.other_pair(k)[0]
            arrive(pack_all.at[pp, pl.ds(d * n_ctx, n_ctx)], pair_sem.at[3, pp])
        for k in range(1, n_dp):
            dd = here.other_dp(k)[0]
            arrive(pack_all.at[p, pl.ds(dd * n_ctx, n_ctx)], dp_sem.at[3, dd])

    rows_own = [
        pltpu.make_async_copy(source.at[mine, side_rows], target.at[z], own_sem.at[4 + i])
        for i, (source, target) in enumerate(((tokens, tok), (out_grad, og)))
    ]

    def rows_start(i, source, target):
        for zz, device in line_order:
            sends.go(source.at[p * n_ctx + zz, side_rows], target.at[z], rows_sem.at[i, z], device)

    def grad_slot(ref, pp, dd, k):
        return ref.at[pp, shard_rows(dd * n_ctx + (z + k) % n_ctx)]

    def pair_leads(a, k):
        return a > 0 and near.index(k) % 2 == 0

    def scatter_start(a, ref, ks):
        for k in ks:
            if pair_leads(a, k):
                for j in range(1, n_pair):
                    pp, device = here.other_pair(j)
                    for i in range(n_dp):
                        sends.go(grad_slot(ref, pp, i, k), first_land[a].at[j - 1, i, k], first_sem.at[a, j - 1, i, k], device)
            else:
                for j in range(1, n_dp):
                    dd, device = here.other_dp(j)
                    for i in range(n_pair):
                        sends.go(grad_slot(ref, i, dd, k), first_land[a].at[j - 1, i, k], first_sem.at[a, j - 1, i, k], device)

    def add_into(target, parts):
        total = target[...].astype(F32)
        for part in parts:
            total = total + part[...].astype(F32)
        target[...] = total.astype(BF16)

    def scatter_turn(a, ref, ks):
        for k in ks:
            leads = pair_leads(a, k)
            n_lead, n_next = (n_pair, n_dp) if leads else (n_dp, n_pair)
            for i in range(n_next):
                parts = [first_land[a].at[j - 1, i, k] for j in range(1, n_lead)]
                for j in range(1, n_lead):
                    arrive(parts[j - 1], first_sem.at[a, j - 1, i, k])
                target = grad_slot(ref, p, i, k) if leads else grad_slot(ref, i, d, k)
                add_into(target, parts)
            for j in range(1, n_next):
                other, device = here.other_dp(j) if leads else here.other_pair(j)
                source = grad_slot(ref, p, other, k) if leads else grad_slot(ref, other, d, k)
                sends.go(source, second_land[a].at[j - 1, k], second_sem.at[a, j - 1, k], device)

    def scatter_line(a, ref, ks):
        for k in ks:
            n_next = n_dp if pair_leads(a, k) else n_pair
            parts = [second_land[a].at[j - 1, k] for j in range(1, n_next)]
            for j in range(1, n_next):
                arrive(parts[j - 1], second_sem.at[a, j - 1, k])
            add_into(grad_slot(ref, p, d, k), parts)
            if k % 2 == 1:
                scatter_give(a, ref, 1, k)

    def scatter_give(a, ref, h, k):
        zz, device = flipped(h)
        at = n_ctx - n_ctx // h + ((z + k - zz + n_ctx) % n_ctx) // (2 * h)
        sends.go(grad_slot(ref, p, d, k), ctx_land[a].at[at], ctx_sem.at[a, at], device)

    def scatter_across(a, ref):
        for h in strides[1:]:
            for i in range(n_ctx // h):
                at = n_ctx - 2 * n_ctx // h + i
                arrive(ctx_land[a].at[at], ctx_sem.at[a, at])
                add_into(grad_slot(ref, p, d, i * h), [ctx_land[a].at[at]])
            for k in range(h, n_ctx, 2 * h):
                scatter_give(a, ref, h, k)

    def scatter_end(a, ref):
        last = n_ctx - 2
        arrive(ctx_land[a].at[last], ctx_sem.at[a, last])
        owned[a][...] = ref[p, shard_rows(own_row), :].astype(F32) + ctx_land[a][last].astype(F32)
        pltpu.make_async_copy(owned[a], owned_out[a], own_sem.at[8 + a]).start()

    near = [k for h in strides for k in range(h, n_ctx, 2 * h)] + [0]
    early, late = near[:two], near[two:]
    others = list(range(1, n_ctx))

    def out_slot(i, s, rows):
        return rows_out[i].at[s, rows]

    def out_start(i, source):
        for zz, device in line_order:
            sends.go(source.at[zz], out_slot(i, mine, side_rows), out_line.at[i, z], device)
        copy = pltpu.make_async_copy(source.at[z], out_slot(i, mine, side_rows), own_sem.at[6 + i])
        copy.start()
        return copy

    def out_pass(i, s, source):
        piece = out_slot(i, s, side_rows)
        for j in range(1, n_pair):
            sends.go(source, piece, out_pair.at[i, s], here.other_pair(j)[1])
        sends.go(source, piece, out_side.at[i, s], partner)

    def out_hop(i, ks):
        for k in ks:
            s = p * n_ctx + here.other_ctx(k)[0]
            piece = out_slot(i, s, side_rows)
            arrive(piece, out_line.at[i, here.other_ctx(k)[0]])
            out_pass(i, s, piece)

    def out_cross(i):
        for j in range(1, n_pair):
            pp = here.other_pair(j)[0]
            for k in range(n_ctx):
                s = pp * n_ctx + (z + k) % n_ctx
                piece = out_slot(i, s, side_rows)
                arrive(piece, out_pair.at[i, s])
                sends.go(piece, piece, out_side.at[i, s], partner)

    def out_end(i):
        for s in range(n_pair * n_ctx):
            arrive(out_slot(i, s, far_side), out_side.at[i, s])

    def own_rows(b):
        return pl.ds(pl.multiple_of(b * block + c * half, half), half)

    def far_rows(b):
        return pl.ds(pl.multiple_of(b * block + (1 - c) * half, half), half)

    def block_rows(b):
        return pl.ds(pl.multiple_of(b * block, block), block)

    def swap(stage, b, src, dst):
        return remote(src, dst, swap_send.at[stage, b], swap_recv.at[stage, b], partner)

    def rows_copy(stage, b, ref):
        return swap(stage, b, ref.at[own_rows(b)], ref.at[own_rows(b)])

    def rows_arrive(stage, b, ref):
        swap(stage, b, ref.at[far_rows(b)], ref.at[far_rows(b)]).wait_recv()

    def part_copy(stage, place, b):
        return swap(stage, b, ssend.at[place, b], srecv.at[place, b])

    def part_store(i, b, value):
        wide[i, pl.ds(pl.multiple_of(b * block, block), half), :] = value[:, :hw]
        wide[i, pl.ds(pl.multiple_of(b * block + half, half), half), :] = value[:, hw:]

    def part_load(i, b):
        left = wide[i, pl.ds(pl.multiple_of(b * block, block), half), :]
        right = wide[i, pl.ds(pl.multiple_of(b * block + half, half), half), :]
        return jnp.concatenate([left, right], axis=1)

    rows_own[0].start()
    rows_own[1].start()
    gather_own[1].start()
    gather_own[2].start()
    for a in range(4):
        full[0][p, shard_rows(own_row), a * cols : (a + 1) * cols] = narrow_shards[a][...]
    own_pack = pack_all.at[p, own_row]
    own_pack[...] = jnp.zeros(own_pack.shape, F32)
    for i in range(6):
        own_pack[i : i + 1, :share] = vectors[i][...].astype(F32)
    row = 6
    for ref in column_biases:
        n = ref.shape[0]
        line = ref[...].astype(F32).reshape(1, n)
        for w in range(0, n, 128):
            m = min(128, n - w)
            own_pack[row : row + 1, :m] = line[:, w : w + m]
            row += 1
    small[...] = jnp.zeros_like(small)
    here.barrier(True)
    pack_start()
    gather_start(0)
    gather_next(0)
    gather_start(1)
    pack_hop()
    pack_end()
    for r in range(n_rows):
        own_part = pack_all[p, r]
        vecs[0:8, r * share : (r + 1) * share] = own_part[0:8, :share]
    for i in range(n_pair):
        piece = pack_all[i, d * n_ctx]
        for line in range(2):
            for w in range(0, cols, 128):
                n = min(128, cols - w)
                row = 6 + 2 * line + w // 128
                cold[line : line + 1, i * cols + w : i * cols + w + n] = piece[row : row + 1, :n]
        for w in range(0, fw, 128):
            row = 10 + w // 128
            cold[2 + i : 3 + i, w : w + 128] = piece[row : row + 1, :]
    gain_one, shift_one, out_shift = vecs[0:1, :], vecs[1:2, :], vecs[2:3, :]
    gain_two, shift_two, down_shift = vecs[3:4, :], vecs[4:5, :], vecs[5:6, :]

    def norm_one(b):
        scaled, _ = normalize(tok[b].astype(F32))
        xn1[own_rows(b), :] = (scaled * gain_one + shift_one).astype(BF16)
        rows_copy(1, b, xn1).start()

    rows_own[0].wait()
    norm_one(z)
    gather_hop(0)
    gather_next(1)
    pl.semaphore_signal(side_sem, inc=1, device_id=partner, device_id_type=MESH)
    pl.semaphore_wait(side_sem, 1)
    rows_start(0, tokens, tok)
    gather_start(2)
    gather_turn(0)
    gather_hop(1)
    for k in range(1, n_ctx):
        b = here.other_ctx(k)[0]
        arrive(tok.at[b], rows_sem.at[0, b])
        norm_one(b)
    gather_end(0)
    for i in range(n_pair):
        for a, base in enumerate((0, hw, 2 * hw)):
            wqkv[:, base + i * cols : base + (i + 1) * cols] = full[0][i, :, a * cols : (a + 1) * cols]
        wo[:, i * cols : (i + 1) * cols] = full[0][i, :, 3 * cols : 4 * cols]
    q_shift, v_shift = cold[0:1, :hw], cold[1:2, :hw]

    @pl.loop(0, n_ctx)
    def _(b):
        rows_arrive(1, b, xn1)
        product = nn_dot(xn1[block_rows(b), :], wqkv[...])
        qs[block_rows(b), :] = (product[:, :hw] + q_shift).astype(BF16) * jnp.asarray(scale, BF16)
        ks[block_rows(b), :] = product[:, hw : 2 * hw].astype(BF16)
        vs[block_rows(b), :] = (product[:, 2 * hw :] + v_shift).astype(BF16)

    gather_next(2)

    for b in range(n_ctx):
        reach = (b + 1) * block
        here_rows = slice(b * block, (b + 1) * block)

        @pl.loop(0, n_twos)
        def _(j):
            at = pl.ds(pl.multiple_of(j * lanes, lanes), lanes)
            queries, keys, values = qs[here_rows, at], ks[:reach, at], vs[:reach, at]
            pieces = []
            for e in range(2):
                head = first_head if e == 0 else jnp.logical_not(first_head)
                scores = nt_dot(jnp.where(head, queries, zero16), keys)
                powers = jnp.exp(scores - jnp.max(scores, axis=-1, keepdims=True))
                inverse = 1.0 / jnp.sum(powers, axis=-1, keepdims=True)
                probs = (powers * inverse).astype(BF16)
                p_first[b][2 * j + e] = probs
                pieces.append(nn_dot(probs, values))
            out = jnp.where(first_head, pieces[0], pieces[1])
            o32[here_rows, at] = out
            mixed[here_rows, at] = out.astype(BF16)

        whole[b % 2] = nt_dot(mixed[here_rows, :], wo[...])
        ssend[0, b] = whole[b % 2, far_side, :].astype(BF16)
        part_copy(2, 0, b).start()
        hid[b] = whole[b % 2, side_rows, :]
        if b == 1:
            gather_turn(1)
            rows_start(1, out_grad, og)
        if b == 2:
            gather_hop(2)

    @pl.loop(0, n_ctx)
    def _(b):
        part_copy(2, 0, b).wait()
        hidden = tok[b].astype(F32) + (hid[b] + srecv[0, b].astype(F32)) + out_shift
        hid[b] = hidden
        scaled, _ = normalize(hidden)
        xn2[own_rows(b), :] = (scaled * gain_two + shift_two).astype(BF16)
        rows_copy(3, b, xn2).start()

    gather_end(1)

    @pl.loop(0, n_ctx)
    def _(b):
        rows_arrive(3, b, xn2)
        normed = xn2[block_rows(b), :]
        for i in range(n_pair):
            upward = nn_dot(normed, full[1][i]) + cold[2 + i : 3 + i, :fw]
            big_phi = 0.5 + 0.5 * lax.erf(upward * root_half)
            act[i, block_rows(b), :] = (upward * big_phi).astype(BF16)
            slope = big_phi + upward * density_scale * jnp.exp(-0.5 * upward * upward)
            ug[i, block_rows(b), :] = slope.astype(BF16)

    rows_own[1].wait()
    for k in range(n_ctx):
        b = (z + k) % n_ctx
        if k > 0:
            arrive(og.at[b], rows_sem.at[1, b])
        swap(0, b, og.at[b], ogf.at[own_rows(b)]).start()
        ogf[own_rows(b), :] = og[b]
    for b in range(n_ctx):
        rows_arrive(0, b, ogf)

    step = 256

    def transposed(ref, out):
        for b in range(n_ctx):
            out[:, b * block : (b + 1) * block] = ref[b * block : (b + 1) * block, :].T

    gather_turn(2)
    gathered = len(sends.started)
    transposed(ogf, trb)

    @pl.loop(0, width // step)
    def _(r):
        rows = pl.ds(pl.multiple_of(r * step, step), step)
        for i in range(n_pair):
            dwd[i, rows, :] = nn_dot(trb[rows, :], act[i]).astype(BF16)

    scatter_start(2, dwd, near)

    def slope_back(i, b):
        slope = ug[i, block_rows(b), :].astype(F32)
        rows_grad = (nn_dot(ogf[block_rows(b), :], full[2][i]) * slope).astype(BF16)
        ug[i, block_rows(b), :] = rows_grad
        small[pl.ds(8 + i, 1), :] += jnp.sum(rows_grad.astype(F32), axis=0, keepdims=True)

    @pl.loop(0, n_ctx)
    def _(b):
        slope_back(p, b)

    gather_end(2)

    def through(ref, weight, rows):
        total = nt_dot(ref[0, rows, :], weight[0])
        for i in range(1, n_pair):
            total = total + nt_dot(ref[i, rows, :], weight[i])
        return total

    def units_back(b):
        for k in range(1, n_pair):
            slope_back(here.other_pair(k)[0], b)
        whole[0] = through(ug, full[1], block_rows(b))
        ssend[0, b] = whole[0, far_side, :].astype(BF16)
        part_copy(5, 0, b).start()
        part_store(1, b, whole[0, side_rows, :])
        whole[1] = through(act, full[2], block_rows(b))
        ssend[1, b] = whole[1, far_side, :].astype(BF16)
        part_copy(4, 1, b).start()
        part_store(0, b, whole[1, side_rows, :])

    pl.loop(0, two)(units_back)
    scatter_turn(2, dwd, early)
    pl.loop(two, n_ctx)(units_back)
    transposed(xn2, tra)
    scatter_turn(2, dwd, late)
    for copy in sends.started[:gathered]:
        copy.wait_send()

    @pl.loop(0, width // step)
    def _(r):
        rows = pl.ds(pl.multiple_of(r * step, step), step)
        for i in range(n_pair):
            full[1][i, rows, :] = nn_dot(tra[rows, :], ug[i]).astype(BF16)

    scatter_start(1, full[1], near)
    scatter_line(2, dwd, early)

    @pl.loop(0, n_ctx)
    def _(b):
        part_copy(5, 0, b).wait()
        grad_two = part_load(1, b) + srecv[0, b].astype(F32)
        part_copy(4, 1, b).wait()
        lo[b] = (hid[b] + (part_load(0, b) + srecv[1, b].astype(F32)) + down_shift).astype(BF16)
        scaled, spread = normalize(hid[b])
        own_grad = og[b].astype(F32)
        hidden_grad = own_grad + norm_back(grad_two * gain_two, scaled, spread)
        hid[b] = hidden_grad
        branch = hidden_grad.astype(BF16)
        bg[own_rows(b), :] = branch
        rows_copy(6, b, bg).start()
        small[2:3, :] += jnp.sum(branch.astype(F32), axis=0, keepdims=True)
        small[3:4, :] += jnp.sum(grad_two * scaled, axis=0, keepdims=True)
        small[4:5, :] += jnp.sum(grad_two, axis=0, keepdims=True)
        small[5:6, :] += jnp.sum(own_grad, axis=0, keepdims=True)

    lo_copy = out_start(0, lo)
    out_pass(0, mine, lo.at[z])

    @pl.loop(0, n_ctx)
    def _(b):
        rows_arrive(6, b, bg)
        dm[block_rows(b), :] = nn_dot(bg[block_rows(b), :], wo[...]).astype(BF16)

    scatter_line(2, dwd, late)
    transposed(bg, trb)

    @pl.loop(0, width // step)
    def _(r):
        rows = pl.ds(pl.multiple_of(r * step, step), step)
        product = nn_dot(trb[rows, :], mixed[...])
        for i in range(n_pair):
            full[0][i, rows, 3 * cols : 4 * cols] = product[:, i * cols : (i + 1) * cols].astype(BF16)

    for b in reversed(range(n_ctx)):
        reach = (b + 1) * block
        here_rows = slice(b * block, (b + 1) * block)

        @pl.loop(0, n_twos)
        def _(j):
            at = pl.ds(pl.multiple_of(j * lanes, lanes), lanes)
            queries, keys, values = qs[here_rows, at], ks[:reach, at], vs[:reach, at]
            mix_grad, mix = dm[here_rows, at], o32[here_rows, at]
            towards = mix_grad.astype(F32) * mix
            query_parts, key_sum, value_sum = [], None, None
            for e in range(2):
                head = first_head if e == 0 else jnp.logical_not(first_head)
                grad_head = jnp.where(head, mix_grad, zero16)
                prob_grad = nt_dot(grad_head, values)
                centre = jnp.sum(jnp.where(head, towards, 0.0), axis=-1, keepdims=True)
                probs = p_first[b][2 * j + e]
                score_grad = (probs.astype(F32) * (prob_grad - centre)).astype(BF16)
                query_parts.append(nn_dot(score_grad, keys))
                key_term = tn_dot(score_grad, jnp.where(head, queries, zero16))
                value_term = tn_dot(probs, grad_head)
                key_sum = key_term if key_sum is None else key_sum + key_term
                value_sum = value_term if value_sum is None else value_sum + value_term
            query_grad = jnp.where(first_head, query_parts[0], query_parts[1]) * scale
            dqkv[here_rows, at] = query_grad.astype(BF16)
            if b == n_ctx - 1:
                wide[0, :, at] = key_sum
                wide[1, :, at] = value_sum
            else:
                wide[0, :reach, at] += key_sum
                wide[1, :reach, at] += value_sum

        if b == 1:
            scatter_turn(1, full[1], near)
        if b == 0:
            out_hop(0, others)

    @pl.loop(0, n_ctx)
    def _(b):
        dqkv[block_rows(b), hw : 2 * hw] = wide[0, block_rows(b), :].astype(BF16)
        dqkv[block_rows(b), 2 * hw :] = wide[1, block_rows(b), :].astype(BF16)
        small[6:7, :hw] += jnp.sum(dqkv[block_rows(b), :hw].astype(F32), axis=0, keepdims=True)
        small[7:8, :hw] += jnp.sum(dqkv[block_rows(b), 2 * hw :].astype(F32), axis=0, keepdims=True)
        whole[0] = nt_dot(dqkv[block_rows(b), :], wqkv[...])
        ssend[1, b] = whole[0, far_side, :].astype(BF16)
        part_copy(7, 1, b).start()
        part_store(0, b, whole[0, side_rows, :])

    transposed(xn1, tra)

    @pl.loop(0, width // step)
    def _(r):
        rows = pl.ds(pl.multiple_of(r * step, step), step)
        product = nn_dot(tra[rows, :], dqkv[...])
        for i in range(n_pair):
            for a in range(3):
                full[0][i, rows, a * cols : (a + 1) * cols] = product[
                    :, a * hw + i * cols : a * hw + (i + 1) * cols
                ].astype(BF16)

    scatter_start(0, full[0], near)

    @pl.loop(0, n_ctx)
    def _(b):
        part_copy(7, 1, b).wait()
        grad_one = part_load(0, b) + srecv[1, b].astype(F32)
        scaled, spread = normalize(tok[b].astype(F32))
        tg[b] = (hid[b] + norm_back(grad_one * gain_one, scaled, spread)).astype(BF16)
        small[0:1, :] += jnp.sum(grad_one * scaled, axis=0, keepdims=True)
        small[1:2, :] += jnp.sum(grad_one, axis=0, keepdims=True)

    sends.go(small.at[pl.ds(0, 8)], side_land, small_sem.at[0, 0], partner)
    tg_copy = out_start(1, tg)
    out_pass(1, mine, tg.at[z])
    scatter_line(1, full[1], near)
    scatter_across(2, dwd)
    arrive(side_land, small_sem.at[0, 0])
    small_b[0:6, :] = small[0:6, :] + side_land[0:6, :]
    small_b[6:16, :] = small[6:16, :]
    for k in range(1, n_pair):
        sends.go(small_b, pair_small.at[k - 1], small_sem.at[2, k - 1], here.other_pair(k)[1])
    scatter_turn(0, full[0], early)
    out_cross(0)
    out_hop(1, others[:1])
    scatter_line(0, full[0], early)
    scatter_turn(0, full[0], late)
    out_hop(1, others[1:])
    scatter_across(1, full[1])
    total = small_b[...]
    for k in range(1, n_pair):
        arrive(pair_small.at[k - 1], small_sem.at[2, k - 1])
        total = total + pair_small[k - 1]
    small_c[...] = total
    for k in range(1, n_dp):
        sends.go(small_c, dp_small.at[k - 1], small_sem.at[3, k - 1], here.other_dp(k)[1])
    scatter_line(0, full[0], late)
    scatter_across(0, full[0])
    scatter_end(2, dwd)
    scatter_end(1, full[1])
    out_end(0)
    total = small_c[...]
    for k in range(1, n_dp):
        arrive(dp_small.at[k - 1], small_sem.at[3, k - 1])
        total = total + dp_small[k - 1]
    small_d[...] = total
    for k in range(1, n_ctx):
        sends.go(small_d, ctx_small.at[k - 1], small_sem.at[1, k - 1], here.other_ctx(k)[1])
    out_cross(1)
    scatter_end(0, full[0])
    total = small_d[...]
    for k in range(1, n_ctx):
        arrive(ctx_small.at[k - 1], small_sem.at[1, k - 1])
        total = total + ctx_small[k - 1]
    small_e[...] = total
    small_copy = pltpu.make_async_copy(small_e, small_out, own_sem.at[11])
    small_copy.start()
    out_end(1)
    lo_copy.wait()
    tg_copy.wait()
    small_copy.wait()
    for a in range(3):
        pltpu.make_async_copy(owned[a], owned_out[a], own_sem.at[8 + a]).wait()

    @pl.loop(0, n_ctx)
    def _(b):
        swap(0, b, og.at[b], ogf.at[own_rows(b)]).wait_send()
        rows_copy(1, b, xn1).wait_send()
        rows_copy(3, b, xn2).wait_send()
        rows_copy(6, b, bg).wait_send()

    for copy in sends.started[gathered:]:
        copy.wait_send()


def fused_call(sizes, tokens, out_grad, shards, vectors, column_biases):
    n_dp, n_ctx, n_tp = sizes
    n_pair = n_tp // 2
    seqs, block, width = tokens.shape
    half = block // 2
    length = n_ctx * block
    share, cols = shards[0].shape
    fw = shards[4].shape[1]
    widths = [4 * cols, fw, fw]
    hw = n_pair * cols
    heads = hw // HEAD_DIM
    two = n_ctx // 2
    any_spec = pl.BlockSpec(memory_space=pl.ANY)
    vmem_spec = pl.BlockSpec(memory_space=pltpu.VMEM)
    shape = jax.ShapeDtypeStruct
    vm = pltpu.VMEM
    dma = pltpu.SemaphoreType.DMA
    out_shape = [shape(tokens.shape, BF16)] * 2
    out_shape += [shape((share, w), F32) for w in widths]
    out_shape += [shape((16, width), F32)]
    scratch = [vm((n_pair, width, w), BF16) for w in widths]
    scratch += [
        vm((n_pair, n_dp * n_ctx, 16, 128), F32),
        vm((8, width), F32),
        vm((8, width), F32),
    ]
    scratch += [vm((n_ctx, half, width), BF16)] * 4
    scratch += [
        vm((length, width), BF16),
        vm((width, 3 * hw), BF16),
        vm((width, hw), BF16),
        vm((length, hw), BF16),
        vm((length, hw), BF16),
        vm((length, hw), BF16),
        vm((length, hw), F32),
        vm((length, hw), BF16),
        vm((n_ctx, half, width), F32),
        vm((length, width), BF16),
        vm((length, width), BF16),
        vm((n_pair, length, fw), BF16),
        vm((n_pair, length, fw), BF16),
        vm((length, width), BF16),
        vm((length, hw), BF16),
        vm((length, 3 * hw), BF16),
        vm((width, length), BF16),
        vm((width, length), BF16),
        vm((2, length, hw), F32),
        vm((2, block, width), F32),
        vm((2, n_ctx, half, width), BF16),
        vm((2, n_ctx, half, width), BF16),
        vm((n_pair, width, fw), BF16),
        vm((16, width), F32),
    ]
    scratch += [vm((heads, block, (b + 1) * block), BF16) for b in range(n_ctx)]
    lead, after = max(n_dp, n_pair) - 1, max(n_dp, n_pair)
    scratch += [vm((lead, after, n_ctx, share, w), BF16) for w in widths]
    scratch += [vm((lead, n_ctx, share, w), BF16) for w in widths]
    scratch += [vm((n_ctx - 1, share, w), BF16) for w in widths]
    scratch += [
        vm((8, width), F32),
        vm((16, width), F32),
        vm((n_ctx - 1, 16, width), F32),
        vm((16, width), F32),
        vm((n_pair - 1, 16, width), F32),
        vm((16, width), F32),
        vm((n_dp - 1, 16, width), F32),
    ]
    scratch += [vm((share, w), F32) for w in widths]
    scratch += [vm((16, width), F32)]
    most = max(n_dp, n_ctx, n_pair)
    scratch += [
        dma((12,)),
        dma((260,)),
        dma((2, n_ctx)),
        dma((4, n_ctx)),
        dma((4, n_pair)),
        dma((4, n_dp)),
        dma((3, n_pair, n_dp)),
        dma((3, n_pair, n_dp)),
        dma((8, n_ctx)),
        dma((8, n_ctx)),
        dma((3, lead, after, n_ctx)),
        dma((3, lead, n_ctx)),
        dma((3, n_ctx)),
        dma((2, n_ctx)),
        dma((2, seqs)),
        dma((2, seqs)),
        dma((4, most)),
        pltpu.SemaphoreType.REGULAR,
    ]
    return pl.pallas_call(
        functools.partial(fused_body, sizes, (half, width, share, cols, fw)),
        out_shape=out_shape,
        in_specs=[any_spec] * 2 + [vmem_spec] * 4 + [any_spec] * 2 + [vmem_spec] * 9,
        out_specs=[any_spec] * 6,
        scratch_shapes=scratch,
        compiler_params=pltpu.CompilerParams(
            collective_id=3, has_side_effects=True, vmem_limit_bytes=67043328
        ),
    )(tokens, out_grad, *shards, *vectors, *column_biases)


def finish_body(n_ctx, share, cols, *refs):
    lo_in, tg_in, attn_in, up_in, down_in, small_in = refs[:6]
    lo, tg, dq, dk, dv, do, du, dd = refs[6:14]
    vectors = refs[14:20]
    shifts = refs[20:22]
    up_shift = refs[22]
    lo_held, tg_held, tg_wide, attn, up, down, small = refs[23:30]
    narrow = refs[30:34]
    in_sem, out_sem, more_in, more_out = refs[34:]
    row = lax.axis_index("dp") * n_ctx + lax.axis_index("ctx")
    pair = lax.axis_index("tp") // 2
    width = small.shape[1]
    seqs = lo_held.shape[0]
    move = pltpu.make_async_copy

    def rows_in(i, s):
        source, held = ((tg_in, tg_held), (lo_in, lo_held))[i]
        return move(source.at[s], held.at[s], in_sem.at[i, s])

    def rows_out(i, s):
        held, target = ((tg_wide, tg), (lo_held, lo))[i]
        return move(held.at[s], target.at[s], out_sem.at[i, s])

    takes = [
        move(source, held, more_in.at[i])
        for i, (source, held) in enumerate(((up_in, up), (down_in, down), (attn_in, attn), (small_in, small)))
    ]
    gives = [
        move(held, target, more_out.at[i])
        for i, (held, target) in enumerate(zip((up, down, *narrow), (du, dd, dq, dk, dv, do)))
    ]

    @pl.loop(0, seqs)
    def _(s):
        rows_in(0, s).start()
        rows_in(1, s).start()

    for copy in takes:
        copy.start()

    @pl.loop(0, seqs)
    def _(s):
        rows_in(0, s).wait()
        tg_wide[s] = tg_held[s].astype(F32)
        rows_out(0, s).start()
        rows_in(1, s).wait()
        rows_out(1, s).start()

    for i in range(2):
        takes[i].wait()
        gives[i].start()
    takes[2].wait()
    for i, ref in enumerate(narrow):
        ref[...] = attn[:, i * cols : (i + 1) * cols]
        gives[2 + i].start()
    takes[3].wait()
    turned = pltpu.roll(small[0:8, :], (width - row * share) % width, 1)
    for i, ref in enumerate(vectors):
        ref[...] = turned[i : i + 1, :share]
    turned = pltpu.roll(small[0:8, :], (width - pair * cols) % width, 1)
    for i, ref in enumerate(shifts):
        ref[...] = turned[6 + i : 7 + i, :cols]
    row_of = small[pl.ds(8 + pair, 1), :]
    for i in range(up_shift.shape[0]):
        up_shift[i : i + 1, :] = row_of[:, i * 128 : (i + 1) * 128]

    @pl.loop(0, seqs)
    def _(s):
        rows_out(0, s).wait()
        rows_out(1, s).wait()

    for copy in gives:
        copy.wait()


def finish_call(sizes, cols, lo, tg, attn, up, down, small):
    n_dp, n_ctx, n_tp = sizes
    seqs, block, width = lo.shape
    share = attn.shape[0]
    shape = jax.ShapeDtypeStruct
    any_spec = pl.BlockSpec(memory_space=pl.ANY)
    vmem_spec = pl.BlockSpec(memory_space=pltpu.VMEM)
    vm = pltpu.VMEM
    dma = pltpu.SemaphoreType.DMA
    out_tail = [(share, cols)] * 4 + [up.shape] * 2 + [(1, share)] * 6 + [(1, cols)] * 2 + [(up.shape[1] // 128, 128)]
    return pl.pallas_call(
        functools.partial(finish_body, n_ctx, share, cols),
        out_shape=[shape(lo.shape, BF16), shape(lo.shape, F32)] + [shape(s, F32) for s in out_tail],
        in_specs=[any_spec] * 6,
        out_specs=[any_spec] * 8 + [vmem_spec] * 9,
        scratch_shapes=[
            vm(lo.shape, BF16),
            vm(lo.shape, BF16),
            vm(lo.shape, F32),
            vm(attn.shape, F32),
            vm(up.shape, F32),
            vm(down.shape, F32),
            vm(small.shape, F32),
        ]
        + [vm((share, cols), F32)] * 4
        + [dma((2, seqs)), dma((2, seqs)), dma((4,)), dma((6,))],
    )(lo, tg, attn, up, down, small)


def fused_layer(sizes, tokens, out_grad, shards, vectors, column_biases):
    cols = shards[0].shape[1]
    lines = [v.reshape(1, -1) for v in vectors]
    results = fused_call(sizes, tokens, out_grad, shards, lines, column_biases)
    final = finish_call(sizes, cols, *results)
    return (*final[:8], *[v.reshape(-1) for v in final[8:]])


def per_device(
    tokens,
    out_grad,
    query_weight,
    key_weight,
    value_weight,
    output_weight,
    up_weight,
    down_weight,
    norm1_gain,
    norm1_bias,
    output_bias,
    norm2_gain,
    norm2_bias,
    down_bias,
    query_bias,
    value_bias,
    up_bias,
):
    sizes = (lax.axis_size("dp"), lax.axis_size("ctx"), lax.axis_size("tp"))
    n_dp, n_ctx, n_tp = sizes
    n_pair = n_tp // 2
    seqs, block, width = tokens.shape
    assert seqs == n_ctx * n_pair
    share = norm1_gain.shape[0]
    cols = query_bias.shape[0]
    pair = lax.axis_index("tp") // 2
    row = lax.axis_index("dp") * n_ctx + lax.axis_index("ctx")
    shards = (query_weight, key_weight, value_weight, output_weight, up_weight, down_weight)
    vectors = (norm1_gain, norm1_bias, output_bias, norm2_gain, norm2_bias, down_bias)
    if share % 16 == 0 and n_ctx % 4 == 0 and n_ctx & (n_ctx - 1) == 0:
        return fused_layer(
            sizes, tokens, out_grad, shards, vectors, (query_bias, value_bias, up_bias)
        )

    six = jnp.stack(vectors).astype(F32)
    vec = jnp.pad(six, ((0, 2), (0, 128 - share)))
    columns = jnp.arange(width) // cols == pair
    narrow = [jnp.where(columns, jnp.tile(b.astype(F32), width // cols), 0.0) for b in (query_bias, value_bias)]
    bias = jnp.pad(jnp.stack(narrow + [up_bias.astype(F32)]), ((0, 5), (0, 0)))

    gathered = gather_call(sizes, tokens, out_grad, shards, vec, bias)
    tok, og = gathered[0:2]
    weights = [w.reshape(n_pair, width, w.shape[3]) for w in gathered[2:8]]
    vecs = gathered[8][:, :, :share].transpose(1, 0, 2).reshape(8, width)
    results = compute_call(sizes, tok, og, weights, vecs, gathered[9])
    lo, tg = results[0:2]
    grads = [
        g.reshape(n_pair, n_dp * n_ctx, s.shape[0], s.shape[1]) for g, s in zip(results[2:8], shards)
    ]
    final = scatter_call(sizes, seqs, lo, tg, grads, results[8])
    layer_out, tokens_grad = final[0], final[1].astype(F32)
    small = final[8]
    owned = [lax.dynamic_slice_in_dim(small[i], row * share, share) for i in range(6)]
    shifts = [lax.dynamic_slice_in_dim(small[6 + i], pair * cols, cols) for i in range(2)]
    up_total = lax.dynamic_index_in_dim(small[8 : 8 + n_pair], pair, 0, keepdims=False)
    return (layer_out, tokens_grad, *final[2:8], *owned, *shifts, up_total)


def solution(mesh):
    rows_spec = P("dp", "ctx", None)
    weight_spec = P(("dp", "ctx"), "tp")
    vector_spec = P(("dp", "ctx"))
    column_spec = P("tp")
    common = (rows_spec,) * 2 + (weight_spec,) * 6 + (vector_spec,) * 6 + (column_spec,) * 3
    return jax.shard_map(
        per_device, mesh=mesh, in_specs=common, out_specs=common, check_vma=False
    )
```

```python
import functools

import jax
import jax.numpy as jnp
from jax import lax
from jax.experimental import pallas as pl
from jax.experimental.pallas import tpu as pltpu
from jax.sharding import PartitionSpec as P

HEAD_DIM = 64
MESH = pl.DeviceIdType.MESH
F32 = jnp.float32
BF16 = jnp.bfloat16
VMEM_LIMIT = 66 * 1000 * 1000

epsilon = 1e-05
root_half = 0.7071067811865476
density_scale = 0.3989422804014327


def remote(src, dst, send_sem, recv_sem, device):
    return pltpu.make_async_remote_copy(
        src_ref=src,
        dst_ref=dst,
        send_sem=send_sem,
        recv_sem=recv_sem,
        device_id=device,
        device_id_type=MESH,
    )


def nn_dot(left, right):
    return lax.dot_general(left, right, (((1,), (0,)), ((), ())), preferred_element_type=F32)


def nt_dot(left, right):
    return lax.dot_general(left, right, (((1,), (1,)), ((), ())), preferred_element_type=F32)


def tn_dot(left, right):
    return lax.dot_general(left, right, (((0,), (0,)), ((), ())), preferred_element_type=F32)


def normalize(values):
    centred = values - jnp.mean(values, axis=-1, keepdims=True)
    spread = lax.rsqrt(jnp.mean(centred * centred, axis=-1, keepdims=True) + epsilon)
    return centred * spread, spread


def norm_back(grad_scaled, scaled, spread):
    inner = grad_scaled - jnp.mean(grad_scaled, axis=-1, keepdims=True)
    inner = inner - scaled * jnp.mean(grad_scaled * scaled, axis=-1, keepdims=True)
    return inner * spread


class Place:
    def __init__(self, sizes):
        self.n_dp, self.n_ctx, self.n_tp = sizes
        self.n_pair = self.n_tp // 2
        self.dp = lax.axis_index("dp")
        self.ctx = lax.axis_index("ctx")
        self.tp = lax.axis_index("tp")
        self.pair = self.tp // 2
        self.side = self.tp % 2

    def other_dp(self, k):
        d = (self.dp + k) % self.n_dp
        return d, (d, self.ctx, self.tp)

    def other_ctx(self, k):
        z = (self.ctx + k) % self.n_ctx
        return z, (self.dp, z, self.tp)

    def other_pair(self, k):
        p = (self.pair + k) % self.n_pair
        return p, (self.dp, self.ctx, 2 * p + self.side)

    def partner(self):
        return (self.dp, self.ctx, 2 * self.pair + 1 - self.side)

    def barrier(self, far):
        sem = pltpu.get_barrier_semaphore()
        count = 1
        pl.semaphore_signal(sem, inc=1, device_id=self.partner(), device_id_type=MESH)
        if far:
            for size, other in (
                (self.n_dp, self.other_dp),
                (self.n_ctx, self.other_ctx),
                (self.n_pair, self.other_pair),
            ):
                for k in range(1, size):
                    pl.semaphore_signal(sem, inc=1, device_id=other(k)[1], device_id_type=MESH)
                    count += 1
        pl.semaphore_wait(sem, count)


class Sends:
    def __init__(self, sems):
        self.sems = sems
        self.started = []

    def go(self, src, dst, recv_sem, device):
        copy = remote(src, dst, self.sems.at[len(self.started)], recv_sem, device)
        copy.start()
        self.started.append(copy)

    def finish(self):
        for copy in self.started:
            copy.wait_send()


def gather_body(sizes, half, *refs):
    here = Place(sizes)
    n_dp, n_ctx, n_pair = here.n_dp, here.n_ctx, here.n_pair
    d, z, p, c = here.dp, here.ctx, here.pair, here.side
    tokens, out_grad = refs[0:2]
    shards = refs[2:8]
    vec, bias = refs[8:10]
    tok_own, og_own = refs[10:12]
    full = refs[12:18]
    vec_all, bias_all = refs[18:20]
    own_sem, send_sem, rows_sem, line_sem, group_sem, vline_sem, vgroup_sem, bias_sem = refs[20:28]
    own_row = d * n_ctx + z
    mine = p * n_ctx + z
    rows = pl.ds(pl.multiple_of(c * half, half), half)

    here.barrier(True)
    sends = Sends(send_sem)
    own = [
        pltpu.make_async_copy(tokens.at[mine, rows], tok_own.at[z], own_sem.at[0]),
        pltpu.make_async_copy(out_grad.at[mine, rows], og_own.at[z], own_sem.at[1]),
        pltpu.make_async_copy(vec, vec_all.at[own_row], own_sem.at[2]),
        pltpu.make_async_copy(bias, bias_all.at[p], own_sem.at[3]),
    ]
    for a in range(6):
        own.append(pltpu.make_async_copy(shards[a], full[a].at[p, own_row], own_sem.at[4 + a]))
    for copy in own:
        copy.start()

    def send_rows(index, source, target):
        for k in range(1, n_ctx):
            zz, device = here.other_ctx(k)
            sends.go(
                source.at[p * n_ctx + zz, rows], target.at[z], rows_sem.at[index, z], device
            )

    def send_line(a):
        for k in range(1, n_ctx):
            zz, device = here.other_ctx(k)
            sends.go(shards[a], full[a].at[p, own_row], line_sem.at[a, z], device)

    send_rows(0, tokens, tok_own)
    for k in range(1, n_ctx):
        zz, device = here.other_ctx(k)
        sends.go(vec, vec_all.at[own_row], vline_sem.at[z], device)
    for k in range(1, n_pair):
        pp, device = here.other_pair(k)
        sends.go(bias, bias_all.at[p], bias_sem.at[p], device)
    for a in range(6):
        send_line(a)
    send_rows(1, out_grad, og_own)

    for copy in own:
        copy.wait()

    def group(a, pp, dd):
        return full[a].at[pp, pl.ds(dd * n_ctx, n_ctx)]

    def wait_line(a):
        for k in range(1, n_ctx):
            zz, device = here.other_ctx(k)
            slot = full[a].at[p, d * n_ctx + zz]
            remote(slot, slot, send_sem.at[0], line_sem.at[a, zz], device).wait_recv()

    def send_pair(a, dd):
        for k in range(1, n_pair):
            pp, device = here.other_pair(k)
            sends.go(group(a, p, dd), group(a, p, dd), group_sem.at[a, p, dd], device)

    def send_dp(a, pp):
        for k in range(1, n_dp):
            dd, device = here.other_dp(k)
            sends.go(group(a, pp, d), group(a, pp, d), group_sem.at[a, pp, d], device)

    def wait_group(a, pp, dd):
        slot = group(a, pp, dd)
        remote(slot, slot, send_sem.at[0], group_sem.at[a, pp, dd], here.partner()).wait_recv()

    for a in range(6):
        wait_line(a)
        send_dp(a, p)
        send_pair(a, d)
    for k in range(1, n_ctx):
        zz, device = here.other_ctx(k)
        slot = vec_all.at[d * n_ctx + zz]
        remote(slot, slot, send_sem.at[0], vline_sem.at[zz], device).wait_recv()
    for k in range(1, n_dp):
        dd, device = here.other_dp(k)
        slot = vec_all.at[pl.ds(d * n_ctx, n_ctx)]
        sends.go(slot, slot, vgroup_sem.at[d], device)
    pair_first = (True, True, True, True, False, True)
    for a in range(6):
        if pair_first[a]:
            for k in range(1, n_pair):
                pp = here.other_pair(k)[0]
                wait_group(a, pp, d)
                send_dp(a, pp)
        else:
            for k in range(1, n_dp):
                dd = here.other_dp(k)[0]
                wait_group(a, p, dd)
                send_pair(a, dd)
    for a in range(6):
        for k in range(1, n_dp):
            dd = here.other_dp(k)[0]
            if pair_first[a]:
                wait_group(a, p, dd)
            for j in range(1, n_pair):
                wait_group(a, here.other_pair(j)[0], dd)
        if not pair_first[a]:
            for j in range(1, n_pair):
                wait_group(a, here.other_pair(j)[0], d)
    for k in range(1, n_dp):
        dd, device = here.other_dp(k)
        slot = vec_all.at[pl.ds(dd * n_ctx, n_ctx)]
        remote(slot, slot, send_sem.at[0], vgroup_sem.at[dd], device).wait_recv()
    for k in range(1, n_pair):
        pp, device = here.other_pair(k)
        slot = bias_all.at[pp]
        remote(slot, slot, send_sem.at[0], bias_sem.at[pp], device).wait_recv()
    for index, target in ((0, tok_own), (1, og_own)):
        for k in range(1, n_ctx):
            zz, device = here.other_ctx(k)
            slot = target.at[zz]
            remote(slot, slot, send_sem.at[0], rows_sem.at[index, zz], device).wait_recv()
    sends.finish()


def gather_call(sizes, tokens, out_grad, shards, vec, bias):
    n_dp, n_ctx, n_tp = sizes
    n_pair = n_tp // 2
    seqs, block, width = tokens.shape
    half = block // 2
    any_spec = pl.BlockSpec(memory_space=pl.ANY)
    vmem_spec = pl.BlockSpec(memory_space=pltpu.VMEM)
    own = jax.ShapeDtypeStruct((n_ctx, half, width), BF16)
    out_shape = [own, own]
    out_shape += [jax.ShapeDtypeStruct((n_pair, n_dp * n_ctx) + s.shape, BF16) for s in shards]
    out_shape += [
        jax.ShapeDtypeStruct((n_dp * n_ctx,) + vec.shape, F32),
        jax.ShapeDtypeStruct((n_pair,) + bias.shape, F32),
    ]
    n_sends = (
        2 * (n_ctx - 1)
        + (n_ctx - 1)
        + (n_pair - 1)
        + 6 * (n_ctx - 1)
        + (n_dp - 1)
        + 6 * ((n_dp - 1) + (n_pair - 1) + (n_dp - 1) * (n_pair - 1))
    )
    dma = pltpu.SemaphoreType.DMA
    return pl.pallas_call(
        functools.partial(gather_body, sizes, half),
        out_shape=out_shape,
        in_specs=[any_spec] * 10,
        out_specs=[vmem_spec] * 10,
        scratch_shapes=[
            dma((10,)),
            dma((n_sends,)),
            dma((2, n_ctx)),
            dma((6, n_ctx)),
            dma((6, n_pair, n_dp)),
            dma((n_ctx,)),
            dma((n_dp,)),
            dma((n_pair,)),
        ],
        compiler_params=pltpu.CompilerParams(
            collective_id=0, has_side_effects=True, vmem_limit_bytes=VMEM_LIMIT
        ),
    )(tokens, out_grad, *shards, vec, bias)


def compute_body(sizes, *refs):
    here = Place(sizes)
    n_ctx, n_pair = here.n_ctx, here.n_pair
    c = here.side
    (tok, og, gq, gk, gv, go, gu, gd, vecs, bias) = refs[:10]
    (lo, tg, dwq, dwk, dwv, dwo, dwu, dwd, small) = refs[10:19]
    (
        xn1, wqkv, wo, qs, ks, vs, o32, mixed, hid, xn2, ogf, act, ug, bg, dm,
        dka, dva, dqkv, tra, trb, part, ssend, srecv, p_first, send_sem, recv_sem,
    ) = refs[19 : 19 + 23] + (refs[42 : 42 + n_ctx],) + refs[42 + n_ctx :]
    half, width = tok.shape[1], tok.shape[2]
    block = 2 * half
    cols = gq.shape[2]
    hw = n_pair * cols
    fw = gu.shape[2]
    lanes = 2 * HEAD_DIM
    n_twos = hw // lanes
    partner = here.partner()
    scale = HEAD_DIM ** -0.5
    first_head = lax.broadcasted_iota(jnp.int32, (1, lanes), 1) < HEAD_DIM
    zero16 = jnp.zeros((), BF16)

    def own_rows(b):
        return pl.ds(pl.multiple_of(b * block + c * half, half), half)

    def far_rows(b):
        return pl.ds(pl.multiple_of(b * block + (1 - c) * half, half), half)

    def block_rows(b):
        return pl.ds(pl.multiple_of(b * block, block), block)

    def exchange(stage, b, src, dst):
        return remote(src, dst, send_sem.at[stage, b], recv_sem.at[stage, b], partner)

    def rows_copy(stage, b, ref):
        return exchange(stage, b, ref.at[own_rows(b)], ref.at[own_rows(b)])

    def rows_arrive(stage, b, ref):
        exchange(stage, b, ref.at[far_rows(b)], ref.at[far_rows(b)]).wait_recv()

    def part_copy(stage, slot, b):
        return exchange(stage, b, ssend.at[slot, b], srecv.at[slot, b])

    here.barrier(False)

    gain_one, shift_one, out_shift = vecs[0:1, :], vecs[1:2, :], vecs[2:3, :]
    gain_two, shift_two, down_shift = vecs[3:4, :], vecs[4:5, :], vecs[5:6, :]

    @pl.loop(0, n_ctx)
    def _(b):
        exchange(0, b, og.at[b], ogf.at[own_rows(b)]).start()
        ogf[own_rows(b), :] = og[b]
        scaled, _ = normalize(tok[b].astype(F32))
        xn1[own_rows(b), :] = (scaled * gain_one + shift_one).astype(BF16)
        rows_copy(1, b, xn1).start()

    for i in range(n_pair):
        at = slice(i * cols, (i + 1) * cols)
        wqkv[:, i * cols : (i + 1) * cols] = gq[i]
        wqkv[:, hw + i * cols : hw + (i + 1) * cols] = gk[i]
        wqkv[:, 2 * hw + i * cols : 2 * hw + (i + 1) * cols] = gv[i]
        wo[:, at] = go[i]
    q_shift = bias[0, 0:1, :hw]
    v_shift = bias[0, 1:2, :hw]
    for i in range(1, n_pair):
        q_shift = q_shift + bias[i, 0:1, :hw]
        v_shift = v_shift + bias[i, 1:2, :hw]

    @pl.loop(0, n_ctx)
    def _(b):
        rows_arrive(1, b, xn1)
        product = nn_dot(xn1[block_rows(b), :], wqkv[...])
        qs[block_rows(b), :] = (product[:, :hw] + q_shift).astype(BF16) * jnp.asarray(scale, BF16)
        ks[block_rows(b), :] = product[:, hw : 2 * hw].astype(BF16)
        vs[block_rows(b), :] = (product[:, 2 * hw :] + v_shift).astype(BF16)

    for b in range(n_ctx):
        reach = (b + 1) * block
        here_rows = slice(b * block, (b + 1) * block)

        @pl.loop(0, n_twos)
        def _(j):
            at = pl.ds(pl.multiple_of(j * lanes, lanes), lanes)
            queries, keys, values = qs[here_rows, at], ks[:reach, at], vs[:reach, at]
            pieces = []
            for e in range(2):
                head = first_head if e == 0 else jnp.logical_not(first_head)
                scores = nt_dot(jnp.where(head, queries, zero16), keys)
                powers = jnp.exp(scores - jnp.max(scores, axis=-1, keepdims=True))
                inverse = 1.0 / jnp.sum(powers, axis=-1, keepdims=True)
                probs = (powers * inverse).astype(BF16)
                p_first[b][2 * j + e] = probs
                pieces.append(nn_dot(probs, values))
            out = jnp.where(first_head, pieces[0], pieces[1])
            o32[here_rows, at] = out
            mixed[here_rows, at] = out.astype(BF16)

        ssend[0, b] = nt_dot(mixed[far_rows(b), :], wo[...]).astype(BF16)
        part_copy(2, 0, b).start()
        hid[b] = nt_dot(mixed[own_rows(b), :], wo[...])

    @pl.loop(0, n_ctx)
    def _(b):
        part_copy(2, 0, b).wait()
        hidden = tok[b].astype(F32) + (hid[b] + srecv[0, b].astype(F32)) + out_shift
        hid[b] = hidden
        scaled, _ = normalize(hidden)
        xn2[own_rows(b), :] = (scaled * gain_two + shift_two).astype(BF16)
        rows_copy(3, b, xn2).start()

    small[...] = jnp.zeros_like(small)

    @pl.loop(0, n_ctx)
    def _(b):
        rows_arrive(0, b, ogf)
        rows_arrive(3, b, xn2)
        normed = xn2[block_rows(b), :]
        grads = ogf[block_rows(b), :]
        for i in range(n_pair):
            upward = nn_dot(normed, gu[i]) + bias[i, 2:3, :]
            big_phi = 0.5 + 0.5 * lax.erf(upward * root_half)
            act[i, block_rows(b), :] = (upward * big_phi).astype(BF16)
            slope = big_phi + upward * density_scale * jnp.exp(-0.5 * upward * upward)
            rows_grad = (nn_dot(grads, gd[i]) * slope).astype(BF16)
            ug[i, block_rows(b), :] = rows_grad
            small[8 + i : 9 + i, :] += jnp.sum(rows_grad.astype(F32), axis=0, keepdims=True)

        def through(ref, weight, rows):
            total = nt_dot(ref[0, rows, :], weight[0])
            for i in range(1, n_pair):
                total = total + nt_dot(ref[i, rows, :], weight[i])
            return total

        ssend[1, b] = through(act, gd, far_rows(b)).astype(BF16)
        part_copy(4, 1, b).start()
        ssend[0, b] = through(ug, gu, far_rows(b)).astype(BF16)
        part_copy(5, 0, b).start()
        part[0, b] = through(act, gd, own_rows(b))
        part[1, b] = through(ug, gu, own_rows(b))

    def transposed(ref, out):
        for b in range(n_ctx):
            out[:, b * block : (b + 1) * block] = ref[b * block : (b + 1) * block, :].T

    @pl.loop(0, n_ctx)
    def _(b):
        part_copy(4, 1, b).wait()
        lo[b] = (hid[b] + (part[0, b] + srecv[1, b].astype(F32)) + down_shift).astype(BF16)
        part_copy(5, 0, b).wait()
        grad_two = part[1, b] + srecv[0, b].astype(F32)
        scaled, spread = normalize(hid[b])
        own_grad = og[b].astype(F32)
        hidden_grad = own_grad + norm_back(grad_two * gain_two, scaled, spread)
        hid[b] = hidden_grad
        branch = hidden_grad.astype(BF16)
        bg[own_rows(b), :] = branch
        rows_copy(6, b, bg).start()
        small[2:3, :] += jnp.sum(branch.astype(F32), axis=0, keepdims=True)
        small[3:4, :] += jnp.sum(grad_two * scaled, axis=0, keepdims=True)
        small[4:5, :] += jnp.sum(grad_two, axis=0, keepdims=True)
        small[5:6, :] += jnp.sum(own_grad, axis=0, keepdims=True)

    transposed(xn2, tra)
    transposed(ogf, trb)
    step = 256

    @pl.loop(0, width // step)
    def _(r):
        rows = pl.ds(pl.multiple_of(r * step, step), step)
        for i in range(n_pair):
            dwu[i, rows, :] = nn_dot(tra[rows, :], ug[i]).astype(BF16)
            dwd[i, rows, :] = nn_dot(trb[rows, :], act[i]).astype(BF16)

    @pl.loop(0, n_ctx)
    def _(b):
        rows_arrive(6, b, bg)
        dm[block_rows(b), :] = nn_dot(bg[block_rows(b), :], wo[...]).astype(BF16)

    transposed(bg, trb)

    @pl.loop(0, width // step)
    def _(r):
        rows = pl.ds(pl.multiple_of(r * step, step), step)
        product = nn_dot(trb[rows, :], mixed[...])
        for i in range(n_pair):
            dwo[i, rows, :] = product[:, i * cols : (i + 1) * cols].astype(BF16)

    for b in reversed(range(n_ctx)):
        reach = (b + 1) * block
        here_rows = slice(b * block, (b + 1) * block)

        @pl.loop(0, n_twos)
        def _(j):
            at = pl.ds(pl.multiple_of(j * lanes, lanes), lanes)
            queries, keys, values = qs[here_rows, at], ks[:reach, at], vs[:reach, at]
            mix_grad, mix = dm[here_rows, at], o32[here_rows, at]
            towards = mix_grad.astype(F32) * mix
            query_parts, key_sum, value_sum = [], None, None
            for e in range(2):
                head = first_head if e == 0 else jnp.logical_not(first_head)
                grad_head = jnp.where(head, mix_grad, zero16)
                prob_grad = nt_dot(grad_head, values)
                centre = jnp.sum(jnp.where(head, towards, 0.0), axis=-1, keepdims=True)
                probs = p_first[b][2 * j + e]
                score_grad = (probs.astype(F32) * (prob_grad - centre)).astype(BF16)
                query_parts.append(nn_dot(score_grad, keys))
                key_term = tn_dot(score_grad, jnp.where(head, queries, zero16))
                value_term = tn_dot(probs, grad_head)
                key_sum = key_term if key_sum is None else key_sum + key_term
                value_sum = value_term if value_sum is None else value_sum + value_term
            query_grad = jnp.where(first_head, query_parts[0], query_parts[1]) * scale
            dqkv[here_rows, at] = query_grad.astype(BF16)
            if b == n_ctx - 1:
                dka[:, at] = key_sum
                dva[:, at] = value_sum
            else:
                dka[:reach, at] += key_sum
                dva[:reach, at] += value_sum

    @pl.loop(0, n_ctx)
    def _(b):
        dqkv[block_rows(b), hw : 2 * hw] = dka[block_rows(b), :].astype(BF16)
        dqkv[block_rows(b), 2 * hw :] = dva[block_rows(b), :].astype(BF16)
        small[6:7, :hw] += jnp.sum(dqkv[block_rows(b), :hw].astype(F32), axis=0, keepdims=True)
        small[7:8, :hw] += jnp.sum(dqkv[block_rows(b), 2 * hw :].astype(F32), axis=0, keepdims=True)
        ssend[1, b] = nt_dot(dqkv[far_rows(b), :], wqkv[...]).astype(BF16)
        part_copy(7, 1, b).start()
        part[0, b] = nt_dot(dqkv[own_rows(b), :], wqkv[...])

    transposed(xn1, tra)

    @pl.loop(0, width // step)
    def _(r):
        rows = pl.ds(pl.multiple_of(r * step, step), step)
        product = nn_dot(tra[rows, :], dqkv[...])
        for i in range(n_pair):
            dwq[i, rows, :] = product[:, i * cols : (i + 1) * cols].astype(BF16)
            dwk[i, rows, :] = product[:, hw + i * cols : hw + (i + 1) * cols].astype(BF16)
            dwv[i, rows, :] = product[:, 2 * hw + i * cols : 2 * hw + (i + 1) * cols].astype(BF16)

    @pl.loop(0, n_ctx)
    def _(b):
        part_copy(7, 1, b).wait()
        grad_one = part[0, b] + srecv[1, b].astype(F32)
        scaled, spread = normalize(tok[b].astype(F32))
        tg[b] = (hid[b] + norm_back(grad_one * gain_one, scaled, spread)).astype(BF16)
        small[0:1, :] += jnp.sum(grad_one * scaled, axis=0, keepdims=True)
        small[1:2, :] += jnp.sum(grad_one, axis=0, keepdims=True)
        exchange(0, b, og.at[b], ogf.at[own_rows(b)]).wait_send()
        rows_copy(1, b, xn1).wait_send()
        rows_copy(3, b, xn2).wait_send()
        rows_copy(6, b, bg).wait_send()


def compute_call(sizes, tok, og, weights, vecs, bias):
    n_dp, n_ctx, n_tp = sizes
    n_pair = n_tp // 2
    half, width = tok.shape[1:]
    block = 2 * half
    length = n_ctx * block
    cols = weights[0].shape[2]
    hw = n_pair * cols
    fw = weights[4].shape[2]
    heads = hw // HEAD_DIM
    vmem_spec = pl.BlockSpec(memory_space=pltpu.VMEM)
    shape = jax.ShapeDtypeStruct
    out_shape = [
        shape(tok.shape, BF16),
        shape(tok.shape, BF16),
    ]
    out_shape += [shape(w.shape, BF16) for w in weights]
    out_shape += [shape((16, width), F32)]
    vm = pltpu.VMEM
    scratch = [
        vm((length, width), BF16),
        vm((width, 3 * hw), BF16),
        vm((width, hw), BF16),
        vm((length, hw), BF16),
        vm((length, hw), BF16),
        vm((length, hw), BF16),
        vm((length, hw), F32),
        vm((length, hw), BF16),
        vm((n_ctx, half, width), F32),
        vm((length, width), BF16),
        vm((length, width), BF16),
        vm((n_pair, length, fw), BF16),
        vm((n_pair, length, fw), BF16),
        vm((length, width), BF16),
        vm((length, hw), BF16),
        vm((length, hw), F32),
        vm((length, hw), F32),
        vm((length, 3 * hw), BF16),
        vm((width, length), BF16),
        vm((width, length), BF16),
        vm((2, n_ctx, half, width), F32),
        vm((2, n_ctx, half, width), BF16),
        vm((2, n_ctx, half, width), BF16),
    ]
    scratch += [vm((heads, block, (b + 1) * block), BF16) for b in range(n_ctx)]
    scratch += [pltpu.SemaphoreType.DMA((8, n_ctx)), pltpu.SemaphoreType.DMA((8, n_ctx))]
    return pl.pallas_call(
        functools.partial(compute_body, sizes),
        out_shape=out_shape,
        in_specs=[vmem_spec] * 10,
        out_specs=[vmem_spec] * 9,
        scratch_shapes=scratch,
        compiler_params=pltpu.CompilerParams(
            collective_id=1, has_side_effects=True, vmem_limit_bytes=VMEM_LIMIT
        ),
    )(tok, og, *weights, vecs, bias)


def scatter_body(sizes, half, *refs):
    here = Place(sizes)
    n_dp, n_ctx, n_pair = here.n_dp, here.n_ctx, here.n_pair
    d, z, p, c = here.dp, here.ctx, here.pair, here.side
    rows_in = refs[0:2]
    grads = refs[2:8]
    small = refs[8]
    rows_out = refs[9:11]
    owned = refs[11:17]
    small_out = refs[17]
    it = iter(refs[18:])
    dp_land = [next(it) for _ in range(6)]
    dp_sum = [next(it) for _ in range(6)]
    keep = [next(it) for _ in range(6)]
    pair_land = [next(it) for _ in range(6)]
    pair_sum = [next(it) for _ in range(6)]
    ctx_land = [next(it) for _ in range(6)]
    side_land, small_b, ctx_small, small_c, pair_small, small_d, dp_small = [next(it) for _ in range(7)]
    own_sem, send_sem, line_sem, far_sem, side_sem, dp_sem, pair_sem, ctx_sem, small_sem = it
    mine = p * n_ctx + z
    rows = pl.ds(pl.multiple_of(c * half, half), half)

    here.barrier(True)
    sends = Sends(send_sem)

    for a in range(6):
        for k in range(1, n_dp):
            dd, device = here.other_dp(k)
            sends.go(
                grads[a].at[:, pl.ds(dd * n_ctx, n_ctx)],
                dp_land[a].at[k - 1],
                dp_sem.at[a, k - 1],
                device,
            )
    own = []
    for i in range(2):
        for k in range(1, n_ctx):
            zz, device = here.other_ctx(k)
            sends.go(rows_in[i].at[zz], rows_out[i].at[mine, rows], line_sem.at[i, z], device)
        own.append(pltpu.make_async_copy(rows_in[i].at[z], rows_out[i].at[mine, rows], own_sem.at[i]))
        own[-1].start()
    sends.go(small.at[pl.ds(0, 8)], side_land, small_sem.at[0, 0], here.partner())

    def small_arrive(stage, k, land):
        remote(land, land, send_sem.at[0], small_sem.at[stage, k - 1], here.partner()).wait_recv()

    for i in range(2):
        own[i].wait()
        for k in range(1, n_ctx):
            zz, device = here.other_ctx(k)
            slot = rows_out[i].at[p * n_ctx + zz, rows]
            remote(slot, slot, send_sem.at[0], line_sem.at[i, zz], device).wait_recv()
        for k in range(1, n_pair):
            pp, device = here.other_pair(k)
            slot = rows_out[i].at[pl.ds(p * n_ctx, n_ctx), rows]
            sends.go(slot, slot, far_sem.at[i, p], device)

    small_arrive(0, 1, side_land)
    small_b[0:8, :] = small[0:8, :] + side_land[...]
    small_b[8:16, :] = small[8:16, :]
    small_b[6:8, :] = small[6:8, :]
    for k in range(1, n_ctx):
        zz, device = here.other_ctx(k)
        sends.go(small_b, ctx_small.at[k - 1], small_sem.at[1, k - 1], device)

    for a in range(6):
        for k in range(1, n_dp):
            remote(
                dp_land[a].at[k - 1], dp_land[a].at[k - 1], send_sem.at[0], dp_sem.at[a, k - 1],
                here.partner(),
            ).wait_recv()
        for i in range(n_pair):
            total = grads[a][i, pl.ds(d * n_ctx, n_ctx)].astype(F32)
            for k in range(1, n_dp):
                total = total + dp_land[a][k - 1, i].astype(F32)
            dp_sum[a][i] = total.astype(BF16)
        for k in range(1, n_pair):
            pp, device = here.other_pair(k)
            sends.go(dp_sum[a].at[pp], pair_land[a].at[k - 1], pair_sem.at[a, k - 1], device)

    total = small_b[...]
    for k in range(1, n_ctx):
        small_arrive(1, k, ctx_small.at[k - 1])
        total = total + ctx_small[k - 1]
    small_c[...] = total
    for k in range(1, n_pair):
        pp, device = here.other_pair(k)
        sends.go(small_c, pair_small.at[k - 1], small_sem.at[2, k - 1], device)

    for a in range(6):
        for k in range(1, n_pair):
            remote(
                pair_land[a].at[k - 1], pair_land[a].at[k - 1], send_sem.at[0], pair_sem.at[a, k - 1],
                here.partner(),
            ).wait_recv()
        total = dp_sum[a][p].astype(F32)
        for k in range(1, n_pair):
            total = total + pair_land[a][k - 1].astype(F32)
        keep[a][...] = total
        pair_sum[a][...] = total.astype(BF16)
        for k in range(1, n_ctx):
            zz, device = here.other_ctx(k)
            sends.go(pair_sum[a].at[zz], ctx_land[a].at[k - 1], ctx_sem.at[a, k - 1], device)

    total = small_c[...]
    for k in range(1, n_pair):
        small_arrive(2, k, pair_small.at[k - 1])
        total = total + pair_small[k - 1]
    small_d[...] = total
    for k in range(1, n_dp):
        dd, device = here.other_dp(k)
        sends.go(small_d, dp_small.at[k - 1], small_sem.at[3, k - 1], device)

    for i in range(2):
        for k in range(1, n_pair):
            pp, device = here.other_pair(k)
            slot = rows_out[i].at[pl.ds(pp * n_ctx, n_ctx), rows]
            remote(slot, slot, send_sem.at[0], far_sem.at[i, pp], device).wait_recv()
        slot = rows_out[i].at[:, rows]
        sends.go(slot, slot, side_sem.at[i], here.partner())

    for a in range(6):
        total = keep[a][z]
        for k in range(1, n_ctx):
            remote(
                ctx_land[a].at[k - 1], ctx_land[a].at[k - 1], send_sem.at[0], ctx_sem.at[a, k - 1],
                here.partner(),
            ).wait_recv()
            total = total + ctx_land[a][k - 1].astype(F32)
        owned[a][...] = total

    total = small_d[...]
    for k in range(1, n_dp):
        small_arrive(3, k, dp_small.at[k - 1])
        total = total + dp_small[k - 1]
    small_out[...] = total
    other = pl.ds(pl.multiple_of((1 - c) * half, half), half)
    for i in range(2):
        slot = rows_out[i].at[:, other]
        remote(slot, slot, send_sem.at[0], side_sem.at[i], here.partner()).wait_recv()
    sends.finish()


def scatter_call(sizes, seqs, lo, tg, grads, small):
    n_dp, n_ctx, n_tp = sizes
    n_pair = n_tp // 2
    half, width = lo.shape[1:]
    vmem_spec = pl.BlockSpec(memory_space=pltpu.VMEM)
    shape = jax.ShapeDtypeStruct
    vm = pltpu.VMEM
    tail = [g.shape[2:] for g in grads]
    out_shape = [shape((seqs, 2 * half, width), BF16)] * 2
    out_shape += [shape(t, F32) for t in tail]
    out_shape += [shape(small.shape, F32)]
    scratch = [vm((n_dp - 1, n_pair, n_ctx) + t, BF16) for t in tail]
    scratch += [vm((n_pair, n_ctx) + t, BF16) for t in tail]
    scratch += [vm((n_ctx,) + t, F32) for t in tail]
    scratch += [vm((n_pair - 1, n_ctx) + t, BF16) for t in tail]
    scratch += [vm((n_ctx,) + t, BF16) for t in tail]
    scratch += [vm((n_ctx - 1,) + t, BF16) for t in tail]
    scratch += [
        vm((8, width), F32),
        vm((16, width), F32),
        vm((n_ctx - 1, 16, width), F32),
        vm((16, width), F32),
        vm((n_pair - 1, 16, width), F32),
        vm((16, width), F32),
        vm((n_dp - 1, 16, width), F32),
    ]
    n_sends = (
        6 * ((n_dp - 1) + (n_pair - 1) + (n_ctx - 1))
        + 2 * ((n_ctx - 1) + (n_pair - 1) + 1)
        + 1 + (n_ctx - 1) + (n_pair - 1) + (n_dp - 1)
    )
    dma = pltpu.SemaphoreType.DMA
    most = max(n_dp, n_ctx, n_pair)
    scratch += [
        dma((2,)),
        dma((n_sends,)),
        dma((2, n_ctx)),
        dma((2, n_pair)),
        dma((2,)),
        dma((6, n_dp - 1)),
        dma((6, n_pair - 1)),
        dma((6, n_ctx - 1)),
        dma((4, most)),
    ]
    return pl.pallas_call(
        functools.partial(scatter_body, sizes, half),
        out_shape=out_shape,
        in_specs=[vmem_spec] * 9,
        out_specs=[vmem_spec] * 9,
        scratch_shapes=scratch,
        compiler_params=pltpu.CompilerParams(
            collective_id=2, has_side_effects=True, vmem_limit_bytes=VMEM_LIMIT
        ),
    )(lo, tg, *grads, small)


def fused_body(sizes, dims, *refs):
    here = Place(sizes)
    n_dp, n_ctx, n_pair = here.n_dp, here.n_ctx, here.n_pair
    d, z, p, c = here.dp, here.ctx, here.pair, here.side
    half, width, share, cols, fw = dims
    block = 2 * half
    hw = n_pair * cols
    lanes = 2 * HEAD_DIM
    n_twos = hw // lanes
    n_rows = n_dp * n_ctx
    two = n_ctx // 2
    it = iter(refs)

    def take(n):
        return [next(it) for _ in range(n)]

    tokens, out_grad = take(2)
    narrow_shards = take(4)
    shards = [None] + take(2)
    vectors, column_biases = take(6), take(3)
    rows_out = take(2)
    owned_out = take(3)
    small_out = next(it)
    full = take(3)
    pack_all, vecs, cold = take(3)
    tok, og, lo, tg = take(4)
    (
        xn1, wqkv, wo, qs, ks, vs, o32, mixed, hid, xn2, ogf, act, ug, bg, dm, dqkv, tra, trb,
        wide, whole, ssend, srecv, dwd, small,
    ) = take(24)
    p_first = take(n_ctx)
    first_land, second_land, ctx_land = take(3), take(3), take(3)
    side_land, small_b, ctx_small, small_c, pair_small, small_d, dp_small = take(7)
    owned = take(3)
    small_e = next(it)
    (
        own_sem, put_sem, rows_sem, line_sem, pair_sem, dp_sem, diag_dp_sem, diag_pair_sem, swap_send,
        swap_recv, first_sem, second_sem, ctx_sem, out_line, out_pair, out_side, small_sem,
        side_sem, cross_pair, cross_dp,
    ) = take(20)
    partner = here.partner()
    own_row = d * n_ctx + z
    mine = p * n_ctx + z
    scale = HEAD_DIM ** -0.5
    first_head = lax.broadcasted_iota(jnp.int32, (1, lanes), 1) < HEAD_DIM
    zero16 = jnp.zeros((), BF16)
    side_rows = pl.ds(pl.multiple_of(c * half, half), half)
    far_side = pl.ds(pl.multiple_of((1 - c) * half, half), half)
    sends = Sends(put_sem)

    def arrive(slot, sem):
        remote(slot, slot, put_sem.at[0], sem, partner).wait_recv()

    def far_first():
        upper = z // two
        order = []
        for i in range(n_ctx - 1):
            down = n_ctx - 1 - i
            down = down - (z - down + n_ctx) // n_ctx
            up = i + (i - z + n_ctx) // n_ctx
            zz = upper * up + (1 - upper) * down
            order.append((zz, (d, zz, here.tp)))
        return order

    line_order = far_first()

    def flipped(h):
        zz = z + h - 2 * h * ((z // h) % 2)
        return zz, (d, zz, here.tp)

    strides = [1 << i for i in range(n_ctx.bit_length() - 1)]

    def shard_rows(r, count=1):
        return pl.ds(pl.multiple_of(r * share, 16), count * share)

    def slot(a, pp, dd, zz, count=1):
        return full[a].at[pp, shard_rows(dd * n_ctx + zz, count)]

    gather_own = [None] + [
        pltpu.make_async_copy(shards[a], slot(a, p, d, z), own_sem.at[a]) for a in (1, 2)
    ]

    def gather_give(a, h):
        device = flipped(h)[1]
        for i in range(n_ctx // (2 * h)):
            zz = (z + 2 * h * i) % n_ctx
            source = shards[a] if a > 0 and i == 0 else slot(a, p, d, zz)
            sends.go(source, slot(a, p, d, zz), line_sem.at[a, zz], device)

    def gather_take(a, h):
        q = flipped(h)[0]
        for i in range(n_ctx // (2 * h)):
            zz = (q + 2 * h * i) % n_ctx
            arrive(slot(a, p, d, zz), line_sem.at[a, zz])

    def gather_cross(a, first):
        for i in range(n_ctx // 2):
            zz = (first + 2 * i) % n_ctx
            piece = slot(a, p, d, zz)
            for k in range(1, n_pair):
                sends.go(piece, piece, cross_pair.at[a, p, zz], here.other_pair(k)[1])
            for k in range(1, n_dp):
                sends.go(piece, piece, cross_dp.at[a, d, zz], here.other_dp(k)[1])

    def gather_start(a):
        gather_give(a, strides[-1])

    def gather_next(a):
        for h in reversed(strides[:-1]):
            gather_take(a, 2 * h)
            gather_give(a, h)
        if a > 0:
            gather_own[a].wait()
        gather_cross(a, z)

    def gather_hop(a):
        gather_take(a, 1)
        gather_cross(a, flipped(1)[0])

    def gather_turn(a):
        for k in range(1, n_pair):
            pp = here.other_pair(k)[0]
            for zz in range(n_ctx):
                arrive(slot(a, pp, d, zz), cross_pair.at[a, pp, zz])
            first = slot(a, pp, d, 0, two)
            for j in range(1, n_dp):
                sends.go(first, first, diag_dp_sem.at[a, pp, d], here.other_dp(j)[1])
        for k in range(1, n_dp):
            dd = here.other_dp(k)[0]
            for zz in range(n_ctx):
                arrive(slot(a, p, dd, zz), cross_dp.at[a, dd, zz])
            second = slot(a, p, dd, two, n_ctx - two)
            for j in range(1, n_pair):
                sends.go(second, second, diag_pair_sem.at[a, p, dd], here.other_pair(j)[1])

    def gather_end(a):
        for k in range(1, n_pair):
            pp = here.other_pair(k)[0]
            for j in range(1, n_dp):
                dd = here.other_dp(j)[0]
                arrive(slot(a, pp, dd, 0, two), diag_dp_sem.at[a, pp, dd])
                arrive(slot(a, pp, dd, two, n_ctx - two), diag_pair_sem.at[a, pp, dd])

    def pack_start():
        own = pack_all.at[p, own_row]
        for zz, device in line_order:
            sends.go(own, own, line_sem.at[3, z], device)

    def pack_hop():
        for k in range(1, n_ctx):
            zz = here.other_ctx(k)[0]
            arrive(pack_all.at[p, d * n_ctx + zz], line_sem.at[3, zz])
        group = pack_all.at[p, pl.ds(d * n_ctx, n_ctx)]
        for k in range(1, n_pair):
            sends.go(group, group, pair_sem.at[3, p], here.other_pair(k)[1])
        for k in range(1, n_dp):
            sends.go(group, group, dp_sem.at[3, d], here.other_dp(k)[1])

    def pack_end():
        for k in range(1, n_pair):
            pp = here.other_pair(k)[0]
            arrive(pack_all.at[pp, pl.ds(d * n_ctx, n_ctx)], pair_sem.at[3, pp])
        for k in range(1, n_dp):
            dd = here.other_dp(k)[0]
            arrive(pack_all.at[p, pl.ds(dd * n_ctx, n_ctx)], dp_sem.at[3, dd])

    rows_own = [
        pltpu.make_async_copy(source.at[mine, side_rows], target.at[z], own_sem.at[4 + i])
        for i, (source, target) in enumerate(((tokens, tok), (out_grad, og)))
    ]

    def rows_start(i, source, target):
        for zz, device in line_order:
            sends.go(source.at[p * n_ctx + zz, side_rows], target.at[z], rows_sem.at[i, z], device)

    def grad_slot(ref, pp, dd, k):
        return ref.at[pp, shard_rows(dd * n_ctx + (z + k) % n_ctx)]

    def pair_leads(a, k):
        return a > 0 and near.index(k) % 2 == 0

    def scatter_start(a, ref, ks):
        for k in ks:
            if pair_leads(a, k):
                for j in range(1, n_pair):
                    pp, device = here.other_pair(j)
                    for i in range(n_dp):
                        sends.go(grad_slot(ref, pp, i, k), first_land[a].at[j - 1, i, k], first_sem.at[a, j - 1, i, k], device)
            else:
                for j in range(1, n_dp):
                    dd, device = here.other_dp(j)
                    for i in range(n_pair):
                        sends.go(grad_slot(ref, i, dd, k), first_land[a].at[j - 1, i, k], first_sem.at[a, j - 1, i, k], device)

    def add_into(target, parts):
        total = target[...].astype(F32)
        for part in parts:
            total = total + part[...].astype(F32)
        target[...] = total.astype(BF16)

    def scatter_turn(a, ref, ks):
        for k in ks:
            leads = pair_leads(a, k)
            n_lead, n_next = (n_pair, n_dp) if leads else (n_dp, n_pair)
            for i in range(n_next):
                parts = [first_land[a].at[j - 1, i, k] for j in range(1, n_lead)]
                for j in range(1, n_lead):
                    arrive(parts[j - 1], first_sem.at[a, j - 1, i, k])
                target = grad_slot(ref, p, i, k) if leads else grad_slot(ref, i, d, k)
                add_into(target, parts)
            for j in range(1, n_next):
                other, device = here.other_dp(j) if leads else here.other_pair(j)
                source = grad_slot(ref, p, other, k) if leads else grad_slot(ref, other, d, k)
                sends.go(source, second_land[a].at[j - 1, k], second_sem.at[a, j - 1, k], device)

    def scatter_line(a, ref, ks):
        for k in ks:
            n_next = n_dp if pair_leads(a, k) else n_pair
            parts = [second_land[a].at[j - 1, k] for j in range(1, n_next)]
            for j in range(1, n_next):
                arrive(parts[j - 1], second_sem.at[a, j - 1, k])
            add_into(grad_slot(ref, p, d, k), parts)
            if k % 2 == 1:
                scatter_give(a, ref, 1, k)

    def scatter_give(a, ref, h, k):
        zz, device = flipped(h)
        at = n_ctx - n_ctx // h + ((z + k - zz + n_ctx) % n_ctx) // (2 * h)
        sends.go(grad_slot(ref, p, d, k), ctx_land[a].at[at], ctx_sem.at[a, at], device)

    def scatter_across(a, ref):
        for h in strides[1:]:
            for i in range(n_ctx // h):
                at = n_ctx - 2 * n_ctx // h + i
                arrive(ctx_land[a].at[at], ctx_sem.at[a, at])
                add_into(grad_slot(ref, p, d, i * h), [ctx_land[a].at[at]])
            for k in range(h, n_ctx, 2 * h):
                scatter_give(a, ref, h, k)

    def scatter_end(a, ref):
        last = n_ctx - 2
        arrive(ctx_land[a].at[last], ctx_sem.at[a, last])
        owned[a][...] = ref[p, shard_rows(own_row), :].astype(F32) + ctx_land[a][last].astype(F32)
        pltpu.make_async_copy(owned[a], owned_out[a], own_sem.at[8 + a]).start()

    near = [k for h in strides for k in range(h, n_ctx, 2 * h)] + [0]
    early, late = near[:two], near[two:]
    others = list(range(1, n_ctx))

    def out_slot(i, s, rows):
        return rows_out[i].at[s, rows]

    def out_start(i, source):
        for zz, device in line_order:
            sends.go(source.at[zz], out_slot(i, mine, side_rows), out_line.at[i, z], device)
        copy = pltpu.make_async_copy(source.at[z], out_slot(i, mine, side_rows), own_sem.at[6 + i])
        copy.start()
        return copy

    def out_pass(i, s, source):
        piece = out_slot(i, s, side_rows)
        for j in range(1, n_pair):
            sends.go(source, piece, out_pair.at[i, s], here.other_pair(j)[1])
        sends.go(source, piece, out_side.at[i, s], partner)

    def out_hop(i, ks):
        for k in ks:
            s = p * n_ctx + here.other_ctx(k)[0]
            piece = out_slot(i, s, side_rows)
            arrive(piece, out_line.at[i, here.other_ctx(k)[0]])
            out_pass(i, s, piece)

    def out_cross(i):
        for j in range(1, n_pair):
            pp = here.other_pair(j)[0]
            for k in range(n_ctx):
                s = pp * n_ctx + (z + k) % n_ctx
                piece = out_slot(i, s, side_rows)
                arrive(piece, out_pair.at[i, s])
                sends.go(piece, piece, out_side.at[i, s], partner)

    def out_end(i):
        for s in range(n_pair * n_ctx):
            arrive(out_slot(i, s, far_side), out_side.at[i, s])

    def own_rows(b):
        return pl.ds(pl.multiple_of(b * block + c * half, half), half)

    def far_rows(b):
        return pl.ds(pl.multiple_of(b * block + (1 - c) * half, half), half)

    def block_rows(b):
        return pl.ds(pl.multiple_of(b * block, block), block)

    def swap(stage, b, src, dst):
        return remote(src, dst, swap_send.at[stage, b], swap_recv.at[stage, b], partner)

    def rows_copy(stage, b, ref):
        return swap(stage, b, ref.at[own_rows(b)], ref.at[own_rows(b)])

    def rows_arrive(stage, b, ref):
        swap(stage, b, ref.at[far_rows(b)], ref.at[far_rows(b)]).wait_recv()

    def part_copy(stage, place, b):
        return swap(stage, b, ssend.at[place, b], srecv.at[place, b])

    def part_store(i, b, value):
        wide[i, pl.ds(pl.multiple_of(b * block, block), half), :] = value[:, :hw]
        wide[i, pl.ds(pl.multiple_of(b * block + half, half), half), :] = value[:, hw:]

    def part_load(i, b):
        left = wide[i, pl.ds(pl.multiple_of(b * block, block), half), :]
        right = wide[i, pl.ds(pl.multiple_of(b * block + half, half), half), :]
        return jnp.concatenate([left, right], axis=1)

    rows_own[0].start()
    rows_own[1].start()
    gather_own[1].start()
    gather_own[2].start()
    for a in range(4):
        full[0][p, shard_rows(own_row), a * cols : (a + 1) * cols] = narrow_shards[a][...]
    own_pack = pack_all.at[p, own_row]
    own_pack[...] = jnp.zeros(own_pack.shape, F32)
    for i in range(6):
        own_pack[i : i + 1, :share] = vectors[i][...].astype(F32)
    row = 6
    for ref in column_biases:
        n = ref.shape[0]
        line = ref[...].astype(F32).reshape(1, n)
        for w in range(0, n, 128):
            m = min(128, n - w)
            own_pack[row : row + 1, :m] = line[:, w : w + m]
            row += 1
    small[...] = jnp.zeros_like(small)
    here.barrier(True)
    pack_start()
    gather_start(0)
    gather_next(0)
    gather_start(1)
    pack_hop()
    pack_end()
    for r in range(n_rows):
        own_part = pack_all[p, r]
        vecs[0:8, r * share : (r + 1) * share] = own_part[0:8, :share]
    for i in range(n_pair):
        piece = pack_all[i, d * n_ctx]
        for line in range(2):
            for w in range(0, cols, 128):
                n = min(128, cols - w)
                row = 6 + 2 * line + w // 128
                cold[line : line + 1, i * cols + w : i * cols + w + n] = piece[row : row + 1, :n]
        for w in range(0, fw, 128):
            row = 10 + w // 128
            cold[2 + i : 3 + i, w : w + 128] = piece[row : row + 1, :]
    gain_one, shift_one, out_shift = vecs[0:1, :], vecs[1:2, :], vecs[2:3, :]
    gain_two, shift_two, down_shift = vecs[3:4, :], vecs[4:5, :], vecs[5:6, :]

    def norm_one(b):
        scaled, _ = normalize(tok[b].astype(F32))
        xn1[own_rows(b), :] = (scaled * gain_one + shift_one).astype(BF16)
        rows_copy(1, b, xn1).start()

    rows_own[0].wait()
    norm_one(z)
    gather_hop(0)
    gather_next(1)
    pl.semaphore_signal(side_sem, inc=1, device_id=partner, device_id_type=MESH)
    pl.semaphore_wait(side_sem, 1)
    rows_start(0, tokens, tok)
    gather_start(2)
    gather_turn(0)
    gather_hop(1)
    for k in range(1, n_ctx):
        b = here.other_ctx(k)[0]
        arrive(tok.at[b], rows_sem.at[0, b])
        norm_one(b)
    gather_end(0)
    for i in range(n_pair):
        for a, base in enumerate((0, hw, 2 * hw)):
            wqkv[:, base + i * cols : base + (i + 1) * cols] = full[0][i, :, a * cols : (a + 1) * cols]
        wo[:, i * cols : (i + 1) * cols] = full[0][i, :, 3 * cols : 4 * cols]
    q_shift, v_shift = cold[0:1, :hw], cold[1:2, :hw]

    @pl.loop(0, n_ctx)
    def _(b):
        rows_arrive(1, b, xn1)
        product = nn_dot(xn1[block_rows(b), :], wqkv[...])
        qs[block_rows(b), :] = (product[:, :hw] + q_shift).astype(BF16) * jnp.asarray(scale, BF16)
        ks[block_rows(b), :] = product[:, hw : 2 * hw].astype(BF16)
        vs[block_rows(b), :] = (product[:, 2 * hw :] + v_shift).astype(BF16)

    gather_next(2)

    for b in range(n_ctx):
        reach = (b + 1) * block
        here_rows = slice(b * block, (b + 1) * block)

        @pl.loop(0, n_twos)
        def _(j):
            at = pl.ds(pl.multiple_of(j * lanes, lanes), lanes)
            queries, keys, values = qs[here_rows, at], ks[:reach, at], vs[:reach, at]
            pieces = []
            for e in range(2):
                head = first_head if e == 0 else jnp.logical_not(first_head)
                scores = nt_dot(jnp.where(head, queries, zero16), keys)
                powers = jnp.exp(scores - jnp.max(scores, axis=-1, keepdims=True))
                inverse = 1.0 / jnp.sum(powers, axis=-1, keepdims=True)
                probs = (powers * inverse).astype(BF16)
                p_first[b][2 * j + e] = probs
                pieces.append(nn_dot(probs, values))
            out = jnp.where(first_head, pieces[0], pieces[1])
            o32[here_rows, at] = out
            mixed[here_rows, at] = out.astype(BF16)

        whole[b % 2] = nt_dot(mixed[here_rows, :], wo[...])
        ssend[0, b] = whole[b % 2, far_side, :].astype(BF16)
        part_copy(2, 0, b).start()
        hid[b] = whole[b % 2, side_rows, :]
        if b == 0:
            gather_turn(1)
        if b == 1:
            rows_start(1, out_grad, og)
        if b == 2:
            gather_hop(2)

    @pl.loop(0, n_ctx)
    def _(b):
        part_copy(2, 0, b).wait()
        hidden = tok[b].astype(F32) + (hid[b] + srecv[0, b].astype(F32)) + out_shift
        hid[b] = hidden
        scaled, _ = normalize(hidden)
        xn2[own_rows(b), :] = (scaled * gain_two + shift_two).astype(BF16)
        rows_copy(3, b, xn2).start()

    gather_end(1)

    @pl.loop(0, n_ctx)
    def _(b):
        rows_arrive(3, b, xn2)
        normed = xn2[block_rows(b), :]
        for i in range(n_pair):
            upward = nn_dot(normed, full[1][i]) + cold[2 + i : 3 + i, :fw]
            big_phi = 0.5 + 0.5 * lax.erf(upward * root_half)
            act[i, block_rows(b), :] = (upward * big_phi).astype(BF16)
            slope = big_phi + upward * density_scale * jnp.exp(-0.5 * upward * upward)
            ug[i, block_rows(b), :] = slope.astype(BF16)

    rows_own[1].wait()
    for k in range(n_ctx):
        b = (z + k) % n_ctx
        if k > 0:
            arrive(og.at[b], rows_sem.at[1, b])
        swap(0, b, og.at[b], ogf.at[own_rows(b)]).start()
        ogf[own_rows(b), :] = og[b]
    for b in range(n_ctx):
        rows_arrive(0, b, ogf)

    step = 256

    def transposed(ref, out):
        for b in range(n_ctx):
            out[:, b * block : (b + 1) * block] = ref[b * block : (b + 1) * block, :].T

    gather_turn(2)
    gathered = len(sends.started)
    transposed(ogf, trb)

    @pl.loop(0, width // step)
    def _(r):
        rows = pl.ds(pl.multiple_of(r * step, step), step)
        for i in range(n_pair):
            dwd[i, rows, :] = nn_dot(trb[rows, :], act[i]).astype(BF16)

    scatter_start(2, dwd, near)

    def slope_back(i, b):
        slope = ug[i, block_rows(b), :].astype(F32)
        rows_grad = (nn_dot(ogf[block_rows(b), :], full[2][i]) * slope).astype(BF16)
        ug[i, block_rows(b), :] = rows_grad
        small[pl.ds(8 + i, 1), :] += jnp.sum(rows_grad.astype(F32), axis=0, keepdims=True)

    @pl.loop(0, n_ctx)
    def _(b):
        slope_back(p, b)

    gather_end(2)

    def through(ref, weight, rows):
        total = nt_dot(ref[0, rows, :], weight[0])
        for i in range(1, n_pair):
            total = total + nt_dot(ref[i, rows, :], weight[i])
        return total

    def units_back(b):
        for k in range(1, n_pair):
            slope_back(here.other_pair(k)[0], b)
        whole[0] = through(ug, full[1], block_rows(b))
        ssend[0, b] = whole[0, far_side, :].astype(BF16)
        part_copy(5, 0, b).start()
        part_store(1, b, whole[0, side_rows, :])
        whole[1] = through(act, full[2], block_rows(b))
        ssend[1, b] = whole[1, far_side, :].astype(BF16)
        part_copy(4, 1, b).start()
        part_store(0, b, whole[1, side_rows, :])

    pl.loop(0, two)(units_back)
    scatter_turn(2, dwd, early)
    pl.loop(two, n_ctx)(units_back)
    transposed(xn2, tra)
    scatter_turn(2, dwd, late)
    for copy in sends.started[:gathered]:
        copy.wait_send()

    @pl.loop(0, width // step)
    def _(r):
        rows = pl.ds(pl.multiple_of(r * step, step), step)
        for i in range(n_pair):
            full[1][i, rows, :] = nn_dot(tra[rows, :], ug[i]).astype(BF16)

    scatter_start(1, full[1], near)
    scatter_line(2, dwd, early)

    @pl.loop(0, n_ctx)
    def _(b):
        part_copy(5, 0, b).wait()
        grad_two = part_load(1, b) + srecv[0, b].astype(F32)
        part_copy(4, 1, b).wait()
        lo[b] = (hid[b] + (part_load(0, b) + srecv[1, b].astype(F32)) + down_shift).astype(BF16)
        scaled, spread = normalize(hid[b])
        own_grad = og[b].astype(F32)
        hidden_grad = own_grad + norm_back(grad_two * gain_two, scaled, spread)
        hid[b] = hidden_grad
        branch = hidden_grad.astype(BF16)
        bg[own_rows(b), :] = branch
        rows_copy(6, b, bg).start()
        small[2:3, :] += jnp.sum(branch.astype(F32), axis=0, keepdims=True)
        small[3:4, :] += jnp.sum(grad_two * scaled, axis=0, keepdims=True)
        small[4:5, :] += jnp.sum(grad_two, axis=0, keepdims=True)
        small[5:6, :] += jnp.sum(own_grad, axis=0, keepdims=True)

    lo_copy = out_start(0, lo)
    out_pass(0, mine, lo.at[z])

    @pl.loop(0, n_ctx)
    def _(b):
        rows_arrive(6, b, bg)
        dm[block_rows(b), :] = nn_dot(bg[block_rows(b), :], wo[...]).astype(BF16)

    scatter_line(2, dwd, late)
    transposed(bg, trb)

    @pl.loop(0, width // step)
    def _(r):
        rows = pl.ds(pl.multiple_of(r * step, step), step)
        product = nn_dot(trb[rows, :], mixed[...])
        for i in range(n_pair):
            full[0][i, rows, 3 * cols : 4 * cols] = product[:, i * cols : (i + 1) * cols].astype(BF16)

    for b in reversed(range(n_ctx)):
        reach = (b + 1) * block
        here_rows = slice(b * block, (b + 1) * block)

        @pl.loop(0, n_twos)
        def _(j):
            at = pl.ds(pl.multiple_of(j * lanes, lanes), lanes)
            queries, keys, values = qs[here_rows, at], ks[:reach, at], vs[:reach, at]
            mix_grad, mix = dm[here_rows, at], o32[here_rows, at]
            towards = mix_grad.astype(F32) * mix
            query_parts, key_sum, value_sum = [], None, None
            for e in range(2):
                head = first_head if e == 0 else jnp.logical_not(first_head)
                grad_head = jnp.where(head, mix_grad, zero16)
                prob_grad = nt_dot(grad_head, values)
                centre = jnp.sum(jnp.where(head, towards, 0.0), axis=-1, keepdims=True)
                probs = p_first[b][2 * j + e]
                score_grad = (probs.astype(F32) * (prob_grad - centre)).astype(BF16)
                query_parts.append(nn_dot(score_grad, keys))
                key_term = tn_dot(score_grad, jnp.where(head, queries, zero16))
                value_term = tn_dot(probs, grad_head)
                key_sum = key_term if key_sum is None else key_sum + key_term
                value_sum = value_term if value_sum is None else value_sum + value_term
            query_grad = jnp.where(first_head, query_parts[0], query_parts[1]) * scale
            dqkv[here_rows, at] = query_grad.astype(BF16)
            if b == n_ctx - 1:
                wide[0, :, at] = key_sum
                wide[1, :, at] = value_sum
            else:
                wide[0, :reach, at] += key_sum
                wide[1, :reach, at] += value_sum

        if b == 1:
            scatter_turn(1, full[1], near)
        if b == 0:
            out_hop(0, others)

    @pl.loop(0, n_ctx)
    def _(b):
        dqkv[block_rows(b), hw : 2 * hw] = wide[0, block_rows(b), :].astype(BF16)
        dqkv[block_rows(b), 2 * hw :] = wide[1, block_rows(b), :].astype(BF16)
        small[6:7, :hw] += jnp.sum(dqkv[block_rows(b), :hw].astype(F32), axis=0, keepdims=True)
        small[7:8, :hw] += jnp.sum(dqkv[block_rows(b), 2 * hw :].astype(F32), axis=0, keepdims=True)
        whole[0] = nt_dot(dqkv[block_rows(b), :], wqkv[...])
        ssend[1, b] = whole[0, far_side, :].astype(BF16)
        part_copy(7, 1, b).start()
        part_store(0, b, whole[0, side_rows, :])

    transposed(xn1, tra)

    @pl.loop(0, width // step)
    def _(r):
        rows = pl.ds(pl.multiple_of(r * step, step), step)
        product = nn_dot(tra[rows, :], dqkv[...])
        for i in range(n_pair):
            for a in range(3):
                full[0][i, rows, a * cols : (a + 1) * cols] = product[
                    :, a * hw + i * cols : a * hw + (i + 1) * cols
                ].astype(BF16)

    scatter_start(0, full[0], near)

    @pl.loop(0, n_ctx)
    def _(b):
        part_copy(7, 1, b).wait()
        grad_one = part_load(0, b) + srecv[1, b].astype(F32)
        scaled, spread = normalize(tok[b].astype(F32))
        tg[b] = (hid[b] + norm_back(grad_one * gain_one, scaled, spread)).astype(BF16)
        small[0:1, :] += jnp.sum(grad_one * scaled, axis=0, keepdims=True)
        small[1:2, :] += jnp.sum(grad_one, axis=0, keepdims=True)

    sends.go(small.at[pl.ds(0, 8)], side_land, small_sem.at[0, 0], partner)
    tg_copy = out_start(1, tg)
    out_pass(1, mine, tg.at[z])
    scatter_line(1, full[1], near)
    scatter_across(2, dwd)
    arrive(side_land, small_sem.at[0, 0])
    small_b[0:6, :] = small[0:6, :] + side_land[0:6, :]
    small_b[6:16, :] = small[6:16, :]
    for k in range(1, n_pair):
        sends.go(small_b, pair_small.at[k - 1], small_sem.at[2, k - 1], here.other_pair(k)[1])
    scatter_turn(0, full[0], early)
    out_cross(0)
    out_hop(1, others[:1])
    scatter_line(0, full[0], early)
    scatter_turn(0, full[0], late)
    out_hop(1, others[1:])
    scatter_across(1, full[1])
    total = small_b[...]
    for k in range(1, n_pair):
        arrive(pair_small.at[k - 1], small_sem.at[2, k - 1])
        total = total + pair_small[k - 1]
    small_c[...] = total
    for k in range(1, n_dp):
        sends.go(small_c, dp_small.at[k - 1], small_sem.at[3, k - 1], here.other_dp(k)[1])
    scatter_line(0, full[0], late)
    scatter_across(0, full[0])
    scatter_end(2, dwd)
    scatter_end(1, full[1])
    out_end(0)
    total = small_c[...]
    for k in range(1, n_dp):
        arrive(dp_small.at[k - 1], small_sem.at[3, k - 1])
        total = total + dp_small[k - 1]
    small_d[...] = total
    for k in range(1, n_ctx):
        sends.go(small_d, ctx_small.at[k - 1], small_sem.at[1, k - 1], here.other_ctx(k)[1])
    out_cross(1)
    scatter_end(0, full[0])
    total = small_d[...]
    for k in range(1, n_ctx):
        arrive(ctx_small.at[k - 1], small_sem.at[1, k - 1])
        total = total + ctx_small[k - 1]
    small_e[...] = total
    small_copy = pltpu.make_async_copy(small_e, small_out, own_sem.at[11])
    small_copy.start()
    out_end(1)
    lo_copy.wait()
    tg_copy.wait()
    small_copy.wait()
    for a in range(3):
        pltpu.make_async_copy(owned[a], owned_out[a], own_sem.at[8 + a]).wait()

    @pl.loop(0, n_ctx)
    def _(b):
        swap(0, b, og.at[b], ogf.at[own_rows(b)]).wait_send()
        rows_copy(1, b, xn1).wait_send()
        rows_copy(3, b, xn2).wait_send()
        rows_copy(6, b, bg).wait_send()

    for copy in sends.started[gathered:]:
        copy.wait_send()


def fused_call(sizes, tokens, out_grad, shards, vectors, column_biases):
    n_dp, n_ctx, n_tp = sizes
    n_pair = n_tp // 2
    seqs, block, width = tokens.shape
    half = block // 2
    length = n_ctx * block
    share, cols = shards[0].shape
    fw = shards[4].shape[1]
    widths = [4 * cols, fw, fw]
    hw = n_pair * cols
    heads = hw // HEAD_DIM
    two = n_ctx // 2
    any_spec = pl.BlockSpec(memory_space=pl.ANY)
    vmem_spec = pl.BlockSpec(memory_space=pltpu.VMEM)
    shape = jax.ShapeDtypeStruct
    vm = pltpu.VMEM
    dma = pltpu.SemaphoreType.DMA
    out_shape = [shape(tokens.shape, BF16)] * 2
    out_shape += [shape((share, w), F32) for w in widths]
    out_shape += [shape((16, width), F32)]
    scratch = [vm((n_pair, width, w), BF16) for w in widths]
    scratch += [
        vm((n_pair, n_dp * n_ctx, 16, 128), F32),
        vm((8, width), F32),
        vm((8, width), F32),
    ]
    scratch += [vm((n_ctx, half, width), BF16)] * 4
    scratch += [
        vm((length, width), BF16),
        vm((width, 3 * hw), BF16),
        vm((width, hw), BF16),
        vm((length, hw), BF16),
        vm((length, hw), BF16),
        vm((length, hw), BF16),
        vm((length, hw), F32),
        vm((length, hw), BF16),
        vm((n_ctx, half, width), F32),
        vm((length, width), BF16),
        vm((length, width), BF16),
        vm((n_pair, length, fw), BF16),
        vm((n_pair, length, fw), BF16),
        vm((length, width), BF16),
        vm((length, hw), BF16),
        vm((length, 3 * hw), BF16),
        vm((width, length), BF16),
        vm((width, length), BF16),
        vm((2, length, hw), F32),
        vm((2, block, width), F32),
        vm((2, n_ctx, half, width), BF16),
        vm((2, n_ctx, half, width), BF16),
        vm((n_pair, width, fw), BF16),
        vm((16, width), F32),
    ]
    scratch += [vm((heads, block, (b + 1) * block), BF16) for b in range(n_ctx)]
    lead, after = max(n_dp, n_pair) - 1, max(n_dp, n_pair)
    scratch += [vm((lead, after, n_ctx, share, w), BF16) for w in widths]
    scratch += [vm((lead, n_ctx, share, w), BF16) for w in widths]
    scratch += [vm((n_ctx - 1, share, w), BF16) for w in widths]
    scratch += [
        vm((8, width), F32),
        vm((16, width), F32),
        vm((n_ctx - 1, 16, width), F32),
        vm((16, width), F32),
        vm((n_pair - 1, 16, width), F32),
        vm((16, width), F32),
        vm((n_dp - 1, 16, width), F32),
    ]
    scratch += [vm((share, w), F32) for w in widths]
    scratch += [vm((16, width), F32)]
    most = max(n_dp, n_ctx, n_pair)
    scratch += [
        dma((12,)),
        dma((300,)),
        dma((2, n_ctx)),
        dma((4, n_ctx)),
        dma((4, n_pair)),
        dma((4, n_dp)),
        dma((3, n_pair, n_dp)),
        dma((3, n_pair, n_dp)),
        dma((8, n_ctx)),
        dma((8, n_ctx)),
        dma((3, lead, after, n_ctx)),
        dma((3, lead, n_ctx)),
        dma((3, n_ctx)),
        dma((2, n_ctx)),
        dma((2, seqs)),
        dma((2, seqs)),
        dma((4, most)),
        pltpu.SemaphoreType.REGULAR,
        dma((3, n_pair, n_ctx)),
        dma((3, n_dp, n_ctx)),
    ]
    return pl.pallas_call(
        functools.partial(fused_body, sizes, (half, width, share, cols, fw)),
        out_shape=out_shape,
        in_specs=[any_spec] * 2 + [vmem_spec] * 4 + [any_spec] * 2 + [vmem_spec] * 9,
        out_specs=[any_spec] * 6,
        scratch_shapes=scratch,
        compiler_params=pltpu.CompilerParams(
            collective_id=3, has_side_effects=True, vmem_limit_bytes=67043328
        ),
    )(tokens, out_grad, *shards, *vectors, *column_biases)


def finish_body(n_ctx, share, cols, *refs):
    lo_in, tg_in, attn_in, up_in, down_in, small_in = refs[:6]
    lo, tg, dq, dk, dv, do, du, dd = refs[6:14]
    vectors = refs[14:20]
    shifts = refs[20:22]
    up_shift = refs[22]
    lo_held, tg_held, tg_wide, attn, up, down, small = refs[23:30]
    narrow = refs[30:34]
    in_sem, out_sem, more_in, more_out = refs[34:]
    row = lax.axis_index("dp") * n_ctx + lax.axis_index("ctx")
    pair = lax.axis_index("tp") // 2
    width = small.shape[1]
    seqs = lo_held.shape[0]
    move = pltpu.make_async_copy

    def rows_in(i, s):
        source, held = ((tg_in, tg_held), (lo_in, lo_held))[i]
        return move(source.at[s], held.at[s], in_sem.at[i, s])

    def rows_out(i, s):
        held, target = ((tg_wide, tg), (lo_held, lo))[i]
        return move(held.at[s], target.at[s], out_sem.at[i, s])

    takes = [
        move(source, held, more_in.at[i])
        for i, (source, held) in enumerate(((up_in, up), (down_in, down), (attn_in, attn), (small_in, small)))
    ]
    gives = [
        move(held, target, more_out.at[i])
        for i, (held, target) in enumerate(zip((up, down, *narrow), (du, dd, dq, dk, dv, do)))
    ]

    @pl.loop(0, seqs)
    def _(s):
        rows_in(0, s).start()
        rows_in(1, s).start()

    for copy in takes:
        copy.start()

    @pl.loop(0, seqs)
    def _(s):
        rows_in(0, s).wait()
        tg_wide[s] = tg_held[s].astype(F32)
        rows_out(0, s).start()
        rows_in(1, s).wait()
        rows_out(1, s).start()

    for i in range(2):
        takes[i].wait()
        gives[i].start()
    takes[2].wait()
    for i, ref in enumerate(narrow):
        ref[...] = attn[:, i * cols : (i + 1) * cols]
        gives[2 + i].start()
    takes[3].wait()
    turned = pltpu.roll(small[0:8, :], (width - row * share) % width, 1)
    for i, ref in enumerate(vectors):
        ref[...] = turned[i : i + 1, :share]
    turned = pltpu.roll(small[0:8, :], (width - pair * cols) % width, 1)
    for i, ref in enumerate(shifts):
        ref[...] = turned[6 + i : 7 + i, :cols]
    row_of = small[pl.ds(8 + pair, 1), :]
    for i in range(up_shift.shape[0]):
        up_shift[i : i + 1, :] = row_of[:, i * 128 : (i + 1) * 128]

    @pl.loop(0, seqs)
    def _(s):
        rows_out(0, s).wait()
        rows_out(1, s).wait()

    for copy in gives:
        copy.wait()


def finish_call(sizes, cols, lo, tg, attn, up, down, small):
    n_dp, n_ctx, n_tp = sizes
    seqs, block, width = lo.shape
    share = attn.shape[0]
    shape = jax.ShapeDtypeStruct
    any_spec = pl.BlockSpec(memory_space=pl.ANY)
    vmem_spec = pl.BlockSpec(memory_space=pltpu.VMEM)
    vm = pltpu.VMEM
    dma = pltpu.SemaphoreType.DMA
    out_tail = [(share, cols)] * 4 + [up.shape] * 2 + [(1, share)] * 6 + [(1, cols)] * 2 + [(up.shape[1] // 128, 128)]
    return pl.pallas_call(
        functools.partial(finish_body, n_ctx, share, cols),
        out_shape=[shape(lo.shape, BF16), shape(lo.shape, F32)] + [shape(s, F32) for s in out_tail],
        in_specs=[any_spec] * 6,
        out_specs=[any_spec] * 8 + [vmem_spec] * 9,
        scratch_shapes=[
            vm(lo.shape, BF16),
            vm(lo.shape, BF16),
            vm(lo.shape, F32),
            vm(attn.shape, F32),
            vm(up.shape, F32),
            vm(down.shape, F32),
            vm(small.shape, F32),
        ]
        + [vm((share, cols), F32)] * 4
        + [dma((2, seqs)), dma((2, seqs)), dma((4,)), dma((6,))],
    )(lo, tg, attn, up, down, small)


def fused_layer(sizes, tokens, out_grad, shards, vectors, column_biases):
    cols = shards[0].shape[1]
    lines = [v.reshape(1, -1) for v in vectors]
    results = fused_call(sizes, tokens, out_grad, shards, lines, column_biases)
    final = finish_call(sizes, cols, *results)
    return (*final[:8], *[v.reshape(-1) for v in final[8:]])


def per_device(
    tokens,
    out_grad,
    query_weight,
    key_weight,
    value_weight,
    output_weight,
    up_weight,
    down_weight,
    norm1_gain,
    norm1_bias,
    output_bias,
    norm2_gain,
    norm2_bias,
    down_bias,
    query_bias,
    value_bias,
    up_bias,
):
    sizes = (lax.axis_size("dp"), lax.axis_size("ctx"), lax.axis_size("tp"))
    n_dp, n_ctx, n_tp = sizes
    n_pair = n_tp // 2
    seqs, block, width = tokens.shape
    assert seqs == n_ctx * n_pair
    share = norm1_gain.shape[0]
    cols = query_bias.shape[0]
    pair = lax.axis_index("tp") // 2
    row = lax.axis_index("dp") * n_ctx + lax.axis_index("ctx")
    shards = (query_weight, key_weight, value_weight, output_weight, up_weight, down_weight)
    vectors = (norm1_gain, norm1_bias, output_bias, norm2_gain, norm2_bias, down_bias)
    if share % 16 == 0 and n_ctx % 4 == 0 and n_ctx & (n_ctx - 1) == 0:
        return fused_layer(
            sizes, tokens, out_grad, shards, vectors, (query_bias, value_bias, up_bias)
        )

    six = jnp.stack(vectors).astype(F32)
    vec = jnp.pad(six, ((0, 2), (0, 128 - share)))
    columns = jnp.arange(width) // cols == pair
    narrow = [jnp.where(columns, jnp.tile(b.astype(F32), width // cols), 0.0) for b in (query_bias, value_bias)]
    bias = jnp.pad(jnp.stack(narrow + [up_bias.astype(F32)]), ((0, 5), (0, 0)))

    gathered = gather_call(sizes, tokens, out_grad, shards, vec, bias)
    tok, og = gathered[0:2]
    weights = [w.reshape(n_pair, width, w.shape[3]) for w in gathered[2:8]]
    vecs = gathered[8][:, :, :share].transpose(1, 0, 2).reshape(8, width)
    results = compute_call(sizes, tok, og, weights, vecs, gathered[9])
    lo, tg = results[0:2]
    grads = [
        g.reshape(n_pair, n_dp * n_ctx, s.shape[0], s.shape[1]) for g, s in zip(results[2:8], shards)
    ]
    final = scatter_call(sizes, seqs, lo, tg, grads, results[8])
    layer_out, tokens_grad = final[0], final[1].astype(F32)
    small = final[8]
    owned = [lax.dynamic_slice_in_dim(small[i], row * share, share) for i in range(6)]
    shifts = [lax.dynamic_slice_in_dim(small[6 + i], pair * cols, cols) for i in range(2)]
    up_total = lax.dynamic_index_in_dim(small[8 : 8 + n_pair], pair, 0, keepdims=False)
    return (layer_out, tokens_grad, *final[2:8], *owned, *shifts, up_total)


def solution(mesh):
    rows_spec = P("dp", "ctx", None)
    weight_spec = P(("dp", "ctx"), "tp")
    vector_spec = P(("dp", "ctx"))
    column_spec = P("tp")
    common = (rows_spec,) * 2 + (weight_spec,) * 6 + (vector_spec,) * 6 + (column_spec,) * 3
    return jax.shard_map(
        per_device, mesh=mesh, in_specs=common, out_specs=common, check_vma=False
    )
```

```python
import functools

import jax
import jax.numpy as jnp
from jax import lax
from jax.experimental import pallas as pl
from jax.experimental.pallas import tpu as pltpu
from jax.sharding import PartitionSpec as P

HEAD_DIM = 64
MESH = pl.DeviceIdType.MESH
F32 = jnp.float32
BF16 = jnp.bfloat16
VMEM_LIMIT = 66 * 1000 * 1000

epsilon = 1e-05
root_half = 0.7071067811865476
density_scale = 0.3989422804014327


def remote(src, dst, send_sem, recv_sem, device):
    return pltpu.make_async_remote_copy(
        src_ref=src,
        dst_ref=dst,
        send_sem=send_sem,
        recv_sem=recv_sem,
        device_id=device,
        device_id_type=MESH,
    )


def nn_dot(left, right):
    return lax.dot_general(left, right, (((1,), (0,)), ((), ())), preferred_element_type=F32)


def nt_dot(left, right):
    return lax.dot_general(left, right, (((1,), (1,)), ((), ())), preferred_element_type=F32)


def tn_dot(left, right):
    return lax.dot_general(left, right, (((0,), (0,)), ((), ())), preferred_element_type=F32)


def normalize(values):
    centred = values - jnp.mean(values, axis=-1, keepdims=True)
    spread = lax.rsqrt(jnp.mean(centred * centred, axis=-1, keepdims=True) + epsilon)
    return centred * spread, spread


def norm_back(grad_scaled, scaled, spread):
    inner = grad_scaled - jnp.mean(grad_scaled, axis=-1, keepdims=True)
    inner = inner - scaled * jnp.mean(grad_scaled * scaled, axis=-1, keepdims=True)
    return inner * spread


class Place:
    def __init__(self, sizes):
        self.n_dp, self.n_ctx, self.n_tp = sizes
        self.n_pair = self.n_tp // 2
        self.dp = lax.axis_index("dp")
        self.ctx = lax.axis_index("ctx")
        self.tp = lax.axis_index("tp")
        self.pair = self.tp // 2
        self.side = self.tp % 2

    def other_dp(self, k):
        d = (self.dp + k) % self.n_dp
        return d, (d, self.ctx, self.tp)

    def other_ctx(self, k):
        z = (self.ctx + k) % self.n_ctx
        return z, (self.dp, z, self.tp)

    def other_pair(self, k):
        p = (self.pair + k) % self.n_pair
        return p, (self.dp, self.ctx, 2 * p + self.side)

    def partner(self):
        return (self.dp, self.ctx, 2 * self.pair + 1 - self.side)

    def barrier(self, far):
        sem = pltpu.get_barrier_semaphore()
        count = 1
        pl.semaphore_signal(sem, inc=1, device_id=self.partner(), device_id_type=MESH)
        if far:
            for size, other in (
                (self.n_dp, self.other_dp),
                (self.n_ctx, self.other_ctx),
                (self.n_pair, self.other_pair),
            ):
                for k in range(1, size):
                    pl.semaphore_signal(sem, inc=1, device_id=other(k)[1], device_id_type=MESH)
                    count += 1
        pl.semaphore_wait(sem, count)


class Sends:
    def __init__(self, sems):
        self.sems = sems
        self.started = []

    def go(self, src, dst, recv_sem, device):
        copy = remote(src, dst, self.sems.at[len(self.started)], recv_sem, device)
        copy.start()
        self.started.append(copy)

    def finish(self):
        for copy in self.started:
            copy.wait_send()


def gather_body(sizes, half, *refs):
    here = Place(sizes)
    n_dp, n_ctx, n_pair = here.n_dp, here.n_ctx, here.n_pair
    d, z, p, c = here.dp, here.ctx, here.pair, here.side
    tokens, out_grad = refs[0:2]
    shards = refs[2:8]
    vec, bias = refs[8:10]
    tok_own, og_own = refs[10:12]
    full = refs[12:18]
    vec_all, bias_all = refs[18:20]
    own_sem, send_sem, rows_sem, line_sem, group_sem, vline_sem, vgroup_sem, bias_sem = refs[20:28]
    own_row = d * n_ctx + z
    mine = p * n_ctx + z
    rows = pl.ds(pl.multiple_of(c * half, half), half)

    here.barrier(True)
    sends = Sends(send_sem)
    own = [
        pltpu.make_async_copy(tokens.at[mine, rows], tok_own.at[z], own_sem.at[0]),
        pltpu.make_async_copy(out_grad.at[mine, rows], og_own.at[z], own_sem.at[1]),
        pltpu.make_async_copy(vec, vec_all.at[own_row], own_sem.at[2]),
        pltpu.make_async_copy(bias, bias_all.at[p], own_sem.at[3]),
    ]
    for a in range(6):
        own.append(pltpu.make_async_copy(shards[a], full[a].at[p, own_row], own_sem.at[4 + a]))
    for copy in own:
        copy.start()

    def send_rows(index, source, target):
        for k in range(1, n_ctx):
            zz, device = here.other_ctx(k)
            sends.go(
                source.at[p * n_ctx + zz, rows], target.at[z], rows_sem.at[index, z], device
            )

    def send_line(a):
        for k in range(1, n_ctx):
            zz, device = here.other_ctx(k)
            sends.go(shards[a], full[a].at[p, own_row], line_sem.at[a, z], device)

    send_rows(0, tokens, tok_own)
    for k in range(1, n_ctx):
        zz, device = here.other_ctx(k)
        sends.go(vec, vec_all.at[own_row], vline_sem.at[z], device)
    for k in range(1, n_pair):
        pp, device = here.other_pair(k)
        sends.go(bias, bias_all.at[p], bias_sem.at[p], device)
    for a in range(6):
        send_line(a)
    send_rows(1, out_grad, og_own)

    for copy in own:
        copy.wait()

    def group(a, pp, dd):
        return full[a].at[pp, pl.ds(dd * n_ctx, n_ctx)]

    def wait_line(a):
        for k in range(1, n_ctx):
            zz, device = here.other_ctx(k)
            slot = full[a].at[p, d * n_ctx + zz]
            remote(slot, slot, send_sem.at[0], line_sem.at[a, zz], device).wait_recv()

    def send_pair(a, dd):
        for k in range(1, n_pair):
            pp, device = here.other_pair(k)
            sends.go(group(a, p, dd), group(a, p, dd), group_sem.at[a, p, dd], device)

    def send_dp(a, pp):
        for k in range(1, n_dp):
            dd, device = here.other_dp(k)
            sends.go(group(a, pp, d), group(a, pp, d), group_sem.at[a, pp, d], device)

    def wait_group(a, pp, dd):
        slot = group(a, pp, dd)
        remote(slot, slot, send_sem.at[0], group_sem.at[a, pp, dd], here.partner()).wait_recv()

    for a in range(6):
        wait_line(a)
        send_dp(a, p)
        send_pair(a, d)
    for k in range(1, n_ctx):
        zz, device = here.other_ctx(k)
        slot = vec_all.at[d * n_ctx + zz]
        remote(slot, slot, send_sem.at[0], vline_sem.at[zz], device).wait_recv()
    for k in range(1, n_dp):
        dd, device = here.other_dp(k)
        slot = vec_all.at[pl.ds(d * n_ctx, n_ctx)]
        sends.go(slot, slot, vgroup_sem.at[d], device)
    pair_first = (True, True, True, True, False, True)
    for a in range(6):
        if pair_first[a]:
            for k in range(1, n_pair):
                pp = here.other_pair(k)[0]
                wait_group(a, pp, d)
                send_dp(a, pp)
        else:
            for k in range(1, n_dp):
                dd = here.other_dp(k)[0]
                wait_group(a, p, dd)
                send_pair(a, dd)
    for a in range(6):
        for k in range(1, n_dp):
            dd = here.other_dp(k)[0]
            if pair_first[a]:
                wait_group(a, p, dd)
            for j in range(1, n_pair):
                wait_group(a, here.other_pair(j)[0], dd)
        if not pair_first[a]:
            for j in range(1, n_pair):
                wait_group(a, here.other_pair(j)[0], d)
    for k in range(1, n_dp):
        dd, device = here.other_dp(k)
        slot = vec_all.at[pl.ds(dd * n_ctx, n_ctx)]
        remote(slot, slot, send_sem.at[0], vgroup_sem.at[dd], device).wait_recv()
    for k in range(1, n_pair):
        pp, device = here.other_pair(k)
        slot = bias_all.at[pp]
        remote(slot, slot, send_sem.at[0], bias_sem.at[pp], device).wait_recv()
    for index, target in ((0, tok_own), (1, og_own)):
        for k in range(1, n_ctx):
            zz, device = here.other_ctx(k)
            slot = target.at[zz]
            remote(slot, slot, send_sem.at[0], rows_sem.at[index, zz], device).wait_recv()
    sends.finish()


def gather_call(sizes, tokens, out_grad, shards, vec, bias):
    n_dp, n_ctx, n_tp = sizes
    n_pair = n_tp // 2
    seqs, block, width = tokens.shape
    half = block // 2
    any_spec = pl.BlockSpec(memory_space=pl.ANY)
    vmem_spec = pl.BlockSpec(memory_space=pltpu.VMEM)
    own = jax.ShapeDtypeStruct((n_ctx, half, width), BF16)
    out_shape = [own, own]
    out_shape += [jax.ShapeDtypeStruct((n_pair, n_dp * n_ctx) + s.shape, BF16) for s in shards]
    out_shape += [
        jax.ShapeDtypeStruct((n_dp * n_ctx,) + vec.shape, F32),
        jax.ShapeDtypeStruct((n_pair,) + bias.shape, F32),
    ]
    n_sends = (
        2 * (n_ctx - 1)
        + (n_ctx - 1)
        + (n_pair - 1)
        + 6 * (n_ctx - 1)
        + (n_dp - 1)
        + 6 * ((n_dp - 1) + (n_pair - 1) + (n_dp - 1) * (n_pair - 1))
    )
    dma = pltpu.SemaphoreType.DMA
    return pl.pallas_call(
        functools.partial(gather_body, sizes, half),
        out_shape=out_shape,
        in_specs=[any_spec] * 10,
        out_specs=[vmem_spec] * 10,
        scratch_shapes=[
            dma((10,)),
            dma((n_sends,)),
            dma((2, n_ctx)),
            dma((6, n_ctx)),
            dma((6, n_pair, n_dp)),
            dma((n_ctx,)),
            dma((n_dp,)),
            dma((n_pair,)),
        ],
        compiler_params=pltpu.CompilerParams(
            collective_id=0, has_side_effects=True, vmem_limit_bytes=VMEM_LIMIT
        ),
    )(tokens, out_grad, *shards, vec, bias)


def compute_body(sizes, *refs):
    here = Place(sizes)
    n_ctx, n_pair = here.n_ctx, here.n_pair
    c = here.side
    (tok, og, gq, gk, gv, go, gu, gd, vecs, bias) = refs[:10]
    (lo, tg, dwq, dwk, dwv, dwo, dwu, dwd, small) = refs[10:19]
    (
        xn1, wqkv, wo, qs, ks, vs, o32, mixed, hid, xn2, ogf, act, ug, bg, dm,
        dka, dva, dqkv, tra, trb, part, ssend, srecv, p_first, send_sem, recv_sem,
    ) = refs[19 : 19 + 23] + (refs[42 : 42 + n_ctx],) + refs[42 + n_ctx :]
    half, width = tok.shape[1], tok.shape[2]
    block = 2 * half
    cols = gq.shape[2]
    hw = n_pair * cols
    fw = gu.shape[2]
    lanes = 2 * HEAD_DIM
    n_twos = hw // lanes
    partner = here.partner()
    scale = HEAD_DIM ** -0.5
    first_head = lax.broadcasted_iota(jnp.int32, (1, lanes), 1) < HEAD_DIM
    zero16 = jnp.zeros((), BF16)

    def own_rows(b):
        return pl.ds(pl.multiple_of(b * block + c * half, half), half)

    def far_rows(b):
        return pl.ds(pl.multiple_of(b * block + (1 - c) * half, half), half)

    def block_rows(b):
        return pl.ds(pl.multiple_of(b * block, block), block)

    def exchange(stage, b, src, dst):
        return remote(src, dst, send_sem.at[stage, b], recv_sem.at[stage, b], partner)

    def rows_copy(stage, b, ref):
        return exchange(stage, b, ref.at[own_rows(b)], ref.at[own_rows(b)])

    def rows_arrive(stage, b, ref):
        exchange(stage, b, ref.at[far_rows(b)], ref.at[far_rows(b)]).wait_recv()

    def part_copy(stage, slot, b):
        return exchange(stage, b, ssend.at[slot, b], srecv.at[slot, b])

    here.barrier(False)

    gain_one, shift_one, out_shift = vecs[0:1, :], vecs[1:2, :], vecs[2:3, :]
    gain_two, shift_two, down_shift = vecs[3:4, :], vecs[4:5, :], vecs[5:6, :]

    @pl.loop(0, n_ctx)
    def _(b):
        exchange(0, b, og.at[b], ogf.at[own_rows(b)]).start()
        ogf[own_rows(b), :] = og[b]
        scaled, _ = normalize(tok[b].astype(F32))
        xn1[own_rows(b), :] = (scaled * gain_one + shift_one).astype(BF16)
        rows_copy(1, b, xn1).start()

    for i in range(n_pair):
        at = slice(i * cols, (i + 1) * cols)
        wqkv[:, i * cols : (i + 1) * cols] = gq[i]
        wqkv[:, hw + i * cols : hw + (i + 1) * cols] = gk[i]
        wqkv[:, 2 * hw + i * cols : 2 * hw + (i + 1) * cols] = gv[i]
        wo[:, at] = go[i]
    q_shift = bias[0, 0:1, :hw]
    v_shift = bias[0, 1:2, :hw]
    for i in range(1, n_pair):
        q_shift = q_shift + bias[i, 0:1, :hw]
        v_shift = v_shift + bias[i, 1:2, :hw]

    @pl.loop(0, n_ctx)
    def _(b):
        rows_arrive(1, b, xn1)
        product = nn_dot(xn1[block_rows(b), :], wqkv[...])
        qs[block_rows(b), :] = (product[:, :hw] + q_shift).astype(BF16) * jnp.asarray(scale, BF16)
        ks[block_rows(b), :] = product[:, hw : 2 * hw].astype(BF16)
        vs[block_rows(b), :] = (product[:, 2 * hw :] + v_shift).astype(BF16)

    for b in range(n_ctx):
        reach = (b + 1) * block
        here_rows = slice(b * block, (b + 1) * block)

        @pl.loop(0, n_twos)
        def _(j):
            at = pl.ds(pl.multiple_of(j * lanes, lanes), lanes)
            queries, keys, values = qs[here_rows, at], ks[:reach, at], vs[:reach, at]
            pieces = []
            for e in range(2):
                head = first_head if e == 0 else jnp.logical_not(first_head)
                scores = nt_dot(jnp.where(head, queries, zero16), keys)
                powers = jnp.exp(scores - jnp.max(scores, axis=-1, keepdims=True))
                inverse = 1.0 / jnp.sum(powers, axis=-1, keepdims=True)
                probs = (powers * inverse).astype(BF16)
                p_first[b][2 * j + e] = probs
                pieces.append(nn_dot(probs, values))
            out = jnp.where(first_head, pieces[0], pieces[1])
            o32[here_rows, at] = out
            mixed[here_rows, at] = out.astype(BF16)

        ssend[0, b] = nt_dot(mixed[far_rows(b), :], wo[...]).astype(BF16)
        part_copy(2, 0, b).start()
        hid[b] = nt_dot(mixed[own_rows(b), :], wo[...])

    @pl.loop(0, n_ctx)
    def _(b):
        part_copy(2, 0, b).wait()
        hidden = tok[b].astype(F32) + (hid[b] + srecv[0, b].astype(F32)) + out_shift
        hid[b] = hidden
        scaled, _ = normalize(hidden)
        xn2[own_rows(b), :] = (scaled * gain_two + shift_two).astype(BF16)
        rows_copy(3, b, xn2).start()

    small[...] = jnp.zeros_like(small)

    @pl.loop(0, n_ctx)
    def _(b):
        rows_arrive(0, b, ogf)
        rows_arrive(3, b, xn2)
        normed = xn2[block_rows(b), :]
        grads = ogf[block_rows(b), :]
        for i in range(n_pair):
            upward = nn_dot(normed, gu[i]) + bias[i, 2:3, :]
            big_phi = 0.5 + 0.5 * lax.erf(upward * root_half)
            act[i, block_rows(b), :] = (upward * big_phi).astype(BF16)
            slope = big_phi + upward * density_scale * jnp.exp(-0.5 * upward * upward)
            rows_grad = (nn_dot(grads, gd[i]) * slope).astype(BF16)
            ug[i, block_rows(b), :] = rows_grad
            small[8 + i : 9 + i, :] += jnp.sum(rows_grad.astype(F32), axis=0, keepdims=True)

        def through(ref, weight, rows):
            total = nt_dot(ref[0, rows, :], weight[0])
            for i in range(1, n_pair):
                total = total + nt_dot(ref[i, rows, :], weight[i])
            return total

        ssend[1, b] = through(act, gd, far_rows(b)).astype(BF16)
        part_copy(4, 1, b).start()
        ssend[0, b] = through(ug, gu, far_rows(b)).astype(BF16)
        part_copy(5, 0, b).start()
        part[0, b] = through(act, gd, own_rows(b))
        part[1, b] = through(ug, gu, own_rows(b))

    def transposed(ref, out):
        for b in range(n_ctx):
            out[:, b * block : (b + 1) * block] = ref[b * block : (b + 1) * block, :].T

    @pl.loop(0, n_ctx)
    def _(b):
        part_copy(4, 1, b).wait()
        lo[b] = (hid[b] + (part[0, b] + srecv[1, b].astype(F32)) + down_shift).astype(BF16)
        part_copy(5, 0, b).wait()
        grad_two = part[1, b] + srecv[0, b].astype(F32)
        scaled, spread = normalize(hid[b])
        own_grad = og[b].astype(F32)
        hidden_grad = own_grad + norm_back(grad_two * gain_two, scaled, spread)
        hid[b] = hidden_grad
        branch = hidden_grad.astype(BF16)
        bg[own_rows(b), :] = branch
        rows_copy(6, b, bg).start()
        small[2:3, :] += jnp.sum(branch.astype(F32), axis=0, keepdims=True)
        small[3:4, :] += jnp.sum(grad_two * scaled, axis=0, keepdims=True)
        small[4:5, :] += jnp.sum(grad_two, axis=0, keepdims=True)
        small[5:6, :] += jnp.sum(own_grad, axis=0, keepdims=True)

    transposed(xn2, tra)
    transposed(ogf, trb)
    step = 256

    @pl.loop(0, width // step)
    def _(r):
        rows = pl.ds(pl.multiple_of(r * step, step), step)
        for i in range(n_pair):
            dwu[i, rows, :] = nn_dot(tra[rows, :], ug[i]).astype(BF16)
            dwd[i, rows, :] = nn_dot(trb[rows, :], act[i]).astype(BF16)

    @pl.loop(0, n_ctx)
    def _(b):
        rows_arrive(6, b, bg)
        dm[block_rows(b), :] = nn_dot(bg[block_rows(b), :], wo[...]).astype(BF16)

    transposed(bg, trb)

    @pl.loop(0, width // step)
    def _(r):
        rows = pl.ds(pl.multiple_of(r * step, step), step)
        product = nn_dot(trb[rows, :], mixed[...])
        for i in range(n_pair):
            dwo[i, rows, :] = product[:, i * cols : (i + 1) * cols].astype(BF16)

    for b in reversed(range(n_ctx)):
        reach = (b + 1) * block
        here_rows = slice(b * block, (b + 1) * block)

        @pl.loop(0, n_twos)
        def _(j):
            at = pl.ds(pl.multiple_of(j * lanes, lanes), lanes)
            queries, keys, values = qs[here_rows, at], ks[:reach, at], vs[:reach, at]
            mix_grad, mix = dm[here_rows, at], o32[here_rows, at]
            towards = mix_grad.astype(F32) * mix
            query_parts, key_sum, value_sum = [], None, None
            for e in range(2):
                head = first_head if e == 0 else jnp.logical_not(first_head)
                grad_head = jnp.where(head, mix_grad, zero16)
                prob_grad = nt_dot(grad_head, values)
                centre = jnp.sum(jnp.where(head, towards, 0.0), axis=-1, keepdims=True)
                probs = p_first[b][2 * j + e]
                score_grad = (probs.astype(F32) * (prob_grad - centre)).astype(BF16)
                query_parts.append(nn_dot(score_grad, keys))
                key_term = tn_dot(score_grad, jnp.where(head, queries, zero16))
                value_term = tn_dot(probs, grad_head)
                key_sum = key_term if key_sum is None else key_sum + key_term
                value_sum = value_term if value_sum is None else value_sum + value_term
            query_grad = jnp.where(first_head, query_parts[0], query_parts[1]) * scale
            dqkv[here_rows, at] = query_grad.astype(BF16)
            if b == n_ctx - 1:
                dka[:, at] = key_sum
                dva[:, at] = value_sum
            else:
                dka[:reach, at] += key_sum
                dva[:reach, at] += value_sum

    @pl.loop(0, n_ctx)
    def _(b):
        dqkv[block_rows(b), hw : 2 * hw] = dka[block_rows(b), :].astype(BF16)
        dqkv[block_rows(b), 2 * hw :] = dva[block_rows(b), :].astype(BF16)
        small[6:7, :hw] += jnp.sum(dqkv[block_rows(b), :hw].astype(F32), axis=0, keepdims=True)
        small[7:8, :hw] += jnp.sum(dqkv[block_rows(b), 2 * hw :].astype(F32), axis=0, keepdims=True)
        ssend[1, b] = nt_dot(dqkv[far_rows(b), :], wqkv[...]).astype(BF16)
        part_copy(7, 1, b).start()
        part[0, b] = nt_dot(dqkv[own_rows(b), :], wqkv[...])

    transposed(xn1, tra)

    @pl.loop(0, width // step)
    def _(r):
        rows = pl.ds(pl.multiple_of(r * step, step), step)
        product = nn_dot(tra[rows, :], dqkv[...])
        for i in range(n_pair):
            dwq[i, rows, :] = product[:, i * cols : (i + 1) * cols].astype(BF16)
            dwk[i, rows, :] = product[:, hw + i * cols : hw + (i + 1) * cols].astype(BF16)
            dwv[i, rows, :] = product[:, 2 * hw + i * cols : 2 * hw + (i + 1) * cols].astype(BF16)

    @pl.loop(0, n_ctx)
    def _(b):
        part_copy(7, 1, b).wait()
        grad_one = part[0, b] + srecv[1, b].astype(F32)
        scaled, spread = normalize(tok[b].astype(F32))
        tg[b] = (hid[b] + norm_back(grad_one * gain_one, scaled, spread)).astype(BF16)
        small[0:1, :] += jnp.sum(grad_one * scaled, axis=0, keepdims=True)
        small[1:2, :] += jnp.sum(grad_one, axis=0, keepdims=True)
        exchange(0, b, og.at[b], ogf.at[own_rows(b)]).wait_send()
        rows_copy(1, b, xn1).wait_send()
        rows_copy(3, b, xn2).wait_send()
        rows_copy(6, b, bg).wait_send()


def compute_call(sizes, tok, og, weights, vecs, bias):
    n_dp, n_ctx, n_tp = sizes
    n_pair = n_tp // 2
    half, width = tok.shape[1:]
    block = 2 * half
    length = n_ctx * block
    cols = weights[0].shape[2]
    hw = n_pair * cols
    fw = weights[4].shape[2]
    heads = hw // HEAD_DIM
    vmem_spec = pl.BlockSpec(memory_space=pltpu.VMEM)
    shape = jax.ShapeDtypeStruct
    out_shape = [
        shape(tok.shape, BF16),
        shape(tok.shape, BF16),
    ]
    out_shape += [shape(w.shape, BF16) for w in weights]
    out_shape += [shape((16, width), F32)]
    vm = pltpu.VMEM
    scratch = [
        vm((length, width), BF16),
        vm((width, 3 * hw), BF16),
        vm((width, hw), BF16),
        vm((length, hw), BF16),
        vm((length, hw), BF16),
        vm((length, hw), BF16),
        vm((length, hw), F32),
        vm((length, hw), BF16),
        vm((n_ctx, half, width), F32),
        vm((length, width), BF16),
        vm((length, width), BF16),
        vm((n_pair, length, fw), BF16),
        vm((n_pair, length, fw), BF16),
        vm((length, width), BF16),
        vm((length, hw), BF16),
        vm((length, hw), F32),
        vm((length, hw), F32),
        vm((length, 3 * hw), BF16),
        vm((width, length), BF16),
        vm((width, length), BF16),
        vm((2, n_ctx, half, width), F32),
        vm((2, n_ctx, half, width), BF16),
        vm((2, n_ctx, half, width), BF16),
    ]
    scratch += [vm((heads, block, (b + 1) * block), BF16) for b in range(n_ctx)]
    scratch += [pltpu.SemaphoreType.DMA((8, n_ctx)), pltpu.SemaphoreType.DMA((8, n_ctx))]
    return pl.pallas_call(
        functools.partial(compute_body, sizes),
        out_shape=out_shape,
        in_specs=[vmem_spec] * 10,
        out_specs=[vmem_spec] * 9,
        scratch_shapes=scratch,
        compiler_params=pltpu.CompilerParams(
            collective_id=1, has_side_effects=True, vmem_limit_bytes=VMEM_LIMIT
        ),
    )(tok, og, *weights, vecs, bias)


def scatter_body(sizes, half, *refs):
    here = Place(sizes)
    n_dp, n_ctx, n_pair = here.n_dp, here.n_ctx, here.n_pair
    d, z, p, c = here.dp, here.ctx, here.pair, here.side
    rows_in = refs[0:2]
    grads = refs[2:8]
    small = refs[8]
    rows_out = refs[9:11]
    owned = refs[11:17]
    small_out = refs[17]
    it = iter(refs[18:])
    dp_land = [next(it) for _ in range(6)]
    dp_sum = [next(it) for _ in range(6)]
    keep = [next(it) for _ in range(6)]
    pair_land = [next(it) for _ in range(6)]
    pair_sum = [next(it) for _ in range(6)]
    ctx_land = [next(it) for _ in range(6)]
    side_land, small_b, ctx_small, small_c, pair_small, small_d, dp_small = [next(it) for _ in range(7)]
    own_sem, send_sem, line_sem, far_sem, side_sem, dp_sem, pair_sem, ctx_sem, small_sem = it
    mine = p * n_ctx + z
    rows = pl.ds(pl.multiple_of(c * half, half), half)

    here.barrier(True)
    sends = Sends(send_sem)

    for a in range(6):
        for k in range(1, n_dp):
            dd, device = here.other_dp(k)
            sends.go(
                grads[a].at[:, pl.ds(dd * n_ctx, n_ctx)],
                dp_land[a].at[k - 1],
                dp_sem.at[a, k - 1],
                device,
            )
    own = []
    for i in range(2):
        for k in range(1, n_ctx):
            zz, device = here.other_ctx(k)
            sends.go(rows_in[i].at[zz], rows_out[i].at[mine, rows], line_sem.at[i, z], device)
        own.append(pltpu.make_async_copy(rows_in[i].at[z], rows_out[i].at[mine, rows], own_sem.at[i]))
        own[-1].start()
    sends.go(small.at[pl.ds(0, 8)], side_land, small_sem.at[0, 0], here.partner())

    def small_arrive(stage, k, land):
        remote(land, land, send_sem.at[0], small_sem.at[stage, k - 1], here.partner()).wait_recv()

    for i in range(2):
        own[i].wait()
        for k in range(1, n_ctx):
            zz, device = here.other_ctx(k)
            slot = rows_out[i].at[p * n_ctx + zz, rows]
            remote(slot, slot, send_sem.at[0], line_sem.at[i, zz], device).wait_recv()
        for k in range(1, n_pair):
            pp, device = here.other_pair(k)
            slot = rows_out[i].at[pl.ds(p * n_ctx, n_ctx), rows]
            sends.go(slot, slot, far_sem.at[i, p], device)

    small_arrive(0, 1, side_land)
    small_b[0:8, :] = small[0:8, :] + side_land[...]
    small_b[8:16, :] = small[8:16, :]
    small_b[6:8, :] = small[6:8, :]
    for k in range(1, n_ctx):
        zz, device = here.other_ctx(k)
        sends.go(small_b, ctx_small.at[k - 1], small_sem.at[1, k - 1], device)

    for a in range(6):
        for k in range(1, n_dp):
            remote(
                dp_land[a].at[k - 1], dp_land[a].at[k - 1], send_sem.at[0], dp_sem.at[a, k - 1],
                here.partner(),
            ).wait_recv()
        for i in range(n_pair):
            total = grads[a][i, pl.ds(d * n_ctx, n_ctx)].astype(F32)
            for k in range(1, n_dp):
                total = total + dp_land[a][k - 1, i].astype(F32)
            dp_sum[a][i] = total.astype(BF16)
        for k in range(1, n_pair):
            pp, device = here.other_pair(k)
            sends.go(dp_sum[a].at[pp], pair_land[a].at[k - 1], pair_sem.at[a, k - 1], device)

    total = small_b[...]
    for k in range(1, n_ctx):
        small_arrive(1, k, ctx_small.at[k - 1])
        total = total + ctx_small[k - 1]
    small_c[...] = total
    for k in range(1, n_pair):
        pp, device = here.other_pair(k)
        sends.go(small_c, pair_small.at[k - 1], small_sem.at[2, k - 1], device)

    for a in range(6):
        for k in range(1, n_pair):
            remote(
                pair_land[a].at[k - 1], pair_land[a].at[k - 1], send_sem.at[0], pair_sem.at[a, k - 1],
                here.partner(),
            ).wait_recv()
        total = dp_sum[a][p].astype(F32)
        for k in range(1, n_pair):
            total = total + pair_land[a][k - 1].astype(F32)
        keep[a][...] = total
        pair_sum[a][...] = total.astype(BF16)
        for k in range(1, n_ctx):
            zz, device = here.other_ctx(k)
            sends.go(pair_sum[a].at[zz], ctx_land[a].at[k - 1], ctx_sem.at[a, k - 1], device)

    total = small_c[...]
    for k in range(1, n_pair):
        small_arrive(2, k, pair_small.at[k - 1])
        total = total + pair_small[k - 1]
    small_d[...] = total
    for k in range(1, n_dp):
        dd, device = here.other_dp(k)
        sends.go(small_d, dp_small.at[k - 1], small_sem.at[3, k - 1], device)

    for i in range(2):
        for k in range(1, n_pair):
            pp, device = here.other_pair(k)
            slot = rows_out[i].at[pl.ds(pp * n_ctx, n_ctx), rows]
            remote(slot, slot, send_sem.at[0], far_sem.at[i, pp], device).wait_recv()
        slot = rows_out[i].at[:, rows]
        sends.go(slot, slot, side_sem.at[i], here.partner())

    for a in range(6):
        total = keep[a][z]
        for k in range(1, n_ctx):
            remote(
                ctx_land[a].at[k - 1], ctx_land[a].at[k - 1], send_sem.at[0], ctx_sem.at[a, k - 1],
                here.partner(),
            ).wait_recv()
            total = total + ctx_land[a][k - 1].astype(F32)
        owned[a][...] = total

    total = small_d[...]
    for k in range(1, n_dp):
        small_arrive(3, k, dp_small.at[k - 1])
        total = total + dp_small[k - 1]
    small_out[...] = total
    other = pl.ds(pl.multiple_of((1 - c) * half, half), half)
    for i in range(2):
        slot = rows_out[i].at[:, other]
        remote(slot, slot, send_sem.at[0], side_sem.at[i], here.partner()).wait_recv()
    sends.finish()


def scatter_call(sizes, seqs, lo, tg, grads, small):
    n_dp, n_ctx, n_tp = sizes
    n_pair = n_tp // 2
    half, width = lo.shape[1:]
    vmem_spec = pl.BlockSpec(memory_space=pltpu.VMEM)
    shape = jax.ShapeDtypeStruct
    vm = pltpu.VMEM
    tail = [g.shape[2:] for g in grads]
    out_shape = [shape((seqs, 2 * half, width), BF16)] * 2
    out_shape += [shape(t, F32) for t in tail]
    out_shape += [shape(small.shape, F32)]
    scratch = [vm((n_dp - 1, n_pair, n_ctx) + t, BF16) for t in tail]
    scratch += [vm((n_pair, n_ctx) + t, BF16) for t in tail]
    scratch += [vm((n_ctx,) + t, F32) for t in tail]
    scratch += [vm((n_pair - 1, n_ctx) + t, BF16) for t in tail]
    scratch += [vm((n_ctx,) + t, BF16) for t in tail]
    scratch += [vm((n_ctx - 1,) + t, BF16) for t in tail]
    scratch += [
        vm((8, width), F32),
        vm((16, width), F32),
        vm((n_ctx - 1, 16, width), F32),
        vm((16, width), F32),
        vm((n_pair - 1, 16, width), F32),
        vm((16, width), F32),
        vm((n_dp - 1, 16, width), F32),
    ]
    n_sends = (
        6 * ((n_dp - 1) + (n_pair - 1) + (n_ctx - 1))
        + 2 * ((n_ctx - 1) + (n_pair - 1) + 1)
        + 1 + (n_ctx - 1) + (n_pair - 1) + (n_dp - 1)
    )
    dma = pltpu.SemaphoreType.DMA
    most = max(n_dp, n_ctx, n_pair)
    scratch += [
        dma((2,)),
        dma((n_sends,)),
        dma((2, n_ctx)),
        dma((2, n_pair)),
        dma((2,)),
        dma((6, n_dp - 1)),
        dma((6, n_pair - 1)),
        dma((6, n_ctx - 1)),
        dma((4, most)),
    ]
    return pl.pallas_call(
        functools.partial(scatter_body, sizes, half),
        out_shape=out_shape,
        in_specs=[vmem_spec] * 9,
        out_specs=[vmem_spec] * 9,
        scratch_shapes=scratch,
        compiler_params=pltpu.CompilerParams(
            collective_id=2, has_side_effects=True, vmem_limit_bytes=VMEM_LIMIT
        ),
    )(lo, tg, *grads, small)


def fused_body(sizes, dims, *refs):
    here = Place(sizes)
    n_dp, n_ctx, n_pair = here.n_dp, here.n_ctx, here.n_pair
    d, z, p, c = here.dp, here.ctx, here.pair, here.side
    half, width, share, cols, fw = dims
    block = 2 * half
    hw = n_pair * cols
    lanes = 2 * HEAD_DIM
    n_twos = hw // lanes
    n_rows = n_dp * n_ctx
    two = n_ctx // 2
    it = iter(refs)

    def take(n):
        return [next(it) for _ in range(n)]

    tokens, out_grad = take(2)
    narrow_shards = take(4)
    shards = [None] + take(2)
    vectors, column_biases = take(6), take(3)
    rows_out = take(2)
    owned_out = take(3)
    small_out = next(it)
    full = take(3)
    pack_all, vecs, cold = take(3)
    tok, og, lo, tg = take(4)
    (
        xn1, wqkv, wo, qs, ks, vs, o32, mixed, hid, xn2, ogf, act, ug, bg, dm, dqkv, tra, trb,
        wide, whole, ssend, srecv, dwd, small,
    ) = take(24)
    p_first = take(n_ctx)
    first_land, second_land, ctx_land = take(3), take(3), take(3)
    side_land, small_b, ctx_small, small_c, pair_small, small_d, dp_small = take(7)
    owned = take(3)
    small_e = next(it)
    (
        own_sem, put_sem, rows_sem, line_sem, pair_sem, dp_sem, diag_dp_sem, diag_pair_sem, swap_send,
        swap_recv, first_sem, second_sem, ctx_sem, out_line, out_pair, out_side, small_sem,
        side_sem, cross_pair, cross_dp,
    ) = take(20)
    partner = here.partner()
    own_row = d * n_ctx + z
    mine = p * n_ctx + z
    scale = HEAD_DIM ** -0.5
    first_head = lax.broadcasted_iota(jnp.int32, (1, lanes), 1) < HEAD_DIM
    zero16 = jnp.zeros((), BF16)
    side_rows = pl.ds(pl.multiple_of(c * half, half), half)
    far_side = pl.ds(pl.multiple_of((1 - c) * half, half), half)
    sends = Sends(put_sem)

    def arrive(slot, sem):
        remote(slot, slot, put_sem.at[0], sem, partner).wait_recv()

    def far_first():
        upper = z // two
        order = []
        for i in range(n_ctx - 1):
            down = n_ctx - 1 - i
            down = down - (z - down + n_ctx) // n_ctx
            up = i + (i - z + n_ctx) // n_ctx
            zz = upper * up + (1 - upper) * down
            order.append((zz, (d, zz, here.tp)))
        return order

    line_order = far_first()

    def flipped(h):
        zz = z + h - 2 * h * ((z // h) % 2)
        return zz, (d, zz, here.tp)

    strides = [1 << i for i in range(n_ctx.bit_length() - 1)]

    def shard_rows(r, count=1):
        return pl.ds(pl.multiple_of(r * share, 16), count * share)

    def slot(a, pp, dd, zz, count=1):
        return full[a].at[pp, shard_rows(dd * n_ctx + zz, count)]

    gather_own = [None] + [
        pltpu.make_async_copy(shards[a], slot(a, p, d, z), own_sem.at[a]) for a in (1, 2)
    ]

    def gather_give(a, h):
        device = flipped(h)[1]
        for i in range(n_ctx // (2 * h)):
            zz = (z + 2 * h * i) % n_ctx
            source = shards[a] if a > 0 and i == 0 else slot(a, p, d, zz)
            sends.go(source, slot(a, p, d, zz), line_sem.at[a, zz], device)

    def gather_take(a, h):
        q = flipped(h)[0]
        for i in range(n_ctx // (2 * h)):
            zz = (q + 2 * h * i) % n_ctx
            arrive(slot(a, p, d, zz), line_sem.at[a, zz])

    def gather_cross(a, first):
        for i in range(n_ctx // 2):
            zz = (first + 2 * i) % n_ctx
            piece = slot(a, p, d, zz)
            for k in range(1, n_pair):
                sends.go(piece, piece, cross_pair.at[a, p, zz], here.other_pair(k)[1])
            for k in range(1, n_dp):
                sends.go(piece, piece, cross_dp.at[a, d, zz], here.other_dp(k)[1])

    def gather_start(a):
        gather_give(a, strides[-1])

    def gather_next(a):
        for h in reversed(strides[:-1]):
            gather_take(a, 2 * h)
            gather_give(a, h)
        if a > 0:
            gather_own[a].wait()
        gather_cross(a, z)

    def gather_hop(a):
        gather_take(a, 1)
        gather_cross(a, flipped(1)[0])

    def gather_turn(a):
        for k in range(1, n_pair):
            pp = here.other_pair(k)[0]
            for zz in range(n_ctx):
                arrive(slot(a, pp, d, zz), cross_pair.at[a, pp, zz])
            first = slot(a, pp, d, 0, two)
            for j in range(1, n_dp):
                sends.go(first, first, diag_dp_sem.at[a, pp, d], here.other_dp(j)[1])
        for k in range(1, n_dp):
            dd = here.other_dp(k)[0]
            for zz in range(n_ctx):
                arrive(slot(a, p, dd, zz), cross_dp.at[a, dd, zz])
            second = slot(a, p, dd, two, n_ctx - two)
            for j in range(1, n_pair):
                sends.go(second, second, diag_pair_sem.at[a, p, dd], here.other_pair(j)[1])

    def gather_end(a):
        for k in range(1, n_pair):
            pp = here.other_pair(k)[0]
            for j in range(1, n_dp):
                dd = here.other_dp(j)[0]
                arrive(slot(a, pp, dd, 0, two), diag_dp_sem.at[a, pp, dd])
                arrive(slot(a, pp, dd, two, n_ctx - two), diag_pair_sem.at[a, pp, dd])

    def pack_start():
        own = pack_all.at[p, own_row]
        for zz, device in line_order:
            sends.go(own, own, line_sem.at[3, z], device)

    def pack_hop():
        for k in range(1, n_ctx):
            zz = here.other_ctx(k)[0]
            arrive(pack_all.at[p, d * n_ctx + zz], line_sem.at[3, zz])
        group = pack_all.at[p, pl.ds(d * n_ctx, n_ctx)]
        for k in range(1, n_pair):
            sends.go(group, group, pair_sem.at[3, p], here.other_pair(k)[1])
        for k in range(1, n_dp):
            sends.go(group, group, dp_sem.at[3, d], here.other_dp(k)[1])

    def pack_end():
        for k in range(1, n_pair):
            pp = here.other_pair(k)[0]
            arrive(pack_all.at[pp, pl.ds(d * n_ctx, n_ctx)], pair_sem.at[3, pp])
        for k in range(1, n_dp):
            dd = here.other_dp(k)[0]
            arrive(pack_all.at[p, pl.ds(dd * n_ctx, n_ctx)], dp_sem.at[3, dd])

    rows_own = [
        pltpu.make_async_copy(source.at[mine, side_rows], target.at[z], own_sem.at[4 + i])
        for i, (source, target) in enumerate(((tokens, tok), (out_grad, og)))
    ]

    def rows_start(i, source, target):
        for zz, device in line_order:
            sends.go(source.at[p * n_ctx + zz, side_rows], target.at[z], rows_sem.at[i, z], device)

    def grad_slot(ref, pp, dd, k):
        return ref.at[pp, shard_rows(dd * n_ctx + (z + k) % n_ctx)]

    def pair_leads(a, k):
        return a > 0 and near.index(k) % 2 == 0

    def scatter_start(a, ref, ks):
        for k in ks:
            if pair_leads(a, k):
                for j in range(1, n_pair):
                    pp, device = here.other_pair(j)
                    for i in range(n_dp):
                        sends.go(grad_slot(ref, pp, i, k), first_land[a].at[j - 1, i, k], first_sem.at[a, j - 1, i, k], device)
            else:
                for j in range(1, n_dp):
                    dd, device = here.other_dp(j)
                    for i in range(n_pair):
                        sends.go(grad_slot(ref, i, dd, k), first_land[a].at[j - 1, i, k], first_sem.at[a, j - 1, i, k], device)

    def add_into(target, parts):
        total = target[...].astype(F32)
        for part in parts:
            total = total + part[...].astype(F32)
        target[...] = total.astype(BF16)

    def scatter_turn(a, ref, ks):
        for k in ks:
            leads = pair_leads(a, k)
            n_lead, n_next = (n_pair, n_dp) if leads else (n_dp, n_pair)
            for i in range(n_next):
                parts = [first_land[a].at[j - 1, i, k] for j in range(1, n_lead)]
                for j in range(1, n_lead):
                    arrive(parts[j - 1], first_sem.at[a, j - 1, i, k])
                target = grad_slot(ref, p, i, k) if leads else grad_slot(ref, i, d, k)
                add_into(target, parts)
            for j in range(1, n_next):
                other, device = here.other_dp(j) if leads else here.other_pair(j)
                source = grad_slot(ref, p, other, k) if leads else grad_slot(ref, other, d, k)
                sends.go(source, second_land[a].at[j - 1, k], second_sem.at[a, j - 1, k], device)

    def scatter_line(a, ref, ks):
        for k in ks:
            n_next = n_dp if pair_leads(a, k) else n_pair
            parts = [second_land[a].at[j - 1, k] for j in range(1, n_next)]
            for j in range(1, n_next):
                arrive(parts[j - 1], second_sem.at[a, j - 1, k])
            add_into(grad_slot(ref, p, d, k), parts)
            if k % 2 == 1:
                scatter_give(a, ref, 1, k)

    def scatter_give(a, ref, h, k):
        zz, device = flipped(h)
        at = n_ctx - n_ctx // h + ((z + k - zz + n_ctx) % n_ctx) // (2 * h)
        sends.go(grad_slot(ref, p, d, k), ctx_land[a].at[at], ctx_sem.at[a, at], device)

    def scatter_across(a, ref):
        for h in strides[1:]:
            for i in range(n_ctx // h):
                at = n_ctx - 2 * n_ctx // h + i
                arrive(ctx_land[a].at[at], ctx_sem.at[a, at])
                add_into(grad_slot(ref, p, d, i * h), [ctx_land[a].at[at]])
            for k in range(h, n_ctx, 2 * h):
                scatter_give(a, ref, h, k)

    def scatter_end(a, ref):
        last = n_ctx - 2
        arrive(ctx_land[a].at[last], ctx_sem.at[a, last])
        owned[a][...] = ref[p, shard_rows(own_row), :].astype(F32) + ctx_land[a][last].astype(F32)
        pltpu.make_async_copy(owned[a], owned_out[a], own_sem.at[8 + a]).start()

    near = [k for h in strides for k in range(h, n_ctx, 2 * h)] + [0]
    early, late = near[:two], near[two:]
    others = list(range(1, n_ctx))

    def out_slot(i, s, rows):
        return rows_out[i].at[s, rows]

    def out_start(i, source):
        for zz, device in line_order:
            sends.go(source.at[zz], out_slot(i, mine, side_rows), out_line.at[i, z], device)
        copy = pltpu.make_async_copy(source.at[z], out_slot(i, mine, side_rows), own_sem.at[6 + i])
        copy.start()
        return copy

    def out_pass(i, s, source):
        piece = out_slot(i, s, side_rows)
        for j in range(1, n_pair):
            sends.go(source, piece, out_pair.at[i, s], here.other_pair(j)[1])
        sends.go(source, piece, out_side.at[i, s], partner)

    def out_hop(i, ks):
        for k in ks:
            s = p * n_ctx + here.other_ctx(k)[0]
            piece = out_slot(i, s, side_rows)
            arrive(piece, out_line.at[i, here.other_ctx(k)[0]])
            out_pass(i, s, piece)

    def out_cross(i):
        for j in range(1, n_pair):
            pp = here.other_pair(j)[0]
            for k in range(n_ctx):
                s = pp * n_ctx + (z + k) % n_ctx
                piece = out_slot(i, s, side_rows)
                arrive(piece, out_pair.at[i, s])
                sends.go(piece, piece, out_side.at[i, s], partner)

    def out_end(i):
        for s in range(n_pair * n_ctx):
            arrive(out_slot(i, s, far_side), out_side.at[i, s])

    def own_rows(b):
        return pl.ds(pl.multiple_of(b * block + c * half, half), half)

    def far_rows(b):
        return pl.ds(pl.multiple_of(b * block + (1 - c) * half, half), half)

    def block_rows(b):
        return pl.ds(pl.multiple_of(b * block, block), block)

    def swap(stage, b, src, dst):
        return remote(src, dst, swap_send.at[stage, b], swap_recv.at[stage, b], partner)

    def rows_copy(stage, b, ref):
        return swap(stage, b, ref.at[own_rows(b)], ref.at[own_rows(b)])

    def rows_arrive(stage, b, ref):
        swap(stage, b, ref.at[far_rows(b)], ref.at[far_rows(b)]).wait_recv()

    def part_copy(stage, place, b):
        return swap(stage, b, ssend.at[place, b], srecv.at[place, b])

    def part_store(i, b, value):
        wide[i, pl.ds(pl.multiple_of(b * block, block), half), :] = value[:, :hw]
        wide[i, pl.ds(pl.multiple_of(b * block + half, half), half), :] = value[:, hw:]

    def part_load(i, b):
        left = wide[i, pl.ds(pl.multiple_of(b * block, block), half), :]
        right = wide[i, pl.ds(pl.multiple_of(b * block + half, half), half), :]
        return jnp.concatenate([left, right], axis=1)

    rows_own[0].start()
    rows_own[1].start()
    gather_own[1].start()
    gather_own[2].start()
    for a in range(4):
        full[0][p, shard_rows(own_row), a * cols : (a + 1) * cols] = narrow_shards[a][...]
    own_pack = pack_all.at[p, own_row]
    own_pack[...] = jnp.zeros(own_pack.shape, F32)
    for i in range(6):
        own_pack[i : i + 1, :share] = vectors[i][...].astype(F32)
    row = 6
    for ref in column_biases:
        n = ref.shape[0]
        line = ref[...].astype(F32).reshape(1, n)
        for w in range(0, n, 128):
            m = min(128, n - w)
            own_pack[row : row + 1, :m] = line[:, w : w + m]
            row += 1
    small[...] = jnp.zeros_like(small)
    here.barrier(True)
    pack_start()
    gather_start(0)
    gather_next(0)
    gather_start(1)
    pack_hop()
    pack_end()
    for r in range(n_rows):
        own_part = pack_all[p, r]
        vecs[0:8, r * share : (r + 1) * share] = own_part[0:8, :share]
    for i in range(n_pair):
        piece = pack_all[i, d * n_ctx]
        for line in range(2):
            for w in range(0, cols, 128):
                n = min(128, cols - w)
                row = 6 + 2 * line + w // 128
                cold[line : line + 1, i * cols + w : i * cols + w + n] = piece[row : row + 1, :n]
        for w in range(0, fw, 128):
            row = 10 + w // 128
            cold[2 + i : 3 + i, w : w + 128] = piece[row : row + 1, :]
    gain_one, shift_one, out_shift = vecs[0:1, :], vecs[1:2, :], vecs[2:3, :]
    gain_two, shift_two, down_shift = vecs[3:4, :], vecs[4:5, :], vecs[5:6, :]

    def norm_one(b):
        scaled, _ = normalize(tok[b].astype(F32))
        xn1[own_rows(b), :] = (scaled * gain_one + shift_one).astype(BF16)
        rows_copy(1, b, xn1).start()

    rows_own[0].wait()
    norm_one(z)
    gather_hop(0)
    gather_next(1)
    pl.semaphore_signal(side_sem, inc=1, device_id=partner, device_id_type=MESH)
    pl.semaphore_wait(side_sem, 1)
    rows_start(0, tokens, tok)
    gather_start(2)
    gather_turn(0)
    gather_hop(1)
    for k in range(1, n_ctx):
        b = here.other_ctx(k)[0]
        arrive(tok.at[b], rows_sem.at[0, b])
        norm_one(b)
    gather_end(0)
    for i in range(n_pair):
        for a, base in enumerate((0, hw, 2 * hw)):
            wqkv[:, base + i * cols : base + (i + 1) * cols] = full[0][i, :, a * cols : (a + 1) * cols]
        wo[:, i * cols : (i + 1) * cols] = full[0][i, :, 3 * cols : 4 * cols]
    q_shift, v_shift = cold[0:1, :hw], cold[1:2, :hw]

    @pl.loop(0, n_ctx)
    def _(b):
        rows_arrive(1, b, xn1)
        product = nn_dot(xn1[block_rows(b), :], wqkv[...])
        qs[block_rows(b), :] = (product[:, :hw] + q_shift).astype(BF16) * jnp.asarray(scale, BF16)
        ks[block_rows(b), :] = product[:, hw : 2 * hw].astype(BF16)
        vs[block_rows(b), :] = (product[:, 2 * hw :] + v_shift).astype(BF16)

    gather_next(2)

    for b in range(n_ctx):
        reach = (b + 1) * block
        here_rows = slice(b * block, (b + 1) * block)

        @pl.loop(0, n_twos)
        def _(j):
            at = pl.ds(pl.multiple_of(j * lanes, lanes), lanes)
            queries, keys, values = qs[here_rows, at], ks[:reach, at], vs[:reach, at]
            pieces = []
            for e in range(2):
                head = first_head if e == 0 else jnp.logical_not(first_head)
                scores = nt_dot(jnp.where(head, queries, zero16), keys)
                powers = jnp.exp(scores - jnp.max(scores, axis=-1, keepdims=True))
                inverse = 1.0 / jnp.sum(powers, axis=-1, keepdims=True)
                probs = (powers * inverse).astype(BF16)
                p_first[b][2 * j + e] = probs
                pieces.append(nn_dot(probs, values))
            out = jnp.where(first_head, pieces[0], pieces[1])
            o32[here_rows, at] = out
            mixed[here_rows, at] = out.astype(BF16)

        whole[b % 2] = nt_dot(mixed[here_rows, :], wo[...])
        ssend[0, b] = whole[b % 2, far_side, :].astype(BF16)
        part_copy(2, 0, b).start()
        hid[b] = whole[b % 2, side_rows, :]
        if b == 0:
            gather_turn(1)
        if b == 1:
            rows_start(1, out_grad, og)
        if b == 2:
            gather_hop(2)

    @pl.loop(0, n_ctx)
    def _(b):
        part_copy(2, 0, b).wait()
        hidden = tok[b].astype(F32) + (hid[b] + srecv[0, b].astype(F32)) + out_shift
        hid[b] = hidden
        scaled, _ = normalize(hidden)
        xn2[own_rows(b), :] = (scaled * gain_two + shift_two).astype(BF16)
        rows_copy(3, b, xn2).start()

    gather_end(1)

    @pl.loop(0, n_ctx)
    def _(b):
        rows_arrive(3, b, xn2)
        normed = xn2[block_rows(b), :]
        for i in range(n_pair):
            upward = nn_dot(normed, full[1][i]) + cold[2 + i : 3 + i, :fw]
            big_phi = 0.5 + 0.5 * lax.erf(upward * root_half)
            act[i, block_rows(b), :] = (upward * big_phi).astype(BF16)
            slope = big_phi + upward * density_scale * jnp.exp(-0.5 * upward * upward)
            ug[i, block_rows(b), :] = slope.astype(BF16)

    rows_own[1].wait()
    for k in range(n_ctx):
        b = (z + k) % n_ctx
        if k > 0:
            arrive(og.at[b], rows_sem.at[1, b])
        swap(0, b, og.at[b], ogf.at[own_rows(b)]).start()
        ogf[own_rows(b), :] = og[b]
    for b in range(n_ctx):
        rows_arrive(0, b, ogf)

    step = 256

    def transposed(ref, out):
        for b in range(n_ctx):
            out[:, b * block : (b + 1) * block] = ref[b * block : (b + 1) * block, :].T

    gather_turn(2)
    gathered = len(sends.started)
    transposed(ogf, trb)

    @pl.loop(0, width // step)
    def _(r):
        rows = pl.ds(pl.multiple_of(r * step, step), step)
        for i in range(n_pair):
            dwd[i, rows, :] = nn_dot(trb[rows, :], act[i]).astype(BF16)

    scatter_start(2, dwd, near)

    def slope_back(i, b):
        slope = ug[i, block_rows(b), :].astype(F32)
        rows_grad = (nn_dot(ogf[block_rows(b), :], full[2][i]) * slope).astype(BF16)
        ug[i, block_rows(b), :] = rows_grad
        small[pl.ds(8 + i, 1), :] += jnp.sum(rows_grad.astype(F32), axis=0, keepdims=True)

    @pl.loop(0, n_ctx)
    def _(b):
        slope_back(p, b)

    gather_end(2)

    def through(ref, weight, rows):
        total = nt_dot(ref[0, rows, :], weight[0])
        for i in range(1, n_pair):
            total = total + nt_dot(ref[i, rows, :], weight[i])
        return total

    def units_back(b):
        for k in range(1, n_pair):
            slope_back(here.other_pair(k)[0], b)
        whole[0] = through(ug, full[1], block_rows(b))
        ssend[0, b] = whole[0, far_side, :].astype(BF16)
        part_copy(5, 0, b).start()
        part_store(1, b, whole[0, side_rows, :])
        whole[1] = through(act, full[2], block_rows(b))
        ssend[1, b] = whole[1, far_side, :].astype(BF16)
        part_copy(4, 1, b).start()
        part_store(0, b, whole[1, side_rows, :])

    pl.loop(0, two)(units_back)
    scatter_turn(2, dwd, early)
    pl.loop(two, n_ctx)(units_back)
    transposed(xn2, tra)
    scatter_turn(2, dwd, late)
    for copy in sends.started[:gathered]:
        copy.wait_send()

    @pl.loop(0, width // step)
    def _(r):
        rows = pl.ds(pl.multiple_of(r * step, step), step)
        for i in range(n_pair):
            full[1][i, rows, :] = nn_dot(tra[rows, :], ug[i]).astype(BF16)

    scatter_start(1, full[1], near)
    scatter_line(2, dwd, early)

    @pl.loop(0, n_ctx)
    def _(b):
        part_copy(5, 0, b).wait()
        grad_two = part_load(1, b) + srecv[0, b].astype(F32)
        part_copy(4, 1, b).wait()
        lo[b] = (hid[b] + (part_load(0, b) + srecv[1, b].astype(F32)) + down_shift).astype(BF16)
        scaled, spread = normalize(hid[b])
        own_grad = og[b].astype(F32)
        hidden_grad = own_grad + norm_back(grad_two * gain_two, scaled, spread)
        hid[b] = hidden_grad
        branch = hidden_grad.astype(BF16)
        bg[own_rows(b), :] = branch
        rows_copy(6, b, bg).start()
        small[2:3, :] += jnp.sum(branch.astype(F32), axis=0, keepdims=True)
        small[3:4, :] += jnp.sum(grad_two * scaled, axis=0, keepdims=True)
        small[4:5, :] += jnp.sum(grad_two, axis=0, keepdims=True)
        small[5:6, :] += jnp.sum(own_grad, axis=0, keepdims=True)

    lo_copy = out_start(0, lo)
    out_pass(0, mine, lo.at[z])

    @pl.loop(0, n_ctx)
    def _(b):
        rows_arrive(6, b, bg)
        dm[block_rows(b), :] = nn_dot(bg[block_rows(b), :], wo[...]).astype(BF16)

    scatter_line(2, dwd, late)
    transposed(bg, trb)

    @pl.loop(0, width // step)
    def _(r):
        rows = pl.ds(pl.multiple_of(r * step, step), step)
        product = nn_dot(trb[rows, :], mixed[...])
        for i in range(n_pair):
            full[0][i, rows, 3 * cols : 4 * cols] = product[:, i * cols : (i + 1) * cols].astype(BF16)

    for b in reversed(range(n_ctx)):
        reach = (b + 1) * block
        here_rows = slice(b * block, (b + 1) * block)

        @pl.loop(0, n_twos)
        def _(j):
            at = pl.ds(pl.multiple_of(j * lanes, lanes), lanes)
            queries, keys, values = qs[here_rows, at], ks[:reach, at], vs[:reach, at]
            mix_grad, mix = dm[here_rows, at], o32[here_rows, at]
            towards = mix_grad.astype(F32) * mix
            query_parts, key_sum, value_sum = [], None, None
            for e in range(2):
                head = first_head if e == 0 else jnp.logical_not(first_head)
                grad_head = jnp.where(head, mix_grad, zero16)
                prob_grad = nt_dot(grad_head, values)
                centre = jnp.sum(jnp.where(head, towards, 0.0), axis=-1, keepdims=True)
                probs = p_first[b][2 * j + e]
                score_grad = (probs.astype(F32) * (prob_grad - centre)).astype(BF16)
                query_parts.append(nn_dot(score_grad, keys))
                key_term = tn_dot(score_grad, jnp.where(head, queries, zero16))
                value_term = tn_dot(probs, grad_head)
                key_sum = key_term if key_sum is None else key_sum + key_term
                value_sum = value_term if value_sum is None else value_sum + value_term
            query_grad = jnp.where(first_head, query_parts[0], query_parts[1]) * scale
            dqkv[here_rows, at] = query_grad.astype(BF16)
            if b == n_ctx - 1:
                wide[0, :, at] = key_sum
                wide[1, :, at] = value_sum
            else:
                wide[0, :reach, at] += key_sum
                wide[1, :reach, at] += value_sum

        if b == 1:
            scatter_turn(1, full[1], near)
        if b == 0:
            out_hop(0, others)

    @pl.loop(0, n_ctx)
    def _(b):
        dqkv[block_rows(b), hw : 2 * hw] = wide[0, block_rows(b), :].astype(BF16)
        dqkv[block_rows(b), 2 * hw :] = wide[1, block_rows(b), :].astype(BF16)
        small[6:7, :hw] += jnp.sum(dqkv[block_rows(b), :hw].astype(F32), axis=0, keepdims=True)
        small[7:8, :hw] += jnp.sum(dqkv[block_rows(b), 2 * hw :].astype(F32), axis=0, keepdims=True)
        whole[0] = nt_dot(dqkv[block_rows(b), :], wqkv[...])
        ssend[1, b] = whole[0, far_side, :].astype(BF16)
        part_copy(7, 1, b).start()
        part_store(0, b, whole[0, side_rows, :])

    transposed(xn1, tra)

    @pl.loop(0, width // step)
    def _(r):
        rows = pl.ds(pl.multiple_of(r * step, step), step)
        product = nn_dot(tra[rows, :], dqkv[...])
        for i in range(n_pair):
            for a in range(3):
                full[0][i, rows, a * cols : (a + 1) * cols] = product[
                    :, a * hw + i * cols : a * hw + (i + 1) * cols
                ].astype(BF16)

    scatter_start(0, full[0], near)

    @pl.loop(0, n_ctx)
    def _(b):
        part_copy(7, 1, b).wait()
        grad_one = part_load(0, b) + srecv[1, b].astype(F32)
        scaled, spread = normalize(tok[b].astype(F32))
        tg[b] = (hid[b] + norm_back(grad_one * gain_one, scaled, spread)).astype(BF16)
        small[0:1, :] += jnp.sum(grad_one * scaled, axis=0, keepdims=True)
        small[1:2, :] += jnp.sum(grad_one, axis=0, keepdims=True)

    sends.go(small.at[pl.ds(0, 8)], side_land, small_sem.at[0, 0], partner)
    tg_copy = out_start(1, tg)
    out_pass(1, mine, tg.at[z])
    scatter_line(1, full[1], near)
    scatter_across(2, dwd)
    arrive(side_land, small_sem.at[0, 0])
    small_b[0:6, :] = small[0:6, :] + side_land[0:6, :]
    small_b[6:16, :] = small[6:16, :]
    for k in range(1, n_pair):
        sends.go(small_b, pair_small.at[k - 1], small_sem.at[2, k - 1], here.other_pair(k)[1])
    scatter_turn(0, full[0], early)
    out_cross(0)
    out_hop(1, others[:1])
    scatter_line(0, full[0], early)
    scatter_turn(0, full[0], late)
    out_hop(1, others[1:])
    scatter_across(1, full[1])
    total = small_b[...]
    for k in range(1, n_pair):
        arrive(pair_small.at[k - 1], small_sem.at[2, k - 1])
        total = total + pair_small[k - 1]
    small_c[...] = total
    for k in range(1, n_dp):
        sends.go(small_c, dp_small.at[k - 1], small_sem.at[3, k - 1], here.other_dp(k)[1])
    scatter_line(0, full[0], late)
    scatter_across(0, full[0])
    total = small_c[...]
    for k in range(1, n_dp):
        arrive(dp_small.at[k - 1], small_sem.at[3, k - 1])
        total = total + dp_small[k - 1]
    small_d[...] = total
    for k in range(1, n_ctx):
        sends.go(small_d, ctx_small.at[k - 1], small_sem.at[1, k - 1], here.other_ctx(k)[1])
    out_cross(1)
    scatter_end(2, dwd)
    scatter_end(1, full[1])
    out_end(0)
    scatter_end(0, full[0])
    total = small_d[...]
    for k in range(1, n_ctx):
        arrive(ctx_small.at[k - 1], small_sem.at[1, k - 1])
        total = total + ctx_small[k - 1]
    small_e[...] = total
    small_copy = pltpu.make_async_copy(small_e, small_out, own_sem.at[11])
    small_copy.start()
    out_end(1)
    lo_copy.wait()
    tg_copy.wait()
    small_copy.wait()
    for a in range(3):
        pltpu.make_async_copy(owned[a], owned_out[a], own_sem.at[8 + a]).wait()

    @pl.loop(0, n_ctx)
    def _(b):
        swap(0, b, og.at[b], ogf.at[own_rows(b)]).wait_send()
        rows_copy(1, b, xn1).wait_send()
        rows_copy(3, b, xn2).wait_send()
        rows_copy(6, b, bg).wait_send()

    for copy in sends.started[gathered:]:
        copy.wait_send()


def fused_call(sizes, tokens, out_grad, shards, vectors, column_biases):
    n_dp, n_ctx, n_tp = sizes
    n_pair = n_tp // 2
    seqs, block, width = tokens.shape
    half = block // 2
    length = n_ctx * block
    share, cols = shards[0].shape
    fw = shards[4].shape[1]
    widths = [4 * cols, fw, fw]
    hw = n_pair * cols
    heads = hw // HEAD_DIM
    two = n_ctx // 2
    any_spec = pl.BlockSpec(memory_space=pl.ANY)
    vmem_spec = pl.BlockSpec(memory_space=pltpu.VMEM)
    shape = jax.ShapeDtypeStruct
    vm = pltpu.VMEM
    dma = pltpu.SemaphoreType.DMA
    out_shape = [shape(tokens.shape, BF16)] * 2
    out_shape += [shape((share, w), F32) for w in widths]
    out_shape += [shape((16, width), F32)]
    scratch = [vm((n_pair, width, w), BF16) for w in widths]
    scratch += [
        vm((n_pair, n_dp * n_ctx, 16, 128), F32),
        vm((8, width), F32),
        vm((8, width), F32),
    ]
    scratch += [vm((n_ctx, half, width), BF16)] * 4
    scratch += [
        vm((length, width), BF16),
        vm((width, 3 * hw), BF16),
        vm((width, hw), BF16),
        vm((length, hw), BF16),
        vm((length, hw), BF16),
        vm((length, hw), BF16),
        vm((length, hw), F32),
        vm((length, hw), BF16),
        vm((n_ctx, half, width), F32),
        vm((length, width), BF16),
        vm((length, width), BF16),
        vm((n_pair, length, fw), BF16),
        vm((n_pair, length, fw), BF16),
        vm((length, width), BF16),
        vm((length, hw), BF16),
        vm((length, 3 * hw), BF16),
        vm((width, length), BF16),
        vm((width, length), BF16),
        vm((2, length, hw), F32),
        vm((2, block, width), F32),
        vm((2, n_ctx, half, width), BF16),
        vm((2, n_ctx, half, width), BF16),
        vm((n_pair, width, fw), BF16),
        vm((16, width), F32),
    ]
    scratch += [vm((heads, block, (b + 1) * block), BF16) for b in range(n_ctx)]
    lead, after = max(n_dp, n_pair) - 1, max(n_dp, n_pair)
    scratch += [vm((lead, after, n_ctx, share, w), BF16) for w in widths]
    scratch += [vm((lead, n_ctx, share, w), BF16) for w in widths]
    scratch += [vm((n_ctx - 1, share, w), BF16) for w in widths]
    scratch += [
        vm((8, width), F32),
        vm((16, width), F32),
        vm((n_ctx - 1, 16, width), F32),
        vm((16, width), F32),
        vm((n_pair - 1, 16, width), F32),
        vm((16, width), F32),
        vm((n_dp - 1, 16, width), F32),
    ]
    scratch += [vm((share, w), F32) for w in widths]
    scratch += [vm((16, width), F32)]
    most = max(n_dp, n_ctx, n_pair)
    scratch += [
        dma((12,)),
        dma((300,)),
        dma((2, n_ctx)),
        dma((4, n_ctx)),
        dma((4, n_pair)),
        dma((4, n_dp)),
        dma((3, n_pair, n_dp)),
        dma((3, n_pair, n_dp)),
        dma((8, n_ctx)),
        dma((8, n_ctx)),
        dma((3, lead, after, n_ctx)),
        dma((3, lead, n_ctx)),
        dma((3, n_ctx)),
        dma((2, n_ctx)),
        dma((2, seqs)),
        dma((2, seqs)),
        dma((4, most)),
        pltpu.SemaphoreType.REGULAR,
        dma((3, n_pair, n_ctx)),
        dma((3, n_dp, n_ctx)),
    ]
    return pl.pallas_call(
        functools.partial(fused_body, sizes, (half, width, share, cols, fw)),
        out_shape=out_shape,
        in_specs=[any_spec] * 2 + [vmem_spec] * 4 + [any_spec] * 2 + [vmem_spec] * 9,
        out_specs=[any_spec] * 6,
        scratch_shapes=scratch,
        compiler_params=pltpu.CompilerParams(
            collective_id=3, has_side_effects=True, vmem_limit_bytes=67043328
        ),
    )(tokens, out_grad, *shards, *vectors, *column_biases)


def finish_body(n_ctx, share, cols, *refs):
    lo_in, tg_in, attn_in, up_in, down_in, small_in = refs[:6]
    lo, tg, dq, dk, dv, do, du, dd = refs[6:14]
    vectors = refs[14:20]
    shifts = refs[20:22]
    up_shift = refs[22]
    lo_held, tg_held, tg_wide, attn, up, down, small = refs[23:30]
    narrow = refs[30:34]
    in_sem, out_sem, more_in, more_out = refs[34:]
    row = lax.axis_index("dp") * n_ctx + lax.axis_index("ctx")
    pair = lax.axis_index("tp") // 2
    width = small.shape[1]
    seqs = lo_held.shape[0]
    move = pltpu.make_async_copy

    def rows_in(i, s):
        source, held = ((tg_in, tg_held), (lo_in, lo_held))[i]
        return move(source.at[s], held.at[s], in_sem.at[i, s])

    def rows_out(i, s):
        held, target = ((tg_wide, tg), (lo_held, lo))[i]
        return move(held.at[s], target.at[s], out_sem.at[i, s])

    takes = [
        move(source, held, more_in.at[i])
        for i, (source, held) in enumerate(((up_in, up), (down_in, down), (attn_in, attn), (small_in, small)))
    ]
    gives = [
        move(held, target, more_out.at[i])
        for i, (held, target) in enumerate(zip((up, down, *narrow), (du, dd, dq, dk, dv, do)))
    ]

    @pl.loop(0, seqs)
    def _(s):
        rows_in(0, s).start()
        rows_in(1, s).start()

    for copy in takes:
        copy.start()

    @pl.loop(0, seqs)
    def _(s):
        rows_in(0, s).wait()
        tg_wide[s] = tg_held[s].astype(F32)
        rows_out(0, s).start()
        rows_in(1, s).wait()
        rows_out(1, s).start()

    for i in range(2):
        takes[i].wait()
        gives[i].start()
    takes[2].wait()
    for i, ref in enumerate(narrow):
        ref[...] = attn[:, i * cols : (i + 1) * cols]
        gives[2 + i].start()
    takes[3].wait()
    turned = pltpu.roll(small[0:8, :], (width - row * share) % width, 1)
    for i, ref in enumerate(vectors):
        ref[...] = turned[i : i + 1, :share]
    turned = pltpu.roll(small[0:8, :], (width - pair * cols) % width, 1)
    for i, ref in enumerate(shifts):
        ref[...] = turned[6 + i : 7 + i, :cols]
    row_of = small[pl.ds(8 + pair, 1), :]
    for i in range(up_shift.shape[0]):
        up_shift[i : i + 1, :] = row_of[:, i * 128 : (i + 1) * 128]

    @pl.loop(0, seqs)
    def _(s):
        rows_out(0, s).wait()
        rows_out(1, s).wait()

    for copy in gives:
        copy.wait()


def finish_call(sizes, cols, lo, tg, attn, up, down, small):
    n_dp, n_ctx, n_tp = sizes
    seqs, block, width = lo.shape
    share = attn.shape[0]
    shape = jax.ShapeDtypeStruct
    any_spec = pl.BlockSpec(memory_space=pl.ANY)
    vmem_spec = pl.BlockSpec(memory_space=pltpu.VMEM)
    vm = pltpu.VMEM
    dma = pltpu.SemaphoreType.DMA
    out_tail = [(share, cols)] * 4 + [up.shape] * 2 + [(1, share)] * 6 + [(1, cols)] * 2 + [(up.shape[1] // 128, 128)]
    return pl.pallas_call(
        functools.partial(finish_body, n_ctx, share, cols),
        out_shape=[shape(lo.shape, BF16), shape(lo.shape, F32)] + [shape(s, F32) for s in out_tail],
        in_specs=[any_spec] * 6,
        out_specs=[any_spec] * 8 + [vmem_spec] * 9,
        scratch_shapes=[
            vm(lo.shape, BF16),
            vm(lo.shape, BF16),
            vm(lo.shape, F32),
            vm(attn.shape, F32),
            vm(up.shape, F32),
            vm(down.shape, F32),
            vm(small.shape, F32),
        ]
        + [vm((share, cols), F32)] * 4
        + [dma((2, seqs)), dma((2, seqs)), dma((4,)), dma((6,))],
    )(lo, tg, attn, up, down, small)


def fused_layer(sizes, tokens, out_grad, shards, vectors, column_biases):
    cols = shards[0].shape[1]
    lines = [v.reshape(1, -1) for v in vectors]
    results = fused_call(sizes, tokens, out_grad, shards, lines, column_biases)
    final = finish_call(sizes, cols, *results)
    return (*final[:8], *[v.reshape(-1) for v in final[8:]])


def per_device(
    tokens,
    out_grad,
    query_weight,
    key_weight,
    value_weight,
    output_weight,
    up_weight,
    down_weight,
    norm1_gain,
    norm1_bias,
    output_bias,
    norm2_gain,
    norm2_bias,
    down_bias,
    query_bias,
    value_bias,
    up_bias,
):
    sizes = (lax.axis_size("dp"), lax.axis_size("ctx"), lax.axis_size("tp"))
    n_dp, n_ctx, n_tp = sizes
    n_pair = n_tp // 2
    seqs, block, width = tokens.shape
    assert seqs == n_ctx * n_pair
    share = norm1_gain.shape[0]
    cols = query_bias.shape[0]
    pair = lax.axis_index("tp") // 2
    row = lax.axis_index("dp") * n_ctx + lax.axis_index("ctx")
    shards = (query_weight, key_weight, value_weight, output_weight, up_weight, down_weight)
    vectors = (norm1_gain, norm1_bias, output_bias, norm2_gain, norm2_bias, down_bias)
    if share % 16 == 0 and n_ctx % 4 == 0 and n_ctx & (n_ctx - 1) == 0:
        return fused_layer(
            sizes, tokens, out_grad, shards, vectors, (query_bias, value_bias, up_bias)
        )

    six = jnp.stack(vectors).astype(F32)
    vec = jnp.pad(six, ((0, 2), (0, 128 - share)))
    columns = jnp.arange(width) // cols == pair
    narrow = [jnp.where(columns, jnp.tile(b.astype(F32), width // cols), 0.0) for b in (query_bias, value_bias)]
    bias = jnp.pad(jnp.stack(narrow + [up_bias.astype(F32)]), ((0, 5), (0, 0)))

    gathered = gather_call(sizes, tokens, out_grad, shards, vec, bias)
    tok, og = gathered[0:2]
    weights = [w.reshape(n_pair, width, w.shape[3]) for w in gathered[2:8]]
    vecs = gathered[8][:, :, :share].transpose(1, 0, 2).reshape(8, width)
    results = compute_call(sizes, tok, og, weights, vecs, gathered[9])
    lo, tg = results[0:2]
    grads = [
        g.reshape(n_pair, n_dp * n_ctx, s.shape[0], s.shape[1]) for g, s in zip(results[2:8], shards)
    ]
    final = scatter_call(sizes, seqs, lo, tg, grads, results[8])
    layer_out, tokens_grad = final[0], final[1].astype(F32)
    small = final[8]
    owned = [lax.dynamic_slice_in_dim(small[i], row * share, share) for i in range(6)]
    shifts = [lax.dynamic_slice_in_dim(small[6 + i], pair * cols, cols) for i in range(2)]
    up_total = lax.dynamic_index_in_dim(small[8 : 8 + n_pair], pair, 0, keepdims=False)
    return (layer_out, tokens_grad, *final[2:8], *owned, *shifts, up_total)


def solution(mesh):
    rows_spec = P("dp", "ctx", None)
    weight_spec = P(("dp", "ctx"), "tp")
    vector_spec = P(("dp", "ctx"))
    column_spec = P("tp")
    common = (rows_spec,) * 2 + (weight_spec,) * 6 + (vector_spec,) * 6 + (column_spec,) * 3
    return jax.shard_map(
        per_device, mesh=mesh, in_specs=common, out_specs=common, check_vma=False
    )
```
